32 devices in a mesh: tile: 16 (over z, x, core), mem: 2 (over y).
Axes of the slice: x: 2, y: 2, z: 4, core: 2. Of those that a mesh axis runs over, the one named last changes fastest.
Arguments:
- atm_latent: bfloat16 [2, 8192, 256], P('mem', 'tile'), may hold values from -6 to 6
- ocean_state: bfloat16 [2, 8, 8192, 256], P('mem', None, 'tile'), may hold values from -6 to 6
- depth: int32 [8192], P('tile'), may hold values from 0 to 8
- src_blocks: int32 [64, 4], P('tile'), may hold values from 0 to 63, as said below
- live: int32 [64], P('tile'), may hold values from 2 to 4
- remap_weight: bfloat16 [64, 4, 128, 128], P('tile'), may hold values from -0.25 to 0.25
- conv_weight: bfloat16 [3, 3, 256, 256], replicated, may hold values from -0.125 to 0.125
- qkv_weight: bfloat16 [256, 768], replicated, may hold values from -5 to 5
- out_weight: bfloat16 [256, 256], replicated, may hold values from -0.375 to 0.375
Outputs:
- ocean_out: bfloat16 [2, 8, 8192, 256], P('mem', None, 'tile')
The draws below stay inside these ranges and needn't reach their ends.
Inputs may be any that keep to these rules, and one draw needn't show every extreme that they name: `src_blocks`: the owner tile of a listed atmosphere block (block // 4) lies within 1 tile indices of the tile owning the ocean block (ocean block // 4); some entry of every tile lies exactly 1 away.
All inputs are finite; a program needn't handle non-finite values.
Results may differ from the reference program's by a relative error of at most 0.0055.
Values may be sent and summed in bfloat16 or wider, within the bound.
No kernel may reach another device: no remote copies, remote signals or barrier semaphores. Data moves between devices by JAX's collectives and lax.ppermute only.
A program may use at most 128 MiB of HBM per device.

```python
import math
import jax
import jax.numpy as jnp
from jax import lax

C = 256
HEADS = 4
HD = 64
LEV = 8
OCOLS = 128
OROWS = 4
ATM_BLK = 4
NPAIR = 4
R = 1
ATMS = 8192
NOROWS = 64
OCELLS = 8192
MEMBERS = 2


def draw_src_blocks(key, part):
    ntile = NOROWS // OROWS
    rows_all = jnp.arange(NOROWS, dtype=jnp.int32)
    owner = rows_all // OROWS
    local_row = rows_all % OROWS
    jitter = jax.random.randint(jax.random.fold_in(key, 11), (NOROWS,), -1, 2, dtype=jnp.int32)
    start = owner * ATM_BLK + local_row * ATM_BLK // OROWS + jitter
    ids = start[:, None] + jnp.arange(NPAIR, dtype=jnp.int32)[None, :]
    lowest = jnp.maximum(owner - R, 0) * ATM_BLK
    highest = jnp.minimum(owner + R, ntile - 1) * ATM_BLK + ATM_BLK - 1
    ids = jnp.clip(ids, lowest[:, None], highest[:, None])
    reach = jnp.where(owner >= R, (owner - R) * ATM_BLK + ATM_BLK - 1, (owner + R) * ATM_BLK)
    ids = ids.at[:, 0].set(jnp.where(local_row == 0, reach, ids[:, 0]))
    return ids.astype(jnp.int32)


def draw_qkv_weight(key, part):
    base_key = jax.random.fold_in(key, 23)
    values = jnp.clip(jax.random.normal(base_key, (C, 3 * C), jnp.float32), -4.0, 4.0) * C ** (-0.5)
    return values.astype(jnp.bfloat16)


def with_ends(result, stream_key, smallest, top_value):
    shape = result.shape
    place = [jax.random.randint(jax.random.fold_in(stream_key, axis), (), 0, shape[axis]) for axis in range(len(shape))]
    result = result.at[tuple(place)].set(smallest)
    longest = shape.index(max(shape))
    place[longest] = (place[longest] + 1) % shape[longest]
    return result.at[tuple(place)].set(top_value)


def level_of(stream_key, dims, pieces, smallest, high):
    loudness, own = 1.0, jax.random.fold_in(stream_key, 6)
    for position, blocks in pieces:
        steps = jnp.exp(jax.random.uniform(jax.random.fold_in(own, position), (blocks,), jnp.float32, smallest / len(pieces), high / len(pieces)))
        loudness = loudness * jnp.repeat(steps, dims[position] // blocks).reshape([-1 if axis == position else 1 for axis in range(len(dims))])
    return loudness


def gaussian(own_key, shape, scale, most, split=(), held_as=jnp.bfloat16):
    level = level_of(own_key, shape, split, -0.22, 0.18) if split else 1.0
    values = jax.random.normal(own_key, shape, jnp.float32) * scale * level
    return jnp.minimum(jnp.maximum(values, -most), most).astype(held_as)


def setup_inputs(seed: int = 0) -> dict:
    seeds = jax.random.split(jax.random.key(seed), 10)
    return {
        "atm_latent": gaussian(seeds[0], (MEMBERS, ATMS, C), 1.0, 6.0, ((0, 2), (1, 16))),
        "ocean_state": gaussian(seeds[1], (MEMBERS, LEV, OCELLS, C), 1.0, 6.0, ((0, 2), (2, 16))),
        "depth": with_ends(jax.random.randint(seeds[2], (OCELLS,), 0, LEV + 1), jax.random.fold_in(seeds[2], 1), 0, LEV).astype(jnp.int32),
        "src_blocks": draw_src_blocks(jax.random.fold_in(seeds[9], 71), 0),
        "live": with_ends(jax.random.randint(seeds[4], (NOROWS,), 2, NPAIR + 1), jax.random.fold_in(seeds[4], 1), 2, NPAIR).astype(jnp.int32),
        "remap_weight": gaussian(seeds[5], (NOROWS, NPAIR, OCOLS, OCOLS), (OCOLS * NPAIR) ** -0.5, 0.25, ((0, 16),)),
        "conv_weight": gaussian(seeds[6], (3, 3, C, C), (9 * C) ** -0.5, 0.125),
        "qkv_weight": draw_qkv_weight(jax.random.fold_in(seeds[9], 71), 0),
        "out_weight": gaussian(seeds[8], (C, C), C ** -0.5, 0.375),
    }


EPS = 1e-06

def attend_block(block, wet_block, qkv_weight, out_weight):
    mem_n, lev, count, width = block.shape
    xf = block.astype(jnp.float32)
    normed = (xf * lax.rsqrt(lax.optimization_barrier(jnp.mean(xf * xf, axis=-1, keepdims=True)) + EPS)).astype(jnp.bfloat16)
    qkv = jnp.dot(normed.reshape(-1, width), qkv_weight, preferred_element_type=jnp.float32).astype(jnp.bfloat16)
    qkv = qkv.reshape(mem_n * lev, count, 3, HEADS, HD)
    query = qkv[:, :, 0].astype(jnp.float32)
    keys = qkv[:, :, 1].astype(jnp.float32)
    values = qkv[:, :, 2].astype(jnp.float32)
    scores = jnp.einsum('tnhd,snhd->nhts', query, keys) * (1.0 / math.sqrt(HD))
    allowed = jnp.maximum(wet_block, 1.0 - wet_block[0:1])
    key_ok = jnp.tile(allowed.T, (1, mem_n))
    scores = jnp.where(key_ok[:, None, None, :] > 0, scores, -jnp.inf)
    top = lax.optimization_barrier(jnp.max(scores, axis=-1, keepdims=True))
    probs = jnp.exp(scores - top)
    probs = probs / lax.optimization_barrier(jnp.sum(probs, axis=-1, keepdims=True))
    attended = jnp.einsum('nhts,snhd->tnhd', probs, values).astype(jnp.bfloat16)
    proj = jnp.dot(attended.reshape(-1, width), out_weight, preferred_element_type=jnp.float32)
    proj = proj.reshape(mem_n, lev, count, width)
    return (xf + wet_block[None, :, :, None] * proj).astype(jnp.bfloat16)

def reference(atm_latent, ocean_state, depth, src_blocks, live, remap_weight, conv_weight, qkv_weight, out_weight):
    levels = jnp.arange(LEV, dtype=jnp.int32)
    wet = (levels[:, None] < depth[None, :]).astype(jnp.float32)
    surface = (levels == 0).astype(jnp.float32)
    pair_on = (jnp.arange(NPAIR, dtype=jnp.int32)[None, :] < live[:, None]).astype(jnp.bfloat16)
    weights = (remap_weight * pair_on[:, :, None, None]).astype(jnp.float32)

    def couple(members):
        atm, state = members
        masked = (state * wet[:, :, None]).astype(jnp.bfloat16)
        grid = jnp.pad(masked.reshape(LEV, NOROWS, OCOLS, C), ((0, 0), (1, 1), (1, 1), (0, 0)))
        conv = jnp.zeros((LEV * NOROWS * OCOLS, C), jnp.float32)
        for shift_row in range(3):
            for shift_col in range(3):
                window = grid[:, shift_row:shift_row + NOROWS, shift_col:shift_col + OCOLS].reshape(-1, C)
                conv = conv + jnp.dot(window, conv_weight[shift_row, shift_col], preferred_element_type=jnp.float32)
        blocks = atm.reshape(-1, OCOLS, C)
        picked = blocks[src_blocks].astype(jnp.float32)
        forcing = jnp.einsum('bpij,bpjc->bic', weights, picked).reshape(OCELLS, C)
        total = conv.reshape(LEV, OCELLS, C) + surface[:, None, None] * forcing[None]
        return (masked.astype(jnp.float32) + wet[:, :, None] * total).astype(jnp.bfloat16)
    mixed = lax.map(couple, (atm_latent, ocean_state))
    rows_first = jnp.moveaxis(mixed.reshape(MEMBERS, LEV, NOROWS, OCOLS, C), 2, 0)
    wet_rows = jnp.moveaxis(wet.reshape(LEV, NOROWS, OCOLS), 1, 0)

    def attend_row(inputs):
        return attend_block(inputs[0], inputs[1], qkv_weight, out_weight)
    done = lax.map(attend_row, (rows_first, wet_rows))
    return jnp.moveaxis(done, 0, 2).reshape(MEMBERS, LEV, OCELLS, C)
```

```python
import functools
import math

import jax
import jax.numpy as jnp
from jax import lax
from jax.experimental import pallas as pl
from jax.experimental.pallas import tpu as pltpu
from jax.sharding import PartitionSpec as P

HEADS = 4
R = 1
GROUP = 16
EPS = 1e-06
NEG = -1e30
F32 = jnp.float32
BF16 = jnp.bfloat16
VMEM_LIMIT = 56 * 1024 * 1024


def params(steps=1):
    return pltpu.CompilerParams(
        dimension_semantics=("arbitrary",) * steps, vmem_limit_bytes=VMEM_LIMIT
    )


def cost(flops, nbytes):
    return pl.CostEstimate(flops=int(flops), bytes_accessed=int(nbytes), transcendentals=0)


def stencil(taps, weight_ref, cols):
    count = taps[0].shape[0]
    sums = []
    for dc in range(3):
        acc = jnp.dot(taps[0], weight_ref[0, dc], preferred_element_type=F32)
        for dr in (1, 2):
            acc = acc + jnp.dot(taps[dr], weight_ref[dr, dc], preferred_element_type=F32)
        sums.append(acc)
    col = lax.broadcasted_iota(jnp.int32, (count, 1), 0) % cols
    left = jnp.where(col == 0, 0.0, pltpu.roll(sums[0], 1, axis=0))
    right = jnp.where(col == cols - 1, 0.0, pltpu.roll(sums[2], count - 1, axis=0))
    return sums[1] + left + right


def finish(masked, wet, total, mixed_ref, normed_ref):
    mixed = (masked.astype(F32) + wet * total).astype(BF16)
    mixed_ref[0] = mixed
    mf = mixed.astype(F32)
    mean = jnp.mean(mf * mf, axis=-1, keepdims=True)
    normed_ref[0] = (mf * lax.rsqrt(mean + EPS)).astype(BF16)


def wet_of(depth_ref, level, width):
    wet = (depth_ref[...] > level.astype(F32)).astype(F32)
    return jnp.concatenate([wet] * (width // wet.shape[1]), axis=1)


def inner_kernel(cols, first, state_ref, depth_ref, weight_ref, mixed_ref, normed_ref):
    width = state_ref.shape[-1]
    wet = wet_of(depth_ref, pl.program_id(0) + first, width)
    x = state_ref[0, 0] * wet.astype(BF16)
    count = x.shape[0] - 2 * cols
    taps = [x[dr * cols : dr * cols + count] for dr in range(3)]
    total = stencil(taps, weight_ref, cols)
    finish(taps[1], wet[cols : cols + count], total, mixed_ref, normed_ref)


def surface_kernel(
    cols,
    ids_ref,
    live_ref,
    state_ref,
    depth_ref,
    weight_ref,
    before_ref,
    atm_ref,
    after_ref,
    remap_ref,
    mixed_ref,
    normed_ref,
    edge_ref,
    window_ref,
    forcing_ref,
):
    width = state_ref.shape[-1]
    own = atm_ref.shape[1]
    blocks, pairs = remap_ref.shape[0], remap_ref.shape[1]
    window_ref[0:own] = before_ref[...]
    window_ref[own : 2 * own] = atm_ref[0]
    window_ref[2 * own : 3 * own] = after_ref[...]
    for b in range(blocks):
        acc = jnp.zeros((cols, width), F32)
        for p in range(pairs):
            on = (p < live_ref[b]).astype(F32)
            start = pl.multiple_of(ids_ref[b, p] * cols, cols)
            acc = acc + on * jnp.dot(
                remap_ref[b, p], window_ref[pl.ds(start, cols), :], preferred_element_type=F32
            )
        forcing_ref[b * cols : (b + 1) * cols] = acc
    wet = wet_of(depth_ref, jnp.int32(0), width)
    x = state_ref[0, 0] * wet.astype(BF16)
    count = x.shape[0] - 2 * cols
    taps = [x[dr * cols : dr * cols + count] for dr in range(3)]
    total = stencil(taps, weight_ref, cols) + forcing_ref[cols : cols + count]
    finish(taps[1], wet[cols : cols + count], total, mixed_ref, normed_ref)
    edge_ref[0:cols] = forcing_ref[0:cols]
    edge_ref[cols : 2 * cols] = forcing_ref[cols + count :]


def edge_kernel(
    cols,
    state_ref,
    depth_ref,
    weight_ref,
    before_ref,
    after_ref,
    forcing_ref,
    mixed_ref,
    normed_ref,
):
    width = state_ref.shape[-1]
    level = pl.program_id(0)
    wet = wet_of(depth_ref, level, width)
    x = state_ref[0, 0] * wet.astype(BF16)
    cells = x.shape[0]
    top = [before_ref[...], x[0:cols], x[cols : 2 * cols]]
    low = [x[cells - 2 * cols : cells - cols], x[cells - cols :], after_ref[...]]
    taps = [jnp.concatenate([a, b], axis=0) for a, b in zip(top, low)]
    total = stencil(taps, weight_ref, cols)
    total = total + jnp.where(level == 0, 1.0, 0.0) * forcing_ref[...]
    edge_wet = jnp.concatenate([wet[0:cols], wet[cells - cols :]], axis=0)
    finish(taps[1], edge_wet, total, mixed_ref, normed_ref)


def attend_kernel(members, nparts, *refs):
    refs = list(refs)
    take = lambda k: [refs.pop(0) for _ in range(k)]
    normed = [take(nparts) for _ in range(members)]
    mixed = take(nparts)
    depth_ref, bias_ref, qkv_ref, wo_ref = take(4)
    if len(refs) == 6:
        take(1)
    out_ref, q_ref, k_ref, v_ref, att_ref = refs
    lev, count, width = q_ref.shape
    head = width // HEADS
    pair = 2 * head
    for m in range(members):
        x = jnp.concatenate([p[...].reshape(-1, width) for p in normed[m]], axis=0)
        rows = slice(m * lev, (m + 1) * lev)
        if m == 0:
            q = jnp.dot(x, qkv_ref[:, 0:width], preferred_element_type=F32).astype(BF16)
            q_ref[...] = (q * (1.0 / math.sqrt(head))).astype(BF16).reshape(lev, count, width)
        k = jnp.dot(x, qkv_ref[:, width : 2 * width], preferred_element_type=F32)
        k_ref[rows] = k.astype(BF16).reshape(lev, count, width)
        v = jnp.dot(x, qkv_ref[:, 2 * width :], preferred_element_type=F32)
        v_ref[rows] = v.astype(BF16).reshape(lev, count, width)
    nq, nk = lev * GROUP, members * lev * GROUP
    qc = lax.broadcasted_iota(jnp.int32, (nq, nk), 0) % GROUP
    kc = lax.broadcasted_iota(jnp.int32, (nq, nk), 1) % GROUP
    same = jnp.where(qc == kc, 0.0, NEG)
    lane = lax.broadcasted_iota(jnp.int32, (1, pair), 1)
    low = (lane < head).astype(F32).astype(BF16)
    high = (lane >= head).astype(F32).astype(BF16)
    for g in range(count // GROUP):
        cells = slice(g * GROUP, (g + 1) * GROUP)
        bias = same + jnp.concatenate([bias_ref[g]] * members, axis=1)
        bias = jnp.concatenate([bias, bias], axis=0)
        for h in range(HEADS // 2):
            lanes = slice(h * pair, (h + 1) * pair)
            q = q_ref[:, cells, lanes].reshape(nq, pair)
            q = jnp.concatenate([q * low, q * high], axis=0)
            k = k_ref[:, cells, lanes].reshape(nk, pair)
            v = v_ref[:, cells, lanes].reshape(nk, pair)
            s = lax.dot_general(q, k, (((1,), (1,)), ((), ())), preferred_element_type=F32) + bias
            p = jnp.exp(s - jnp.max(s, axis=-1, keepdims=True))
            norm = 1.0 / jnp.sum(p, axis=-1, keepdims=True)
            o = jnp.dot(p.astype(BF16), v, preferred_element_type=F32) * norm
            o = jnp.where(lane < head, o[:nq], o[nq:])
            att_ref[:, cells, lanes] = o.astype(BF16).reshape(lev, GROUP, pair)
    proj = jnp.dot(att_ref[...].reshape(-1, width), wo_ref[...], preferred_element_type=F32)
    base = jnp.concatenate([p[...].reshape(-1, width) for p in mixed], axis=0).astype(F32)
    for l in range(lev):
        rows = slice(l * count, (l + 1) * count)
        wet = wet_of(depth_ref, jnp.int32(l), width)
        out_ref[0, l] = (base[rows] + wet * proj[rows]).astype(BF16)


def attend(normed, mixed, depth_b, bias, qkv_weight, out_weight, cols, place, out, shape):
    members, nparts = len(normed), len(mixed)
    lev = sum(p.shape[0] for p in mixed)
    width = shape[-1]
    nblocks = mixed[0].shape[1] // cols
    groups = cols // GROUP
    part = [pl.BlockSpec((p.shape[0], cols, width), lambda i: (0, i, 0)) for p in mixed]
    in_specs = part * (members + 1) + [
        pl.BlockSpec((cols, depth_b.shape[1]), lambda i: (place(i), 0)),
        pl.BlockSpec((groups, 1, bias.shape[2]), lambda i: (place(i), 0, 0)),
        pl.BlockSpec(qkv_weight.shape, lambda i: (0, 0)),
        pl.BlockSpec(out_weight.shape, lambda i: (0, 0)),
    ]
    args = sum(normed, []) + mixed + [depth_b, bias, qkv_weight, out_weight]
    alias = {}
    if out is not None:
        in_specs.append(pl.BlockSpec(memory_space=pl.ANY))
        alias = {len(args): 0}
        args.append(out)
    tokens = lev * cols * nblocks
    return pl.pallas_call(
        functools.partial(attend_kernel, members, nparts),
        grid=(nblocks,),
        in_specs=in_specs,
        out_specs=pl.BlockSpec((1, lev, cols, width), lambda i: (0, 0, place(i), 0)),
        out_shape=jax.ShapeDtypeStruct(shape, BF16),
        scratch_shapes=[
            pltpu.VMEM((lev, cols, width), BF16),
            pltpu.VMEM((members * lev, cols, width), BF16),
            pltpu.VMEM((members * lev, cols, width), BF16),
            pltpu.VMEM((lev, cols, width), BF16),
        ],
        input_output_aliases=alias,
        compiler_params=params(),
        cost_estimate=cost(tokens * width * width * 8 * (members + 2), tokens * width * 2 * 5),
        name="attend",
    )(*args)


def body(
    atm_latent,
    ocean_state,
    depth,
    src_blocks,
    live,
    remap_weight,
    conv_weight,
    qkv_weight,
    out_weight,
):
    _, lev, cells, width = ocean_state.shape
    cols = remap_weight.shape[2]
    rows = cells // cols
    inner = cells - 2 * cols
    own = atm_latent.shape[1]
    atm_blk = own // cols
    tiles = lax.axis_size("tile")
    members = lax.axis_size("mem")
    depth_f = depth.astype(F32)
    depth_b = jnp.broadcast_to(depth_f[:, None], (cells, 128))
    levels = jnp.arange(lev, dtype=F32)
    bias = jnp.where(
        depth_f.reshape(-1, 1, GROUP) > levels[None, :, None], 0.0, NEG
    ).reshape(cells // GROUP, 1, lev * GROUP)

    grid = ocean_state[0].reshape(lev, rows, cols, width)
    dgrid = depth_f.reshape(rows, cols)

    def message(row):
        wet = (levels[:, None] < dgrid[row][None, :]).astype(BF16)
        edge = (grid[:, row] * wet[:, :, None]).reshape(lev * cols, width)
        return jnp.concatenate([edge, atm_latent[0]], axis=0)

    before = lax.ppermute(message(rows - 1), "tile", [(i, i + 1) for i in range(tiles - 1)])
    after = lax.ppermute(message(0), "tile", [(i + 1, i) for i in range(tiles - 1)])

    def exchange(x):
        out = []
        for k in range(1, members):
            out.append(lax.ppermute(x, "mem", [(i, (i + k) % members) for i in range(members)]))
        return out

    weight_spec = lambda nd: pl.BlockSpec(conv_weight.shape, lambda *i: (0, 0, 0, 0))
    depth_spec = pl.BlockSpec(depth_b.shape, lambda *i: (0, 0))
    tok = lambda n, c: jax.ShapeDtypeStruct((n, c, width), BF16)
    conv_flops = lambda n, c: 2 * 9 * n * c * width * width

    deep_mixed, deep_normed = pl.pallas_call(
        functools.partial(inner_kernel, cols, 1),
        grid=(lev - 1,),
        in_specs=[
            pl.BlockSpec((1, 1, cells, width), lambda l: (0, l + 1, 0, 0)),
            depth_spec,
            weight_spec(1),
        ],
        out_specs=[pl.BlockSpec((1, inner, width), lambda l: (l, 0, 0))] * 2,
        out_shape=[tok(lev - 1, inner)] * 2,
        compiler_params=params(),
        cost_estimate=cost(conv_flops(lev - 1, inner), lev * inner * width * 8),
        name="inner",
    )(ocean_state, depth_b, conv_weight)
    deep_other = exchange(deep_normed)

    first = (lax.axis_index("tile") - R) * atm_blk
    ids = jnp.clip(src_blocks - first, 0, 3 * atm_blk - 1)
    atm_at = lev * cols // own
    surf_mixed, surf_normed, edge_forcing = pl.pallas_call(
        functools.partial(surface_kernel, cols),
        grid_spec=pltpu.PrefetchScalarGridSpec(
            num_scalar_prefetch=2,
            grid=(1,),
            in_specs=[
                pl.BlockSpec((1, 1, cells, width), lambda i, *_: (0, 0, 0, 0)),
                depth_spec,
                weight_spec(1),
                pl.BlockSpec((own, width), lambda i, *_: (atm_at, 0)),
                pl.BlockSpec((1, own, width), lambda i, *_: (0, 0, 0)),
                pl.BlockSpec((own, width), lambda i, *_: (atm_at, 0)),
                pl.BlockSpec(remap_weight.shape, lambda i, *_: (0, 0, 0, 0)),
            ],
            out_specs=[
                pl.BlockSpec((1, inner, width), lambda i, *_: (0, 0, 0)),
                pl.BlockSpec((1, inner, width), lambda i, *_: (0, 0, 0)),
                pl.BlockSpec((2 * cols, width), lambda i, *_: (0, 0)),
            ],
            scratch_shapes=[pltpu.VMEM((3 * own, width), BF16), pltpu.VMEM((cells, width), F32)],
        ),
        out_shape=[tok(1, inner), tok(1, inner), jax.ShapeDtypeStruct((2 * cols, width), F32)],
        compiler_params=params(),
        cost_estimate=cost(conv_flops(1, inner) * 2, cells * width * 16),
        name="surface",
    )(ids, live, ocean_state, depth_b, conv_weight, before, atm_latent, after, remap_weight)
    surf_other = exchange(surf_normed)

    edge_mixed, edge_normed = pl.pallas_call(
        functools.partial(edge_kernel, cols),
        grid=(lev,),
        in_specs=[
            pl.BlockSpec((1, 1, cells, width), lambda l: (0, l, 0, 0)),
            depth_spec,
            weight_spec(1),
            pl.BlockSpec((cols, width), lambda l: (l, 0)),
            pl.BlockSpec((cols, width), lambda l: (l, 0)),
            pl.BlockSpec((2 * cols, width), lambda l: (0, 0)),
        ],
        out_specs=[pl.BlockSpec((1, 2 * cols, width), lambda l: (l, 0, 0))] * 2,
        out_shape=[tok(lev, 2 * cols)] * 2,
        compiler_params=params(),
        cost_estimate=cost(conv_flops(lev, 2 * cols), lev * cols * width * 16),
        name="edge",
    )(ocean_state, depth_b, conv_weight, before, after, edge_forcing)
    edge_other = exchange(edge_normed)

    shape = ocean_state.shape
    inner_normed = [[surf_normed, deep_normed]] + [list(p) for p in zip(surf_other, deep_other)]
    out = attend(
        inner_normed,
        [surf_mixed, deep_mixed],
        depth_b,
        bias,
        qkv_weight,
        out_weight,
        cols,
        lambda i: i + 1,
        None,
        shape,
    )
    return attend(
        [[edge_normed]] + [[p] for p in edge_other],
        [edge_mixed],
        depth_b,
        bias,
        qkv_weight,
        out_weight,
        cols,
        lambda i: i * (rows - 1),
        out,
        shape,
    )


def solution(mesh):
    return jax.shard_map(
        body,
        mesh=mesh,
        in_specs=(
            P("mem", "tile", None),
            P("mem", None, "tile", None),
            P("tile"),
            P("tile", None),
            P("tile"),
            P("tile", None, None, None),
            P(),
            P(),
            P(),
        ),
        out_specs=P("mem", None, "tile", None),
        check_vma=False,
    )
```

```python
import functools
import math

import jax
import jax.numpy as jnp
from jax import lax
from jax.experimental import pallas as pl
from jax.experimental.pallas import tpu as pltpu
from jax.sharding import PartitionSpec as P

HEADS = 4
R = 1
GROUP = 16
EPS = 1e-06
NEG = -1e30
F32 = jnp.float32
BF16 = jnp.bfloat16
MIB = 1024 * 1024


def params(mib, steps=0):
    return pltpu.CompilerParams(
        dimension_semantics=("arbitrary",) * steps if steps else None, vmem_limit_bytes=mib * MIB
    )


def cost(flops, nbytes):
    return pl.CostEstimate(flops=int(flops), bytes_accessed=int(nbytes), transcendentals=0)


def capacity(tokens, share):
    return -(-int(tokens * share) // 16) * 16


def row_plan(depth_row, lev):
    cols = depth_row.shape[1]
    level = lax.broadcasted_iota(jnp.int32, (lev, cols), 0).astype(F32)
    wet = (depth_row > level).astype(F32)
    upper = (
        lax.broadcasted_iota(jnp.int32, (cols, cols), 0)
        < lax.broadcasted_iota(jnp.int32, (cols, cols), 1)
    )
    upper = upper.astype(F32).astype(BF16)
    rank = jnp.dot(wet.astype(BF16), upper, preferred_element_type=F32)
    counts = [jnp.sum(wet[l : l + 1]).astype(jnp.int32) for l in range(lev)]
    return wet, rank, counts


def offsets(plans, first, lev):
    at, place = jnp.int32(0), {}
    for l in range(first, lev):
        for r, plan in enumerate(plans):
            place[l, r] = at
            at = at + plan[2][l]
    return place


def segment(wet, rank, offset, cap):
    cols = wet.shape[1]
    base = jnp.minimum((offset // 16) * 16, cap)
    target = jnp.where(wet > 0, rank + (offset - base).astype(F32), -1.0)
    slot = lax.broadcasted_iota(jnp.int32, (cols + 16, cols), 0).astype(F32)
    return pl.multiple_of(base, 16), (slot == target).astype(F32).astype(BF16)


def pack(buf_ref, wet, rank, offset, cap, tokens):
    base, hot = segment(wet, rank, offset, cap)
    rows = jnp.dot(hot, tokens, preferred_element_type=F32).astype(BF16)
    head = pl.ds(base, 16)
    buf_ref[head, :] = buf_ref[head, :] + rows[:16]
    buf_ref[pl.ds(pl.multiple_of(base + 16, 16), rows.shape[0] - 16), :] = rows[16:]


def unpack(buf_ref, wet, rank, offset, cap):
    base, hot = segment(wet, rank, offset, cap)
    rows = buf_ref[pl.ds(base, hot.shape[0]), :]
    return lax.dot_general(
        hot, rows, (((0,), (0,)), ((), ())), preferred_element_type=F32
    ).astype(BF16)


def column(depth_row, width):
    cols = depth_row.shape[1]
    turned = jnp.broadcast_to(depth_row, (cols, cols)).T
    return jnp.concatenate([turned] * (width // cols), axis=1)


def stencil(taps, weight_ref, cols):
    count, width = taps[0].shape
    x = jnp.concatenate(taps, axis=1)
    sums = [
        jnp.dot(x, weight_ref[:, dc].reshape(3 * width, -1), preferred_element_type=F32)
        for dc in range(3)
    ]
    col = lax.broadcasted_iota(jnp.int32, (count, 1), 0) % cols
    left = jnp.where(col == 0, 0.0, pltpu.roll(sums[0], 1, axis=0))
    right = jnp.where(col == cols - 1, 0.0, pltpu.roll(sums[2], count - 1, axis=0))
    return sums[1] + left + right


def normalise(mixed):
    mf = mixed.astype(F32)
    mean = jnp.mean(mf * mf, axis=-1, keepdims=True)
    return (mf * lax.rsqrt(mean + EPS)).astype(BF16)


def inner_kernel(
    cap,
    state_hbm,
    depth_ref,
    weight_hbm,
    mixed_hbm,
    normed_hbm,
    packed_hbm,
    base_ref,
    state,
    weight,
    mixed,
    normed,
    packed,
    in_sem,
    weight_sem,
    out_sem,
    packed_sem,
):
    _, lev, cells, width = state_hbm.shape
    rows, cols = depth_ref.shape
    order = list(range(1, lev)) + [0]
    load_w = pltpu.make_async_copy(weight_hbm, weight, weight_sem)
    loads = [pltpu.make_async_copy(state_hbm.at[0, l], state.at[l], in_sem.at[l]) for l in range(lev)]
    loads[1].start()
    load_w.start()
    for l in order[1:]:
        loads[l].start()
    packed[...] = jnp.zeros_like(packed)
    d = depth_ref[...].astype(F32)
    plans = [row_plan(d[r : r + 1], lev) for r in range(1, rows - 1)]
    place = offsets(plans, 1, lev)
    deep = jnp.concatenate([column(d[r : r + 1], width) for r in range(rows)], axis=0)
    count = cells - 2 * cols
    stores = []
    for l in order:
        wet = (deep > l).astype(F32)
        loads[l].wait()
        if l == 1:
            load_w.wait()
        x = state[l] * wet.astype(BF16)
        taps = [x[dr * cols : dr * cols + count] for dr in range(3)]
        total = stencil(taps, weight, cols)
        new = taps[1].astype(F32) + wet[cols : cols + count] * total
        if l == 0:
            base_ref[...] = new
            continue
        new = new.astype(BF16)
        mixed[l - 1] = new
        tokens = normalise(new)
        normed[l - 1] = tokens
        for k, (buf, out) in enumerate(((mixed, mixed_hbm), (normed, normed_hbm))):
            store = pltpu.make_async_copy(buf.at[l - 1], out.at[l - 1], out_sem.at[l - 1, k])
            store.start()
            stores.append(store)
        for r, plan in enumerate(plans):
            pack(
                packed,
                plan[0][l : l + 1],
                plan[1][l : l + 1],
                place[l, r],
                cap,
                tokens[r * cols : (r + 1) * cols],
            )
        if l == lev - 1:
            store = pltpu.make_async_copy(packed.at[pl.ds(0, cap)], packed_hbm, packed_sem)
            store.start()
            stores.append(store)
    for store in stores:
        store.wait()


def surface_kernel(
    ids_ref,
    live_ref,
    base_ref,
    depth_ref,
    before_ref,
    atm_ref,
    after_ref,
    remap_ref,
    mixed_ref,
    normed_ref,
    edge_ref,
    window_ref,
    forcing_ref,
):
    rows, cols = depth_ref.shape
    width = base_ref.shape[-1]
    own = atm_ref.shape[1]
    blocks, pairs = remap_ref.shape[0], remap_ref.shape[1]
    window_ref[0:own] = before_ref[0]
    window_ref[own : 2 * own] = atm_ref[0]
    window_ref[2 * own : 3 * own] = after_ref[0]
    for b in range(blocks):
        acc = jnp.zeros((cols, width), F32)
        for p in range(pairs):
            on = (p < live_ref[b]).astype(F32)
            start = pl.multiple_of(ids_ref[b, p] * cols, cols)
            acc = acc + on * jnp.dot(
                remap_ref[b, p], window_ref[pl.ds(start, cols), :], preferred_element_type=F32
            )
        forcing_ref[b * cols : (b + 1) * cols] = acc
    d = depth_ref[...].astype(F32)
    for r in range(1, rows - 1):
        at = slice((r - 1) * cols, r * cols)
        wet = (column(d[r : r + 1], width) > 0).astype(F32)
        new = (base_ref[at] + wet * forcing_ref[r * cols : (r + 1) * cols]).astype(BF16)
        mixed_ref[0, at] = new
        normed_ref[0, at] = normalise(new)
    edge_ref[0:cols] = forcing_ref[0:cols]
    edge_ref[cols : 2 * cols] = forcing_ref[(rows - 1) * cols :]


def edge_kernel(
    cap,
    state_hbm,
    depth_ref,
    weight_hbm,
    before_hbm,
    after_hbm,
    forcing_ref,
    mixed_hbm,
    normed_hbm,
    top_hbm,
    low_hbm,
    state,
    weight,
    before,
    after,
    mixed,
    normed,
    top,
    low,
    in_sem,
    weight_sem,
    out_sem,
    packed_sem,
):
    _, lev, cells, width = state_hbm.shape
    rows, cols = depth_ref.shape
    load_w = pltpu.make_async_copy(weight_hbm, weight, weight_sem)
    loads = []
    for l in range(lev):
        halo = pl.ds(l * cols, cols)
        loads.append(
            [
                pltpu.make_async_copy(state_hbm.at[0, l], state.at[l], in_sem.at[l, 0]),
                pltpu.make_async_copy(before_hbm.at[halo], before.at[halo], in_sem.at[l, 1]),
                pltpu.make_async_copy(after_hbm.at[halo], after.at[halo], in_sem.at[l, 2]),
            ]
        )
    for copy in loads[0]:
        copy.start()
    load_w.start()
    for l in range(1, lev):
        for copy in loads[l]:
            copy.start()
    top[...] = jnp.zeros_like(top)
    low[...] = jnp.zeros_like(low)
    d = depth_ref[...].astype(F32)
    ends = [d[0:1], d[rows - 1 : rows]]
    plans = [row_plan(e, lev) for e in ends]
    places = [offsets([plan], 0, lev) for plan in plans]
    deep = jnp.concatenate([column(d[r : r + 1], width) for r in range(rows)], axis=0)
    stores = []
    for l in range(lev):
        wet = (deep > l).astype(F32)
        for copy in loads[l]:
            copy.wait()
        if l == 0:
            load_w.wait()
        x = state[l] * wet.astype(BF16)
        halo = slice(l * cols, (l + 1) * cols)
        up = [before[halo], x[0:cols], x[cols : 2 * cols]]
        down = [x[cells - 2 * cols : cells - cols], x[cells - cols :], after[halo]]
        taps = [jnp.concatenate([a, b], axis=0) for a, b in zip(up, down)]
        total = stencil(taps, weight, cols)
        if l == 0:
            total = total + forcing_ref[...]
        edge_wet = jnp.concatenate([wet[0:cols], wet[cells - cols :]], axis=0)
        new = (taps[1].astype(F32) + edge_wet * total).astype(BF16)
        mixed[l] = new
        tokens = normalise(new)
        normed[l] = tokens
        for k, (buf, out) in enumerate(((mixed, mixed_hbm), (normed, normed_hbm))):
            store = pltpu.make_async_copy(buf.at[l], out.at[l], out_sem.at[l, k])
            store.start()
            stores.append(store)
        for r, buf in enumerate((top, low)):
            pack(
                buf,
                plans[r][0][l : l + 1],
                plans[r][1][l : l + 1],
                places[r][l, 0],
                cap,
                tokens[r * cols : (r + 1) * cols],
            )
    for k, (buf, out) in enumerate(((top, top_hbm), (low, low_hbm))):
        store = pltpu.make_async_copy(buf.at[pl.ds(0, cap)], out, packed_sem.at[k])
        store.start()
        stores.append(store)
    for store in stores:
        store.wait()


def attend_kernel(others, nparts, rows_of, first, cap, aliased, flag_ref, *refs):
    refs = list(refs)
    take = lambda k: [refs.pop(0) for _ in range(k)]
    own_normed = take(nparts)
    own_mixed = take(nparts)
    surf = take(others) if first else []
    packed = take(others)
    whole = take(others)
    depth_ref, qkv_ref, wo_ref = take(3)
    if aliased:
        take(1)
    out_ref, q_ref, k_ref, v_ref, att_ref, buf_ref, token_ref, sem = refs
    lev, count, width = q_ref.shape
    members = others + 1
    head = width // HEADS
    pair = 2 * head
    step = pl.program_id(0)

    def keys_values(x, m):
        rows = slice(m * lev, (m + 1) * lev)
        kv = jnp.dot(x, qkv_ref[:, width:], preferred_element_type=F32).astype(BF16)
        k_ref[rows] = kv[:, :width].reshape(lev, count, width)
        v_ref[rows] = kv[:, width:].reshape(lev, count, width)

    d = depth_ref[...].astype(F32)
    plans = [row_plan(d[r : r + 1], lev) for r in rows_of]
    place = offsets(plans, first, lev)
    two = len(rows_of) == 2
    pick = lambda a, b: jnp.where(step == 0, a, b)
    wet_row = pick(plans[0][0], plans[1][0]) if two else plans[0][0]
    rank = pick(plans[0][1], plans[1][1]) if two else plans[0][1]
    depth_row = d[rows_of[0] : rows_of[0] + 1]
    if two:
        depth_row = pick(depth_row, d[rows_of[1] : rows_of[1] + 1])

    x = jnp.concatenate([p[...].reshape(-1, width) for p in own_normed], axis=0)
    q = jnp.dot(x, qkv_ref[:, 0:width], preferred_element_type=F32).astype(BF16)
    q_ref[...] = (q * (1.0 / math.sqrt(head))).astype(BF16).reshape(lev, count, width)
    keys_values(x, 0)
    for o in range(others):
        if first:
            token_ref[0] = surf[o][0]

        @pl.when(flag_ref[0] == 0)
        def _():
            buf_ref[0:cap] = packed[o][...]
            buf_ref[cap:] = jnp.zeros((buf_ref.shape[0] - cap, width), BF16)
            for l in range(first, lev):
                at = pick(place[l, 0], place[l, 1]) if two else place[l, 0]
                token_ref[l] = unpack(
                    buf_ref, wet_row[l : l + 1], rank[l : l + 1], at, cap
                )

        @pl.when(flag_ref[0] != 0)
        def _():
            which = step if two else (0 if rows_of[0] == 0 else 1)
            copy = pltpu.make_async_copy(
                whole[o].at[:, pl.ds(which * count, count)], token_ref.at[pl.ds(first, lev - first)], sem
            )
            copy.start()
            copy.wait()

        keys_values(token_ref[...].reshape(-1, width), o + 1)

    nq, nk = lev * GROUP, members * lev * GROUP
    groups = count // GROUP
    lanes_n = lev * GROUP
    cell = lax.broadcasted_iota(jnp.int32, (groups, count), 1)
    mine = (cell // GROUP == lax.broadcasted_iota(jnp.int32, (groups, count), 0)).astype(F32)
    spread = lax.broadcasted_iota(jnp.int32, (count, lanes_n), 0) % GROUP
    spread = (spread == lax.broadcasted_iota(jnp.int32, (count, lanes_n), 1) % GROUP).astype(F32)
    key_depth = jnp.dot(
        (mine * depth_row).astype(BF16), spread.astype(BF16), preferred_element_type=F32
    )
    key_level = lax.broadcasted_iota(jnp.int32, (groups, lanes_n), 1) // GROUP
    key_bias = jnp.where(key_depth > key_level.astype(F32), 0.0, NEG)
    qc = lax.broadcasted_iota(jnp.int32, (nq, nk), 0) % GROUP
    kc = lax.broadcasted_iota(jnp.int32, (nq, nk), 1) % GROUP
    same = jnp.where(qc == kc, 0.0, NEG)
    lane = lax.broadcasted_iota(jnp.int32, (1, pair), 1)
    low = (lane < head).astype(F32).astype(BF16)
    high = (lane >= head).astype(F32).astype(BF16)
    for g in range(groups):
        cells = slice(g * GROUP, (g + 1) * GROUP)
        bias = same + jnp.concatenate([key_bias[g : g + 1]] * members, axis=1)
        bias = jnp.concatenate([bias, bias], axis=0)
        for h in range(HEADS // 2):
            lanes = slice(h * pair, (h + 1) * pair)
            q = q_ref[:, cells, lanes].reshape(nq, pair)
            q = jnp.concatenate([q * low, q * high], axis=0)
            k = k_ref[:, cells, lanes].reshape(nk, pair)
            v = v_ref[:, cells, lanes].reshape(nk, pair)
            s = lax.dot_general(q, k, (((1,), (1,)), ((), ())), preferred_element_type=F32) + bias
            p = jnp.exp(s - jnp.max(s, axis=-1, keepdims=True))
            norm = 1.0 / jnp.sum(p, axis=-1, keepdims=True)
            o = jnp.dot(p.astype(BF16), v, preferred_element_type=F32) * norm
            o = jnp.where(lane < head, o[:nq], o[nq:])
            att_ref[:, cells, lanes] = o.astype(BF16).reshape(lev, GROUP, pair)
    proj = jnp.dot(att_ref[...].reshape(-1, width), wo_ref[...], preferred_element_type=F32)
    base = jnp.concatenate([p[...].reshape(-1, width) for p in own_mixed], axis=0).astype(F32)
    deep = column(depth_row, width)
    for l in range(lev):
        rows = slice(l * count, (l + 1) * count)
        wet = (deep > l).astype(F32)
        out_ref[0, l] = (base[rows] + wet * proj[rows]).astype(BF16)


def attend(flag, normed, mixed, surf, packed, whole, depth, qkv_weight, out_weight, rows_of, out, shape):
    others, nparts = len(packed), len(mixed)
    lev = sum(p.shape[0] for p in mixed)
    width = shape[-1]
    rows, cols = depth.shape
    cap = packed[0].shape[0]
    first = 1 if surf else 0
    shift = 1 if rows_of[0] == rows - 1 else 0
    index = lambda i, *_: (0, i + shift, 0)
    full2 = lambda a: pl.BlockSpec(a.shape, lambda i, *_: (0, 0))
    part = [pl.BlockSpec((p.shape[0], cols, width), index) for p in mixed]
    hbm = pl.BlockSpec(memory_space=pl.ANY)
    in_specs = part * 2
    in_specs += [pl.BlockSpec((1, cols, width), index)] * len(surf)
    in_specs += [full2(p) for p in packed]
    in_specs += [hbm] * others
    in_specs += [full2(depth), full2(qkv_weight), full2(out_weight)]
    args = normed + mixed + surf + packed + whole + [depth, qkv_weight, out_weight]
    alias = {}
    if out is not None:
        in_specs.append(hbm)
        alias = {len(args) + 1: 0}
        args.append(out)
    tokens = lev * cols * len(rows_of)
    members = others + 1
    return pl.pallas_call(
        functools.partial(
            attend_kernel, others, nparts, tuple(rows_of), first, cap, out is not None
        ),
        grid_spec=pltpu.PrefetchScalarGridSpec(
            num_scalar_prefetch=1,
            grid=(len(rows_of),),
            in_specs=in_specs,
            out_specs=pl.BlockSpec(
                (1, lev, cols, width), lambda i, *_: (0, 0, i + rows_of[0], 0)
            ),
            scratch_shapes=[
                pltpu.VMEM((lev, cols, width), BF16),
                pltpu.VMEM((members * lev, cols, width), BF16),
                pltpu.VMEM((members * lev, cols, width), BF16),
                pltpu.VMEM((lev, cols, width), BF16),
                pltpu.VMEM((cap + cols + 16, width), BF16),
                pltpu.VMEM((lev, cols, width), BF16),
                pltpu.SemaphoreType.DMA,
            ],
        ),
        out_shape=jax.ShapeDtypeStruct(shape, BF16),
        input_output_aliases=alias,
        compiler_params=params(24 if members <= 2 else 48, 1),
        cost_estimate=cost(tokens * width * width * 8 * (members + 2), tokens * width * 2 * 5),
        name="attend",
    )(flag, *args)


def body(
    atm_latent,
    ocean_state,
    depth,
    src_blocks,
    live,
    remap_weight,
    conv_weight,
    qkv_weight,
    out_weight,
):
    _, lev, cells, width = ocean_state.shape
    cols = remap_weight.shape[2]
    rows = cells // cols
    inner = cells - 2 * cols
    own = atm_latent.shape[1]
    atm_blk = own // cols
    tiles = lax.axis_size("tile")
    members = lax.axis_size("mem")
    ups = [(i, i + 1) for i in range(tiles - 1)]
    downs = [(i + 1, i) for i in range(tiles - 1)]
    atm_before = lax.ppermute(atm_latent, "tile", ups)
    atm_after = lax.ppermute(atm_latent, "tile", downs)

    depth = depth.reshape(rows, cols)
    levels = jnp.arange(lev, dtype=jnp.int32)
    grid = ocean_state[0].reshape(lev, rows, cols, width)

    def edge(row):
        wet = (levels[:, None] < depth[row][None, :]).astype(BF16)
        return (grid[:, row] * wet[:, :, None]).reshape(lev * cols, width)

    before = lax.ppermute(edge(rows - 1), "tile", ups)
    after = lax.ppermute(edge(0), "tile", downs)

    def exchange(x):
        return [
            lax.ppermute(x, "mem", [(i, (i + k) % members) for i in range(members)])
            for k in range(1, members)
        ]

    deep_cap = capacity((lev - 1) * inner, 0.5625)
    edge_cap = capacity(lev * cols, 0.65625)
    wet_deep = jnp.sum(jnp.maximum(depth[1 : rows - 1] - 1, 0))
    wet_top = jnp.sum(jnp.maximum(depth[0], 0))
    wet_low = jnp.sum(jnp.maximum(depth[rows - 1], 0))
    over = (wet_deep > deep_cap) | (wet_top > edge_cap) | (wet_low > edge_cap)
    flag = over.astype(jnp.int32).reshape(1)

    hbm = pl.BlockSpec(memory_space=pl.ANY)
    vmem = pl.BlockSpec(memory_space=pltpu.VMEM)
    tok = lambda *s: jax.ShapeDtypeStruct((*s, width), BF16)
    conv_flops = lambda n, c: 2 * 9 * n * c * width * width
    dma = pltpu.SemaphoreType.DMA
    slack = cols + 16

    deep_mixed, deep_normed, deep_packed, base = pl.pallas_call(
        functools.partial(inner_kernel, deep_cap),
        in_specs=[hbm, vmem, hbm],
        out_specs=[hbm, hbm, hbm, vmem],
        out_shape=[
            tok(lev - 1, inner),
            tok(lev - 1, inner),
            tok(deep_cap),
            jax.ShapeDtypeStruct((inner, width), F32),
        ],
        scratch_shapes=[
            pltpu.VMEM((lev, cells, width), BF16),
            pltpu.VMEM(conv_weight.shape, BF16),
            pltpu.VMEM((lev - 1, inner, width), BF16),
            pltpu.VMEM((lev - 1, inner, width), BF16),
            pltpu.VMEM((deep_cap + slack, width), BF16),
            dma((lev,)),
            dma,
            dma((lev - 1, 2)),
            dma,
        ],
        compiler_params=params(24),
        cost_estimate=cost(conv_flops(lev, inner), lev * inner * width * 8),
        name="inner",
    )(ocean_state, depth, conv_weight)
    deep_others = exchange(deep_packed)

    first = (lax.axis_index("tile") - R) * atm_blk
    ids = jnp.clip(src_blocks - first, 0, 3 * atm_blk - 1)
    full = lambda a: pl.BlockSpec(a.shape, lambda i, *_: (0,) * a.ndim)
    surf_mixed, surf_normed, edge_forcing = pl.pallas_call(
        surface_kernel,
        grid_spec=pltpu.PrefetchScalarGridSpec(
            num_scalar_prefetch=2,
            grid=(1,),
            in_specs=[full(a) for a in (base, depth, atm_before, atm_latent, atm_after, remap_weight)],
            out_specs=[
                pl.BlockSpec((1, inner, width), lambda i, *_: (0, 0, 0)),
                pl.BlockSpec((1, inner, width), lambda i, *_: (0, 0, 0)),
                pl.BlockSpec((2 * cols, width), lambda i, *_: (0, 0)),
            ],
            scratch_shapes=[pltpu.VMEM((3 * own, width), BF16), pltpu.VMEM((cells, width), F32)],
        ),
        out_shape=[tok(1, inner), tok(1, inner), jax.ShapeDtypeStruct((2 * cols, width), F32)],
        compiler_params=params(24, 1),
        cost_estimate=cost(conv_flops(1, inner), cells * width * 16),
        name="surface",
    )(ids, live, base, depth, atm_before, atm_latent, atm_after, remap_weight)
    surf_others = exchange(surf_normed)

    edge_mixed, edge_normed, top_packed, low_packed = pl.pallas_call(
        functools.partial(edge_kernel, edge_cap),
        in_specs=[hbm, vmem, hbm, hbm, hbm, vmem],
        out_specs=[hbm] * 4,
        out_shape=[tok(lev, 2 * cols), tok(lev, 2 * cols), tok(edge_cap), tok(edge_cap)],
        scratch_shapes=[
            pltpu.VMEM((lev, cells, width), BF16),
            pltpu.VMEM(conv_weight.shape, BF16),
            pltpu.VMEM((lev * cols, width), BF16),
            pltpu.VMEM((lev * cols, width), BF16),
            pltpu.VMEM((lev, 2 * cols, width), BF16),
            pltpu.VMEM((lev, 2 * cols, width), BF16),
            pltpu.VMEM((edge_cap + slack, width), BF16),
            pltpu.VMEM((edge_cap + slack, width), BF16),
            dma((lev, 3)),
            dma,
            dma((lev, 2)),
            dma((2,)),
        ],
        compiler_params=params(24),
        cost_estimate=cost(conv_flops(lev, 2 * cols), lev * cols * width * 16),
        name="edge",
    )(ocean_state, depth, conv_weight, before, after, edge_forcing)
    top_others = exchange(top_packed)
    low_others = exchange(low_packed)

    deep_whole, edge_whole = lax.cond(
        over,
        lambda a, b: (exchange(a), exchange(b)),
        lambda a, b: ([a] * (members - 1), [b] * (members - 1)),
        deep_normed,
        edge_normed,
    )
    shape = ocean_state.shape
    weights = (depth, qkv_weight, out_weight)
    out = attend(
        flag,
        [surf_normed, deep_normed],
        [surf_mixed, deep_mixed],
        surf_others,
        deep_others,
        deep_whole,
        *weights,
        list(range(1, rows - 1)),
        None,
        shape,
    )
    for row, got in ((0, top_others), (rows - 1, low_others)):
        out = attend(
            flag, [edge_normed], [edge_mixed], [], got, edge_whole, *weights, [row], out, shape
        )
    return out


def solution(mesh):
    return jax.shard_map(
        body,
        mesh=mesh,
        in_specs=(
            P("mem", "tile", None),
            P("mem", None, "tile", None),
            P("tile"),
            P("tile", None),
            P("tile"),
            P("tile", None, None, None),
            P(),
            P(),
            P(),
        ),
        out_specs=P("mem", None, "tile", None),
        check_vma=False,
    )
```

```python
import functools
import math

import jax
import jax.numpy as jnp
from jax import lax
from jax.experimental import pallas as pl
from jax.experimental.pallas import tpu as pltpu
from jax.sharding import PartitionSpec as P

HEADS = 4
R = 1
GROUP = 16
EPS = 1e-06
NEG = -1e30
F32 = jnp.float32
BF16 = jnp.bfloat16
MIB = 1024 * 1024


def params(mib, steps=0):
    return pltpu.CompilerParams(
        dimension_semantics=("arbitrary",) * steps if steps else None, vmem_limit_bytes=mib * MIB
    )


def cost(flops, nbytes):
    return pl.CostEstimate(flops=int(flops), bytes_accessed=int(nbytes), transcendentals=0)


def capacity(tokens, share):
    return -(-int(tokens * share) // 16) * 16


def row_plan(depth_row, lev):
    cols = depth_row.shape[1]
    level = lax.broadcasted_iota(jnp.int32, (lev, cols), 0).astype(F32)
    wet = (depth_row > level).astype(F32)
    upper = (
        lax.broadcasted_iota(jnp.int32, (cols, cols), 0)
        < lax.broadcasted_iota(jnp.int32, (cols, cols), 1)
    )
    upper = upper.astype(F32).astype(BF16)
    rank = jnp.dot(wet.astype(BF16), upper, preferred_element_type=F32)
    counts = [jnp.sum(wet[l : l + 1]).astype(jnp.int32) for l in range(lev)]
    return wet, rank, counts


def offsets(plans, first, lev):
    at, place = jnp.int32(0), {}
    for l in range(first, lev):
        for r, plan in enumerate(plans):
            place[l, r] = at
            at = at + plan[2][l]
    return place


def segment(wet, rank, offset, cap):
    cols = wet.shape[1]
    base = jnp.minimum((offset // 16) * 16, cap)
    target = jnp.where(wet > 0, rank + (offset - base).astype(F32), -1.0)
    slot = lax.broadcasted_iota(jnp.int32, (cols + 16, cols), 0).astype(F32)
    return pl.multiple_of(base, 16), (slot == target).astype(F32).astype(BF16)


def pack(buf_ref, wet, rank, offset, cap, tokens):
    base, hot = segment(wet, rank, offset, cap)
    rows = jnp.dot(hot, tokens, preferred_element_type=F32).astype(BF16)
    head = pl.ds(base, 16)
    buf_ref[head, :] = buf_ref[head, :] + rows[:16]
    buf_ref[pl.ds(pl.multiple_of(base + 16, 16), rows.shape[0] - 16), :] = rows[16:]


def unpack(buf_ref, wet, rank, offset, cap):
    base, hot = segment(wet, rank, offset, cap)
    rows = buf_ref[pl.ds(base, hot.shape[0]), :]
    return lax.dot_general(
        hot, rows, (((0,), (0,)), ((), ())), preferred_element_type=F32
    ).astype(BF16)


def column(depth_row):
    cols = depth_row.shape[1]
    return jnp.broadcast_to(depth_row, (cols, cols)).T


def widen(x, width):
    return jnp.concatenate([x] * (width // x.shape[1]), axis=1)


def stencil(taps, weight_ref, cols):
    count, width = taps[0].shape
    x = jnp.concatenate(taps, axis=1)
    sums = [
        jnp.dot(x, weight_ref[:, dc].reshape(3 * width, -1), preferred_element_type=F32)
        for dc in range(3)
    ]
    col = lax.broadcasted_iota(jnp.int32, (count, 1), 0) % cols
    left = jnp.where(col == 0, 0.0, pltpu.roll(sums[0], 1, axis=0))
    right = jnp.where(col == cols - 1, 0.0, pltpu.roll(sums[2], count - 1, axis=0))
    return sums[1] + left + right


def normalise(mixed):
    mf = mixed.astype(F32)
    mean = jnp.mean(mf * mf, axis=-1, keepdims=True)
    return (mf * lax.rsqrt(mean + EPS)).astype(BF16)


def prep_kernel(caps, side_ref, near_ref, far_ref, atm_ref, depth_ref, on_ref, off_ref, flag_ref):
    _, lev, cols, width = near_ref.shape
    rows = depth_ref.shape[0]
    for block, row, out in ((near_ref, 0, on_ref), (far_ref, 1, off_ref)):
        deep = column(depth_ref[pl.ds(side_ref[row], 1), :].astype(F32))
        for l in range(lev):
            wet = (deep > l).astype(F32).astype(BF16)
            out[l * cols : (l + 1) * cols] = block[0, l] * widen(wet, width)
    on_ref[lev * cols :] = atm_ref[0]
    d = depth_ref[...].astype(F32)
    near = depth_ref[pl.ds(side_ref[0], 1), :].astype(F32)
    far = depth_ref[pl.ds(side_ref[1], 1), :].astype(F32)
    counts = [
        jnp.sum(jnp.maximum(d[1 : rows - 1] - 1.0, 0.0)),
        jnp.sum(jnp.maximum(near - 1.0, 0.0)),
        jnp.sum(far),
    ]
    over = jnp.int32(0)
    for count, cap in zip(counts, caps):
        over = over | (count > cap).astype(jnp.int32)
    flag_ref[0] = over


def inner_kernel(
    cap,
    state,
    depth_ref,
    weight,
    mixed_hbm,
    normed_hbm,
    packed_hbm,
    base_ref,
    mixed,
    normed,
    packed,
    out_sem,
    packed_sem,
):
    _, lev, cells, width = state.shape
    rows, cols = depth_ref.shape
    packed[...] = jnp.zeros_like(packed)
    d = depth_ref[...].astype(F32)
    plans = [row_plan(d[r : r + 1], lev) for r in range(1, rows - 1)]
    place = offsets(plans, 1, lev)
    deep = jnp.concatenate([column(d[r : r + 1]) for r in range(rows)], axis=0)
    count = cells - 2 * cols
    stores = []
    for l in list(range(1, lev)) + [0]:
        wet = (deep > l).astype(F32)
        x = state[0, l] * widen(wet.astype(BF16), width)
        taps = [x[dr * cols : dr * cols + count] for dr in range(3)]
        total = stencil(taps, weight, cols)
        new = taps[1].astype(F32) + widen(wet[cols : cols + count], width) * total
        if l == 0:
            base_ref[...] = new
            continue
        new = new.astype(BF16)
        mixed[l - 1] = new
        tokens = normalise(new)
        normed[l - 1] = tokens
        for k, (buf, out) in enumerate(((mixed, mixed_hbm), (normed, normed_hbm))):
            store = pltpu.make_async_copy(buf.at[l - 1], out.at[l - 1], out_sem.at[l - 1, k])
            store.start()
            stores.append(store)
        for r, plan in enumerate(plans):
            pack(
                packed,
                plan[0][l : l + 1],
                plan[1][l : l + 1],
                place[l, r],
                cap,
                tokens[r * cols : (r + 1) * cols],
            )
        if l == lev - 1:
            store = pltpu.make_async_copy(packed.at[pl.ds(0, cap)], packed_hbm, packed_sem)
            store.start()
            stores.append(store)
    for store in stores:
        store.wait()


def surface_kernel(
    ids_ref,
    live_ref,
    side_ref,
    base_ref,
    near_base_ref,
    depth_ref,
    on_ref,
    off_ref,
    atm_ref,
    remap_ref,
    mixed_ref,
    normed_ref,
    far_ref,
    window_ref,
    forcing_ref,
):
    rows, cols = depth_ref.shape
    width = base_ref.shape[-1]
    own = atm_ref.shape[1]
    blocks, pairs = remap_ref.shape[0], remap_ref.shape[1]
    near, far = side_ref[0], side_ref[1]
    on_at = jnp.where(near == 0, 0, 2 * own)
    window_ref[pl.ds(pl.multiple_of(on_at, own), own)] = on_ref[on_ref.shape[0] - own :]
    window_ref[pl.ds(pl.multiple_of(2 * own - on_at, own), own)] = off_ref[0]
    window_ref[own : 2 * own] = atm_ref[0]
    for b in range(blocks):
        acc = jnp.zeros((cols, width), F32)
        for p in range(pairs):
            on = (p < live_ref[b]).astype(F32)
            start = pl.multiple_of(ids_ref[b, p] * cols, cols)
            acc = acc + on * jnp.dot(
                remap_ref[b, p], window_ref[pl.ds(start, cols), :], preferred_element_type=F32
            )
        forcing_ref[b] = acc
    d = depth_ref[...].astype(F32)
    near_row = depth_ref[pl.ds(near, 1), :].astype(F32)
    for k in range(rows - 1):
        at = slice(k * cols, (k + 1) * cols)
        last = k == rows - 2
        wet = (column(near_row if last else d[k + 1 : k + 2]) > 0).astype(F32)
        part = near_base_ref[...] if last else base_ref[at]
        forcing = forcing_ref[near] if last else forcing_ref[k + 1]
        new = (part + widen(wet, width) * forcing).astype(BF16)
        mixed_ref[0, at] = new
        normed_ref[0, at] = normalise(new)
    far_ref[...] = forcing_ref[far]


def row_kernel(cap, first, which, side_ref, state, depth_ref, weight, halo, *refs):
    refs = list(refs)
    forcing_ref = None if first else refs.pop(0)
    mixed_hbm, normed_hbm, packed_hbm = refs[:3]
    refs = refs[3:]
    base_ref = refs.pop(0) if first else None
    tap, mixed, normed, packed, out_sem, packed_sem = refs
    _, lev, cells, width = state.shape
    rows, cols = depth_ref.shape
    row = side_ref[which]
    top = row == 0
    beside = jnp.where(top, 1, rows - 2)
    outer = jnp.where(top, 0, 2)
    packed[...] = jnp.zeros_like(packed)
    own_depth = depth_ref[pl.ds(row, 1), :].astype(F32)
    plan = row_plan(own_depth, lev)
    place = offsets([plan], first, lev)
    deep, deep_beside = column(own_depth), column(depth_ref[pl.ds(beside, 1), :].astype(F32))
    at = pl.multiple_of(row * cols, cols)
    at_beside = pl.multiple_of(beside * cols, cols)
    wets = []
    for l in range(lev):
        rows_l = slice(l * cols, (l + 1) * cols)
        wet = (deep > l).astype(F32)
        wets.append(wet)
        wet_beside = (deep_beside > l).astype(F32)
        tap[1, rows_l] = state[0, l, pl.ds(at, cols)] * widen(wet.astype(BF16), width)
        tap[2 - outer, rows_l] = state[0, l, pl.ds(at_beside, cols)] * widen(
            wet_beside.astype(BF16), width
        )
        tap[outer, rows_l] = halo[rows_l]
    stores = []
    half = lev // 2
    for start in range(0, lev, half):
        rows_b = slice(start * cols, (start + half) * cols)
        taps = [tap[dr, rows_b] for dr in range(3)]
        total = stencil(taps, weight, cols)
        for k in range(half):
            l = start + k
            rows_k = slice(k * cols, (k + 1) * cols)
            part = total[rows_k]
            if l == 0 and not first:
                part = part + forcing_ref[...]
            new = taps[1][rows_k].astype(F32) + widen(wets[l], width) * part
            if l < first:
                base_ref[...] = new
                continue
            new = new.astype(BF16)
            mixed[l - first] = new
            tokens = normalise(new)
            normed[l - first] = tokens
            pack(packed, plan[0][l : l + 1], plan[1][l : l + 1], place[l, 0], cap, tokens)
    for k, (buf, out) in enumerate(((mixed, mixed_hbm), (normed, normed_hbm))):
        store = pltpu.make_async_copy(buf, out, out_sem.at[k])
        store.start()
        stores.append(store)
    store = pltpu.make_async_copy(packed.at[pl.ds(0, cap)], packed_hbm, packed_sem)
    store.start()
    stores.append(store)
    for store in stores:
        store.wait()


def attend_kernel(others, nparts, which, first, cap, aliased, flag_ref, side_ref, *refs):
    refs = list(refs)
    take = lambda k: [refs.pop(0) for _ in range(k)]
    own_normed = take(nparts)
    own_mixed = take(nparts)
    surf = take(others) if first else []
    packed = take(others)
    whole = take(others)
    depth_ref, qkv_ref, wo_ref = take(3)
    if aliased:
        take(1)
    out_ref, q_ref, k_ref, v_ref, att_ref, buf_ref, token_ref, sem = refs
    lev, count, width = q_ref.shape
    members = others + 1
    head = width // HEADS
    pair = 2 * head
    step = pl.program_id(0)

    def keys_values(x, m):
        rows = slice(m * lev, (m + 1) * lev)
        kv = jnp.dot(x, qkv_ref[:, width:], preferred_element_type=F32).astype(BF16)
        k_ref[rows] = kv[:, :width].reshape(lev, count, width)
        v_ref[rows] = kv[:, width:].reshape(lev, count, width)

    two = which is None
    pick = lambda a, b: jnp.where(step == 0, a, b)
    if two:
        rows_d = [depth_ref[r : r + 1, :].astype(F32) for r in range(1, depth_ref.shape[0] - 1)]
        plans = [row_plan(row, lev) for row in rows_d]
        place = offsets(plans, first, lev)
        wet_row = pick(plans[0][0], plans[1][0])
        rank = pick(plans[0][1], plans[1][1])
        depth_row = pick(*rows_d)
    else:
        depth_row = depth_ref[pl.ds(side_ref[which], 1), :].astype(F32)
        plan = row_plan(depth_row, lev)
        place = offsets([plan], first, lev)
        wet_row, rank, _ = plan

    x = jnp.concatenate([p[...].reshape(-1, width) for p in own_normed], axis=0)
    q = jnp.dot(x, qkv_ref[:, 0:width], preferred_element_type=F32).astype(BF16)
    q_ref[...] = (q * (1.0 / math.sqrt(head))).astype(BF16).reshape(lev, count, width)
    keys_values(x, 0)
    for o in range(others):
        if first:
            token_ref[0] = surf[o][0]

        @pl.when(flag_ref[0] == 0)
        def _():
            buf_ref[0:cap] = packed[o][...]
            buf_ref[cap:] = jnp.zeros((buf_ref.shape[0] - cap, width), BF16)
            for l in range(first, lev):
                at = pick(place[l, 0], place[l, 1]) if two else place[l, 0]
                token_ref[l] = unpack(
                    buf_ref, wet_row[l : l + 1], rank[l : l + 1], at, cap
                )

        @pl.when(flag_ref[0] != 0)
        def _():
            copy = pltpu.make_async_copy(
                whole[o].at[:, pl.ds(pl.multiple_of(step * count, count), count)], token_ref.at[pl.ds(first, lev - first)], sem
            )
            copy.start()
            copy.wait()

        keys_values(token_ref[...].reshape(-1, width), o + 1)

    nq, nk = lev * GROUP, members * lev * GROUP
    groups = count // GROUP
    lanes_n = lev * GROUP
    cell = lax.broadcasted_iota(jnp.int32, (groups, count), 1)
    mine = (cell // GROUP == lax.broadcasted_iota(jnp.int32, (groups, count), 0)).astype(F32)
    spread = lax.broadcasted_iota(jnp.int32, (count, lanes_n), 0) % GROUP
    spread = (spread == lax.broadcasted_iota(jnp.int32, (count, lanes_n), 1) % GROUP).astype(F32)
    key_depth = jnp.dot(
        (mine * depth_row).astype(BF16), spread.astype(BF16), preferred_element_type=F32
    )
    key_level = lax.broadcasted_iota(jnp.int32, (groups, lanes_n), 1) // GROUP
    key_bias = jnp.where(key_depth > key_level.astype(F32), 0.0, NEG)
    qc = lax.broadcasted_iota(jnp.int32, (nq, nk), 0) % GROUP
    kc = lax.broadcasted_iota(jnp.int32, (nq, nk), 1) % GROUP
    same = jnp.where(qc == kc, 0.0, NEG)
    lane = lax.broadcasted_iota(jnp.int32, (1, pair), 1)
    low = (lane < head).astype(F32).astype(BF16)
    high = (lane >= head).astype(F32).astype(BF16)
    for g in range(groups):
        cells = slice(g * GROUP, (g + 1) * GROUP)
        bias = same + jnp.concatenate([key_bias[g : g + 1]] * members, axis=1)
        bias = jnp.concatenate([bias, bias], axis=0)
        for h in range(HEADS // 2):
            lanes = slice(h * pair, (h + 1) * pair)
            q = q_ref[:, cells, lanes].reshape(nq, pair)
            q = jnp.concatenate([q * low, q * high], axis=0)
            k = k_ref[:, cells, lanes].reshape(nk, pair)
            v = v_ref[:, cells, lanes].reshape(nk, pair)
            s = lax.dot_general(q, k, (((1,), (1,)), ((), ())), preferred_element_type=F32) + bias
            p = jnp.exp(s - jnp.max(s, axis=-1, keepdims=True))
            norm = 1.0 / jnp.sum(p, axis=-1, keepdims=True)
            o = jnp.dot(p.astype(BF16), v, preferred_element_type=F32) * norm
            o = jnp.where(lane < head, o[:nq], o[nq:])
            att_ref[:, cells, lanes] = o.astype(BF16).reshape(lev, GROUP, pair)
    proj = jnp.dot(att_ref[...].reshape(-1, width), wo_ref[...], preferred_element_type=F32)
    base = jnp.concatenate([p[...].reshape(-1, width) for p in own_mixed], axis=0).astype(F32)
    deep = column(depth_row)
    for l in range(lev):
        rows = slice(l * count, (l + 1) * count)
        wet = widen((deep > l).astype(F32), width)
        out_ref[0, l] = (base[rows] + wet * proj[rows]).astype(BF16)


def attend(
    flag, side, normed, mixed, surf, packed, whole, depth, qkv_weight, out_weight, which, out, shape
):
    others, nparts = len(packed), len(mixed)
    lev = sum(p.shape[0] for p in mixed)
    width = shape[-1]
    rows, cols = depth.shape
    cap = packed[0].shape[0]
    first = 1 if surf else 0
    steps = rows - 2 if which is None else 1
    row_of = lambda i, s: i + 1 if which is None else s[which]
    surf_at = 0 if which is None else rows - 2
    full2 = lambda a: pl.BlockSpec(a.shape, lambda i, *_: (0, 0))
    block = lambda n, at: pl.BlockSpec((n, cols, width), lambda i, *_: (0, i + at, 0))
    part = [block(p.shape[0], surf_at if first and k == 0 else 0) for k, p in enumerate(mixed)]
    hbm = pl.BlockSpec(memory_space=pl.ANY)
    in_specs = part * 2
    in_specs += [block(1, surf_at)] * len(surf)
    in_specs += [full2(p) for p in packed]
    in_specs += [hbm] * others
    in_specs += [full2(depth), full2(qkv_weight), full2(out_weight)]
    args = normed + mixed + surf + packed + whole + [depth, qkv_weight, out_weight]
    alias = {}
    if out is not None:
        in_specs.append(hbm)
        alias = {len(args) + 2: 0}
        args.append(out)
    tokens = lev * cols * steps
    members = others + 1
    return pl.pallas_call(
        functools.partial(attend_kernel, others, nparts, which, first, cap, out is not None),
        grid_spec=pltpu.PrefetchScalarGridSpec(
            num_scalar_prefetch=2,
            grid=(steps,),
            in_specs=in_specs,
            out_specs=pl.BlockSpec(
                (1, lev, cols, width), lambda i, f, s: (0, 0, row_of(i, s), 0)
            ),
            scratch_shapes=[
                pltpu.VMEM((lev, cols, width), BF16),
                pltpu.VMEM((members * lev, cols, width), BF16),
                pltpu.VMEM((members * lev, cols, width), BF16),
                pltpu.VMEM((lev, cols, width), BF16),
                pltpu.VMEM((cap + cols + 16, width), BF16),
                pltpu.VMEM((lev, cols, width), BF16),
                pltpu.SemaphoreType.DMA,
            ],
        ),
        out_shape=jax.ShapeDtypeStruct(shape, BF16),
        input_output_aliases=alias,
        compiler_params=params(20 if members <= 2 else 48, 1),
        cost_estimate=cost(tokens * width * width * 8 * (members + 2), tokens * width * 2 * 5),
        name="attend",
    )(flag, side, *args)


def body(
    atm_latent,
    ocean_state,
    depth,
    src_blocks,
    live,
    remap_weight,
    conv_weight,
    qkv_weight,
    out_weight,
):
    _, lev, cells, width = ocean_state.shape
    cols = remap_weight.shape[2]
    rows = cells // cols
    inner = cells - 2 * cols
    own = atm_latent.shape[1]
    atm_blk = own // cols
    tiles = lax.axis_size("tile")
    members = lax.axis_size("mem")
    tile = lax.axis_index("tile")

    def swap(x, first):
        pairs = [(i, i + 1) for i in range(first, tiles - 1, 2)]
        return lax.ppermute(x, "tile", pairs + [(b, a) for a, b in pairs])

    def exchange(x):
        return [
            lax.ppermute(x, "mem", [(i, (i + k) % members) for i in range(members)])
            for k in range(1, members)
        ]

    odd = tile % 2
    side = jnp.stack([(1 - odd) * (rows - 1), odd * (rows - 1)]).astype(jnp.int32)
    depth = depth.reshape(rows, cols)
    deep_cap = capacity((lev - 1) * inner, 0.5625)
    near_cap = capacity((lev - 1) * cols, 0.605)
    far_cap = capacity(lev * cols, 0.65625)

    hbm = pl.BlockSpec(memory_space=pltpu.HBM)
    vmem = pl.BlockSpec(memory_space=pltpu.VMEM)
    smem = pl.BlockSpec(memory_space=pltpu.SMEM)
    tok = lambda *s: jax.ShapeDtypeStruct((*s, width), BF16)
    row_f32 = jax.ShapeDtypeStruct((cols, width), F32)
    conv_flops = lambda n, c: 2 * 9 * n * c * width * width
    dma = pltpu.SemaphoreType.DMA
    slack = cols + 16
    full = lambda a: pl.BlockSpec(a.shape, lambda i, *_: (0,) * a.ndim)
    state_row = lambda k: pl.BlockSpec((1, lev, cols, width), lambda i, s: (0, 0, s[k], 0))

    off_atm = swap(atm_latent, 1)
    on_msg, off_msg, flag = pl.pallas_call(
        functools.partial(prep_kernel, (deep_cap, near_cap, far_cap)),
        grid_spec=pltpu.PrefetchScalarGridSpec(
            num_scalar_prefetch=1,
            grid=(1,),
            in_specs=[state_row(0), state_row(1), full(atm_latent), full(depth)],
            out_specs=[
                pl.BlockSpec((lev * cols + own, width), lambda i, s: (0, 0)),
                pl.BlockSpec((lev * cols, width), lambda i, s: (0, 0)),
                smem,
            ],
        ),
        out_shape=[
            tok(lev * cols + own),
            tok(lev * cols),
            jax.ShapeDtypeStruct((1,), jnp.int32),
        ],
        compiler_params=params(16, 1),
        cost_estimate=cost(lev * cols * width * 4, lev * cols * width * 10),
        name="prep",
    )(side, ocean_state, ocean_state, atm_latent, depth)
    off_halo = swap(off_msg, 1)
    on_halo = swap(on_msg, 0)

    deep_mixed, deep_normed, deep_packed, base = pl.pallas_call(
        functools.partial(inner_kernel, deep_cap),
        in_specs=[vmem, vmem, vmem],
        out_specs=[hbm, hbm, hbm, vmem],
        out_shape=[
            tok(lev - 1, inner),
            tok(lev - 1, inner),
            tok(deep_cap),
            jax.ShapeDtypeStruct((inner, width), F32),
        ],
        scratch_shapes=[
            pltpu.VMEM((lev - 1, inner, width), BF16),
            pltpu.VMEM((lev - 1, inner, width), BF16),
            pltpu.VMEM((deep_cap + slack, width), BF16),
            dma((lev - 1, 2)),
            dma,
        ],
        compiler_params=params(20),
        cost_estimate=cost(conv_flops(lev, inner), lev * inner * width * 8),
        name="inner",
    )(ocean_state, depth, conv_weight)
    deep_others = exchange(deep_packed)

    def row_conv(which, first, cap, halo, forcing):
        n = lev - first
        extra = [] if forcing is None else [forcing]
        return pl.pallas_call(
            functools.partial(row_kernel, cap, first, which),
            in_specs=[smem] + [vmem] * (4 + len(extra)),
            out_specs=[hbm] * 3 + [vmem] * first,
            out_shape=[tok(n, cols), tok(n, cols), tok(cap)] + [row_f32] * first,
            scratch_shapes=[
                pltpu.VMEM((3, lev * cols, width), BF16),
                pltpu.VMEM((n, cols, width), BF16),
                pltpu.VMEM((n, cols, width), BF16),
                pltpu.VMEM((cap + slack, width), BF16),
                dma((2,)),
                dma,
            ],
            compiler_params=params(20),
            cost_estimate=cost(conv_flops(lev, cols), lev * cols * width * 16),
            name="row",
        )(side, ocean_state, depth, conv_weight, halo, *extra)

    near_mixed, near_normed, near_packed, near_base = row_conv(0, 1, near_cap, on_halo, None)

    ids = jnp.clip(src_blocks - (tile - R) * atm_blk, 0, 3 * atm_blk - 1)
    surf_mixed, surf_normed, far_forcing = pl.pallas_call(
        surface_kernel,
        in_specs=[smem] * 3 + [vmem] * 7,
        out_specs=[pl.BlockSpec((1, inner + cols, width), lambda *_: (0, 0, 0))] * 2 + [vmem],
        out_shape=[tok(1, inner + cols), tok(1, inner + cols), row_f32],
        scratch_shapes=[pltpu.VMEM((3 * own, width), BF16), pltpu.VMEM((rows, cols, width), F32)],
        compiler_params=params(20),
        cost_estimate=cost(conv_flops(1, inner), cells * width * 16),
        name="surface",
    )(ids, live, side, base, near_base, depth, on_halo, off_atm, atm_latent, remap_weight)
    surf_others = exchange(surf_normed)
    near_others = exchange(near_packed)

    far_mixed, far_normed, far_packed = row_conv(1, 0, far_cap, off_halo, far_forcing)
    far_others = exchange(far_packed)

    deep_whole, near_whole, far_whole = lax.cond(
        flag[0] > 0,
        lambda *a: tuple(exchange(x) for x in a),
        lambda *a: tuple([x] * (members - 1) for x in a),
        deep_normed,
        near_normed,
        far_normed,
    )
    shape = ocean_state.shape
    weights = (depth, qkv_weight, out_weight)
    out = None
    for which, normed, mixed, surf, packed, whole in (
        (
            None,
            [surf_normed, deep_normed],
            [surf_mixed, deep_mixed],
            surf_others,
            deep_others,
            deep_whole,
        ),
        (
            0,
            [surf_normed, near_normed],
            [surf_mixed, near_mixed],
            surf_others,
            near_others,
            near_whole,
        ),
        (1, [far_normed], [far_mixed], [], far_others, far_whole),
    ):
        out = attend(
            flag, side, normed, mixed, surf, packed, whole, *weights, which, out, shape
        )
    return out


def solution(mesh):
    return jax.shard_map(
        body,
        mesh=mesh,
        in_specs=(
            P("mem", "tile", None),
            P("mem", None, "tile", None),
            P("tile"),
            P("tile", None),
            P("tile"),
            P("tile", None, None, None),
            P(),
            P(),
            P(),
        ),
        out_specs=P("mem", None, "tile", None),
        check_vma=False,
    )
```

```python
import functools
import math

import jax
import jax.numpy as jnp
from jax import lax
from jax.experimental import pallas as pl
from jax.experimental.pallas import tpu as pltpu
from jax.sharding import PartitionSpec as P

HEADS = 4
R = 1
GROUP = 16
EPS = 1e-06
NEG = -1e30
F32 = jnp.float32
BF16 = jnp.bfloat16
MIB = 1024 * 1024


def params(mib, steps=0):
    return pltpu.CompilerParams(
        dimension_semantics=("arbitrary",) * steps if steps else None, vmem_limit_bytes=mib * MIB
    )


def cost(flops, nbytes):
    return pl.CostEstimate(flops=int(flops), bytes_accessed=int(nbytes), transcendentals=0)


def capacity(tokens, share):
    return -(-int(tokens * share) // 16) * 16


def row_plan(depth_row, lev):
    cols = depth_row.shape[1]
    level = lax.broadcasted_iota(jnp.int32, (lev, cols), 0).astype(F32)
    wet = (depth_row > level).astype(F32)
    upper = (
        lax.broadcasted_iota(jnp.int32, (cols, cols), 0)
        < lax.broadcasted_iota(jnp.int32, (cols, cols), 1)
    )
    upper = upper.astype(F32).astype(BF16)
    rank = jnp.dot(wet.astype(BF16), upper, preferred_element_type=F32)
    counts = [jnp.sum(wet[l : l + 1]).astype(jnp.int32) for l in range(lev)]
    return wet, rank, counts


def offsets(plans, first, lev):
    at, place = jnp.int32(0), {}
    for l in range(first, lev):
        for r, plan in enumerate(plans):
            place[l, r] = at
            at = at + plan[2][l]
    return place


def segment(wet, rank, offset, cap):
    cols = wet.shape[1]
    base = jnp.minimum((offset // 16) * 16, cap)
    target = jnp.where(wet > 0, rank + (offset - base).astype(F32), -1.0)
    slot = lax.broadcasted_iota(jnp.int32, (cols + 16, cols), 0).astype(F32)
    return pl.multiple_of(base, 16), (slot == target).astype(F32).astype(BF16)


def pack(buf_ref, wet, rank, offset, cap, tokens):
    base, hot = segment(wet, rank, offset, cap)
    rows = jnp.dot(hot, tokens, preferred_element_type=F32).astype(BF16)
    head = pl.ds(base, 16)
    buf_ref[head, :] = buf_ref[head, :] + rows[:16]
    buf_ref[pl.ds(pl.multiple_of(base + 16, 16), rows.shape[0] - 16), :] = rows[16:]


def unpack(buf_ref, wet, rank, offset, cap):
    base, hot = segment(wet, rank, offset, cap)
    rows = buf_ref[pl.ds(base, hot.shape[0]), :]
    return lax.dot_general(
        hot, rows, (((0,), (0,)), ((), ())), preferred_element_type=F32
    ).astype(BF16)


def column(depth_row):
    cols = depth_row.shape[1]
    return jnp.broadcast_to(depth_row, (cols, cols)).T


def widen(x, width):
    return jnp.concatenate([x] * (width // x.shape[1]), axis=1)


def stencil(taps, weight_ref, cols):
    count, width = taps[0].shape
    x = jnp.concatenate(taps, axis=1)
    sums = [
        jnp.dot(x, weight_ref[:, dc].reshape(3 * width, -1), preferred_element_type=F32)
        for dc in range(3)
    ]
    col = lax.broadcasted_iota(jnp.int32, (count, 1), 0) % cols
    left = jnp.where(col == 0, 0.0, pltpu.roll(sums[0], 1, axis=0))
    right = jnp.where(col == cols - 1, 0.0, pltpu.roll(sums[2], count - 1, axis=0))
    return sums[1] + left + right


def normalise(mixed):
    mf = mixed.astype(F32)
    mean = jnp.mean(mf * mf, axis=-1, keepdims=True)
    return (mf * lax.rsqrt(mean + EPS)).astype(BF16)


def prep_kernel(caps, side_ref, near_ref, far_ref, atm_ref, depth_ref, on_ref, off_ref, flag_ref):
    _, lev, cols, width = near_ref.shape
    rows = depth_ref.shape[0]
    for block, row, out in ((near_ref, 0, on_ref), (far_ref, 1, off_ref)):
        deep = column(depth_ref[pl.ds(side_ref[row], 1), :].astype(F32))
        for l in range(lev):
            wet = (deep > l).astype(F32).astype(BF16)
            out[l * cols : (l + 1) * cols] = block[0, l] * widen(wet, width)
    on_ref[lev * cols :] = atm_ref[0]
    d = depth_ref[...].astype(F32)
    counts = [
        jnp.sum(jnp.maximum(d[1 : rows - 1] - 1.0, 0.0)),
        jnp.sum(d[0:1]),
        jnp.sum(d[rows - 1 :]),
    ]
    over = jnp.int32(0)
    for count, cap in zip(counts, caps):
        over = over | (count > cap).astype(jnp.int32)
    flag_ref[0] = over


def inner_kernel(
    cap,
    state,
    depth_ref,
    weight,
    mixed_hbm,
    normed_hbm,
    packed_hbm,
    mixed,
    normed,
    packed,
    out_sem,
    packed_sem,
):
    _, lev, cells, width = state.shape
    rows, cols = depth_ref.shape
    packed[...] = jnp.zeros_like(packed)
    d = depth_ref[...].astype(F32)
    plans = [row_plan(d[r : r + 1], lev) for r in range(1, rows - 1)]
    place = offsets(plans, 1, lev)
    deep = jnp.concatenate([column(d[r : r + 1]) for r in range(rows)], axis=0)
    count = cells - 2 * cols
    stores = []
    for l in range(1, lev):
        wet = (deep > l).astype(F32)
        x = state[0, l] * widen(wet.astype(BF16), width)
        taps = [x[dr * cols : dr * cols + count] for dr in range(3)]
        total = stencil(taps, weight, cols)
        new = taps[1].astype(F32) + widen(wet[cols : cols + count], width) * total
        new = new.astype(BF16)
        mixed[l - 1] = new
        tokens = normalise(new)
        normed[l - 1] = tokens
        for k, (buf, out) in enumerate(((mixed, mixed_hbm), (normed, normed_hbm))):
            store = pltpu.make_async_copy(buf.at[l - 1], out.at[l - 1], out_sem.at[l - 1, k])
            store.start()
            stores.append(store)
        for r, plan in enumerate(plans):
            pack(
                packed,
                plan[0][l : l + 1],
                plan[1][l : l + 1],
                place[l, r],
                cap,
                tokens[r * cols : (r + 1) * cols],
            )
        if l == lev - 1:
            store = pltpu.make_async_copy(packed.at[pl.ds(0, cap)], packed_hbm, packed_sem)
            store.start()
            stores.append(store)
    for store in stores:
        store.wait()


def surface_kernel(
    ids_ref,
    live_ref,
    side_ref,
    state,
    depth_ref,
    weight,
    on_hbm,
    off_hbm,
    atm_hbm,
    remap_hbm,
    mixed_ref,
    normed_ref,
    edge_ref,
    window,
    remap,
    forcing_ref,
    sem,
):
    rows, cols = depth_ref.shape
    _, own, width = atm_hbm.shape
    cells = state.shape[2]
    blocks, pairs = remap_hbm.shape[0], remap_hbm.shape[1]
    on_at = jnp.where(side_ref[0] == 0, 0, 2 * own)
    copies = [
        pltpu.make_async_copy(
            on_hbm.at[pl.ds(on_hbm.shape[0] - own, own)],
            window.at[pl.ds(pl.multiple_of(on_at, own), own)],
            sem.at[0],
        ),
        pltpu.make_async_copy(
            off_hbm.at[0], window.at[pl.ds(pl.multiple_of(2 * own - on_at, own), own)], sem.at[1]
        ),
        pltpu.make_async_copy(atm_hbm.at[0], window.at[pl.ds(own, own)], sem.at[2]),
        pltpu.make_async_copy(remap_hbm, remap, sem.at[3]),
    ]
    for copy in copies:
        copy.start()
    d = depth_ref[...].astype(F32)
    wet = (jnp.concatenate([column(d[r : r + 1]) for r in range(rows)], axis=0) > 0).astype(F32)
    x = state[0, 0] * widen(wet.astype(BF16), width)
    count = cells - 2 * cols
    taps = [x[dr * cols : dr * cols + count] for dr in range(3)]
    total = stencil(taps, weight, cols)
    for copy in copies:
        copy.wait()
    for b in range(blocks):
        acc = jnp.zeros((cols, width), F32)
        for p in range(pairs):
            on = (p < live_ref[b]).astype(F32)
            start = pl.multiple_of(ids_ref[b, p] * cols, cols)
            acc = acc + on * jnp.dot(
                remap[b, p], window[pl.ds(start, cols), :], preferred_element_type=F32
            )
        forcing_ref[b * cols : (b + 1) * cols] = acc
    total = total + forcing_ref[cols : cols + count]
    new = (taps[1].astype(F32) + widen(wet[cols : cols + count], width) * total).astype(BF16)
    mixed_ref[0] = new
    normed_ref[0] = normalise(new)
    edge_ref[0:cols] = forcing_ref[0:cols]
    edge_ref[cols : 2 * cols] = forcing_ref[cols + count :]


def edge_kernel(
    cap,
    side_ref,
    state,
    depth_ref,
    weight_hbm,
    on_hbm,
    off_hbm,
    forcing_hbm,
    mixed_hbm,
    normed_hbm,
    top_hbm,
    low_hbm,
    weight,
    halos,
    forcing,
    mixed,
    normed,
    top,
    low,
    in_sem,
    out_sem,
    packed_sem,
):
    _, lev, cells, width = state.shape
    rows, cols = depth_ref.shape
    on_at = jnp.where(side_ref[0] == 0, 0, 1)
    copies = [
        pltpu.make_async_copy(weight_hbm, weight, in_sem.at[0]),
        pltpu.make_async_copy(on_hbm.at[pl.ds(0, lev * cols)], halos.at[on_at], in_sem.at[1]),
        pltpu.make_async_copy(off_hbm, halos.at[1 - on_at], in_sem.at[2]),
        pltpu.make_async_copy(forcing_hbm, forcing, in_sem.at[3]),
    ]
    for copy in copies:
        copy.start()
    top[...] = jnp.zeros_like(top)
    low[...] = jnp.zeros_like(low)
    d = depth_ref[...].astype(F32)
    plans = [row_plan(d[r : r + 1], lev) for r in (0, rows - 1)]
    places = [offsets([plan], 0, lev) for plan in plans]
    deep = jnp.concatenate([column(d[r : r + 1]) for r in range(rows)], axis=0)
    for copy in copies:
        copy.wait()
    stores = []
    for l in range(lev):
        wet = (deep > l).astype(F32)
        x = state[0, l] * widen(wet.astype(BF16), width)
        halo = slice(l * cols, (l + 1) * cols)
        up = [halos[0, halo], x[0:cols], x[cols : 2 * cols]]
        down = [x[cells - 2 * cols : cells - cols], x[cells - cols :], halos[1, halo]]
        taps = [jnp.concatenate([a, b], axis=0) for a, b in zip(up, down)]
        total = stencil(taps, weight, cols)
        if l == 0:
            total = total + forcing[...]
        edge_wet = jnp.concatenate([wet[0:cols], wet[cells - cols :]], axis=0)
        new = (taps[1].astype(F32) + widen(edge_wet, width) * total).astype(BF16)
        mixed[l] = new
        tokens = normalise(new)
        normed[l] = tokens
        for k, (buf, out) in enumerate(((mixed, mixed_hbm), (normed, normed_hbm))):
            store = pltpu.make_async_copy(buf.at[l], out.at[l], out_sem.at[l, k])
            store.start()
            stores.append(store)
        for r, buf in enumerate((top, low)):
            pack(
                buf,
                plans[r][0][l : l + 1],
                plans[r][1][l : l + 1],
                places[r][l, 0],
                cap,
                tokens[r * cols : (r + 1) * cols],
            )
    for k, (buf, out) in enumerate(((top, top_hbm), (low, low_hbm))):
        store = pltpu.make_async_copy(buf.at[pl.ds(0, cap)], out, packed_sem.at[k])
        store.start()
        stores.append(store)
    for store in stores:
        store.wait()


def attend_kernel(others, nparts, rows_of, first, cap, aliased, flag_ref, *refs):
    refs = list(refs)
    take = lambda k: [refs.pop(0) for _ in range(k)]
    own_normed = take(nparts)
    own_mixed = take(nparts)
    surf = take(others) if first else []
    packed = take(others)
    whole = take(others)
    depth_ref, qkv_ref, wo_ref = take(3)
    if aliased:
        take(1)
    out_ref, q_ref, k_ref, v_ref, att_ref, buf_ref, token_ref, sem = refs
    lev, count, width = q_ref.shape
    members = others + 1
    head = width // HEADS
    pair = 2 * head
    step = pl.program_id(0)

    def keys_values(x, m):
        rows = slice(m * lev, (m + 1) * lev)
        kv = jnp.dot(x, qkv_ref[:, width:], preferred_element_type=F32).astype(BF16)
        k_ref[rows] = kv[:, :width].reshape(lev, count, width)
        v_ref[rows] = kv[:, width:].reshape(lev, count, width)

    two = len(rows_of) == 2
    pick = lambda a, b: jnp.where(step == 0, a, b)
    d = depth_ref[...].astype(F32)
    rows_d = [d[r : r + 1] for r in rows_of]
    plans = [row_plan(row, lev) for row in rows_d]
    place = offsets(plans, first, lev)
    wet_row, rank, _ = plans[0]
    depth_row = rows_d[0]
    if two:
        wet_row, rank = pick(wet_row, plans[1][0]), pick(rank, plans[1][1])
        depth_row = pick(*rows_d)

    x = jnp.concatenate([p[...].reshape(-1, width) for p in own_normed], axis=0)
    q = jnp.dot(x, qkv_ref[:, 0:width], preferred_element_type=F32).astype(BF16)
    q_ref[...] = (q * (1.0 / math.sqrt(head))).astype(BF16).reshape(lev, count, width)
    keys_values(x, 0)
    for o in range(others):
        if first:
            token_ref[0] = surf[o][0]

        @pl.when(flag_ref[0] == 0)
        def _():
            buf_ref[0:cap] = packed[o][...]
            buf_ref[cap:] = jnp.zeros((buf_ref.shape[0] - cap, width), BF16)
            for l in range(first, lev):
                at = pick(place[l, 0], place[l, 1]) if two else place[l, 0]
                token_ref[l] = unpack(
                    buf_ref, wet_row[l : l + 1], rank[l : l + 1], at, cap
                )

        @pl.when(flag_ref[0] != 0)
        def _():
            which = step if two else (0 if rows_of[0] == 0 else 1)
            copy = pltpu.make_async_copy(
                whole[o].at[:, pl.ds(which * count, count)], token_ref.at[pl.ds(first, lev - first)], sem
            )
            copy.start()
            copy.wait()

        keys_values(token_ref[...].reshape(-1, width), o + 1)

    nq, nk = lev * GROUP, members * lev * GROUP
    groups = count // GROUP
    lanes_n = lev * GROUP
    cell = lax.broadcasted_iota(jnp.int32, (groups, count), 1)
    mine = (cell // GROUP == lax.broadcasted_iota(jnp.int32, (groups, count), 0)).astype(F32)
    spread = lax.broadcasted_iota(jnp.int32, (count, lanes_n), 0) % GROUP
    spread = (spread == lax.broadcasted_iota(jnp.int32, (count, lanes_n), 1) % GROUP).astype(F32)
    key_depth = jnp.dot(
        (mine * depth_row).astype(BF16), spread.astype(BF16), preferred_element_type=F32
    )
    key_level = lax.broadcasted_iota(jnp.int32, (groups, lanes_n), 1) // GROUP
    key_bias = jnp.where(key_depth > key_level.astype(F32), 0.0, NEG)
    qc = lax.broadcasted_iota(jnp.int32, (nq, nk), 0) % GROUP
    kc = lax.broadcasted_iota(jnp.int32, (nq, nk), 1) % GROUP
    same = jnp.where(qc == kc, 0.0, NEG)
    lane = lax.broadcasted_iota(jnp.int32, (1, pair), 1)
    low = (lane < head).astype(F32).astype(BF16)
    high = (lane >= head).astype(F32).astype(BF16)
    for g in range(groups):
        cells = slice(g * GROUP, (g + 1) * GROUP)
        bias = same + jnp.concatenate([key_bias[g : g + 1]] * members, axis=1)
        bias = jnp.concatenate([bias, bias], axis=0)
        for h in range(HEADS // 2):
            lanes = slice(h * pair, (h + 1) * pair)
            q = q_ref[:, cells, lanes].reshape(nq, pair)
            q = jnp.concatenate([q * low, q * high], axis=0)
            k = k_ref[:, cells, lanes].reshape(nk, pair)
            v = v_ref[:, cells, lanes].reshape(nk, pair)
            s = lax.dot_general(q, k, (((1,), (1,)), ((), ())), preferred_element_type=F32) + bias
            p = jnp.exp(s - jnp.max(s, axis=-1, keepdims=True))
            norm = 1.0 / jnp.sum(p, axis=-1, keepdims=True)
            o = jnp.dot(p.astype(BF16), v, preferred_element_type=F32) * norm
            o = jnp.where(lane < head, o[:nq], o[nq:])
            att_ref[:, cells, lanes] = o.astype(BF16).reshape(lev, GROUP, pair)
    proj = jnp.dot(att_ref[...].reshape(-1, width), wo_ref[...], preferred_element_type=F32)
    base = jnp.concatenate([p[...].reshape(-1, width) for p in own_mixed], axis=0).astype(F32)
    deep = column(depth_row)
    for l in range(lev):
        rows = slice(l * count, (l + 1) * count)
        wet = widen((deep > l).astype(F32), width)
        out_ref[0, l] = (base[rows] + wet * proj[rows]).astype(BF16)


def attend(flag, normed, mixed, surf, packed, whole, depth, qkv_weight, out_weight, rows_of, out, shape):
    others, nparts = len(packed), len(mixed)
    lev = sum(p.shape[0] for p in mixed)
    width = shape[-1]
    rows, cols = depth.shape
    cap = packed[0].shape[0]
    first = 1 if surf else 0
    shift = 1 if rows_of[0] == rows - 1 else 0
    index = lambda i, *_: (0, i + shift, 0)
    full2 = lambda a: pl.BlockSpec(a.shape, lambda i, *_: (0, 0))
    part = [pl.BlockSpec((p.shape[0], cols, width), index) for p in mixed]
    hbm = pl.BlockSpec(memory_space=pl.ANY)
    in_specs = part * 2
    in_specs += [pl.BlockSpec((1, cols, width), index)] * len(surf)
    in_specs += [full2(p) for p in packed]
    in_specs += [hbm] * others
    in_specs += [full2(depth), full2(qkv_weight), full2(out_weight)]
    args = normed + mixed + surf + packed + whole + [depth, qkv_weight, out_weight]
    alias = {}
    if out is not None:
        in_specs.append(hbm)
        alias = {len(args) + 1: 0}
        args.append(out)
    tokens = lev * cols * len(rows_of)
    members = others + 1
    return pl.pallas_call(
        functools.partial(
            attend_kernel, others, nparts, tuple(rows_of), first, cap, out is not None
        ),
        grid_spec=pltpu.PrefetchScalarGridSpec(
            num_scalar_prefetch=1,
            grid=(len(rows_of),),
            in_specs=in_specs,
            out_specs=pl.BlockSpec(
                (1, lev, cols, width), lambda i, *_: (0, 0, i + rows_of[0], 0)
            ),
            scratch_shapes=[
                pltpu.VMEM((lev, cols, width), BF16),
                pltpu.VMEM((members * lev, cols, width), BF16),
                pltpu.VMEM((members * lev, cols, width), BF16),
                pltpu.VMEM((lev, cols, width), BF16),
                pltpu.VMEM((cap + cols + 16, width), BF16),
                pltpu.VMEM((lev, cols, width), BF16),
                pltpu.SemaphoreType.DMA,
            ],
        ),
        out_shape=jax.ShapeDtypeStruct(shape, BF16),
        input_output_aliases=alias,
        compiler_params=params(20 if members <= 2 else 48, 1),
        cost_estimate=cost(tokens * width * width * 8 * (members + 2), tokens * width * 2 * 5),
        name="attend",
    )(flag, *args)


def body(
    atm_latent,
    ocean_state,
    depth,
    src_blocks,
    live,
    remap_weight,
    conv_weight,
    qkv_weight,
    out_weight,
):
    _, lev, cells, width = ocean_state.shape
    cols = remap_weight.shape[2]
    rows = cells // cols
    inner = cells - 2 * cols
    own = atm_latent.shape[1]
    atm_blk = own // cols
    tiles = lax.axis_size("tile")
    members = lax.axis_size("mem")
    tile = lax.axis_index("tile")

    def swap(x, first):
        pairs = [(i, i + 1) for i in range(first, tiles - 1, 2)]
        return lax.ppermute(x, "tile", pairs + [(b, a) for a, b in pairs])

    def exchange(x):
        return [
            lax.ppermute(x, "mem", [(i, (i + k) % members) for i in range(members)])
            for k in range(1, members)
        ]

    odd = tile % 2
    side = jnp.stack([(1 - odd) * (rows - 1), odd * (rows - 1)]).astype(jnp.int32)
    depth = depth.reshape(rows, cols)
    deep_cap = capacity((lev - 1) * inner, 0.5625)
    edge_cap = capacity(lev * cols, 0.65625)

    hbm = pl.BlockSpec(memory_space=pltpu.HBM)
    anywhere = pl.BlockSpec(memory_space=pl.ANY)
    vmem = pl.BlockSpec(memory_space=pltpu.VMEM)
    smem = pl.BlockSpec(memory_space=pltpu.SMEM)
    tok = lambda *s: pltpu.HBM((*s, width), BF16)
    stay = lambda x: pltpu.with_memory_space_constraint(x, pltpu.HBM)
    conv_flops = lambda n, c: 2 * 9 * n * c * width * width
    dma = pltpu.SemaphoreType.DMA
    slack = cols + 16
    full = lambda a: pl.BlockSpec(a.shape, lambda i, *_: (0,) * a.ndim)
    state_row = lambda k: pl.BlockSpec((1, lev, cols, width), lambda i, s: (0, 0, s[k], 0))

    off_atm = swap(atm_latent, 1)
    on_msg, off_msg, flag = pl.pallas_call(
        functools.partial(prep_kernel, (deep_cap, edge_cap, edge_cap)),
        grid_spec=pltpu.PrefetchScalarGridSpec(
            num_scalar_prefetch=1,
            grid=(1,),
            in_specs=[state_row(0), state_row(1), full(atm_latent), full(depth)],
            out_specs=[
                pl.BlockSpec((lev * cols + own, width), lambda i, s: (0, 0)),
                pl.BlockSpec((lev * cols, width), lambda i, s: (0, 0)),
                smem,
            ],
        ),
        out_shape=[
            tok(lev * cols + own),
            tok(lev * cols),
            jax.ShapeDtypeStruct((1,), jnp.int32),
        ],
        compiler_params=params(16, 1),
        cost_estimate=cost(lev * cols * width * 4, lev * cols * width * 10),
        name="prep",
    )(side, stay(ocean_state), stay(ocean_state), stay(atm_latent), stay(depth))
    off_halo = swap(off_msg, 1)
    on_halo = swap(on_msg, 0)

    deep_mixed, deep_normed, deep_packed = pl.pallas_call(
        functools.partial(inner_kernel, deep_cap),
        in_specs=[vmem, vmem, vmem],
        out_specs=[hbm] * 3,
        out_shape=[tok(lev - 1, inner), tok(lev - 1, inner), tok(deep_cap)],
        scratch_shapes=[
            pltpu.VMEM((lev - 1, inner, width), BF16),
            pltpu.VMEM((lev - 1, inner, width), BF16),
            pltpu.VMEM((deep_cap + slack, width), BF16),
            dma((lev - 1, 2)),
            dma,
        ],
        compiler_params=params(20),
        cost_estimate=cost(conv_flops(lev, inner), lev * inner * width * 8),
        name="inner",
    )(ocean_state, depth, conv_weight)
    deep_others = exchange(deep_packed)

    ids = jnp.clip(src_blocks - (tile - R) * atm_blk, 0, 3 * atm_blk - 1)
    whole_spec = lambda *sh: pl.BlockSpec(sh, lambda *_: (0,) * len(sh))
    surf_mixed, surf_normed, edge_forcing = pl.pallas_call(
        surface_kernel,
        in_specs=[smem] * 3 + [vmem] * 3 + [anywhere] * 2 + [hbm] * 2,
        out_specs=[whole_spec(1, inner, width)] * 2 + [whole_spec(2 * cols, width)],
        out_shape=[tok(1, inner), tok(1, inner), pltpu.HBM((2 * cols, width), F32)],
        scratch_shapes=[
            pltpu.VMEM((3 * own, width), BF16),
            pltpu.VMEM(remap_weight.shape, BF16),
            pltpu.VMEM((cells, width), F32),
            dma((4,)),
        ],
        compiler_params=params(20),
        cost_estimate=cost(conv_flops(1, inner), cells * width * 16),
        name="surface",
    )(
        ids,
        live,
        side,
        ocean_state,
        depth,
        conv_weight,
        on_halo,
        off_atm,
        stay(atm_latent),
        stay(remap_weight),
    )
    surf_others = exchange(surf_normed)

    edge_mixed, edge_normed, top_packed, low_packed = pl.pallas_call(
        functools.partial(edge_kernel, edge_cap),
        in_specs=[smem, vmem, vmem, hbm, anywhere, anywhere, hbm],
        out_specs=[hbm] * 4,
        out_shape=[tok(lev, 2 * cols), tok(lev, 2 * cols), tok(edge_cap), tok(edge_cap)],
        scratch_shapes=[
            pltpu.VMEM(conv_weight.shape, BF16),
            pltpu.VMEM((2, lev * cols, width), BF16),
            pltpu.VMEM((2 * cols, width), F32),
            pltpu.VMEM((lev, 2 * cols, width), BF16),
            pltpu.VMEM((lev, 2 * cols, width), BF16),
            pltpu.VMEM((edge_cap + slack, width), BF16),
            pltpu.VMEM((edge_cap + slack, width), BF16),
            dma((4,)),
            dma((lev, 2)),
            dma((2,)),
        ],
        compiler_params=params(20),
        cost_estimate=cost(conv_flops(lev, 2 * cols), lev * cols * width * 16),
        name="edge",
    )(side, ocean_state, depth, stay(conv_weight), on_halo, off_halo, edge_forcing)
    top_others = exchange(top_packed)
    low_others = exchange(low_packed)

    def unread(shape):
        return pl.pallas_call(
            lambda out_ref: None,
            out_specs=hbm,
            out_shape=pltpu.HBM(shape, BF16),
            name="unread",
        )()

    deep_whole, edge_whole = lax.cond(
        flag[0] > 0,
        lambda *a: tuple(exchange(x) for x in a),
        lambda *a: tuple([unread(x.shape) for _ in range(members - 1)] for x in a),
        deep_normed,
        edge_normed,
    )
    shape = ocean_state.shape
    weights = (depth, qkv_weight, out_weight)
    out = attend(
        flag,
        [surf_normed, deep_normed],
        [surf_mixed, deep_mixed],
        surf_others,
        deep_others,
        deep_whole,
        *weights,
        list(range(1, rows - 1)),
        None,
        shape,
    )
    for row, got in ((0, top_others), (rows - 1, low_others)):
        out = attend(
            flag, [edge_normed], [edge_mixed], [], got, edge_whole, *weights, [row], out, shape
        )
    return out


def solution(mesh):
    return jax.shard_map(
        body,
        mesh=mesh,
        in_specs=(
            P("mem", "tile", None),
            P("mem", None, "tile", None),
            P("tile"),
            P("tile", None),
            P("tile"),
            P("tile", None, None, None),
            P(),
            P(),
            P(),
        ),
        out_specs=P("mem", None, "tile", None),
        check_vma=False,
    )
```

```python
import functools
import math

import jax
import jax.numpy as jnp
from jax import lax
from jax.experimental import pallas as pl
from jax.experimental.pallas import tpu as pltpu
from jax.sharding import PartitionSpec as P

HEADS = 4
R = 1
GROUP = 16
EPS = 1e-06
NEG = -1e30
F32 = jnp.float32
BF16 = jnp.bfloat16
MIB = 1024 * 1024


def params(mib, steps=0):
    return pltpu.CompilerParams(
        dimension_semantics=("arbitrary",) * steps if steps else None, vmem_limit_bytes=mib * MIB
    )


def cost(flops, nbytes):
    return pl.CostEstimate(flops=int(flops), bytes_accessed=int(nbytes), transcendentals=0)


def capacity(tokens, share):
    return -(-int(tokens * share) // 16) * 16


def row_plan(depth_row, lev):
    cols = depth_row.shape[1]
    level = lax.broadcasted_iota(jnp.int32, (lev, cols), 0).astype(F32)
    wet = (depth_row > level).astype(F32)
    upper = (
        lax.broadcasted_iota(jnp.int32, (cols, cols), 0)
        < lax.broadcasted_iota(jnp.int32, (cols, cols), 1)
    )
    upper = upper.astype(F32).astype(BF16)
    rank = jnp.dot(wet.astype(BF16), upper, preferred_element_type=F32)
    counts = [jnp.sum(wet[l : l + 1]).astype(jnp.int32) for l in range(lev)]
    return wet, rank, counts


def offsets(plans, first, lev):
    at, place = jnp.int32(0), {}
    for l in range(first, lev):
        for r, plan in enumerate(plans):
            place[l, r] = at
            at = at + plan[2][l]
    return place


def segment(wet, rank, offset, cap):
    cols = wet.shape[1]
    base = jnp.minimum((offset // 16) * 16, cap)
    target = jnp.where(wet > 0, rank + (offset - base).astype(F32), -1.0)
    slot = lax.broadcasted_iota(jnp.int32, (cols + 16, cols), 0).astype(F32)
    return pl.multiple_of(base, 16), (slot == target).astype(F32).astype(BF16)


def pack(buf_ref, wet, rank, offset, cap, tokens):
    base, hot = segment(wet, rank, offset, cap)
    rows = jnp.dot(hot, tokens, preferred_element_type=F32).astype(BF16)
    head = pl.ds(base, 16)
    buf_ref[head, :] = buf_ref[head, :] + rows[:16]
    buf_ref[pl.ds(pl.multiple_of(base + 16, 16), rows.shape[0] - 16), :] = rows[16:]


def unpack(buf_ref, wet, rank, offset, cap):
    base, hot = segment(wet, rank, offset, cap)
    rows = buf_ref[pl.ds(base, hot.shape[0]), :]
    return lax.dot_general(
        hot, rows, (((0,), (0,)), ((), ())), preferred_element_type=F32
    ).astype(BF16)


def column(depth_row):
    cols = depth_row.shape[1]
    return jnp.broadcast_to(depth_row, (cols, cols)).T


def widen(x, width):
    return jnp.concatenate([x] * (width // x.shape[1]), axis=1)


def stencil(taps, weight_ref, cols):
    count, width = taps[0].shape
    x = jnp.concatenate(taps, axis=1)
    sums = [
        jnp.dot(x, weight_ref[:, dc].reshape(3 * width, -1), preferred_element_type=F32)
        for dc in range(3)
    ]
    col = lax.broadcasted_iota(jnp.int32, (count, 1), 0) % cols
    left = jnp.where(col == 0, 0.0, pltpu.roll(sums[0], 1, axis=0))
    right = jnp.where(col == cols - 1, 0.0, pltpu.roll(sums[2], count - 1, axis=0))
    return sums[1] + left + right


def normalise(mixed):
    mf = mixed.astype(F32)
    mean = jnp.mean(mf * mf, axis=-1, keepdims=True)
    return (mf * lax.rsqrt(mean + EPS)).astype(BF16)


def prep_kernel(
    caps, side_ref, state_hbm, atm_hbm, depth_ref, on_hbm, off_hbm, flag_ref, rows_in, in_sem, out_sem, atm_sem
):
    _, lev, cells, width = state_hbm.shape
    rows, cols = depth_ref.shape
    own = atm_hbm.shape[1]
    sides = (on_hbm, off_hbm)
    loads, stores = [], []
    for k in (1, 0):
        at = pl.multiple_of(side_ref[k] * cols, cols)
        for l in range(lev):
            load = pltpu.make_async_copy(
                state_hbm.at[0, l, pl.ds(at, cols)], rows_in.at[k, l], in_sem.at[k, l]
            )
            load.start()
            loads.append((k, l, load))
    for k, out in enumerate(sides):
        store = pltpu.make_async_copy(
            atm_hbm.at[0], out.at[pl.ds(lev * cols, own)], atm_sem.at[k]
        )
        store.start()
        stores.append(store)
    d = depth_ref[...].astype(F32)
    deep = [column(jnp.where(side_ref[k] == 0, d[0:1], d[rows - 1 :])) for k in range(2)]
    for k, l, load in loads:
        wet = widen((deep[k] > l).astype(F32).astype(BF16), width)
        load.wait()
        rows_in[k, l] = rows_in[k, l] * wet
        store = pltpu.make_async_copy(
            rows_in.at[k, l], sides[k].at[pl.ds(l * cols, cols)], out_sem.at[k, l]
        )
        store.start()
        stores.append(store)
    counts = [
        jnp.sum(jnp.maximum(d[1 : rows - 1] - 1.0, 0.0)),
        jnp.sum(d[0:1]),
        jnp.sum(d[rows - 1 :]),
    ]
    over = jnp.int32(0)
    for count, cap in zip(counts, caps):
        over = over | (count > cap).astype(jnp.int32)
    flag_ref[0] = over
    for store in stores:
        store.wait()


def inner_kernel(
    cap,
    state,
    depth_ref,
    weight,
    mixed_hbm,
    normed_hbm,
    packed_hbm,
    mixed,
    normed,
    packed,
    out_sem,
    packed_sem,
):
    _, lev, cells, width = state.shape
    rows, cols = depth_ref.shape
    packed[...] = jnp.zeros_like(packed)
    d = depth_ref[...].astype(F32)
    plans = [row_plan(d[r : r + 1], lev) for r in range(1, rows - 1)]
    place = offsets(plans, 1, lev)
    deep = jnp.concatenate([column(d[r : r + 1]) for r in range(rows)], axis=0)
    count = cells - 2 * cols
    stores = []
    for l in range(1, lev):
        wet = (deep > l).astype(F32)
        x = state[0, l] * widen(wet.astype(BF16), width)
        taps = [x[dr * cols : dr * cols + count] for dr in range(3)]
        total = stencil(taps, weight, cols)
        new = taps[1].astype(F32) + widen(wet[cols : cols + count], width) * total
        new = new.astype(BF16)
        mixed[l - 1] = new
        tokens = normalise(new)
        normed[l - 1] = tokens
        for k, (buf, out) in enumerate(((mixed, mixed_hbm), (normed, normed_hbm))):
            store = pltpu.make_async_copy(buf.at[l - 1], out.at[l - 1], out_sem.at[l - 1, k])
            store.start()
            stores.append(store)
        for r, plan in enumerate(plans):
            pack(
                packed,
                plan[0][l : l + 1],
                plan[1][l : l + 1],
                place[l, r],
                cap,
                tokens[r * cols : (r + 1) * cols],
            )
        if l == lev - 1:
            store = pltpu.make_async_copy(packed.at[pl.ds(0, cap)], packed_hbm, packed_sem)
            store.start()
            stores.append(store)
    for store in stores:
        store.wait()


def surface_kernel(
    ids_ref,
    live_ref,
    side_ref,
    state,
    depth_ref,
    weight,
    on_hbm,
    off_hbm,
    atm_hbm,
    remap_hbm,
    mixed_ref,
    normed_ref,
    edge_ref,
    window,
    remap,
    forcing_ref,
    sem,
):
    rows, cols = depth_ref.shape
    _, own, width = atm_hbm.shape
    cells = state.shape[2]
    blocks, pairs = remap_hbm.shape[0], remap_hbm.shape[1]
    on_at = jnp.where(side_ref[0] == 0, 0, 2 * own)
    copies = [
        pltpu.make_async_copy(
            on_hbm.at[pl.ds(on_hbm.shape[0] - own, own)],
            window.at[pl.ds(pl.multiple_of(on_at, own), own)],
            sem.at[0],
        ),
        pltpu.make_async_copy(
            off_hbm.at[pl.ds(off_hbm.shape[0] - own, own)],
            window.at[pl.ds(pl.multiple_of(2 * own - on_at, own), own)],
            sem.at[1],
        ),
        pltpu.make_async_copy(atm_hbm.at[0], window.at[pl.ds(own, own)], sem.at[2]),
        pltpu.make_async_copy(remap_hbm, remap, sem.at[3]),
    ]
    for copy in copies:
        copy.start()
    d = depth_ref[...].astype(F32)
    wet = (jnp.concatenate([column(d[r : r + 1]) for r in range(rows)], axis=0) > 0).astype(F32)
    x = state[0, 0] * widen(wet.astype(BF16), width)
    count = cells - 2 * cols
    taps = [x[dr * cols : dr * cols + count] for dr in range(3)]
    total = stencil(taps, weight, cols)
    for copy in copies:
        copy.wait()
    for b in range(blocks):
        acc = jnp.zeros((cols, width), F32)
        for p in range(pairs):
            on = (p < live_ref[b]).astype(F32)
            start = pl.multiple_of(ids_ref[b, p] * cols, cols)
            acc = acc + on * jnp.dot(
                remap[b, p], window[pl.ds(start, cols), :], preferred_element_type=F32
            )
        forcing_ref[b * cols : (b + 1) * cols] = acc
    total = total + forcing_ref[cols : cols + count]
    new = (taps[1].astype(F32) + widen(wet[cols : cols + count], width) * total).astype(BF16)
    mixed_ref[0] = new
    normed_ref[0] = normalise(new)
    edge_ref[0:cols] = forcing_ref[0:cols]
    edge_ref[cols : 2 * cols] = forcing_ref[cols + count :]


def edge_kernel(
    cap,
    side_ref,
    state,
    depth_ref,
    weight_hbm,
    on_hbm,
    off_hbm,
    forcing_hbm,
    mixed_hbm,
    normed_hbm,
    top_hbm,
    low_hbm,
    weight,
    halos,
    forcing,
    mixed,
    normed,
    top,
    low,
    in_sem,
    out_sem,
    packed_sem,
):
    _, lev, cells, width = state.shape
    rows, cols = depth_ref.shape
    on_at = jnp.where(side_ref[0] == 0, 0, 1)
    copies = [
        pltpu.make_async_copy(weight_hbm, weight, in_sem.at[0]),
        pltpu.make_async_copy(on_hbm.at[pl.ds(0, lev * cols)], halos.at[on_at], in_sem.at[1]),
        pltpu.make_async_copy(off_hbm.at[pl.ds(0, lev * cols)], halos.at[1 - on_at], in_sem.at[2]),
        pltpu.make_async_copy(forcing_hbm, forcing, in_sem.at[3]),
    ]
    for copy in copies:
        copy.start()
    top[...] = jnp.zeros_like(top)
    low[...] = jnp.zeros_like(low)
    d = depth_ref[...].astype(F32)
    plans = [row_plan(d[r : r + 1], lev) for r in (0, rows - 1)]
    places = [offsets([plan], 0, lev) for plan in plans]
    deep = jnp.concatenate([column(d[r : r + 1]) for r in range(rows)], axis=0)
    for copy in copies:
        copy.wait()
    stores = []
    for l in range(lev):
        wet = (deep > l).astype(F32)
        x = state[0, l] * widen(wet.astype(BF16), width)
        halo = slice(l * cols, (l + 1) * cols)
        up = [halos[0, halo], x[0:cols], x[cols : 2 * cols]]
        down = [x[cells - 2 * cols : cells - cols], x[cells - cols :], halos[1, halo]]
        taps = [jnp.concatenate([a, b], axis=0) for a, b in zip(up, down)]
        total = stencil(taps, weight, cols)
        if l == 0:
            total = total + forcing[...]
        edge_wet = jnp.concatenate([wet[0:cols], wet[cells - cols :]], axis=0)
        new = (taps[1].astype(F32) + widen(edge_wet, width) * total).astype(BF16)
        mixed[l] = new
        tokens = normalise(new)
        normed[l] = tokens
        for k, (buf, out) in enumerate(((mixed, mixed_hbm), (normed, normed_hbm))):
            store = pltpu.make_async_copy(buf.at[l], out.at[l], out_sem.at[l, k])
            store.start()
            stores.append(store)
        for r, buf in enumerate((top, low)):
            pack(
                buf,
                plans[r][0][l : l + 1],
                plans[r][1][l : l + 1],
                places[r][l, 0],
                cap,
                tokens[r * cols : (r + 1) * cols],
            )
    for k, (buf, out) in enumerate(((top, top_hbm), (low, low_hbm))):
        store = pltpu.make_async_copy(buf.at[pl.ds(0, cap)], out, packed_sem.at[k])
        store.start()
        stores.append(store)
    for store in stores:
        store.wait()


def attend_kernel(others, nparts, rows_of, first, cap, aliased, flag_ref, *refs):
    refs = list(refs)
    take = lambda k: [refs.pop(0) for _ in range(k)]
    own_normed = take(nparts)
    own_mixed = take(nparts)
    surf = take(others) if first else []
    packed = take(others)
    whole = take(others)
    depth_ref, qkv_ref, wo_ref = take(3)
    if aliased:
        take(1)
    out_ref, q_ref, k_ref, v_ref, att_ref, buf_ref, token_ref, sem = refs
    lev, count, width = q_ref.shape
    members = others + 1
    head = width // HEADS
    pair = 2 * head
    step = pl.program_id(0)

    def keys_values(x, m):
        rows = slice(m * lev, (m + 1) * lev)
        kv = jnp.dot(x, qkv_ref[:, width:], preferred_element_type=F32).astype(BF16)
        k_ref[rows] = kv[:, :width].reshape(lev, count, width)
        v_ref[rows] = kv[:, width:].reshape(lev, count, width)

    two = len(rows_of) == 2
    pick = lambda a, b: jnp.where(step == 0, a, b)
    d = depth_ref[...].astype(F32)
    rows_d = [d[r : r + 1] for r in rows_of]
    plans = [row_plan(row, lev) for row in rows_d]
    place = offsets(plans, first, lev)
    wet_row, rank, _ = plans[0]
    depth_row = rows_d[0]
    if two:
        wet_row, rank = pick(wet_row, plans[1][0]), pick(rank, plans[1][1])
        depth_row = pick(*rows_d)

    x = jnp.concatenate([p[...].reshape(-1, width) for p in own_normed], axis=0)
    q = jnp.dot(x, qkv_ref[:, 0:width], preferred_element_type=F32).astype(BF16)
    q_ref[...] = (q * (1.0 / math.sqrt(head))).astype(BF16).reshape(lev, count, width)
    keys_values(x, 0)
    for o in range(others):
        if first:
            token_ref[0] = surf[o][0]

        @pl.when(flag_ref[0] == 0)
        def _():
            buf_ref[0:cap] = packed[o][...]
            buf_ref[cap:] = jnp.zeros((buf_ref.shape[0] - cap, width), BF16)
            for l in range(first, lev):
                at = pick(place[l, 0], place[l, 1]) if two else place[l, 0]
                token_ref[l] = unpack(
                    buf_ref, wet_row[l : l + 1], rank[l : l + 1], at, cap
                )

        @pl.when(flag_ref[0] != 0)
        def _():
            which = step if two else (0 if rows_of[0] == 0 else 1)
            copy = pltpu.make_async_copy(
                whole[o].at[:, pl.ds(which * count, count)], token_ref.at[pl.ds(first, lev - first)], sem
            )
            copy.start()
            copy.wait()

        keys_values(token_ref[...].reshape(-1, width), o + 1)

    nq, nk = lev * GROUP, members * lev * GROUP
    groups = count // GROUP
    lanes_n = lev * GROUP
    cell = lax.broadcasted_iota(jnp.int32, (groups, count), 1)
    mine = (cell // GROUP == lax.broadcasted_iota(jnp.int32, (groups, count), 0)).astype(F32)
    spread = lax.broadcasted_iota(jnp.int32, (count, lanes_n), 0) % GROUP
    spread = (spread == lax.broadcasted_iota(jnp.int32, (count, lanes_n), 1) % GROUP).astype(F32)
    key_depth = jnp.dot(
        (mine * depth_row).astype(BF16), spread.astype(BF16), preferred_element_type=F32
    )
    key_level = lax.broadcasted_iota(jnp.int32, (groups, lanes_n), 1) // GROUP
    key_bias = jnp.where(key_depth > key_level.astype(F32), 0.0, NEG)
    qc = lax.broadcasted_iota(jnp.int32, (nq, nk), 0) % GROUP
    kc = lax.broadcasted_iota(jnp.int32, (nq, nk), 1) % GROUP
    same = jnp.where(qc == kc, 0.0, NEG)
    lane = lax.broadcasted_iota(jnp.int32, (1, pair), 1)
    low = (lane < head).astype(F32).astype(BF16)
    high = (lane >= head).astype(F32).astype(BF16)
    for g in range(groups):
        cells = slice(g * GROUP, (g + 1) * GROUP)
        bias = same + jnp.concatenate([key_bias[g : g + 1]] * members, axis=1)
        bias = jnp.concatenate([bias, bias], axis=0)
        for h in range(HEADS // 2):
            lanes = slice(h * pair, (h + 1) * pair)
            q = q_ref[:, cells, lanes].reshape(nq, pair)
            q = jnp.concatenate([q * low, q * high], axis=0)
            k = k_ref[:, cells, lanes].reshape(nk, pair)
            v = v_ref[:, cells, lanes].reshape(nk, pair)
            s = lax.dot_general(q, k, (((1,), (1,)), ((), ())), preferred_element_type=F32) + bias
            p = jnp.exp(s - jnp.max(s, axis=-1, keepdims=True))
            norm = 1.0 / jnp.sum(p, axis=-1, keepdims=True)
            o = jnp.dot(p.astype(BF16), v, preferred_element_type=F32) * norm
            o = jnp.where(lane < head, o[:nq], o[nq:])
            att_ref[:, cells, lanes] = o.astype(BF16).reshape(lev, GROUP, pair)
    proj = jnp.dot(att_ref[...].reshape(-1, width), wo_ref[...], preferred_element_type=F32)
    base = jnp.concatenate([p[...].reshape(-1, width) for p in own_mixed], axis=0).astype(F32)
    deep = column(depth_row)
    for l in range(lev):
        rows = slice(l * count, (l + 1) * count)
        wet = widen((deep > l).astype(F32), width)
        out_ref[0, l] = (base[rows] + wet * proj[rows]).astype(BF16)


def attend(flag, normed, mixed, surf, packed, whole, depth, qkv_weight, out_weight, rows_of, out, shape):
    others, nparts = len(packed), len(mixed)
    lev = sum(p.shape[0] for p in mixed)
    width = shape[-1]
    rows, cols = depth.shape
    cap = packed[0].shape[0]
    first = 1 if surf else 0
    shift = 1 if rows_of[0] == rows - 1 else 0
    index = lambda i, *_: (0, i + shift, 0)
    full2 = lambda a: pl.BlockSpec(a.shape, lambda i, *_: (0, 0))
    part = [pl.BlockSpec((p.shape[0], cols, width), index) for p in mixed]
    hbm = pl.BlockSpec(memory_space=pl.ANY)
    in_specs = part * 2
    in_specs += [pl.BlockSpec((1, cols, width), index)] * len(surf)
    in_specs += [full2(p) for p in packed]
    in_specs += [hbm] * others
    in_specs += [full2(depth), full2(qkv_weight), full2(out_weight)]
    args = normed + mixed + surf + packed + whole + [depth, qkv_weight, out_weight]
    alias = {}
    if out is not None:
        in_specs.append(hbm)
        alias = {len(args) + 1: 0}
        args.append(out)
    tokens = lev * cols * len(rows_of)
    members = others + 1
    return pl.pallas_call(
        functools.partial(
            attend_kernel, others, nparts, tuple(rows_of), first, cap, out is not None
        ),
        grid_spec=pltpu.PrefetchScalarGridSpec(
            num_scalar_prefetch=1,
            grid=(len(rows_of),),
            in_specs=in_specs,
            out_specs=pl.BlockSpec(
                (1, lev, cols, width), lambda i, *_: (0, 0, i + rows_of[0], 0)
            ),
            scratch_shapes=[
                pltpu.VMEM((lev, cols, width), BF16),
                pltpu.VMEM((members * lev, cols, width), BF16),
                pltpu.VMEM((members * lev, cols, width), BF16),
                pltpu.VMEM((lev, cols, width), BF16),
                pltpu.VMEM((cap + cols + 16, width), BF16),
                pltpu.VMEM((lev, cols, width), BF16),
                pltpu.SemaphoreType.DMA,
            ],
        ),
        out_shape=jax.ShapeDtypeStruct(shape, BF16),
        input_output_aliases=alias,
        compiler_params=params(20 if members <= 2 else 48, 1),
        cost_estimate=cost(tokens * width * width * 8 * (members + 2), tokens * width * 2 * 5),
        name="attend",
    )(flag, *args)


def body(
    atm_latent,
    ocean_state,
    depth,
    src_blocks,
    live,
    remap_weight,
    conv_weight,
    qkv_weight,
    out_weight,
):
    _, lev, cells, width = ocean_state.shape
    cols = remap_weight.shape[2]
    rows = cells // cols
    inner = cells - 2 * cols
    own = atm_latent.shape[1]
    atm_blk = own // cols
    tiles = lax.axis_size("tile")
    members = lax.axis_size("mem")
    tile = lax.axis_index("tile")

    def swap(x, first):
        pairs = [(i, i + 1) for i in range(first, tiles - 1, 2)]
        return lax.ppermute(x, "tile", pairs + [(b, a) for a, b in pairs])

    def exchange(x):
        return [
            lax.ppermute(x, "mem", [(i, (i + k) % members) for i in range(members)])
            for k in range(1, members)
        ]

    odd = tile % 2
    side = jnp.stack([(1 - odd) * (rows - 1), odd * (rows - 1)]).astype(jnp.int32)
    depth = depth.reshape(rows, cols)
    deep_cap = capacity((lev - 1) * inner, 0.5625)
    edge_cap = capacity(lev * cols, 0.65625)

    hbm = pl.BlockSpec(memory_space=pltpu.HBM)
    anywhere = pl.BlockSpec(memory_space=pl.ANY)
    vmem = pl.BlockSpec(memory_space=pltpu.VMEM)
    smem = pl.BlockSpec(memory_space=pltpu.SMEM)
    tok = lambda *s: pltpu.HBM((*s, width), BF16)
    stay = lambda x: pltpu.with_memory_space_constraint(x, pltpu.HBM)
    conv_flops = lambda n, c: 2 * 9 * n * c * width * width
    dma = pltpu.SemaphoreType.DMA
    slack = cols + 16
    message = lev * cols + own
    on_msg, off_msg, flag = pl.pallas_call(
        functools.partial(prep_kernel, (deep_cap, edge_cap, edge_cap)),
        in_specs=[smem, hbm, hbm, vmem],
        out_specs=[hbm, hbm, smem],
        out_shape=[tok(message), tok(message), jax.ShapeDtypeStruct((1,), jnp.int32)],
        scratch_shapes=[
            pltpu.VMEM((2, lev, cols, width), BF16),
            dma((2, lev)),
            dma((2, lev)),
            dma((2,)),
        ],
        compiler_params=params(16),
        cost_estimate=cost(lev * cols * width * 4, lev * cols * width * 10),
        name="prep",
    )(side, stay(ocean_state), stay(atm_latent), depth)
    off_halo = swap(off_msg, 1)
    on_halo = swap(on_msg, 0)

    deep_mixed, deep_normed, deep_packed = pl.pallas_call(
        functools.partial(inner_kernel, deep_cap),
        in_specs=[vmem, vmem, vmem],
        out_specs=[hbm] * 3,
        out_shape=[tok(lev - 1, inner), tok(lev - 1, inner), tok(deep_cap)],
        scratch_shapes=[
            pltpu.VMEM((lev - 1, inner, width), BF16),
            pltpu.VMEM((lev - 1, inner, width), BF16),
            pltpu.VMEM((deep_cap + slack, width), BF16),
            dma((lev - 1, 2)),
            dma,
        ],
        compiler_params=params(20),
        cost_estimate=cost(conv_flops(lev, inner), lev * inner * width * 8),
        name="inner",
    )(ocean_state, depth, conv_weight)
    deep_others = exchange(deep_packed)

    ids = jnp.clip(src_blocks - (tile - R) * atm_blk, 0, 3 * atm_blk - 1)
    whole_spec = lambda *sh: pl.BlockSpec(sh, lambda *_: (0,) * len(sh))
    surf_mixed, surf_normed, edge_forcing = pl.pallas_call(
        surface_kernel,
        in_specs=[smem] * 3 + [vmem] * 3 + [anywhere] * 2 + [hbm] * 2,
        out_specs=[whole_spec(1, inner, width)] * 2 + [whole_spec(2 * cols, width)],
        out_shape=[tok(1, inner), tok(1, inner), pltpu.HBM((2 * cols, width), F32)],
        scratch_shapes=[
            pltpu.VMEM((3 * own, width), BF16),
            pltpu.VMEM(remap_weight.shape, BF16),
            pltpu.VMEM((cells, width), F32),
            dma((4,)),
        ],
        compiler_params=params(20),
        cost_estimate=cost(conv_flops(1, inner), cells * width * 16),
        name="surface",
    )(
        ids,
        live,
        side,
        ocean_state,
        depth,
        conv_weight,
        on_halo,
        off_halo,
        stay(atm_latent),
        stay(remap_weight),
    )
    surf_others = exchange(surf_normed)

    edge_mixed, edge_normed, top_packed, low_packed = pl.pallas_call(
        functools.partial(edge_kernel, edge_cap),
        in_specs=[smem, vmem, vmem, hbm, anywhere, anywhere, hbm],
        out_specs=[hbm] * 4,
        out_shape=[tok(lev, 2 * cols), tok(lev, 2 * cols), tok(edge_cap), tok(edge_cap)],
        scratch_shapes=[
            pltpu.VMEM(conv_weight.shape, BF16),
            pltpu.VMEM((2, lev * cols, width), BF16),
            pltpu.VMEM((2 * cols, width), F32),
            pltpu.VMEM((lev, 2 * cols, width), BF16),
            pltpu.VMEM((lev, 2 * cols, width), BF16),
            pltpu.VMEM((edge_cap + slack, width), BF16),
            pltpu.VMEM((edge_cap + slack, width), BF16),
            dma((4,)),
            dma((lev, 2)),
            dma((2,)),
        ],
        compiler_params=params(20),
        cost_estimate=cost(conv_flops(lev, 2 * cols), lev * cols * width * 16),
        name="edge",
    )(side, ocean_state, depth, stay(conv_weight), on_halo, off_halo, stay(edge_forcing))
    top_others = exchange(top_packed)
    low_others = exchange(low_packed)

    def unread(shape):
        return pl.pallas_call(
            lambda out_ref: None,
            out_specs=hbm,
            out_shape=pltpu.HBM(shape, BF16),
            name="unread",
        )()

    deep_whole, edge_whole = lax.cond(
        flag[0] > 0,
        lambda *a: tuple(exchange(x) for x in a),
        lambda *a: tuple([unread(x.shape) for _ in range(members - 1)] for x in a),
        deep_normed,
        edge_normed,
    )
    shape = ocean_state.shape
    weights = (depth, qkv_weight, out_weight)
    out = attend(
        flag,
        [surf_normed, deep_normed],
        [surf_mixed, deep_mixed],
        surf_others,
        deep_others,
        deep_whole,
        *weights,
        list(range(1, rows - 1)),
        None,
        shape,
    )
    for row, got in ((0, top_others), (rows - 1, low_others)):
        out = attend(
            flag, [edge_normed], [edge_mixed], [], got, edge_whole, *weights, [row], out, shape
        )
    return out


def solution(mesh):
    return jax.shard_map(
        body,
        mesh=mesh,
        in_specs=(
            P("mem", "tile", None),
            P("mem", None, "tile", None),
            P("tile"),
            P("tile", None),
            P("tile"),
            P("tile", None, None, None),
            P(),
            P(),
            P(),
        ),
        out_specs=P("mem", None, "tile", None),
        check_vma=False,
    )
```

```python
import functools
import math

import jax
import jax.numpy as jnp
from jax import lax
from jax.experimental import pallas as pl
from jax.experimental.pallas import tpu as pltpu
from jax.sharding import PartitionSpec as P

HEADS = 4
R = 1
GROUP = 16
EPS = 1e-06
NEG = -1e30
F32 = jnp.float32
BF16 = jnp.bfloat16
MIB = 1024 * 1024


def params(mib, steps=0):
    return pltpu.CompilerParams(
        dimension_semantics=("arbitrary",) * steps if steps else None, vmem_limit_bytes=mib * MIB
    )


def cost(flops, nbytes):
    return pl.CostEstimate(flops=int(flops), bytes_accessed=int(nbytes), transcendentals=0)


def capacity(tokens, share):
    return -(-int(tokens * share) // 16) * 16


def row_plan(depth_row, lev):
    cols = depth_row.shape[1]
    level = lax.broadcasted_iota(jnp.int32, (lev, cols), 0).astype(F32)
    wet = (depth_row > level).astype(F32)
    upper = (
        lax.broadcasted_iota(jnp.int32, (cols, cols), 0)
        < lax.broadcasted_iota(jnp.int32, (cols, cols), 1)
    )
    upper = upper.astype(F32).astype(BF16)
    rank = jnp.dot(wet.astype(BF16), upper, preferred_element_type=F32)
    counts = [jnp.sum(wet[l : l + 1]).astype(jnp.int32) for l in range(lev)]
    return wet, rank, counts


def offsets(plans, first, lev):
    at, place = jnp.int32(0), {}
    for l in range(first, lev):
        for r, plan in enumerate(plans):
            place[l, r] = at
            at = at + plan[2][l]
    return place


def segment(wet, rank, offset, cap):
    cols = wet.shape[1]
    base = jnp.minimum((offset // 16) * 16, cap)
    target = jnp.where(wet > 0, rank + (offset - base).astype(F32), -1.0)
    slot = lax.broadcasted_iota(jnp.int32, (cols + 16, cols), 0).astype(F32)
    return pl.multiple_of(base, 16), (slot == target).astype(F32).astype(BF16)


def pack(buf_ref, wet, rank, offset, cap, tokens):
    base, hot = segment(wet, rank, offset, cap)
    rows = jnp.dot(hot, tokens, preferred_element_type=F32).astype(BF16)
    head = pl.ds(base, 16)
    buf_ref[head, :] = buf_ref[head, :] + rows[:16]
    buf_ref[pl.ds(pl.multiple_of(base + 16, 16), rows.shape[0] - 16), :] = rows[16:]


def unpack(buf_ref, wet, rank, offset, cap):
    base, hot = segment(wet, rank, offset, cap)
    rows = buf_ref[pl.ds(base, hot.shape[0]), :]
    return lax.dot_general(
        hot, rows, (((0,), (0,)), ((), ())), preferred_element_type=F32
    ).astype(BF16)


def column(depth_row):
    cols = depth_row.shape[1]
    return jnp.broadcast_to(depth_row, (cols, cols)).T


def widen(x, width):
    return jnp.concatenate([x] * (width // x.shape[1]), axis=1)


def stencil(taps, weight_ref, cols):
    count, width = taps[0].shape
    x = jnp.concatenate(taps, axis=1)
    sums = [
        jnp.dot(x, weight_ref[:, dc].reshape(3 * width, -1), preferred_element_type=F32)
        for dc in range(3)
    ]
    col = lax.broadcasted_iota(jnp.int32, (count, 1), 0) % cols
    left = jnp.where(col == 0, 0.0, pltpu.roll(sums[0], 1, axis=0))
    right = jnp.where(col == cols - 1, 0.0, pltpu.roll(sums[2], count - 1, axis=0))
    return sums[1] + left + right


def normalise(mixed):
    mf = mixed.astype(F32)
    mean = jnp.mean(mf * mf, axis=-1, keepdims=True)
    return (mf * lax.rsqrt(mean + EPS)).astype(BF16)


def prep_kernel(
    caps, side_ref, state_hbm, atm_ref, depth_ref, on_hbm, off_hbm, flag_ref, rows_in, in_sem, out_sem, atm_sem
):
    _, lev, cells, width = state_hbm.shape
    rows, cols = depth_ref.shape
    own = atm_ref.shape[1]
    sides = (on_hbm, off_hbm)
    loads, stores = [], []
    for k in (1, 0):
        at = pl.multiple_of(side_ref[k] * cols, cols)
        for l in range(lev):
            load = pltpu.make_async_copy(
                state_hbm.at[0, l, pl.ds(at, cols)], rows_in.at[k, l], in_sem.at[k, l]
            )
            load.start()
            loads.append((k, l, load))
    for k, out in enumerate(sides):
        store = pltpu.make_async_copy(
            atm_ref.at[0], out.at[pl.ds(lev * cols, own)], atm_sem.at[k]
        )
        store.start()
        stores.append(store)
    d = depth_ref[...].astype(F32)
    pick = lambda k: jnp.where(side_ref[k] == 0, d[0:1], d[rows - 1 :])
    deep = [column(pick(k)) for k in range(2)]
    for k, l, load in loads:
        wet = widen((deep[k] > l).astype(F32).astype(BF16), width)
        load.wait()
        rows_in[k, l] = rows_in[k, l] * wet
        store = pltpu.make_async_copy(
            rows_in.at[k, l], sides[k].at[pl.ds(l * cols, cols)], out_sem.at[k, l]
        )
        store.start()
        stores.append(store)
    counts = [
        jnp.sum(jnp.maximum(d[1 : rows - 1] - 1.0, 0.0)),
        jnp.sum(jnp.maximum(pick(0) - 1.0, 0.0)),
        jnp.sum(pick(1)),
    ]
    over = jnp.int32(0)
    for count, cap in zip(counts, caps):
        over = over | (count > cap).astype(jnp.int32)
    flag_ref[0] = over
    for store in stores:
        store.wait()


def inner_kernel(
    cap,
    state,
    depth_ref,
    weight,
    mixed_hbm,
    normed_hbm,
    packed_hbm,
    mixed,
    normed,
    packed,
    out_sem,
    packed_sem,
):
    _, lev, cells, width = state.shape
    rows, cols = depth_ref.shape
    packed[...] = jnp.zeros_like(packed)
    d = depth_ref[...].astype(F32)
    plans = [row_plan(d[r : r + 1], lev) for r in range(1, rows - 1)]
    place = offsets(plans, 1, lev)
    deep = jnp.concatenate([column(d[r : r + 1]) for r in range(rows)], axis=0)
    count = cells - 2 * cols
    stores = []
    for l in range(1, lev):
        wet = (deep > l).astype(F32)
        x = state[0, l] * widen(wet.astype(BF16), width)
        taps = [x[dr * cols : dr * cols + count] for dr in range(3)]
        total = stencil(taps, weight, cols)
        new = taps[1].astype(F32) + widen(wet[cols : cols + count], width) * total
        new = new.astype(BF16)
        mixed[l - 1] = new
        tokens = normalise(new)
        normed[l - 1] = tokens
        for k, (buf, out) in enumerate(((mixed, mixed_hbm), (normed, normed_hbm))):
            store = pltpu.make_async_copy(buf.at[l - 1], out.at[l - 1], out_sem.at[l - 1, k])
            store.start()
            stores.append(store)
        for r, plan in enumerate(plans):
            pack(
                packed,
                plan[0][l : l + 1],
                plan[1][l : l + 1],
                place[l, r],
                cap,
                tokens[r * cols : (r + 1) * cols],
            )
        if l == lev - 1:
            store = pltpu.make_async_copy(packed.at[pl.ds(0, cap)], packed_hbm, packed_sem)
            store.start()
            stores.append(store)
    for store in stores:
        store.wait()


def surface_kernel(
    ids_ref,
    live_ref,
    side_ref,
    state,
    depth_ref,
    weight,
    on_hbm,
    off_hbm,
    atm_hbm,
    remap_hbm,
    near_base,
    mixed_ref,
    normed_ref,
    far_ref,
    window,
    remap,
    forcing_ref,
    sem,
):
    rows, cols = depth_ref.shape
    _, own, width = atm_hbm.shape
    cells = state.shape[2]
    blocks, pairs = remap_hbm.shape[0], remap_hbm.shape[1]
    on_at = jnp.where(side_ref[0] == 0, 0, 2 * own)
    copies = [
        pltpu.make_async_copy(
            on_hbm.at[pl.ds(on_hbm.shape[0] - own, own)],
            window.at[pl.ds(pl.multiple_of(on_at, own), own)],
            sem.at[0],
        ),
        pltpu.make_async_copy(
            off_hbm.at[pl.ds(off_hbm.shape[0] - own, own)],
            window.at[pl.ds(pl.multiple_of(2 * own - on_at, own), own)],
            sem.at[1],
        ),
        pltpu.make_async_copy(atm_hbm.at[0], window.at[pl.ds(own, own)], sem.at[2]),
        pltpu.make_async_copy(remap_hbm, remap, sem.at[3]),
    ]
    for copy in copies:
        copy.start()
    d = depth_ref[...].astype(F32)
    wet = (jnp.concatenate([column(d[r : r + 1]) for r in range(rows)], axis=0) > 0).astype(F32)
    x = state[0, 0] * widen(wet.astype(BF16), width)
    count = cells - 2 * cols
    taps = [x[dr * cols : dr * cols + count] for dr in range(3)]
    total = stencil(taps, weight, cols)
    for copy in copies:
        copy.wait()
    for b in range(blocks):
        acc = jnp.zeros((cols, width), F32)
        for p in range(pairs):
            on = (p < live_ref[b]).astype(F32)
            start = pl.multiple_of(ids_ref[b, p] * cols, cols)
            acc = acc + on * jnp.dot(
                remap[b, p], window[pl.ds(start, cols), :], preferred_element_type=F32
            )
        forcing_ref[b] = acc
    near = side_ref[0]
    parts = [
        (taps[1][r * cols : (r + 1) * cols].astype(F32), total[r * cols : (r + 1) * cols], r + 1)
        for r in range(rows - 2)
    ]
    for k, (base, conv, r) in enumerate(parts):
        at = slice(k * cols, (k + 1) * cols)
        wet_k = widen(wet[r * cols : (r + 1) * cols], width)
        new = (base + wet_k * (conv + forcing_ref[r])).astype(BF16)
        mixed_ref[0, at] = new
        normed_ref[0, at] = normalise(new)
    at = slice((rows - 2) * cols, (rows - 1) * cols)
    wet_near = jnp.where(near == 0, wet[0:cols], wet[cells - cols :])
    new = (near_base[...] + widen(wet_near, width) * forcing_ref[near]).astype(BF16)
    mixed_ref[0, at] = new
    normed_ref[0, at] = normalise(new)
    far_ref[...] = forcing_ref[side_ref[1]]


def row_kernel(cap, first, which, side_ref, state, depth_ref, weight_hbm, halo_hbm, *refs):
    refs = list(refs)
    forcing_ref = None if first else refs.pop(0)
    mixed_hbm, normed_hbm, packed_hbm = refs[:3]
    refs = refs[3:]
    base_ref = refs.pop(0) if first else None
    weight, tap, mixed, normed, packed, weight_sem, halo_sem, out_sem, packed_sem = refs
    load = pltpu.make_async_copy(weight_hbm, weight, weight_sem)
    load.start()
    _, lev, cells, width = state.shape
    rows, cols = depth_ref.shape
    row = side_ref[which]
    top = row == 0
    beside = jnp.where(top, 1, rows - 2)
    outer = jnp.where(top, 0, 2)
    halo = pltpu.make_async_copy(
        halo_hbm.at[pl.ds(0, lev * cols)], tap.at[outer], halo_sem
    )
    halo.start()
    packed[...] = jnp.zeros_like(packed)
    d = depth_ref[...].astype(F32)
    own_depth = jnp.where(top, d[0:1], d[rows - 1 :])
    plan = row_plan(own_depth, lev)
    place = offsets([plan], first, lev)
    deep = column(own_depth)
    deep_beside = column(jnp.where(top, d[1:2], d[rows - 2 : rows - 1]))
    at = pl.multiple_of(row * cols, cols)
    at_beside = pl.multiple_of(beside * cols, cols)
    wets = []
    for l in range(lev):
        rows_l = slice(l * cols, (l + 1) * cols)
        wet = (deep > l).astype(F32)
        wets.append(wet)
        wet_beside = (deep_beside > l).astype(F32)
        tap[1, rows_l] = state[0, l, pl.ds(at, cols)] * widen(wet.astype(BF16), width)
        tap[2 - outer, rows_l] = state[0, l, pl.ds(at_beside, cols)] * widen(
            wet_beside.astype(BF16), width
        )
    stores = []
    half = lev // 2
    load.wait()
    halo.wait()
    for start in range(0, lev, half):
        rows_b = slice(start * cols, (start + half) * cols)
        taps = [tap[dr, rows_b] for dr in range(3)]
        total = stencil(taps, weight, cols)
        for k in range(half):
            l = start + k
            rows_k = slice(k * cols, (k + 1) * cols)
            part = total[rows_k]
            if l == 0 and not first:
                part = part + forcing_ref[...]
            new = taps[1][rows_k].astype(F32) + widen(wets[l], width) * part
            if l < first:
                base_ref[...] = new
                continue
            new = new.astype(BF16)
            mixed[l - first] = new
            tokens = normalise(new)
            normed[l - first] = tokens
            pack(packed, plan[0][l : l + 1], plan[1][l : l + 1], place[l, 0], cap, tokens)
    for k, (buf, out) in enumerate(((mixed, mixed_hbm), (normed, normed_hbm))):
        store = pltpu.make_async_copy(buf, out, out_sem.at[k])
        store.start()
        stores.append(store)
    store = pltpu.make_async_copy(packed.at[pl.ds(0, cap)], packed_hbm, packed_sem)
    store.start()
    stores.append(store)
    for store in stores:
        store.wait()


def attend_kernel(others, nparts, which, first, cap, aliased, flag_ref, side_ref, *refs):
    refs = list(refs)
    take = lambda k: [refs.pop(0) for _ in range(k)]
    own_normed = take(nparts)
    own_mixed = take(nparts)
    surf = take(others) if first else []
    packed = take(others)
    whole = take(others)
    depth_ref, qkv_ref, wo_ref = take(3)
    if aliased:
        take(1)
    out_ref, q_ref, k_ref, v_ref, att_ref, buf_ref, token_ref, sem = refs
    lev, count, width = q_ref.shape
    members = others + 1
    head = width // HEADS
    pair = 2 * head
    step = pl.program_id(0)

    def keys_values(x, m):
        rows = slice(m * lev, (m + 1) * lev)
        kv = jnp.dot(x, qkv_ref[:, width:], preferred_element_type=F32).astype(BF16)
        k_ref[rows] = kv[:, :width].reshape(lev, count, width)
        v_ref[rows] = kv[:, width:].reshape(lev, count, width)

    two = which is None
    pick = lambda a, b: jnp.where(step == 0, a, b)
    d = depth_ref[...].astype(F32)
    last = d.shape[0] - 1
    if two:
        rows_d = [d[r : r + 1] for r in range(1, last)]
    else:
        rows_d = [jnp.where(side_ref[which] == 0, d[0:1], d[last:])]
    plans = [row_plan(row, lev) for row in rows_d]
    place = offsets(plans, first, lev)
    wet_row, rank, _ = plans[0]
    depth_row = rows_d[0]
    if two:
        wet_row, rank = pick(wet_row, plans[1][0]), pick(rank, plans[1][1])
        depth_row = pick(*rows_d)

    x = jnp.concatenate([p[...].reshape(-1, width) for p in own_normed], axis=0)
    q = jnp.dot(x, qkv_ref[:, 0:width], preferred_element_type=F32).astype(BF16)
    q_ref[...] = (q * (1.0 / math.sqrt(head))).astype(BF16).reshape(lev, count, width)
    keys_values(x, 0)
    for o in range(others):
        if first:
            token_ref[0] = surf[o][0]

        @pl.when(flag_ref[0] == 0)
        def _():
            buf_ref[0:cap] = packed[o][...]
            buf_ref[cap:] = jnp.zeros((buf_ref.shape[0] - cap, width), BF16)
            for l in range(first, lev):
                at = pick(place[l, 0], place[l, 1]) if two else place[l, 0]
                token_ref[l] = unpack(
                    buf_ref, wet_row[l : l + 1], rank[l : l + 1], at, cap
                )

        @pl.when(flag_ref[0] != 0)
        def _():
            copy = pltpu.make_async_copy(
                whole[o].at[:, pl.ds(pl.multiple_of(step * count, count), count)], token_ref.at[pl.ds(first, lev - first)], sem
            )
            copy.start()
            copy.wait()

        keys_values(token_ref[...].reshape(-1, width), o + 1)

    nq, nk = lev * GROUP, members * lev * GROUP
    groups = count // GROUP
    lanes_n = lev * GROUP
    cell = lax.broadcasted_iota(jnp.int32, (groups, count), 1)
    mine = (cell // GROUP == lax.broadcasted_iota(jnp.int32, (groups, count), 0)).astype(F32)
    spread = lax.broadcasted_iota(jnp.int32, (count, lanes_n), 0) % GROUP
    spread = (spread == lax.broadcasted_iota(jnp.int32, (count, lanes_n), 1) % GROUP).astype(F32)
    key_depth = jnp.dot(
        (mine * depth_row).astype(BF16), spread.astype(BF16), preferred_element_type=F32
    )
    key_level = lax.broadcasted_iota(jnp.int32, (groups, lanes_n), 1) // GROUP
    key_bias = jnp.where(key_depth > key_level.astype(F32), 0.0, NEG)
    qc = lax.broadcasted_iota(jnp.int32, (nq, nk), 0) % GROUP
    kc = lax.broadcasted_iota(jnp.int32, (nq, nk), 1) % GROUP
    same = jnp.where(qc == kc, 0.0, NEG)
    lane = lax.broadcasted_iota(jnp.int32, (1, width), 1)
    masks = [(lane // head == h).astype(F32).astype(BF16) for h in range(HEADS)]
    for g in range(groups):
        cells = slice(g * GROUP, (g + 1) * GROUP)
        bias = same + jnp.concatenate([key_bias[g : g + 1]] * members, axis=1)
        bias = jnp.concatenate([bias] * HEADS, axis=0)
        q = q_ref[:, cells].reshape(nq, width)
        q = jnp.concatenate([q * mask for mask in masks], axis=0)
        k = k_ref[:, cells].reshape(nk, width)
        v = v_ref[:, cells].reshape(nk, width)
        s = lax.dot_general(q, k, (((1,), (1,)), ((), ())), preferred_element_type=F32) + bias
        p = jnp.exp(s - jnp.max(s, axis=-1, keepdims=True))
        norm = 1.0 / jnp.sum(p, axis=-1, keepdims=True)
        p = p.astype(BF16)
        for h in range(HEADS // 2):
            lanes = slice(h * pair, (h + 1) * pair)
            mine = slice(h * 2 * nq, (h + 1) * 2 * nq)
            o = jnp.dot(p[mine], v[:, lanes], preferred_element_type=F32) * norm[mine]
            o = jnp.where(lane[:, :pair] < head, o[:nq], o[nq:])
            att_ref[:, cells, lanes] = o.astype(BF16).reshape(lev, GROUP, pair)
    proj = jnp.dot(att_ref[...].reshape(-1, width), wo_ref[...], preferred_element_type=F32)
    base = jnp.concatenate([p[...].reshape(-1, width) for p in own_mixed], axis=0).astype(F32)
    deep = column(depth_row)
    for l in range(lev):
        rows = slice(l * count, (l + 1) * count)
        wet = widen((deep > l).astype(F32), width)
        out_ref[0, l] = (base[rows] + wet * proj[rows]).astype(BF16)


def attend(
    flag, side, normed, mixed, surf, packed, whole, depth, qkv_weight, out_weight, which, out, shape
):
    others, nparts = len(packed), len(mixed)
    lev = sum(p.shape[0] for p in mixed)
    width = shape[-1]
    rows, cols = depth.shape
    cap = packed[0].shape[0]
    first = 1 if surf else 0
    steps = rows - 2 if which is None else 1
    row_of = lambda i, s: i + 1 if which is None else s[which]
    surf_at = 0 if which is None else rows - 2
    full2 = lambda a: pl.BlockSpec(a.shape, lambda i, *_: (0, 0))
    block = lambda n, at: pl.BlockSpec((n, cols, width), lambda i, *_: (0, i + at, 0))
    part = [block(p.shape[0], surf_at if first and k == 0 else 0) for k, p in enumerate(mixed)]
    hbm = pl.BlockSpec(memory_space=pl.ANY)
    in_specs = part * 2
    in_specs += [block(1, surf_at)] * len(surf)
    in_specs += [full2(p) for p in packed]
    in_specs += [hbm] * others
    in_specs += [full2(depth), full2(qkv_weight), full2(out_weight)]
    args = normed + mixed + surf + packed + whole + [depth, qkv_weight, out_weight]
    alias = {}
    if out is not None:
        in_specs.append(hbm)
        alias = {len(args) + 2: 0}
        args.append(out)
    tokens = lev * cols * steps
    members = others + 1
    return pl.pallas_call(
        functools.partial(attend_kernel, others, nparts, which, first, cap, out is not None),
        grid_spec=pltpu.PrefetchScalarGridSpec(
            num_scalar_prefetch=2,
            grid=(steps,),
            in_specs=in_specs,
            out_specs=pl.BlockSpec(
                (1, lev, cols, width), lambda i, f, s: (0, 0, row_of(i, s), 0)
            ),
            scratch_shapes=[
                pltpu.VMEM((lev, cols, width), BF16),
                pltpu.VMEM((members * lev, cols, width), BF16),
                pltpu.VMEM((members * lev, cols, width), BF16),
                pltpu.VMEM((lev, cols, width), BF16),
                pltpu.VMEM((cap + cols + 16, width), BF16),
                pltpu.VMEM((lev, cols, width), BF16),
                pltpu.SemaphoreType.DMA,
            ],
        ),
        out_shape=jax.ShapeDtypeStruct(shape, BF16),
        input_output_aliases=alias,
        compiler_params=params(20 if members <= 2 else 48, 1),
        cost_estimate=cost(tokens * width * width * 8 * (members + 2), tokens * width * 2 * 5),
        name="attend",
    )(flag, side, *args)


def body(
    atm_latent,
    ocean_state,
    depth,
    src_blocks,
    live,
    remap_weight,
    conv_weight,
    qkv_weight,
    out_weight,
):
    _, lev, cells, width = ocean_state.shape
    cols = remap_weight.shape[2]
    rows = cells // cols
    inner = cells - 2 * cols
    own = atm_latent.shape[1]
    atm_blk = own // cols
    tiles = lax.axis_size("tile")
    members = lax.axis_size("mem")
    tile = lax.axis_index("tile")

    def swap(x, first):
        pairs = [(i, i + 1) for i in range(first, tiles - 1, 2)]
        return lax.ppermute(x, "tile", pairs + [(b, a) for a, b in pairs])

    def exchange(x):
        return [
            lax.ppermute(x, "mem", [(i, (i + k) % members) for i in range(members)])
            for k in range(1, members)
        ]

    odd = tile % 2
    side = jnp.stack([(1 - odd) * (rows - 1), odd * (rows - 1)]).astype(jnp.int32)
    depth = depth.reshape(rows, cols)
    deep_cap = capacity((lev - 1) * inner, 0.5625)
    near_cap = capacity((lev - 1) * cols, 0.605)
    far_cap = capacity(lev * cols, 0.65625)

    hbm = pl.BlockSpec(memory_space=pltpu.HBM)
    anywhere = pl.BlockSpec(memory_space=pl.ANY)
    vmem = pl.BlockSpec(memory_space=pltpu.VMEM)
    smem = pl.BlockSpec(memory_space=pltpu.SMEM)
    tok = lambda *s: pltpu.HBM((*s, width), BF16)
    stay = lambda x: pltpu.with_memory_space_constraint(x, pltpu.HBM)
    conv_flops = lambda n, c: 2 * 9 * n * c * width * width
    dma = pltpu.SemaphoreType.DMA
    slack = cols + 16
    message = lev * cols + own
    on_msg, off_msg, flag = pl.pallas_call(
        functools.partial(prep_kernel, (deep_cap, near_cap, far_cap)),
        in_specs=[smem, hbm, vmem, vmem],
        out_specs=[hbm, hbm, smem],
        out_shape=[tok(message), tok(message), jax.ShapeDtypeStruct((1,), jnp.int32)],
        scratch_shapes=[
            pltpu.VMEM((2, lev, cols, width), BF16),
            dma((2, lev)),
            dma((2, lev)),
            dma((2,)),
        ],
        compiler_params=params(16),
        cost_estimate=cost(lev * cols * width * 4, lev * cols * width * 10),
        name="prep",
    )(side, stay(ocean_state), atm_latent, depth)
    off_halo = swap(off_msg, 1)
    on_halo = swap(on_msg, 0)

    deep_mixed, deep_normed, deep_packed = pl.pallas_call(
        functools.partial(inner_kernel, deep_cap),
        in_specs=[vmem, vmem, vmem],
        out_specs=[hbm] * 3,
        out_shape=[tok(lev - 1, inner), tok(lev - 1, inner), tok(deep_cap)],
        scratch_shapes=[
            pltpu.VMEM((lev - 1, inner, width), BF16),
            pltpu.VMEM((lev - 1, inner, width), BF16),
            pltpu.VMEM((deep_cap + slack, width), BF16),
            dma((lev - 1, 2)),
            dma,
        ],
        compiler_params=params(20),
        cost_estimate=cost(conv_flops(lev, inner), lev * inner * width * 8),
        name="inner",
    )(ocean_state, depth, conv_weight)
    deep_others = exchange(deep_packed)

    whole_spec = lambda *sh: pl.BlockSpec(sh, lambda *_: (0,) * len(sh))
    row_f32 = pltpu.HBM((cols, width), F32)

    def row_conv(which, first, cap, halo, forcing):
        n = lev - first
        extra = [] if forcing is None else [forcing]
        return pl.pallas_call(
            functools.partial(row_kernel, cap, first, which),
            in_specs=[smem, vmem, vmem, hbm, anywhere] + [vmem] * len(extra),
            out_specs=[hbm] * 3 + [whole_spec(cols, width)] * first,
            out_shape=[tok(n, cols), tok(n, cols), tok(cap)] + [row_f32] * first,
            scratch_shapes=[
                pltpu.VMEM(conv_weight.shape, BF16),
                pltpu.VMEM((3, lev * cols, width), BF16),
                pltpu.VMEM((n, cols, width), BF16),
                pltpu.VMEM((n, cols, width), BF16),
                pltpu.VMEM((cap + slack, width), BF16),
                dma,
                dma,
                dma((2,)),
                dma,
            ],
            compiler_params=params(20),
            cost_estimate=cost(conv_flops(lev, cols), lev * cols * width * 16),
            name="row",
        )(side, ocean_state, depth, stay(conv_weight), halo, *extra)

    near_mixed, near_normed, near_packed, near_base = row_conv(0, 1, near_cap, on_halo, None)

    ids = jnp.clip(src_blocks - (tile - R) * atm_blk, 0, 3 * atm_blk - 1)
    surf_mixed, surf_normed, far_forcing = pl.pallas_call(
        surface_kernel,
        in_specs=[smem] * 3 + [vmem] * 3 + [anywhere] * 2 + [hbm] * 2 + [vmem],
        out_specs=[whole_spec(1, inner + cols, width)] * 2 + [whole_spec(cols, width)],
        out_shape=[tok(1, inner + cols), tok(1, inner + cols), row_f32],
        scratch_shapes=[
            pltpu.VMEM((3 * own, width), BF16),
            pltpu.VMEM(remap_weight.shape, BF16),
            pltpu.VMEM((rows, cols, width), F32),
            dma((4,)),
        ],
        compiler_params=params(20),
        cost_estimate=cost(conv_flops(1, inner), cells * width * 16),
        name="surface",
    )(
        ids,
        live,
        side,
        ocean_state,
        depth,
        conv_weight,
        on_halo,
        off_halo,
        stay(atm_latent),
        stay(remap_weight),
        near_base,
    )
    surf_others = exchange(surf_normed)
    near_others = exchange(near_packed)

    far_mixed, far_normed, far_packed = row_conv(1, 0, far_cap, off_halo, far_forcing)
    far_others = exchange(far_packed)

    def unread(shape):
        return pl.pallas_call(
            lambda out_ref: None,
            out_specs=hbm,
            out_shape=pltpu.HBM(shape, BF16),
            name="unread",
        )()

    def send_all(*arrays):
        sizes = [x.shape[0] * x.shape[1] for x in arrays]
        joined = jnp.concatenate([x.reshape(-1, width) for x in arrays], axis=0)
        got = [[] for _ in arrays]
        for part in exchange(joined):
            at = 0
            for k, (x, size) in enumerate(zip(arrays, sizes)):
                got[k].append(part[at : at + size].reshape(x.shape))
                at += size
        return tuple(got)

    deep_whole, near_whole, far_whole = lax.cond(
        flag[0] > 0,
        send_all,
        lambda *a: tuple([unread(x.shape) for _ in range(members - 1)] for x in a),
        deep_normed,
        near_normed,
        far_normed,
    )
    shape = ocean_state.shape
    weights = (depth, qkv_weight, out_weight)
    out = None
    for which, normed, mixed, surf, packed, whole in (
        (
            None,
            [surf_normed, deep_normed],
            [surf_mixed, deep_mixed],
            surf_others,
            deep_others,
            deep_whole,
        ),
        (
            0,
            [surf_normed, near_normed],
            [surf_mixed, near_mixed],
            surf_others,
            near_others,
            near_whole,
        ),
        (1, [far_normed], [far_mixed], [], far_others, far_whole),
    ):
        out = attend(
            flag, side, normed, mixed, surf, packed, whole, *weights, which, out, shape
        )
    return out


def solution(mesh):
    return jax.shard_map(
        body,
        mesh=mesh,
        in_specs=(
            P("mem", "tile", None),
            P("mem", None, "tile", None),
            P("tile"),
            P("tile", None),
            P("tile"),
            P("tile", None, None, None),
            P(),
            P(),
            P(),
        ),
        out_specs=P("mem", None, "tile", None),
        check_vma=False,
    )
```

```python
import functools
import math

import jax
import jax.numpy as jnp
from jax import lax
from jax.experimental import pallas as pl
from jax.experimental.pallas import tpu as pltpu
from jax.sharding import PartitionSpec as P

HEADS = 4
R = 1
GROUP = 16
EPS = 1e-06
NEG = -1e30
F32 = jnp.float32
BF16 = jnp.bfloat16
MIB = 1024 * 1024


def params(mib, steps=0):
    return pltpu.CompilerParams(
        dimension_semantics=("arbitrary",) * steps if steps else None, vmem_limit_bytes=mib * MIB
    )


def cost(flops, nbytes):
    return pl.CostEstimate(flops=int(flops), bytes_accessed=int(nbytes), transcendentals=0)


def capacity(tokens, share):
    return -(-int(tokens * share) // 16) * 16


def row_plan(depth_row, lev):
    cols = depth_row.shape[1]
    level = lax.broadcasted_iota(jnp.int32, (lev, cols), 0).astype(F32)
    wet = (depth_row > level).astype(F32)
    upper = (
        lax.broadcasted_iota(jnp.int32, (cols, cols), 0)
        < lax.broadcasted_iota(jnp.int32, (cols, cols), 1)
    )
    upper = upper.astype(F32).astype(BF16)
    rank = jnp.dot(wet.astype(BF16), upper, preferred_element_type=F32)
    counts = [jnp.sum(wet[l : l + 1]).astype(jnp.int32) for l in range(lev)]
    return wet, rank, counts


def offsets(plans, first, lev):
    at, place = jnp.int32(0), {}
    for l in range(first, lev):
        for r, plan in enumerate(plans):
            place[l, r] = at
            at = at + plan[2][l]
    return place


def segment(wet, rank, offset, cap):
    cols = wet.shape[1]
    base = jnp.minimum((offset // 16) * 16, cap)
    target = jnp.where(wet > 0, rank + (offset - base).astype(F32), -1.0)
    slot = lax.broadcasted_iota(jnp.int32, (cols + 16, cols), 0).astype(F32)
    return pl.multiple_of(base, 16), (slot == target).astype(F32).astype(BF16)


def pack(buf_ref, wet, rank, offset, cap, tokens):
    base, hot = segment(wet, rank, offset, cap)
    rows = jnp.dot(hot, tokens, preferred_element_type=F32).astype(BF16)
    head = pl.ds(base, 16)
    buf_ref[head, :] = buf_ref[head, :] + rows[:16]
    buf_ref[pl.ds(pl.multiple_of(base + 16, 16), rows.shape[0] - 16), :] = rows[16:]


def unpack(buf_ref, wet, rank, offset, cap):
    base, hot = segment(wet, rank, offset, cap)
    rows = buf_ref[pl.ds(base, hot.shape[0]), :]
    return lax.dot_general(
        hot, rows, (((0,), (0,)), ((), ())), preferred_element_type=F32
    ).astype(BF16)


def column(depth_row):
    cols = depth_row.shape[1]
    return jnp.broadcast_to(depth_row, (cols, cols)).T


def widen(x, width):
    return jnp.concatenate([x] * (width // x.shape[1]), axis=1)


def stencil(taps, weight_ref, cols):
    count, width = taps[0].shape
    x = jnp.concatenate(taps, axis=1)
    sums = [
        jnp.dot(x, weight_ref[:, dc].reshape(3 * width, -1), preferred_element_type=F32)
        for dc in range(3)
    ]
    col = lax.broadcasted_iota(jnp.int32, (count, 1), 0) % cols
    left = jnp.where(col == 0, 0.0, pltpu.roll(sums[0], 1, axis=0))
    right = jnp.where(col == cols - 1, 0.0, pltpu.roll(sums[2], count - 1, axis=0))
    return sums[1] + left + right


def normalise(mixed):
    mf = mixed.astype(F32)
    mean = jnp.mean(mf * mf, axis=-1, keepdims=True)
    return (mf * lax.rsqrt(mean + EPS)).astype(BF16)


def prep_kernel(
    caps,
    side_ref,
    state_hbm,
    atm_hbm,
    depth_hbm,
    on_hbm,
    off_hbm,
    flag_ref,
    depth_ref,
    atm,
    rows_in,
    in_sem,
    out_sem,
    atm_sem,
    own_sem,
):
    _, lev, cells, width = state_hbm.shape
    rows, cols = depth_ref.shape
    own = atm_hbm.shape[1]
    sides = (on_hbm, off_hbm)
    load_depth = pltpu.make_async_copy(depth_hbm, depth_ref, own_sem.at[0])
    load_depth.start()
    loads, stores = [], []
    for k in (1, 0):
        at = pl.multiple_of(side_ref[k] * cols, cols)
        for l in range(lev):
            load = pltpu.make_async_copy(
                state_hbm.at[0, l, pl.ds(at, cols)], rows_in.at[k, l], in_sem.at[k, l]
            )
            load.start()
            loads.append((k, l, load))
    load_atm = pltpu.make_async_copy(atm_hbm.at[0], atm, own_sem.at[1])
    load_atm.start()
    load_depth.wait()
    d = depth_ref[...].astype(F32)
    pick = lambda k: jnp.where(side_ref[k] == 0, d[0:1], d[rows - 1 :])
    deep = [column(pick(k)) for k in range(2)]
    for k, l, load in loads:
        wet = widen((deep[k] > l).astype(F32).astype(BF16), width)
        load.wait()
        rows_in[k, l] = rows_in[k, l] * wet
        store = pltpu.make_async_copy(
            rows_in.at[k, l], sides[k].at[pl.ds(l * cols, cols)], out_sem.at[k, l]
        )
        store.start()
        stores.append(store)
    load_atm.wait()
    for k in (1, 0):
        store = pltpu.make_async_copy(
            atm, sides[k].at[pl.ds(lev * cols, own)], atm_sem.at[k]
        )
        store.start()
        stores.append(store)
    counts = [
        jnp.sum(jnp.maximum(d[1 : rows - 1] - 1.0, 0.0)),
        jnp.sum(jnp.maximum(pick(0) - 1.0, 0.0)),
        jnp.sum(pick(1)),
    ]
    over = jnp.int32(0)
    for count, cap in zip(counts, caps):
        over = over | (count > cap).astype(jnp.int32)
    flag_ref[0] = over
    for store in stores:
        store.wait()


def inner_kernel(
    cap,
    state,
    depth_ref,
    weight_hbm,
    mixed_hbm,
    normed_hbm,
    packed_hbm,
    weight,
    mixed,
    normed,
    packed,
    weight_sem,
    out_sem,
    packed_sem,
):
    _, lev, cells, width = state.shape
    rows, cols = depth_ref.shape
    load = pltpu.make_async_copy(weight_hbm, weight, weight_sem)
    load.start()
    packed[...] = jnp.zeros_like(packed)
    d = depth_ref[...].astype(F32)
    plans = [row_plan(d[r : r + 1], lev) for r in range(1, rows - 1)]
    place = offsets(plans, 1, lev)
    deep = jnp.concatenate([column(d[r : r + 1]) for r in range(rows)], axis=0)
    count = cells - 2 * cols
    stores = []
    for l in range(1, lev):
        wet = (deep > l).astype(F32)
        x = state[0, l] * widen(wet.astype(BF16), width)
        taps = [x[dr * cols : dr * cols + count] for dr in range(3)]
        if l == 1:
            load.wait()
        total = stencil(taps, weight, cols)
        new = taps[1].astype(F32) + widen(wet[cols : cols + count], width) * total
        new = new.astype(BF16)
        mixed[l - 1] = new
        tokens = normalise(new)
        normed[l - 1] = tokens
        for k, (buf, out) in enumerate(((mixed, mixed_hbm), (normed, normed_hbm))):
            store = pltpu.make_async_copy(buf.at[l - 1], out.at[l - 1], out_sem.at[l - 1, k])
            store.start()
            stores.append(store)
        for r, plan in enumerate(plans):
            pack(
                packed,
                plan[0][l : l + 1],
                plan[1][l : l + 1],
                place[l, r],
                cap,
                tokens[r * cols : (r + 1) * cols],
            )
        if l == lev - 1:
            store = pltpu.make_async_copy(packed.at[pl.ds(0, cap)], packed_hbm, packed_sem)
            store.start()
            stores.append(store)
    for store in stores:
        store.wait()


def surface_kernel(
    ids_ref,
    live_ref,
    side_ref,
    state,
    depth_ref,
    weight_hbm,
    on_hbm,
    off_hbm,
    atm_hbm,
    remap_hbm,
    base_hbm,
    mixed_ref,
    normed_ref,
    far_ref,
    weight,
    near_base,
    window,
    remap,
    forcing_ref,
    sem,
):
    rows, cols = depth_ref.shape
    _, own, width = atm_hbm.shape
    cells = state.shape[2]
    blocks, pairs = remap_hbm.shape[0], remap_hbm.shape[1]
    on_at = jnp.where(side_ref[0] == 0, 0, 2 * own)
    load = pltpu.make_async_copy(weight_hbm, weight, sem.at[4])
    load.start()
    copies = [
        pltpu.make_async_copy(
            on_hbm.at[pl.ds(on_hbm.shape[0] - own, own)],
            window.at[pl.ds(pl.multiple_of(on_at, own), own)],
            sem.at[0],
        ),
        pltpu.make_async_copy(
            off_hbm.at[pl.ds(off_hbm.shape[0] - own, own)],
            window.at[pl.ds(pl.multiple_of(2 * own - on_at, own), own)],
            sem.at[1],
        ),
        pltpu.make_async_copy(atm_hbm.at[0], window.at[pl.ds(own, own)], sem.at[2]),
        pltpu.make_async_copy(remap_hbm, remap, sem.at[3]),
        pltpu.make_async_copy(base_hbm, near_base, sem.at[5]),
    ]
    for copy in copies:
        copy.start()
    d = depth_ref[...].astype(F32)
    wet = (jnp.concatenate([column(d[r : r + 1]) for r in range(rows)], axis=0) > 0).astype(F32)
    x = state[0, 0] * widen(wet.astype(BF16), width)
    count = cells - 2 * cols
    taps = [x[dr * cols : dr * cols + count] for dr in range(3)]
    for copy in copies:
        copy.wait()
    for b in range(blocks):
        acc = jnp.zeros((cols, width), F32)
        for p in range(pairs):
            on = (p < live_ref[b]).astype(F32)
            start = pl.multiple_of(ids_ref[b, p] * cols, cols)
            acc = acc + on * jnp.dot(
                remap[b, p], window[pl.ds(start, cols), :], preferred_element_type=F32
            )
        forcing_ref[b] = acc
    load.wait()
    total = stencil(taps, weight, cols)
    near = side_ref[0]
    parts = [
        (taps[1][r * cols : (r + 1) * cols].astype(F32), total[r * cols : (r + 1) * cols], r + 1)
        for r in range(rows - 2)
    ]
    for k, (base, conv, r) in enumerate(parts):
        at = slice(k * cols, (k + 1) * cols)
        wet_k = widen(wet[r * cols : (r + 1) * cols], width)
        new = (base + wet_k * (conv + forcing_ref[r])).astype(BF16)
        mixed_ref[0, at] = new
        normed_ref[0, at] = normalise(new)
    at = slice((rows - 2) * cols, (rows - 1) * cols)
    wet_near = jnp.where(near == 0, wet[0:cols], wet[cells - cols :])
    new = (near_base[...] + widen(wet_near, width) * forcing_ref[near]).astype(BF16)
    mixed_ref[0, at] = new
    normed_ref[0, at] = normalise(new)
    far_ref[...] = forcing_ref[side_ref[1]]


def row_kernel(cap, first, which, side_ref, state, depth_ref, weight_hbm, halo_hbm, *refs):
    refs = list(refs)
    forcing_hbm = None if first else refs.pop(0)
    mixed_hbm, normed_hbm, packed_hbm = refs[:3]
    refs = refs[3:]
    base_ref = refs.pop(0) if first else None
    forcing_ref, weight, tap, mixed, normed, packed, weight_sem, halo_sem, out_sem, packed_sem = refs
    load = pltpu.make_async_copy(weight_hbm, weight, weight_sem)
    load.start()
    _, lev, cells, width = state.shape
    rows, cols = depth_ref.shape
    row = side_ref[which]
    top = row == 0
    beside = jnp.where(top, 1, rows - 2)
    outer = jnp.where(top, 0, 2)
    halo = pltpu.make_async_copy(
        halo_hbm.at[pl.ds(0, lev * cols)], tap.at[outer], halo_sem
    )
    halo.start()
    if not first:
        forcing = pltpu.make_async_copy(forcing_hbm, forcing_ref, packed_sem)
        forcing.start()
    packed[...] = jnp.zeros_like(packed)
    d = depth_ref[...].astype(F32)
    own_depth = jnp.where(top, d[0:1], d[rows - 1 :])
    plan = row_plan(own_depth, lev)
    place = offsets([plan], first, lev)
    deep = column(own_depth)
    deep_beside = column(jnp.where(top, d[1:2], d[rows - 2 : rows - 1]))
    at = pl.multiple_of(row * cols, cols)
    at_beside = pl.multiple_of(beside * cols, cols)
    wets = []
    for l in range(lev):
        rows_l = slice(l * cols, (l + 1) * cols)
        wet = (deep > l).astype(F32)
        wets.append(wet)
        wet_beside = (deep_beside > l).astype(F32)
        tap[1, rows_l] = state[0, l, pl.ds(at, cols)] * widen(wet.astype(BF16), width)
        tap[2 - outer, rows_l] = state[0, l, pl.ds(at_beside, cols)] * widen(
            wet_beside.astype(BF16), width
        )
    stores = []
    half = lev // 2
    load.wait()
    halo.wait()
    if not first:
        forcing.wait()
    for start in range(0, lev, half):
        rows_b = slice(start * cols, (start + half) * cols)
        taps = [tap[dr, rows_b] for dr in range(3)]
        total = stencil(taps, weight, cols)
        for k in range(half):
            l = start + k
            rows_k = slice(k * cols, (k + 1) * cols)
            part = total[rows_k]
            if l == 0 and not first:
                part = part + forcing_ref[...]
            new = taps[1][rows_k].astype(F32) + widen(wets[l], width) * part
            if l < first:
                base_ref[...] = new
                continue
            new = new.astype(BF16)
            mixed[l - first] = new
            tokens = normalise(new)
            normed[l - first] = tokens
            pack(packed, plan[0][l : l + 1], plan[1][l : l + 1], place[l, 0], cap, tokens)
    for k, (buf, out) in enumerate(((mixed, mixed_hbm), (normed, normed_hbm))):
        store = pltpu.make_async_copy(buf, out, out_sem.at[k])
        store.start()
        stores.append(store)
    store = pltpu.make_async_copy(packed.at[pl.ds(0, cap)], packed_hbm, packed_sem)
    store.start()
    stores.append(store)
    for store in stores:
        store.wait()


def attend_kernel(others, nparts, which, first, cap, aliased, flag_ref, side_ref, *refs):
    refs = list(refs)
    take = lambda k: [refs.pop(0) for _ in range(k)]
    own_normed = take(nparts)
    own_mixed = take(nparts)
    surf = take(others) if first else []
    packed = take(others)
    whole = take(others)
    depth_ref, qkv_ref, wo_ref = take(3)
    if aliased:
        take(1)
    out_ref, q_ref, k_ref, v_ref, att_ref, buf_ref, token_ref, sem = refs
    lev, count, width = q_ref.shape
    members = others + 1
    head = width // HEADS
    pair = 2 * head
    step = pl.program_id(0)

    def keys_values(x, m):
        rows = slice(m * lev, (m + 1) * lev)
        kv = jnp.dot(x, qkv_ref[:, width:], preferred_element_type=F32).astype(BF16)
        k_ref[rows] = kv[:, :width].reshape(lev, count, width)
        v_ref[rows] = kv[:, width:].reshape(lev, count, width)

    two = which is None
    pick = lambda a, b: jnp.where(step == 0, a, b)
    d = depth_ref[...].astype(F32)
    last = d.shape[0] - 1
    if two:
        rows_d = [d[r : r + 1] for r in range(1, last)]
    else:
        rows_d = [jnp.where(side_ref[which] == 0, d[0:1], d[last:])]
    plans = [row_plan(row, lev) for row in rows_d]
    place = offsets(plans, first, lev)
    wet_row, rank, _ = plans[0]
    depth_row = rows_d[0]
    if two:
        wet_row, rank = pick(wet_row, plans[1][0]), pick(rank, plans[1][1])
        depth_row = pick(*rows_d)

    x = jnp.concatenate([p[...].reshape(-1, width) for p in own_normed], axis=0)
    q = jnp.dot(x, qkv_ref[:, 0:width], preferred_element_type=F32).astype(BF16)
    q_ref[...] = (q * (1.0 / math.sqrt(head))).astype(BF16).reshape(lev, count, width)
    keys_values(x, 0)
    for o in range(others):
        if first:
            token_ref[0] = surf[o][0]

        @pl.when(flag_ref[0] == 0)
        def _():
            buf_ref[0:cap] = packed[o][...]
            buf_ref[cap:] = jnp.zeros((buf_ref.shape[0] - cap, width), BF16)
            for l in range(first, lev):
                at = pick(place[l, 0], place[l, 1]) if two else place[l, 0]
                token_ref[l] = unpack(
                    buf_ref, wet_row[l : l + 1], rank[l : l + 1], at, cap
                )

        @pl.when(flag_ref[0] != 0)
        def _():
            copy = pltpu.make_async_copy(
                whole[o].at[:, pl.ds(pl.multiple_of(step * count, count), count)], token_ref.at[pl.ds(first, lev - first)], sem
            )
            copy.start()
            copy.wait()

        keys_values(token_ref[...].reshape(-1, width), o + 1)

    nq, nk = lev * GROUP, members * lev * GROUP
    groups = count // GROUP
    lanes_n = lev * GROUP
    cell = lax.broadcasted_iota(jnp.int32, (groups, count), 1)
    mine = (cell // GROUP == lax.broadcasted_iota(jnp.int32, (groups, count), 0)).astype(F32)
    spread = lax.broadcasted_iota(jnp.int32, (count, lanes_n), 0) % GROUP
    spread = (spread == lax.broadcasted_iota(jnp.int32, (count, lanes_n), 1) % GROUP).astype(F32)
    key_depth = jnp.dot(
        (mine * depth_row).astype(BF16), spread.astype(BF16), preferred_element_type=F32
    )
    key_level = lax.broadcasted_iota(jnp.int32, (groups, lanes_n), 1) // GROUP
    key_bias = jnp.where(key_depth > key_level.astype(F32), 0.0, NEG)
    qc = lax.broadcasted_iota(jnp.int32, (nq, nk), 0) % GROUP
    kc = lax.broadcasted_iota(jnp.int32, (nq, nk), 1) % GROUP
    same = jnp.where(qc == kc, 0.0, NEG)
    lane = lax.broadcasted_iota(jnp.int32, (1, width), 1)
    masks = [(lane // head == h).astype(F32).astype(BF16) for h in range(HEADS)]
    for g in range(groups):
        cells = slice(g * GROUP, (g + 1) * GROUP)
        bias = same + jnp.concatenate([key_bias[g : g + 1]] * members, axis=1)
        bias = jnp.concatenate([bias] * HEADS, axis=0)
        q = q_ref[:, cells].reshape(nq, width)
        q = jnp.concatenate([q * mask for mask in masks], axis=0)
        k = k_ref[:, cells].reshape(nk, width)
        v = v_ref[:, cells].reshape(nk, width)
        s = lax.dot_general(q, k, (((1,), (1,)), ((), ())), preferred_element_type=F32) + bias
        p = jnp.exp(s - jnp.max(s, axis=-1, keepdims=True))
        norm = 1.0 / jnp.sum(p, axis=-1, keepdims=True)
        p = p.astype(BF16)
        for h in range(HEADS // 2):
            lanes = slice(h * pair, (h + 1) * pair)
            mine = slice(h * 2 * nq, (h + 1) * 2 * nq)
            o = jnp.dot(p[mine], v[:, lanes], preferred_element_type=F32) * norm[mine]
            o = jnp.where(lane[:, :pair] < head, o[:nq], o[nq:])
            att_ref[:, cells, lanes] = o.astype(BF16).reshape(lev, GROUP, pair)
    proj = jnp.dot(att_ref[...].reshape(-1, width), wo_ref[...], preferred_element_type=F32)
    base = jnp.concatenate([p[...].reshape(-1, width) for p in own_mixed], axis=0).astype(F32)
    deep = column(depth_row)
    for l in range(lev):
        rows = slice(l * count, (l + 1) * count)
        wet = widen((deep > l).astype(F32), width)
        out_ref[0, l] = (base[rows] + wet * proj[rows]).astype(BF16)


def attend(
    flag, side, normed, mixed, surf, packed, whole, depth, qkv_weight, out_weight, which, out, shape
):
    others, nparts = len(packed), len(mixed)
    lev = sum(p.shape[0] for p in mixed)
    width = shape[-1]
    rows, cols = depth.shape
    cap = packed[0].shape[0]
    first = 1 if surf else 0
    steps = rows - 2 if which is None else 1
    row_of = lambda i, s: i + 1 if which is None else s[which]
    surf_at = 0 if which is None else rows - 2
    full2 = lambda a: pl.BlockSpec(a.shape, lambda i, *_: (0, 0))
    block = lambda n, at: pl.BlockSpec((n, cols, width), lambda i, *_: (0, i + at, 0))
    part = [block(p.shape[0], surf_at if first and k == 0 else 0) for k, p in enumerate(mixed)]
    hbm = pl.BlockSpec(memory_space=pl.ANY)
    in_specs = part * 2
    in_specs += [block(1, surf_at)] * len(surf)
    in_specs += [full2(p) for p in packed]
    in_specs += [hbm] * others
    in_specs += [full2(depth), full2(qkv_weight), full2(out_weight)]
    stay = lambda x: pltpu.with_memory_space_constraint(x, pltpu.HBM)
    args = [stay(x) for x in normed + mixed] + surf + packed + whole
    args += [depth, qkv_weight, out_weight]
    alias = {}
    if out is not None:
        in_specs.append(hbm)
        alias = {len(args) + 2: 0}
        args.append(out)
    tokens = lev * cols * steps
    members = others + 1
    return pl.pallas_call(
        functools.partial(attend_kernel, others, nparts, which, first, cap, out is not None),
        grid_spec=pltpu.PrefetchScalarGridSpec(
            num_scalar_prefetch=2,
            grid=(steps,),
            in_specs=in_specs,
            out_specs=pl.BlockSpec(
                (1, lev, cols, width), lambda i, f, s: (0, 0, row_of(i, s), 0)
            ),
            scratch_shapes=[
                pltpu.VMEM((lev, cols, width), BF16),
                pltpu.VMEM((members * lev, cols, width), BF16),
                pltpu.VMEM((members * lev, cols, width), BF16),
                pltpu.VMEM((lev, cols, width), BF16),
                pltpu.VMEM((cap + cols + 16, width), BF16),
                pltpu.VMEM((lev, cols, width), BF16),
                pltpu.SemaphoreType.DMA,
            ],
        ),
        out_shape=jax.ShapeDtypeStruct(shape, BF16),
        input_output_aliases=alias,
        compiler_params=params(16 if members <= 2 else 48, 1),
        cost_estimate=cost(tokens * width * width * 8 * (members + 2), tokens * width * 2 * 5),
        name="attend",
    )(flag, side, *args)


def body(
    atm_latent,
    ocean_state,
    depth,
    src_blocks,
    live,
    remap_weight,
    conv_weight,
    qkv_weight,
    out_weight,
):
    _, lev, cells, width = ocean_state.shape
    cols = remap_weight.shape[2]
    rows = cells // cols
    inner = cells - 2 * cols
    own = atm_latent.shape[1]
    atm_blk = own // cols
    tiles = lax.axis_size("tile")
    members = lax.axis_size("mem")
    tile = lax.axis_index("tile")

    def swap(x, first):
        pairs = [(i, i + 1) for i in range(first, tiles - 1, 2)]
        return lax.ppermute(x, "tile", pairs + [(b, a) for a, b in pairs])

    def exchange(x):
        return [
            lax.ppermute(x, "mem", [(i, (i + k) % members) for i in range(members)])
            for k in range(1, members)
        ]

    odd = tile % 2
    side = jnp.stack([(1 - odd) * (rows - 1), odd * (rows - 1)]).astype(jnp.int32)
    depth = depth.reshape(rows, cols)
    deep_cap = capacity((lev - 1) * inner, 0.5625)
    near_cap = capacity((lev - 1) * cols, 0.605)
    far_cap = capacity(lev * cols, 0.65625)

    hbm = pl.BlockSpec(memory_space=pltpu.HBM)
    anywhere = pl.BlockSpec(memory_space=pl.ANY)
    vmem = pl.BlockSpec(memory_space=pltpu.VMEM)
    smem = pl.BlockSpec(memory_space=pltpu.SMEM)
    tok = lambda *s: pltpu.HBM((*s, width), BF16)
    stay = lambda x: pltpu.with_memory_space_constraint(x, pltpu.HBM)
    conv_flops = lambda n, c: 2 * 9 * n * c * width * width
    dma = pltpu.SemaphoreType.DMA
    slack = cols + 16
    message = lev * cols + own
    on_msg, off_msg, flag = pl.pallas_call(
        functools.partial(prep_kernel, (deep_cap, near_cap, far_cap)),
        in_specs=[smem, hbm, hbm, hbm],
        out_specs=[hbm, hbm, smem],
        out_shape=[tok(message), tok(message), jax.ShapeDtypeStruct((1,), jnp.int32)],
        scratch_shapes=[
            pltpu.VMEM((rows, cols), jnp.int32),
            pltpu.VMEM((own, width), BF16),
            pltpu.VMEM((2, lev, cols, width), BF16),
            dma((2, lev)),
            dma((2, lev)),
            dma((2,)),
            dma((2,)),
        ],
        compiler_params=params(16),
        cost_estimate=cost(lev * cols * width * 4, lev * cols * width * 10),
        name="prep",
    )(side, stay(ocean_state), stay(atm_latent), stay(depth))
    off_halo = swap(off_msg, 1)
    on_halo = swap(on_msg, 0)

    deep_mixed, deep_normed, deep_packed = pl.pallas_call(
        functools.partial(inner_kernel, deep_cap),
        in_specs=[vmem, vmem, hbm],
        out_specs=[hbm] * 3,
        out_shape=[tok(lev - 1, inner), tok(lev - 1, inner), tok(deep_cap)],
        scratch_shapes=[
            pltpu.VMEM(conv_weight.shape, BF16),
            pltpu.VMEM((lev - 1, inner, width), BF16),
            pltpu.VMEM((lev - 1, inner, width), BF16),
            pltpu.VMEM((deep_cap + slack, width), BF16),
            dma,
            dma((lev - 1, 2)),
            dma,
        ],
        compiler_params=params(12),
        cost_estimate=cost(conv_flops(lev, inner), lev * inner * width * 8),
        name="inner",
    )(ocean_state, depth, stay(conv_weight))
    deep_others = exchange(deep_packed)

    whole_spec = lambda *sh: pl.BlockSpec(sh, lambda *_: (0,) * len(sh))
    row_f32 = pltpu.HBM((cols, width), F32)

    def row_conv(which, first, cap, halo, forcing):
        n = lev - first
        extra = [] if forcing is None else [stay(forcing)]
        return pl.pallas_call(
            functools.partial(row_kernel, cap, first, which),
            in_specs=[smem, vmem, vmem, hbm, anywhere] + [hbm] * len(extra),
            out_specs=[hbm] * 3 + [whole_spec(cols, width)] * first,
            out_shape=[tok(n, cols), tok(n, cols), tok(cap)] + [row_f32] * first,
            scratch_shapes=[
                pltpu.VMEM((cols, width), F32),
                pltpu.VMEM(conv_weight.shape, BF16),
                pltpu.VMEM((3, lev * cols, width), BF16),
                pltpu.VMEM((n, cols, width), BF16),
                pltpu.VMEM((n, cols, width), BF16),
                pltpu.VMEM((cap + slack, width), BF16),
                dma,
                dma,
                dma((2,)),
                dma,
            ],
            compiler_params=params(12),
            cost_estimate=cost(conv_flops(lev, cols), lev * cols * width * 16),
            name="row",
        )(side, ocean_state, depth, stay(conv_weight), halo, *extra)

    near_mixed, near_normed, near_packed, near_base = row_conv(0, 1, near_cap, on_halo, None)

    ids = jnp.clip(src_blocks - (tile - R) * atm_blk, 0, 3 * atm_blk - 1)
    surf_mixed, surf_normed, far_forcing = pl.pallas_call(
        surface_kernel,
        in_specs=[smem] * 3 + [vmem] * 2 + [hbm] + [anywhere] * 2 + [hbm] * 3,
        out_specs=[whole_spec(1, inner + cols, width)] * 2 + [whole_spec(cols, width)],
        out_shape=[tok(1, inner + cols), tok(1, inner + cols), row_f32],
        scratch_shapes=[
            pltpu.VMEM(conv_weight.shape, BF16),
            pltpu.VMEM((cols, width), F32),
            pltpu.VMEM((3 * own, width), BF16),
            pltpu.VMEM(remap_weight.shape, BF16),
            pltpu.VMEM((rows, cols, width), F32),
            dma((6,)),
        ],
        compiler_params=params(12),
        cost_estimate=cost(conv_flops(1, inner), cells * width * 16),
        name="surface",
    )(
        ids,
        live,
        side,
        ocean_state,
        depth,
        stay(conv_weight),
        on_halo,
        off_halo,
        stay(atm_latent),
        stay(remap_weight),
        stay(near_base),
    )
    surf_others = exchange(surf_normed)
    near_others = exchange(near_packed)

    far_mixed, far_normed, far_packed = row_conv(1, 0, far_cap, off_halo, far_forcing)
    far_others = exchange(far_packed)

    def unread(shape):
        return pl.pallas_call(
            lambda out_ref: None,
            out_specs=hbm,
            out_shape=pltpu.HBM(shape, BF16),
            name="unread",
        )()

    def send_all(*arrays):
        sizes = [x.shape[0] * x.shape[1] for x in arrays]
        joined = jnp.concatenate([x.reshape(-1, width) for x in arrays], axis=0)
        got = [[] for _ in arrays]
        for part in exchange(joined):
            at = 0
            for k, (x, size) in enumerate(zip(arrays, sizes)):
                got[k].append(part[at : at + size].reshape(x.shape))
                at += size
        return tuple(got)

    deep_whole, near_whole, far_whole = lax.cond(
        flag[0] > 0,
        send_all,
        lambda *a: tuple([unread(x.shape) for _ in range(members - 1)] for x in a),
        deep_normed,
        near_normed,
        far_normed,
    )
    shape = ocean_state.shape
    weights = (depth, qkv_weight, out_weight)
    out = None
    for which, normed, mixed, surf, packed, whole in (
        (
            None,
            [surf_normed, deep_normed],
            [surf_mixed, deep_mixed],
            surf_others,
            deep_others,
            deep_whole,
        ),
        (
            0,
            [surf_normed, near_normed],
            [surf_mixed, near_mixed],
            surf_others,
            near_others,
            near_whole,
        ),
        (1, [far_normed], [far_mixed], [], far_others, far_whole),
    ):
        out = attend(
            flag, side, normed, mixed, surf, packed, whole, *weights, which, out, shape
        )
    return out


def solution(mesh):
    return jax.shard_map(
        body,
        mesh=mesh,
        in_specs=(
            P("mem", "tile", None),
            P("mem", None, "tile", None),
            P("tile"),
            P("tile", None),
            P("tile"),
            P("tile", None, None, None),
            P(),
            P(),
            P(),
        ),
        out_specs=P("mem", None, "tile", None),
        check_vma=False,
    )
```

```python
import functools
import math

import jax
import jax.numpy as jnp
from jax import lax
from jax.experimental import pallas as pl
from jax.experimental.pallas import tpu as pltpu
from jax.sharding import PartitionSpec as P

HEADS = 4
R = 1
GROUP = 16
EPS = 1e-06
NEG = -1e30
F32 = jnp.float32
BF16 = jnp.bfloat16
MIB = 1024 * 1024


def params(mib, steps=0):
    return pltpu.CompilerParams(
        dimension_semantics=("arbitrary",) * steps if steps else None, vmem_limit_bytes=mib * MIB
    )


def cost(flops, nbytes):
    return pl.CostEstimate(flops=int(flops), bytes_accessed=int(nbytes), transcendentals=0)


def capacity(tokens, share):
    return -(-int(tokens * share) // 16) * 16


def row_plan(depth_row, lev):
    cols = depth_row.shape[1]
    level = lax.broadcasted_iota(jnp.int32, (lev, cols), 0).astype(F32)
    wet = (depth_row > level).astype(F32)
    upper = (
        lax.broadcasted_iota(jnp.int32, (cols, cols), 0)
        < lax.broadcasted_iota(jnp.int32, (cols, cols), 1)
    )
    upper = upper.astype(F32).astype(BF16)
    rank = jnp.dot(wet.astype(BF16), upper, preferred_element_type=F32)
    counts = [jnp.sum(wet[l : l + 1]).astype(jnp.int32) for l in range(lev)]
    return wet, rank, counts


def offsets(plans, first, lev):
    at, place = jnp.int32(0), {}
    for l in range(first, lev):
        for r, plan in enumerate(plans):
            place[l, r] = at
            at = at + plan[2][l]
    return place


def segment(wet, rank, offset, cap):
    cols = wet.shape[1]
    base = jnp.minimum((offset // 16) * 16, cap)
    target = jnp.where(wet > 0, rank + (offset - base).astype(F32), -1.0)
    slot = lax.broadcasted_iota(jnp.int32, (cols + 16, cols), 0).astype(F32)
    return pl.multiple_of(base, 16), (slot == target).astype(F32).astype(BF16)


def pack(buf_ref, wet, rank, offset, cap, tokens):
    base, hot = segment(wet, rank, offset, cap)
    rows = jnp.dot(hot, tokens, preferred_element_type=F32).astype(BF16)
    head = pl.ds(base, 16)
    buf_ref[head, :] = buf_ref[head, :] + rows[:16]
    buf_ref[pl.ds(pl.multiple_of(base + 16, 16), rows.shape[0] - 16), :] = rows[16:]


def unpack(buf_ref, wet, rank, offset, cap):
    base, hot = segment(wet, rank, offset, cap)
    rows = buf_ref[pl.ds(base, hot.shape[0]), :]
    return lax.dot_general(
        hot, rows, (((0,), (0,)), ((), ())), preferred_element_type=F32
    ).astype(BF16)


def column(depth_row):
    cols = depth_row.shape[1]
    return jnp.broadcast_to(depth_row, (cols, cols)).T


def widen(x, width):
    return jnp.concatenate([x] * (width // x.shape[1]), axis=1)


def stencil(taps, weight_ref, cols):
    count, width = taps[0].shape
    x = jnp.concatenate(taps, axis=1)
    sums = [
        jnp.dot(x, weight_ref[:, dc].reshape(3 * width, -1), preferred_element_type=F32)
        for dc in range(3)
    ]
    col = lax.broadcasted_iota(jnp.int32, (count, 1), 0) % cols
    left = jnp.where(col == 0, 0.0, pltpu.roll(sums[0], 1, axis=0))
    right = jnp.where(col == cols - 1, 0.0, pltpu.roll(sums[2], count - 1, axis=0))
    return sums[1] + left + right


def normalise(mixed):
    mf = mixed.astype(F32)
    mean = jnp.mean(mf * mf, axis=-1, keepdims=True)
    return (mf * lax.rsqrt(mean + EPS)).astype(BF16)


def prep_kernel(
    caps,
    side_ref,
    state_hbm,
    atm_hbm,
    depth_hbm,
    on_hbm,
    off_hbm,
    flag_ref,
    depth_ref,
    atm,
    rows_in,
    in_sem,
    out_sem,
    atm_sem,
    own_sem,
):
    _, lev, cells, width = state_hbm.shape
    rows, cols = depth_ref.shape
    own = atm_hbm.shape[1]
    sides = (on_hbm, off_hbm)
    load_depth = pltpu.make_async_copy(depth_hbm, depth_ref, own_sem.at[0])
    load_depth.start()
    loads, stores = [], []
    for k in (1, 0):
        at = pl.multiple_of(side_ref[k] * cols, cols)
        for l in range(lev):
            load = pltpu.make_async_copy(
                state_hbm.at[0, l, pl.ds(at, cols)], rows_in.at[k, l], in_sem.at[k, l]
            )
            load.start()
            loads.append((k, l, load))
    load_atm = pltpu.make_async_copy(atm_hbm.at[0], atm, own_sem.at[1])
    load_atm.start()
    load_depth.wait()
    d = depth_ref[...].astype(F32)
    pick = lambda k: jnp.where(side_ref[k] == 0, d[0:1], d[rows - 1 :])
    deep = [column(pick(k)) for k in range(2)]
    for k, l, load in loads:
        wet = widen((deep[k] > l).astype(F32).astype(BF16), width)
        load.wait()
        rows_in[k, l] = rows_in[k, l] * wet
        store = pltpu.make_async_copy(
            rows_in.at[k, l], sides[k].at[pl.ds(l * cols, cols)], out_sem.at[k, l]
        )
        store.start()
        stores.append(store)
    load_atm.wait()
    for k in (1, 0):
        store = pltpu.make_async_copy(
            atm, sides[k].at[pl.ds(lev * cols, own)], atm_sem.at[k]
        )
        store.start()
        stores.append(store)
    counts = [
        jnp.sum(jnp.maximum(d[1 : rows - 1] - 1.0, 0.0)),
        jnp.sum(jnp.maximum(pick(0) - 1.0, 0.0)),
        jnp.sum(pick(1)),
    ]
    over = jnp.int32(0)
    for count, cap in zip(counts, caps):
        over = over | (count > cap).astype(jnp.int32)
    flag_ref[0] = over
    for store in stores:
        store.wait()


def inner_kernel(
    cap,
    state,
    depth_ref,
    weight_hbm,
    mixed_hbm,
    normed_hbm,
    packed_hbm,
    weight,
    mixed,
    normed,
    packed,
    weight_sem,
    out_sem,
    packed_sem,
):
    _, lev, cells, width = state.shape
    rows, cols = depth_ref.shape
    load = pltpu.make_async_copy(weight_hbm, weight, weight_sem)
    load.start()
    packed[...] = jnp.zeros_like(packed)
    d = depth_ref[...].astype(F32)
    plans = [row_plan(d[r : r + 1], lev) for r in range(1, rows - 1)]
    place = offsets(plans, 1, lev)
    deep = jnp.concatenate([column(d[r : r + 1]) for r in range(rows)], axis=0)
    count = cells - 2 * cols
    stores = []
    for l in range(1, lev):
        wet = (deep > l).astype(F32)
        x = state[0, l] * widen(wet.astype(BF16), width)
        taps = [x[dr * cols : dr * cols + count] for dr in range(3)]
        if l == 1:
            load.wait()
        total = stencil(taps, weight, cols)
        new = taps[1].astype(F32) + widen(wet[cols : cols + count], width) * total
        new = new.astype(BF16)
        mixed[l - 1] = new
        tokens = normalise(new)
        normed[l - 1] = tokens
        for k, (buf, out) in enumerate(((mixed, mixed_hbm), (normed, normed_hbm))):
            store = pltpu.make_async_copy(buf.at[l - 1], out.at[l - 1], out_sem.at[l - 1, k])
            store.start()
            stores.append(store)
        for r, plan in enumerate(plans):
            pack(
                packed,
                plan[0][l : l + 1],
                plan[1][l : l + 1],
                place[l, r],
                cap,
                tokens[r * cols : (r + 1) * cols],
            )
        if l == lev - 1:
            store = pltpu.make_async_copy(packed.at[pl.ds(0, cap)], packed_hbm, packed_sem)
            store.start()
            stores.append(store)
    for store in stores:
        store.wait()


def surface_kernel(
    ids_ref,
    live_ref,
    side_ref,
    depth_ref,
    on_hbm,
    off_hbm,
    atm_hbm,
    remap_hbm,
    base_hbm,
    edge_mixed_in,
    edge_normed_in,
    mixed_ref,
    normed_ref,
    far_ref,
    edge_mixed_hbm,
    edge_normed_hbm,
    base,
    window,
    remap,
    forcing_ref,
    sem,
):
    rows, cols = depth_ref.shape
    _, own, width = atm_hbm.shape
    blocks, pairs = remap_hbm.shape[0], remap_hbm.shape[1]
    on_at = jnp.where(side_ref[0] == 0, 0, 2 * own)
    copies = [
        pltpu.make_async_copy(
            on_hbm.at[pl.ds(on_hbm.shape[0] - own, own)],
            window.at[pl.ds(pl.multiple_of(on_at, own), own)],
            sem.at[0],
        ),
        pltpu.make_async_copy(
            off_hbm.at[pl.ds(off_hbm.shape[0] - own, own)],
            window.at[pl.ds(pl.multiple_of(2 * own - on_at, own), own)],
            sem.at[1],
        ),
        pltpu.make_async_copy(atm_hbm.at[0], window.at[pl.ds(own, own)], sem.at[2]),
        pltpu.make_async_copy(remap_hbm, remap, sem.at[3]),
        pltpu.make_async_copy(base_hbm, base, sem.at[4]),
    ]
    for copy in copies:
        copy.start()
    d = depth_ref[...].astype(F32)
    near, far = side_ref[0], side_ref[1]
    rows_d = [d[r : r + 1] for r in range(1, rows - 1)]
    rows_d.append(jnp.where(near == 0, d[0:1], d[rows - 1 :]))
    wets = [widen((column(row) > 0).astype(F32), width) for row in rows_d]
    for copy in copies:
        copy.wait()
    for b in range(blocks):
        acc = jnp.zeros((cols, width), F32)
        for p in range(pairs):
            on = (p < live_ref[b]).astype(F32)
            start = pl.multiple_of(ids_ref[b, p] * cols, cols)
            acc = acc + on * jnp.dot(
                remap[b, p], window[pl.ds(start, cols), :], preferred_element_type=F32
            )
        forcing_ref[b] = acc
    for k, wet in enumerate(wets):
        at = slice(k * cols, (k + 1) * cols)
        forcing = forcing_ref[near] if k == rows - 2 else forcing_ref[k + 1]
        new = (base[at] + wet * forcing).astype(BF16)
        mixed_ref[0, at] = new
        normed_ref[0, at] = normalise(new)
    far_ref[...] = forcing_ref[far]
    at = pl.ds((rows - 2) * cols, cols)
    stores = [
        pltpu.make_async_copy(mixed_ref.at[0, at], edge_mixed_hbm.at[0, pl.ds(0, cols)], sem.at[5]),
        pltpu.make_async_copy(normed_ref.at[0, at], edge_normed_hbm.at[0, pl.ds(0, cols)], sem.at[6]),
    ]
    for store in stores:
        store.start()
    for store in stores:
        store.wait()


def row_kernel(cap, first, which, side_ref, state, depth_ref, weight_hbm, halo_hbm, *refs):
    refs = list(refs)
    forcing_hbm = None
    if not first:
        forcing_hbm = refs[0]
        refs = refs[3:]
    mixed_hbm, normed_hbm, packed_hbm = refs[:3]
    refs = refs[3:]
    base_ref = refs.pop(0) if first else None
    forcing_ref, weight, tap, mixed, normed, packed, weight_sem, halo_sem, out_sem, packed_sem = refs
    load = pltpu.make_async_copy(weight_hbm, weight, weight_sem)
    load.start()
    _, lev, cells, width = state.shape
    rows, cols = depth_ref.shape
    row = side_ref[which]
    top = row == 0
    beside = jnp.where(top, 1, rows - 2)
    outer = jnp.where(top, 0, 2)
    halo = pltpu.make_async_copy(
        halo_hbm.at[pl.ds(0, lev * cols)], tap.at[outer], halo_sem
    )
    halo.start()
    if not first:
        forcing = pltpu.make_async_copy(forcing_hbm, forcing_ref, packed_sem)
        forcing.start()
    packed[...] = jnp.zeros_like(packed)
    d = depth_ref[...].astype(F32)
    own_depth = jnp.where(top, d[0:1], d[rows - 1 :])
    plan = row_plan(own_depth, lev)
    place = offsets([plan], first, lev)
    deep = column(own_depth)
    deep_beside = column(jnp.where(top, d[1:2], d[rows - 2 : rows - 1]))
    at = pl.multiple_of(row * cols, cols)
    at_beside = pl.multiple_of(beside * cols, cols)
    wets = []
    for l in range(lev):
        rows_l = slice(l * cols, (l + 1) * cols)
        wet = (deep > l).astype(F32)
        wets.append(wet)
        wet_beside = (deep_beside > l).astype(F32)
        tap[1, rows_l] = state[0, l, pl.ds(at, cols)] * widen(wet.astype(BF16), width)
        tap[2 - outer, rows_l] = state[0, l, pl.ds(at_beside, cols)] * widen(
            wet_beside.astype(BF16), width
        )
    stores = []
    half = lev // 2
    load.wait()
    halo.wait()
    if not first:
        forcing.wait()
    for start in range(0, lev, half):
        rows_b = slice(start * cols, (start + half) * cols)
        taps = [tap[dr, rows_b] for dr in range(3)]
        total = stencil(taps, weight, cols)
        for k in range(half):
            l = start + k
            rows_k = slice(k * cols, (k + 1) * cols)
            part = total[rows_k]
            if l == 0 and not first:
                part = part + forcing_ref[...]
            new = taps[1][rows_k].astype(F32) + widen(wets[l], width) * part
            if l < first:
                base_ref[cells - 2 * cols :] = new
                continue
            new = new.astype(BF16)
            mixed[l - first] = new
            tokens = normalise(new)
            normed[l - first] = tokens
            pack(packed, plan[0][l : l + 1], plan[1][l : l + 1], place[l, 0], cap, tokens)
    if first:
        wet = (jnp.concatenate([column(d[r : r + 1]) for r in range(rows)], axis=0) > 0).astype(F32)
        x = state[0, 0] * widen(wet.astype(BF16), width)
        taps = [x[dr * cols : dr * cols + cells - 2 * cols] for dr in range(3)]
        inside = widen(wet[cols : cells - cols], width)
        base_ref[0 : cells - 2 * cols] = taps[1].astype(F32) + inside * stencil(taps, weight, cols)
    block = (pl.ds(first, lev - first), pl.ds(which * cols, cols))
    for k, (buf, out) in enumerate(((mixed, mixed_hbm), (normed, normed_hbm))):
        store = pltpu.make_async_copy(buf, out.at[block], out_sem.at[k])
        store.start()
        stores.append(store)
    store = pltpu.make_async_copy(packed.at[pl.ds(0, cap)], packed_hbm, packed_sem)
    store.start()
    stores.append(store)
    for store in stores:
        store.wait()


def attend_kernel(others, nparts, edges, flag_ref, side_ref, *refs):
    refs = list(refs)
    take = lambda k: [refs.pop(0) for _ in range(k)]
    own_normed = take(nparts)
    own_mixed = take(nparts)
    surf = take(others)
    packed = [take(others) for _ in range(1 + edges)]
    whole = take(others)
    depth_ref, qkv_ref, wo_ref = take(3)
    if edges:
        take(1)
    out_ref, q_ref, k_ref, v_ref, att_ref, buf_ref, token_ref, sem = refs
    lev, count, width = q_ref.shape
    members = others + 1
    head = width // HEADS
    pair = 2 * head
    step = pl.program_id(0)
    cap = max(p[0].shape[0] for p in packed)

    def keys_values(x, m):
        rows = slice(m * lev, (m + 1) * lev)
        kv = jnp.dot(x, qkv_ref[:, width:], preferred_element_type=F32).astype(BF16)
        k_ref[rows] = kv[:, :width].reshape(lev, count, width)
        v_ref[rows] = kv[:, width:].reshape(lev, count, width)

    pick = lambda a, b: jnp.where(step == 0, a, b)
    d = depth_ref[...].astype(F32)
    last = d.shape[0] - 1
    if edges:
        rows_d = [jnp.where(side_ref[k] == 0, d[0:1], d[last:]) for k in range(2)]
        plans = [row_plan(row, lev) for row in rows_d]
        near, far = offsets(plans[:1], 1, lev), offsets(plans[1:], 0, lev)
        place = [far[0, 0]] + [pick(near[l, 0], far[l, 0]) for l in range(1, lev)]
    else:
        rows_d = [d[r : r + 1] for r in range(1, last)]
        plans = [row_plan(row, lev) for row in rows_d]
        both = offsets(plans, 1, lev)
        place = [None] + [pick(both[l, 0], both[l, 1]) for l in range(1, lev)]
    wet_row, rank = pick(plans[0][0], plans[1][0]), pick(plans[0][1], plans[1][1])
    depth_row = pick(*rows_d)

    def fill(packed_ref):
        size = packed_ref.shape[0]
        buf_ref[0:size] = packed_ref[...]
        buf_ref[size : size + count + 16] = jnp.zeros((count + 16, width), BF16)

    def restore(l):
        token_ref[l] = unpack(buf_ref, wet_row[l : l + 1], rank[l : l + 1], place[l], cap)

    x = jnp.concatenate([p[...].reshape(-1, width) for p in own_normed], axis=0)
    q = jnp.dot(x, qkv_ref[:, 0:width], preferred_element_type=F32).astype(BF16)
    q_ref[...] = (q * (1.0 / math.sqrt(head))).astype(BF16).reshape(lev, count, width)
    keys_values(x, 0)
    for o in range(others):

        @pl.when(flag_ref[0] == 0)
        def _():
            if edges:

                @pl.when(step == 0)
                def _():
                    token_ref[0] = surf[o][0]
                    fill(packed[0][o])

                @pl.when(step == 1)
                def _():
                    fill(packed[1][o])
                    restore(0)

            else:
                token_ref[0] = surf[o][0]
                fill(packed[0][o])
            for l in range(1, lev):
                restore(l)

        @pl.when(flag_ref[0] != 0)
        def _():
            if not edges:
                token_ref[0] = surf[o][0]
            first = lev - whole[o].shape[0]
            copy = pltpu.make_async_copy(
                whole[o].at[:, pl.ds(pl.multiple_of(step * count, count), count)],
                token_ref.at[pl.ds(first, lev - first)],
                sem,
            )
            copy.start()
            copy.wait()

        keys_values(token_ref[...].reshape(-1, width), o + 1)

    nq, nk = lev * GROUP, members * lev * GROUP
    groups = count // GROUP
    lanes_n = lev * GROUP
    cell = lax.broadcasted_iota(jnp.int32, (groups, count), 1)
    mine = (cell // GROUP == lax.broadcasted_iota(jnp.int32, (groups, count), 0)).astype(F32)
    spread = lax.broadcasted_iota(jnp.int32, (count, lanes_n), 0) % GROUP
    spread = (spread == lax.broadcasted_iota(jnp.int32, (count, lanes_n), 1) % GROUP).astype(F32)
    key_depth = jnp.dot(
        (mine * depth_row).astype(BF16), spread.astype(BF16), preferred_element_type=F32
    )
    key_level = lax.broadcasted_iota(jnp.int32, (groups, lanes_n), 1) // GROUP
    key_bias = jnp.where(key_depth > key_level.astype(F32), 0.0, NEG)
    qc = lax.broadcasted_iota(jnp.int32, (nq, nk), 0) % GROUP
    kc = lax.broadcasted_iota(jnp.int32, (nq, nk), 1) % GROUP
    same = jnp.where(qc == kc, 0.0, NEG)
    lane = lax.broadcasted_iota(jnp.int32, (1, width), 1)
    masks = [(lane // head == h).astype(F32).astype(BF16) for h in range(HEADS)]
    for g in range(groups):
        cells = slice(g * GROUP, (g + 1) * GROUP)
        bias = same + jnp.concatenate([key_bias[g : g + 1]] * members, axis=1)
        bias = jnp.concatenate([bias] * HEADS, axis=0)
        q = q_ref[:, cells].reshape(nq, width)
        q = jnp.concatenate([q * mask for mask in masks], axis=0)
        k = k_ref[:, cells].reshape(nk, width)
        v = v_ref[:, cells].reshape(nk, width)
        s = lax.dot_general(q, k, (((1,), (1,)), ((), ())), preferred_element_type=F32) + bias
        p = jnp.exp(s - jnp.max(s, axis=-1, keepdims=True))
        norm = 1.0 / jnp.sum(p, axis=-1, keepdims=True)
        p = p.astype(BF16)
        for h in range(HEADS // 2):
            lanes = slice(h * pair, (h + 1) * pair)
            mine = slice(h * 2 * nq, (h + 1) * 2 * nq)
            o = jnp.dot(p[mine], v[:, lanes], preferred_element_type=F32) * norm[mine]
            o = jnp.where(lane[:, :pair] < head, o[:nq], o[nq:])
            att_ref[:, cells, lanes] = o.astype(BF16).reshape(lev, GROUP, pair)
    proj = jnp.dot(att_ref[...].reshape(-1, width), wo_ref[...], preferred_element_type=F32)
    base = jnp.concatenate([p[...].reshape(-1, width) for p in own_mixed], axis=0).astype(F32)
    deep = column(depth_row)
    for l in range(lev):
        rows = slice(l * count, (l + 1) * count)
        wet = widen((deep > l).astype(F32), width)
        out_ref[0, l] = (base[rows] + wet * proj[rows]).astype(BF16)


def attend(
    flag, side, normed, mixed, surf, packed, whole, depth, qkv_weight, out_weight, out, shape
):
    edges = out is not None
    others, nparts = len(whole), len(mixed)
    lev = sum(p.shape[0] for p in mixed)
    width = shape[-1]
    rows, cols = depth.shape
    cap = max(p.shape[0] for p in packed)
    row_of = lambda i, s: s[i] if edges else i + 1
    full2 = lambda a: pl.BlockSpec(a.shape, lambda i, *_: (0, 0))
    block = lambda n: pl.BlockSpec((n, cols, width), lambda i, *_: (0, i, 0))
    near = pl.BlockSpec((1, cols, width), lambda i, *_: (0, rows - 2, 0))
    part = [block(p.shape[0]) for p in mixed]
    hbm = pl.BlockSpec(memory_space=pl.ANY)
    in_specs = part * 2
    in_specs += [near if edges else block(1)] * others
    in_specs += [full2(p) for p in packed]
    in_specs += [hbm] * others
    in_specs += [full2(depth), full2(qkv_weight), full2(out_weight)]
    stay = lambda x: pltpu.with_memory_space_constraint(x, pltpu.HBM)
    args = [x if edges else stay(x) for x in normed + mixed]
    args += surf + packed + whole + [depth, qkv_weight, out_weight]
    alias = {}
    if edges:
        in_specs.append(hbm)
        alias = {len(args) + 2: 0}
        args.append(out)
    tokens = lev * cols * 2
    members = others + 1
    return pl.pallas_call(
        functools.partial(attend_kernel, others, nparts, edges),
        grid_spec=pltpu.PrefetchScalarGridSpec(
            num_scalar_prefetch=2,
            grid=(2,),
            in_specs=in_specs,
            out_specs=pl.BlockSpec(
                (1, lev, cols, width), lambda i, f, s: (0, 0, row_of(i, s), 0)
            ),
            scratch_shapes=[
                pltpu.VMEM((lev, cols, width), BF16),
                pltpu.VMEM((members * lev, cols, width), BF16),
                pltpu.VMEM((members * lev, cols, width), BF16),
                pltpu.VMEM((lev, cols, width), BF16),
                pltpu.VMEM((cap + cols + 16, width), BF16),
                pltpu.VMEM((lev, cols, width), BF16),
                pltpu.SemaphoreType.DMA,
            ],
        ),
        out_shape=jax.ShapeDtypeStruct(shape, BF16),
        input_output_aliases=alias,
        compiler_params=params(16 if members <= 2 else 48, 1),
        cost_estimate=cost(tokens * width * width * 8 * (members + 2), tokens * width * 2 * 5),
        name="attend",
    )(flag, side, *args)


def body(
    atm_latent,
    ocean_state,
    depth,
    src_blocks,
    live,
    remap_weight,
    conv_weight,
    qkv_weight,
    out_weight,
):
    _, lev, cells, width = ocean_state.shape
    cols = remap_weight.shape[2]
    rows = cells // cols
    inner = cells - 2 * cols
    own = atm_latent.shape[1]
    atm_blk = own // cols
    tiles = lax.axis_size("tile")
    members = lax.axis_size("mem")
    tile = lax.axis_index("tile")

    def swap(x, first):
        pairs = [(i, i + 1) for i in range(first, tiles - 1, 2)]
        return lax.ppermute(x, "tile", pairs + [(b, a) for a, b in pairs])

    def exchange(x):
        return [
            lax.ppermute(x, "mem", [(i, (i + k) % members) for i in range(members)])
            for k in range(1, members)
        ]

    odd = tile % 2
    side = jnp.stack([(1 - odd) * (rows - 1), odd * (rows - 1)]).astype(jnp.int32)
    depth = depth.reshape(rows, cols)
    deep_cap = capacity((lev - 1) * inner, 0.5625)
    near_cap = capacity((lev - 1) * cols, 0.605)
    far_cap = capacity(lev * cols, 0.65625)

    hbm = pl.BlockSpec(memory_space=pltpu.HBM)
    anywhere = pl.BlockSpec(memory_space=pl.ANY)
    vmem = pl.BlockSpec(memory_space=pltpu.VMEM)
    smem = pl.BlockSpec(memory_space=pltpu.SMEM)
    tok = lambda *s: pltpu.HBM((*s, width), BF16)
    stay = lambda x: pltpu.with_memory_space_constraint(x, pltpu.HBM)
    conv_flops = lambda n, c: 2 * 9 * n * c * width * width
    dma = pltpu.SemaphoreType.DMA
    slack = cols + 16
    message = lev * cols + own
    on_msg, off_msg, flag = pl.pallas_call(
        functools.partial(prep_kernel, (deep_cap, near_cap, far_cap)),
        in_specs=[smem, hbm, hbm, hbm],
        out_specs=[hbm, hbm, smem],
        out_shape=[tok(message), tok(message), jax.ShapeDtypeStruct((1,), jnp.int32)],
        scratch_shapes=[
            pltpu.VMEM((rows, cols), jnp.int32),
            pltpu.VMEM((own, width), BF16),
            pltpu.VMEM((2, lev, cols, width), BF16),
            dma((2, lev)),
            dma((2, lev)),
            dma((2,)),
            dma((2,)),
        ],
        compiler_params=params(16),
        cost_estimate=cost(lev * cols * width * 4, lev * cols * width * 10),
        name="prep",
    )(side, stay(ocean_state), stay(atm_latent), stay(depth))
    off_halo = swap(off_msg, 1)
    on_halo = swap(on_msg, 0)

    deep_mixed, deep_normed, deep_packed = pl.pallas_call(
        functools.partial(inner_kernel, deep_cap),
        in_specs=[vmem, vmem, hbm],
        out_specs=[hbm] * 3,
        out_shape=[tok(lev - 1, inner), tok(lev - 1, inner), tok(deep_cap)],
        scratch_shapes=[
            pltpu.VMEM(conv_weight.shape, BF16),
            pltpu.VMEM((lev - 1, inner, width), BF16),
            pltpu.VMEM((lev - 1, inner, width), BF16),
            pltpu.VMEM((deep_cap + slack, width), BF16),
            dma,
            dma((lev - 1, 2)),
            dma,
        ],
        compiler_params=params(12),
        cost_estimate=cost(conv_flops(lev, inner), lev * inner * width * 8),
        name="inner",
    )(ocean_state, depth, stay(conv_weight))
    deep_others = exchange(deep_packed)

    whole_spec = lambda *sh: pl.BlockSpec(sh, lambda *_: (0,) * len(sh))
    row_f32 = pltpu.HBM((cols, width), F32)

    def row_conv(which, first, cap, halo, extra):
        n = lev - first
        base = pltpu.HBM((inner + cols, width), F32)
        return pl.pallas_call(
            functools.partial(row_kernel, cap, first, which),
            in_specs=[smem, vmem, vmem, hbm, anywhere] + [hbm] * len(extra),
            out_specs=[hbm] * 3 + [whole_spec(inner + cols, width)] * first,
            out_shape=[tok(lev, 2 * cols), tok(lev, 2 * cols), tok(cap)] + [base] * first,
            scratch_shapes=[
                pltpu.VMEM((cols, width), F32),
                pltpu.VMEM(conv_weight.shape, BF16),
                pltpu.VMEM((3, lev * cols, width), BF16),
                pltpu.VMEM((n, cols, width), BF16),
                pltpu.VMEM((n, cols, width), BF16),
                pltpu.VMEM((cap + slack, width), BF16),
                dma,
                dma,
                dma((2,)),
                dma,
            ],
            input_output_aliases={6: 0, 7: 1} if extra else {},
            compiler_params=params(12),
            cost_estimate=cost(conv_flops(lev, cols), lev * cols * width * 16),
            name="row",
        )(side, ocean_state, depth, stay(conv_weight), halo, *[stay(x) for x in extra])

    edge_mixed, edge_normed, near_packed, base = row_conv(0, 1, near_cap, on_halo, [])

    ids = jnp.clip(src_blocks - (tile - R) * atm_blk, 0, 3 * atm_blk - 1)
    surf_mixed, surf_normed, far_forcing, edge_mixed, edge_normed = pl.pallas_call(
        surface_kernel,
        in_specs=[smem] * 3 + [vmem] + [anywhere] * 2 + [hbm] * 5,
        out_specs=[whole_spec(1, inner + cols, width)] * 2 + [whole_spec(cols, width)] + [hbm] * 2,
        out_shape=[tok(1, inner + cols), tok(1, inner + cols), row_f32]
        + [tok(lev, 2 * cols)] * 2,
        scratch_shapes=[
            pltpu.VMEM((inner + cols, width), F32),
            pltpu.VMEM((3 * own, width), BF16),
            pltpu.VMEM(remap_weight.shape, BF16),
            pltpu.VMEM((rows, cols, width), F32),
            dma((7,)),
        ],
        input_output_aliases={9: 3, 10: 4},
        compiler_params=params(12),
        cost_estimate=cost(conv_flops(1, inner), cells * width * 16),
        name="surface",
    )(
        ids,
        live,
        side,
        depth,
        on_halo,
        off_halo,
        stay(atm_latent),
        stay(remap_weight),
        stay(base),
        stay(edge_mixed),
        stay(edge_normed),
    )
    surf_others = exchange(surf_normed)
    near_others = exchange(near_packed)

    edge_mixed, edge_normed, far_packed = row_conv(
        1, 0, far_cap, off_halo, [far_forcing, edge_mixed, edge_normed]
    )
    far_others = exchange(far_packed)

    def unread(shape):
        return pl.pallas_call(
            lambda out_ref: None,
            out_specs=hbm,
            out_shape=pltpu.HBM(shape, BF16),
            name="unread",
        )()

    def send_all(*arrays):
        sizes = [x.shape[0] * x.shape[1] for x in arrays]
        joined = jnp.concatenate([x.reshape(-1, width) for x in arrays], axis=0)
        got = [[] for _ in arrays]
        for part in exchange(joined):
            at = 0
            for k, (x, size) in enumerate(zip(arrays, sizes)):
                got[k].append(part[at : at + size].reshape(x.shape))
                at += size
        return tuple(got)

    deep_whole, edge_whole = lax.cond(
        flag[0] > 0,
        send_all,
        lambda *a: tuple([unread(x.shape) for _ in range(members - 1)] for x in a),
        deep_normed,
        edge_normed,
    )
    shape = ocean_state.shape
    weights = (depth, qkv_weight, out_weight)
    out = attend(
        flag,
        side,
        [surf_normed, deep_normed],
        [surf_mixed, deep_mixed],
        surf_others,
        deep_others,
        deep_whole,
        *weights,
        None,
        shape,
    )
    return attend(
        flag,
        side,
        [edge_normed],
        [edge_mixed],
        surf_others,
        near_others + far_others,
        edge_whole,
        *weights,
        out,
        shape,
    )


def solution(mesh):
    return jax.shard_map(
        body,
        mesh=mesh,
        in_specs=(
            P("mem", "tile", None),
            P("mem", None, "tile", None),
            P("tile"),
            P("tile", None),
            P("tile"),
            P("tile", None, None, None),
            P(),
            P(),
            P(),
        ),
        out_specs=P("mem", None, "tile", None),
        check_vma=False,
    )
```

```python
import functools
import math

import jax
import jax.numpy as jnp
from jax import lax
from jax.experimental import pallas as pl
from jax.experimental.pallas import tpu as pltpu
from jax.sharding import PartitionSpec as P

HEADS = 4
R = 1
GROUP = 16
EPS = 1e-06
NEG = -1e30
F32 = jnp.float32
BF16 = jnp.bfloat16
MIB = 1024 * 1024


def params(mib, steps=0):
    return pltpu.CompilerParams(
        dimension_semantics=("arbitrary",) * steps if steps else None, vmem_limit_bytes=mib * MIB
    )


def cost(flops, nbytes):
    return pl.CostEstimate(flops=int(flops), bytes_accessed=int(nbytes), transcendentals=0)


def capacity(tokens, share):
    return -(-int(tokens * share) // 16) * 16


def row_plan(depth_row, lev):
    cols = depth_row.shape[1]
    level = lax.broadcasted_iota(jnp.int32, (lev, cols), 0).astype(F32)
    wet = (depth_row > level).astype(F32)
    upper = (
        lax.broadcasted_iota(jnp.int32, (cols, cols), 0)
        < lax.broadcasted_iota(jnp.int32, (cols, cols), 1)
    )
    upper = upper.astype(F32).astype(BF16)
    rank = jnp.dot(wet.astype(BF16), upper, preferred_element_type=F32)
    counts = [jnp.sum(wet[l : l + 1]).astype(jnp.int32) for l in range(lev)]
    return wet, rank, counts


def offsets(plans, first, lev):
    at, place = jnp.int32(0), {}
    for l in range(first, lev):
        for r, plan in enumerate(plans):
            place[l, r] = at
            at = at + plan[2][l]
    return place


def segment(wet, rank, offset, limit):
    cols = wet.shape[1]
    base = jnp.minimum((offset // 16) * 16, limit)
    target = jnp.where(wet > 0, rank + (offset - base).astype(F32), -1.0)
    slot = lax.broadcasted_iota(jnp.int32, (cols + 16, cols), 0).astype(F32)
    return pl.multiple_of(base, 16), (slot == target).astype(F32).astype(BF16)


def pack(buf_ref, wet, rank, offset, cap, tokens):
    base, hot = segment(wet, rank, offset, cap)
    rows = jnp.dot(hot, tokens, preferred_element_type=F32).astype(BF16)
    head = pl.ds(base, 16)
    buf_ref[head, :] = buf_ref[head, :] + rows[:16]
    buf_ref[pl.ds(pl.multiple_of(base + 16, 16), rows.shape[0] - 16), :] = rows[16:]


def unpack(rows_of, wet, rank, offset, limit):
    base, hot = segment(wet, rank, offset, limit)
    return lax.dot_general(
        hot, rows_of(base, hot.shape[0]), (((0,), (0,)), ((), ())), preferred_element_type=F32
    ).astype(BF16)


def column(depth_row):
    cols = depth_row.shape[1]
    return jnp.broadcast_to(depth_row, (cols, cols)).T


def widen(x, width):
    return jnp.concatenate([x] * (width // x.shape[1]), axis=1)


def stencil(taps, weight_ref, cols):
    count, width = taps[0].shape
    x = jnp.concatenate(taps, axis=1)
    sums = [
        jnp.dot(x, weight_ref[:, dc].reshape(3 * width, -1), preferred_element_type=F32)
        for dc in range(3)
    ]
    col = lax.broadcasted_iota(jnp.int32, (count, 1), 0) % cols
    left = jnp.where(col == 0, 0.0, pltpu.roll(sums[0], 1, axis=0))
    right = jnp.where(col == cols - 1, 0.0, pltpu.roll(sums[2], count - 1, axis=0))
    return sums[1] + left + right


def normalise(mixed):
    mf = mixed.astype(F32)
    mean = jnp.mean(mf * mf, axis=-1, keepdims=True)
    return (mf * lax.rsqrt(mean + EPS)).astype(BF16)


def prep_kernel(
    caps,
    side_ref,
    state_hbm,
    atm_hbm,
    depth_hbm,
    on_hbm,
    off_hbm,
    flag_ref,
    depth_ref,
    atm,
    rows_in,
    in_sem,
    out_sem,
    atm_sem,
    own_sem,
):
    _, lev, cells, width = state_hbm.shape
    rows, cols = depth_ref.shape
    own = atm_hbm.shape[1]
    sides = (on_hbm, off_hbm)
    load_depth = pltpu.make_async_copy(depth_hbm, depth_ref, own_sem.at[0])
    load_depth.start()
    loads, stores = [], []
    for k in (1, 0):
        at = pl.multiple_of(side_ref[k] * cols, cols)
        for l in range(lev):
            load = pltpu.make_async_copy(
                state_hbm.at[0, l, pl.ds(at, cols)], rows_in.at[k, l], in_sem.at[k, l]
            )
            load.start()
            loads.append((k, l, load))
    load_atm = pltpu.make_async_copy(atm_hbm.at[0], atm, own_sem.at[1])
    load_atm.start()
    load_depth.wait()
    d = depth_ref[...].astype(F32)
    pick = lambda k: jnp.where(side_ref[k] == 0, d[0:1], d[rows - 1 :])
    deep = [column(pick(k)) for k in range(2)]
    for k, l, load in loads:
        wet = widen((deep[k] > l).astype(F32).astype(BF16), width)
        load.wait()
        rows_in[k, l] = rows_in[k, l] * wet
        store = pltpu.make_async_copy(
            rows_in.at[k, l], sides[k].at[pl.ds(l * cols, cols)], out_sem.at[k, l]
        )
        store.start()
        stores.append(store)
    load_atm.wait()
    for k in (1, 0):
        store = pltpu.make_async_copy(
            atm, sides[k].at[pl.ds(lev * cols, own)], atm_sem.at[k]
        )
        store.start()
        stores.append(store)
    counts = [
        jnp.sum(jnp.maximum(d[1 : rows - 1] - 1.0, 0.0)),
        jnp.sum(jnp.maximum(pick(0) - 1.0, 0.0)),
        jnp.sum(pick(1)),
    ]
    over = jnp.int32(0)
    for count, cap in zip(counts, caps):
        over = over | (count > cap).astype(jnp.int32)
    flag_ref[0] = over
    for store in stores:
        store.wait()


def inner_kernel(
    cap,
    state,
    depth_ref,
    weight_hbm,
    mixed_hbm,
    normed_hbm,
    packed_hbm,
    weight,
    mixed,
    normed,
    packed,
    weight_sem,
    out_sem,
    packed_sem,
):
    _, lev, cells, width = state.shape
    rows, cols = depth_ref.shape
    load = pltpu.make_async_copy(weight_hbm, weight, weight_sem)
    load.start()
    packed[...] = jnp.zeros_like(packed)
    d = depth_ref[...].astype(F32)
    plans = [row_plan(d[r : r + 1], lev) for r in range(1, rows - 1)]
    place = offsets(plans, 1, lev)
    deep = jnp.concatenate([column(d[r : r + 1]) for r in range(rows)], axis=0)
    count = cells - 2 * cols
    stores = []
    for l in range(1, lev):
        wet = (deep > l).astype(F32)
        x = state[0, l] * widen(wet.astype(BF16), width)
        taps = [x[dr * cols : dr * cols + count] for dr in range(3)]
        if l == 1:
            load.wait()
        total = stencil(taps, weight, cols)
        new = taps[1].astype(F32) + widen(wet[cols : cols + count], width) * total
        new = new.astype(BF16)
        mixed[l - 1] = new
        tokens = normalise(new)
        normed[l - 1] = tokens
        for k, (buf, out) in enumerate(((mixed, mixed_hbm), (normed, normed_hbm))):
            store = pltpu.make_async_copy(buf.at[l - 1], out.at[l - 1], out_sem.at[l - 1, k])
            store.start()
            stores.append(store)
        for r, plan in enumerate(plans):
            pack(
                packed,
                plan[0][l : l + 1],
                plan[1][l : l + 1],
                place[l, r],
                cap,
                tokens[r * cols : (r + 1) * cols],
            )
        if l == lev - 1:
            store = pltpu.make_async_copy(packed.at[pl.ds(0, cap)], packed_hbm, packed_sem)
            store.start()
            stores.append(store)
    for store in stores:
        store.wait()


def surface_kernel(
    ids_ref,
    live_ref,
    side_ref,
    depth_ref,
    on_hbm,
    off_hbm,
    atm_ref,
    remap,
    base_hbm,
    edge_mixed_in,
    edge_normed_in,
    mixed_ref,
    normed_ref,
    far_ref,
    edge_mixed_hbm,
    edge_normed_hbm,
    base,
    window,
    forcing_ref,
    sem,
):
    rows, cols = depth_ref.shape
    _, own, width = atm_ref.shape
    blocks, pairs = remap.shape[0], remap.shape[1]
    on_at = jnp.where(side_ref[0] == 0, 0, 2 * own)
    copies = [
        pltpu.make_async_copy(
            on_hbm.at[pl.ds(on_hbm.shape[0] - own, own)],
            window.at[pl.ds(pl.multiple_of(on_at, own), own)],
            sem.at[0],
        ),
        pltpu.make_async_copy(
            off_hbm.at[pl.ds(off_hbm.shape[0] - own, own)],
            window.at[pl.ds(pl.multiple_of(2 * own - on_at, own), own)],
            sem.at[1],
        ),
        pltpu.make_async_copy(base_hbm, base, sem.at[4]),
    ]
    for copy in copies:
        copy.start()
    window[own : 2 * own] = atm_ref[0]
    d = depth_ref[...].astype(F32)
    near, far = side_ref[0], side_ref[1]
    rows_d = [d[r : r + 1] for r in range(1, rows - 1)]
    rows_d.append(jnp.where(near == 0, d[0:1], d[rows - 1 :]))
    wets = [widen((column(row) > 0).astype(F32), width) for row in rows_d]
    for copy in copies:
        copy.wait()
    for b in range(blocks):
        acc = jnp.zeros((cols, width), F32)
        for p in range(pairs):
            on = (p < live_ref[b]).astype(F32)
            start = pl.multiple_of(ids_ref[b, p] * cols, cols)
            acc = acc + on * jnp.dot(
                remap[b, p], window[pl.ds(start, cols), :], preferred_element_type=F32
            )
        forcing_ref[b] = acc
    for k, wet in enumerate(wets):
        at = slice(k * cols, (k + 1) * cols)
        forcing = forcing_ref[near] if k == rows - 2 else forcing_ref[k + 1]
        new = (base[at] + wet * forcing).astype(BF16)
        mixed_ref[0, at] = new
        normed_ref[0, at] = normalise(new)
    far_ref[...] = forcing_ref[far]
    at = pl.ds((rows - 2) * cols, cols)
    stores = [
        pltpu.make_async_copy(mixed_ref.at[0, at], edge_mixed_hbm.at[0, pl.ds(0, cols)], sem.at[2]),
        pltpu.make_async_copy(normed_ref.at[0, at], edge_normed_hbm.at[0, pl.ds(0, cols)], sem.at[3]),
    ]
    for store in stores:
        store.start()
    for store in stores:
        store.wait()


def row_kernel(cap, first, which, side_ref, state, depth_ref, weight_hbm, halo_hbm, *refs):
    refs = list(refs)
    forcing_hbm = None
    if not first:
        forcing_hbm = refs[0]
        refs = refs[3:]
    mixed_hbm, normed_hbm, packed_hbm = refs[:3]
    refs = refs[3:]
    base_ref = refs.pop(0) if first else None
    forcing_ref, weight, tap, mixed, normed, packed, weight_sem, halo_sem, out_sem, packed_sem = refs
    load = pltpu.make_async_copy(weight_hbm, weight, weight_sem)
    load.start()
    _, lev, cells, width = state.shape
    rows, cols = depth_ref.shape
    row = side_ref[which]
    top = row == 0
    beside = jnp.where(top, 1, rows - 2)
    outer = jnp.where(top, 0, 2)
    halo = pltpu.make_async_copy(
        halo_hbm.at[pl.ds(0, lev * cols)], tap.at[outer], halo_sem
    )
    halo.start()
    if not first:
        forcing = pltpu.make_async_copy(forcing_hbm, forcing_ref, packed_sem)
        forcing.start()
    packed[...] = jnp.zeros_like(packed)
    d = depth_ref[...].astype(F32)
    own_depth = jnp.where(top, d[0:1], d[rows - 1 :])
    plan = row_plan(own_depth, lev)
    place = offsets([plan], first, lev)
    deep = column(own_depth)
    deep_beside = column(jnp.where(top, d[1:2], d[rows - 2 : rows - 1]))
    at = pl.multiple_of(row * cols, cols)
    at_beside = pl.multiple_of(beside * cols, cols)
    wets = []
    for l in range(lev):
        rows_l = slice(l * cols, (l + 1) * cols)
        wet = (deep > l).astype(F32)
        wets.append(wet)
        wet_beside = (deep_beside > l).astype(F32)
        tap[1, rows_l] = state[0, l, pl.ds(at, cols)] * widen(wet.astype(BF16), width)
        tap[2 - outer, rows_l] = state[0, l, pl.ds(at_beside, cols)] * widen(
            wet_beside.astype(BF16), width
        )
    stores = []
    half = lev // 2
    load.wait()
    halo.wait()
    if not first:
        forcing.wait()
    for start in range(0, lev, half):
        rows_b = slice(start * cols, (start + half) * cols)
        taps = [tap[dr, rows_b] for dr in range(3)]
        total = stencil(taps, weight, cols)
        for k in range(half):
            l = start + k
            rows_k = slice(k * cols, (k + 1) * cols)
            part = total[rows_k]
            if l == 0 and not first:
                part = part + forcing_ref[...]
            new = taps[1][rows_k].astype(F32) + widen(wets[l], width) * part
            if l < first:
                base_ref[cells - 2 * cols :] = new
                continue
            new = new.astype(BF16)
            mixed[l - first] = new
            tokens = normalise(new)
            normed[l - first] = tokens
            pack(packed, plan[0][l : l + 1], plan[1][l : l + 1], place[l, 0], cap, tokens)
    if first:
        wet = (jnp.concatenate([column(d[r : r + 1]) for r in range(rows)], axis=0) > 0).astype(F32)
        x = state[0, 0] * widen(wet.astype(BF16), width)
        taps = [x[dr * cols : dr * cols + cells - 2 * cols] for dr in range(3)]
        inside = widen(wet[cols : cells - cols], width)
        base_ref[0 : cells - 2 * cols] = taps[1].astype(F32) + inside * stencil(taps, weight, cols)
    block = (pl.ds(first, lev - first), pl.ds(which * cols, cols))
    for k, (buf, out) in enumerate(((mixed, mixed_hbm), (normed, normed_hbm))):
        store = pltpu.make_async_copy(buf, out.at[block], out_sem.at[k])
        store.start()
        stores.append(store)
    store = pltpu.make_async_copy(packed.at[pl.ds(0, cap)], packed_hbm, packed_sem)
    store.start()
    stores.append(store)
    for store in stores:
        store.wait()


def attend_kernel(others, nparts, edges, flag_ref, side_ref, *refs):
    refs = list(refs)
    take = lambda k: [refs.pop(0) for _ in range(k)]
    own_normed = take(nparts)
    own_mixed = take(nparts)
    surf = take(others)
    packed = [take(others) for _ in range(1 + edges)]
    whole = take(others)
    depth_ref, qkv_ref, wo_ref = take(3)
    if edges:
        take(1)
    out_ref, q_ref, k_ref, v_ref, att_ref, token_ref, sem = refs
    lev, count, width = q_ref.shape
    members = others + 1
    head = width // HEADS
    pair = 2 * head
    step = pl.program_id(0)

    def keys_values(x, m):
        rows = slice(m * lev, (m + 1) * lev)
        kv = jnp.dot(x, qkv_ref[:, width:], preferred_element_type=F32).astype(BF16)
        k_ref[rows] = kv[:, :width].reshape(lev, count, width)
        v_ref[rows] = kv[:, width:].reshape(lev, count, width)

    pick = lambda a, b: jnp.where(step == 0, a, b)
    d = depth_ref[...].astype(F32)
    last = d.shape[0] - 1
    if edges:
        rows_d = [jnp.where(side_ref[k] == 0, d[0:1], d[last:]) for k in range(2)]
        plans = [row_plan(row, lev) for row in rows_d]
        near, far = offsets(plans[:1], 1, lev), offsets(plans[1:], 0, lev)
        place = [far[0, 0]] + [pick(near[l, 0], far[l, 0]) for l in range(1, lev)]
    else:
        rows_d = [d[r : r + 1] for r in range(1, last)]
        plans = [row_plan(row, lev) for row in rows_d]
        both = offsets(plans, 1, lev)
        place = [None] + [pick(both[l, 0], both[l, 1]) for l in range(1, lev)]
    wet_row, rank = pick(plans[0][0], plans[1][0]), pick(plans[0][1], plans[1][1])
    depth_row = pick(*rows_d)

    window = count + 16
    limits = [p[0].shape[0] - window for p in packed]
    limit = pick(*limits) if edges else limits[0]

    def restore(l, o):
        def rows_of(base, size):
            if not edges:
                return packed[0][o][pl.ds(base, size), :]
            near_at, far_at = (pl.multiple_of(jnp.minimum(base, at), 16) for at in limits)
            return pick(packed[0][o][pl.ds(near_at, size), :], packed[1][o][pl.ds(far_at, size), :])

        return unpack(rows_of, wet_row[l : l + 1], rank[l : l + 1], place[l], limit)

    x = jnp.concatenate([p[...].reshape(-1, width) for p in own_normed], axis=0)
    q = jnp.dot(x, qkv_ref[:, 0:width], preferred_element_type=F32).astype(BF16)
    q_ref[...] = (q * (1.0 / math.sqrt(head))).astype(BF16).reshape(lev, count, width)
    keys_values(x, 0)
    for o in range(others):
        token_ref[0] = pick(surf[o][0], restore(0, o)) if edges else surf[o][0]
        for l in range(1, lev):
            token_ref[l] = restore(l, o)

        @pl.when(flag_ref[0] != 0)
        def _():
            first = lev - whole[o].shape[0]
            copy = pltpu.make_async_copy(
                whole[o].at[:, pl.ds(pl.multiple_of(step * count, count), count)],
                token_ref.at[pl.ds(first, lev - first)],
                sem,
            )
            copy.start()
            copy.wait()

        keys_values(token_ref[...].reshape(-1, width), o + 1)

    nq, nk = lev * GROUP, members * lev * GROUP
    groups = count // GROUP
    lanes_n = lev * GROUP
    cell = lax.broadcasted_iota(jnp.int32, (groups, count), 1)
    mine = (cell // GROUP == lax.broadcasted_iota(jnp.int32, (groups, count), 0)).astype(F32)
    spread = lax.broadcasted_iota(jnp.int32, (count, lanes_n), 0) % GROUP
    spread = (spread == lax.broadcasted_iota(jnp.int32, (count, lanes_n), 1) % GROUP).astype(F32)
    key_depth = jnp.dot(
        (mine * depth_row).astype(BF16), spread.astype(BF16), preferred_element_type=F32
    )
    key_level = lax.broadcasted_iota(jnp.int32, (groups, lanes_n), 1) // GROUP
    key_bias = jnp.where(key_depth > key_level.astype(F32), 0.0, NEG)
    qc = lax.broadcasted_iota(jnp.int32, (nq, nk), 0) % GROUP
    kc = lax.broadcasted_iota(jnp.int32, (nq, nk), 1) % GROUP
    same = jnp.where(qc == kc, 0.0, NEG)
    lane = lax.broadcasted_iota(jnp.int32, (1, width), 1)
    masks = [(lane // head == h).astype(F32).astype(BF16) for h in range(HEADS)]
    for g in range(groups):
        cells = slice(g * GROUP, (g + 1) * GROUP)
        bias = same + jnp.concatenate([key_bias[g : g + 1]] * members, axis=1)
        bias = jnp.concatenate([bias] * HEADS, axis=0)
        q = q_ref[:, cells].reshape(nq, width)
        q = jnp.concatenate([q * mask for mask in masks], axis=0)
        k = k_ref[:, cells].reshape(nk, width)
        v = v_ref[:, cells].reshape(nk, width)
        s = lax.dot_general(q, k, (((1,), (1,)), ((), ())), preferred_element_type=F32) + bias
        p = jnp.exp(s - jnp.max(s, axis=-1, keepdims=True))
        norm = 1.0 / jnp.sum(p, axis=-1, keepdims=True)
        p = p.astype(BF16)
        for h in range(HEADS // 2):
            lanes = slice(h * pair, (h + 1) * pair)
            mine = slice(h * 2 * nq, (h + 1) * 2 * nq)
            o = jnp.dot(p[mine], v[:, lanes], preferred_element_type=F32) * norm[mine]
            o = jnp.where(lane[:, :pair] < head, o[:nq], o[nq:])
            att_ref[:, cells, lanes] = o.astype(BF16).reshape(lev, GROUP, pair)
    proj = jnp.dot(att_ref[...].reshape(-1, width), wo_ref[...], preferred_element_type=F32)
    base = jnp.concatenate([p[...].reshape(-1, width) for p in own_mixed], axis=0).astype(F32)
    deep = column(depth_row)
    for l in range(lev):
        rows = slice(l * count, (l + 1) * count)
        wet = widen((deep > l).astype(F32), width)
        out_ref[0, l] = (base[rows] + wet * proj[rows]).astype(BF16)


def attend(
    flag, side, normed, mixed, surf, packed, whole, depth, qkv_weight, out_weight, out, shape
):
    edges = out is not None
    others, nparts = len(whole), len(mixed)
    lev = sum(p.shape[0] for p in mixed)
    width = shape[-1]
    rows, cols = depth.shape
    row_of = lambda i, s: s[i] if edges else i + 1
    full2 = lambda a: pl.BlockSpec(a.shape, lambda i, *_: (0, 0))
    block = lambda n: pl.BlockSpec((n, cols, width), lambda i, *_: (0, i, 0))
    near = pl.BlockSpec((1, cols, width), lambda i, *_: (0, rows - 2, 0))
    part = [block(p.shape[0]) for p in mixed]
    hbm = pl.BlockSpec(memory_space=pl.ANY)
    in_specs = part * 2
    in_specs += [near if edges else block(1)] * others
    in_specs += [full2(p) for p in packed]
    in_specs += [hbm] * others
    in_specs += [full2(depth), full2(qkv_weight), full2(out_weight)]
    stay = lambda x: pltpu.with_memory_space_constraint(x, pltpu.HBM)
    args = [x if edges else stay(x) for x in normed + mixed]
    args += surf + packed + whole + [depth, qkv_weight, out_weight]
    alias = {}
    if edges:
        in_specs.append(hbm)
        alias = {len(args) + 2: 0}
        args.append(out)
    tokens = lev * cols * 2
    members = others + 1
    return pl.pallas_call(
        functools.partial(attend_kernel, others, nparts, edges),
        grid_spec=pltpu.PrefetchScalarGridSpec(
            num_scalar_prefetch=2,
            grid=(2,),
            in_specs=in_specs,
            out_specs=pl.BlockSpec(
                (1, lev, cols, width), lambda i, f, s: (0, 0, row_of(i, s), 0)
            ),
            scratch_shapes=[
                pltpu.VMEM((lev, cols, width), BF16),
                pltpu.VMEM((members * lev, cols, width), BF16),
                pltpu.VMEM((members * lev, cols, width), BF16),
                pltpu.VMEM((lev, cols, width), BF16),
                pltpu.VMEM((lev, cols, width), BF16),
                pltpu.SemaphoreType.DMA,
            ],
        ),
        out_shape=jax.ShapeDtypeStruct(shape, BF16),
        input_output_aliases=alias,
        compiler_params=params(16 if members <= 2 else 48, 1),
        cost_estimate=cost(tokens * width * width * 8 * (members + 2), tokens * width * 2 * 5),
        name="attend",
    )(flag, side, *args)


def body(
    atm_latent,
    ocean_state,
    depth,
    src_blocks,
    live,
    remap_weight,
    conv_weight,
    qkv_weight,
    out_weight,
):
    _, lev, cells, width = ocean_state.shape
    cols = remap_weight.shape[2]
    rows = cells // cols
    inner = cells - 2 * cols
    own = atm_latent.shape[1]
    atm_blk = own // cols
    tiles = lax.axis_size("tile")
    members = lax.axis_size("mem")
    tile = lax.axis_index("tile")

    def swap(x, first):
        pairs = [(i, i + 1) for i in range(first, tiles - 1, 2)]
        return lax.ppermute(x, "tile", pairs + [(b, a) for a, b in pairs])

    def exchange(x):
        return [
            lax.ppermute(x, "mem", [(i, (i + k) % members) for i in range(members)])
            for k in range(1, members)
        ]

    odd = tile % 2
    side = jnp.stack([(1 - odd) * (rows - 1), odd * (rows - 1)]).astype(jnp.int32)
    depth = depth.reshape(rows, cols)
    deep_cap = capacity((lev - 1) * inner, 0.5625)
    near_cap = capacity((lev - 1) * cols, 0.605)
    far_cap = capacity(lev * cols, 0.65625)

    hbm = pl.BlockSpec(memory_space=pltpu.HBM)
    anywhere = pl.BlockSpec(memory_space=pl.ANY)
    vmem = pl.BlockSpec(memory_space=pltpu.VMEM)
    smem = pl.BlockSpec(memory_space=pltpu.SMEM)
    tok = lambda *s: pltpu.HBM((*s, width), BF16)
    stay = lambda x: pltpu.with_memory_space_constraint(x, pltpu.HBM)
    conv_flops = lambda n, c: 2 * 9 * n * c * width * width
    dma = pltpu.SemaphoreType.DMA
    slack = cols + 16
    message = lev * cols + own
    on_msg, off_msg, flag = pl.pallas_call(
        functools.partial(prep_kernel, (deep_cap, near_cap, far_cap)),
        in_specs=[smem, hbm, hbm, hbm],
        out_specs=[hbm, hbm, smem],
        out_shape=[tok(message), tok(message), jax.ShapeDtypeStruct((1,), jnp.int32)],
        scratch_shapes=[
            pltpu.VMEM((rows, cols), jnp.int32),
            pltpu.VMEM((own, width), BF16),
            pltpu.VMEM((2, lev, cols, width), BF16),
            dma((2, lev)),
            dma((2, lev)),
            dma((2,)),
            dma((2,)),
        ],
        compiler_params=params(16),
        cost_estimate=cost(lev * cols * width * 4, lev * cols * width * 10),
        name="prep",
    )(side, stay(ocean_state), stay(atm_latent), stay(depth))
    off_halo = swap(off_msg, 1)
    on_halo = swap(on_msg, 0)

    deep_mixed, deep_normed, deep_packed = pl.pallas_call(
        functools.partial(inner_kernel, deep_cap),
        in_specs=[vmem, vmem, hbm],
        out_specs=[hbm] * 3,
        out_shape=[tok(lev - 1, inner), tok(lev - 1, inner), tok(deep_cap)],
        scratch_shapes=[
            pltpu.VMEM(conv_weight.shape, BF16),
            pltpu.VMEM((lev - 1, inner, width), BF16),
            pltpu.VMEM((lev - 1, inner, width), BF16),
            pltpu.VMEM((deep_cap + slack, width), BF16),
            dma,
            dma((lev - 1, 2)),
            dma,
        ],
        compiler_params=params(12),
        cost_estimate=cost(conv_flops(lev, inner), lev * inner * width * 8),
        name="inner",
    )(ocean_state, depth, stay(conv_weight))
    deep_others = exchange(deep_packed)

    whole_spec = lambda *sh: pl.BlockSpec(sh, lambda *_: (0,) * len(sh))
    row_f32 = pltpu.HBM((cols, width), F32)

    def row_conv(which, first, cap, halo, extra):
        n = lev - first
        base = pltpu.HBM((inner + cols, width), F32)
        return pl.pallas_call(
            functools.partial(row_kernel, cap, first, which),
            in_specs=[smem, vmem, vmem, hbm, anywhere] + [hbm] * len(extra),
            out_specs=[hbm] * 3 + [whole_spec(inner + cols, width)] * first,
            out_shape=[tok(lev, 2 * cols), tok(lev, 2 * cols), tok(cap)] + [base] * first,
            scratch_shapes=[
                pltpu.VMEM((cols, width), F32),
                pltpu.VMEM(conv_weight.shape, BF16),
                pltpu.VMEM((3, lev * cols, width), BF16),
                pltpu.VMEM((n, cols, width), BF16),
                pltpu.VMEM((n, cols, width), BF16),
                pltpu.VMEM((cap + slack, width), BF16),
                dma,
                dma,
                dma((2,)),
                dma,
            ],
            input_output_aliases={6: 0, 7: 1} if extra else {},
            compiler_params=params(12),
            cost_estimate=cost(conv_flops(lev, cols), lev * cols * width * 16),
            name="row",
        )(side, ocean_state, depth, stay(conv_weight), halo, *[stay(x) for x in extra])

    edge_mixed, edge_normed, near_packed, base = row_conv(0, 1, near_cap, on_halo, [])

    ids = jnp.clip(src_blocks - (tile - R) * atm_blk, 0, 3 * atm_blk - 1)
    surf_mixed, surf_normed, far_forcing, edge_mixed, edge_normed = pl.pallas_call(
        surface_kernel,
        in_specs=[smem] * 3 + [vmem] + [anywhere] * 2 + [vmem] * 2 + [hbm] * 3,
        out_specs=[whole_spec(1, inner + cols, width)] * 2 + [whole_spec(cols, width)] + [hbm] * 2,
        out_shape=[tok(1, inner + cols), tok(1, inner + cols), row_f32]
        + [tok(lev, 2 * cols)] * 2,
        scratch_shapes=[
            pltpu.VMEM((inner + cols, width), F32),
            pltpu.VMEM((3 * own, width), BF16),
            pltpu.VMEM((rows, cols, width), F32),
            dma((5,)),
        ],
        input_output_aliases={9: 3, 10: 4},
        compiler_params=params(12),
        cost_estimate=cost(conv_flops(1, inner), cells * width * 16),
        name="surface",
    )(
        ids,
        live,
        side,
        depth,
        on_halo,
        off_halo,
        atm_latent,
        remap_weight,
        stay(base),
        stay(edge_mixed),
        stay(edge_normed),
    )
    surf_others = exchange(surf_normed)
    near_others = exchange(near_packed)

    edge_mixed, edge_normed, far_packed = row_conv(
        1, 0, far_cap, off_halo, [far_forcing, edge_mixed, edge_normed]
    )
    far_others = exchange(far_packed)

    def unread(shape):
        return pl.pallas_call(
            lambda out_ref: None,
            out_specs=hbm,
            out_shape=pltpu.HBM(shape, BF16),
            name="unread",
        )()

    def send_all(*arrays):
        sizes = [x.shape[0] * x.shape[1] for x in arrays]
        joined = jnp.concatenate([x.reshape(-1, width) for x in arrays], axis=0)
        got = [[] for _ in arrays]
        for part in exchange(joined):
            at = 0
            for k, (x, size) in enumerate(zip(arrays, sizes)):
                got[k].append(part[at : at + size].reshape(x.shape))
                at += size
        return tuple(got)

    deep_whole, edge_whole = lax.cond(
        flag[0] > 0,
        send_all,
        lambda *a: tuple([unread(x.shape) for _ in range(members - 1)] for x in a),
        deep_normed,
        edge_normed,
    )
    shape = ocean_state.shape
    weights = (depth, qkv_weight, out_weight)
    out = attend(
        flag,
        side,
        [surf_normed, deep_normed],
        [surf_mixed, deep_mixed],
        surf_others,
        deep_others,
        deep_whole,
        *weights,
        None,
        shape,
    )
    return attend(
        flag,
        side,
        [edge_normed],
        [edge_mixed],
        surf_others,
        near_others + far_others,
        edge_whole,
        *weights,
        out,
        shape,
    )


def solution(mesh):
    return jax.shard_map(
        body,
        mesh=mesh,
        in_specs=(
            P("mem", "tile", None),
            P("mem", None, "tile", None),
            P("tile"),
            P("tile", None),
            P("tile"),
            P("tile", None, None, None),
            P(),
            P(),
            P(),
        ),
        out_specs=P("mem", None, "tile", None),
        check_vma=False,
    )
```

```python
import functools
import math

import jax
import jax.numpy as jnp
from jax import lax
from jax.experimental import pallas as pl
from jax.experimental.pallas import tpu as pltpu
from jax.sharding import PartitionSpec as P

HEADS = 4
R = 1
GROUP = 16
EPS = 1e-06
NEG = -1e30
F32 = jnp.float32
BF16 = jnp.bfloat16
MIB = 1024 * 1024


def params(mib, steps=0):
    return pltpu.CompilerParams(
        dimension_semantics=("arbitrary",) * steps if steps else None, vmem_limit_bytes=mib * MIB
    )


def cost(flops, nbytes):
    return pl.CostEstimate(flops=int(flops), bytes_accessed=int(nbytes), transcendentals=0)


def capacity(tokens, share):
    return -(-int(tokens * share) // 16) * 16


def row_plan(depth_row, lev):
    cols = depth_row.shape[1]
    level = lax.broadcasted_iota(jnp.int32, (lev, cols), 0).astype(F32)
    wet = (depth_row > level).astype(F32)
    upper = (
        lax.broadcasted_iota(jnp.int32, (cols, cols), 0)
        < lax.broadcasted_iota(jnp.int32, (cols, cols), 1)
    )
    upper = upper.astype(F32).astype(BF16)
    rank = jnp.dot(wet.astype(BF16), upper, preferred_element_type=F32)
    counts = [jnp.sum(wet[l : l + 1]).astype(jnp.int32) for l in range(lev)]
    return wet, rank, counts


def offsets(plans, first, lev):
    at, place = jnp.int32(0), {}
    for l in range(first, lev):
        for r, plan in enumerate(plans):
            place[l, r] = at
            at = at + plan[2][l]
    return place


def segment(wet, rank, offset, limit):
    cols = wet.shape[1]
    base = jnp.minimum((offset // 16) * 16, limit)
    target = jnp.where(wet > 0, rank + (offset - base).astype(F32), -1.0)
    slot = lax.broadcasted_iota(jnp.int32, (cols + 16, cols), 0).astype(F32)
    return pl.multiple_of(base, 16), (slot == target).astype(F32).astype(BF16)


def pack(buf_ref, wet, rank, offset, cap, tokens):
    base, hot = segment(wet, rank, offset, cap)
    rows = jnp.dot(hot, tokens, preferred_element_type=F32).astype(BF16)
    head = pl.ds(base, 16)
    buf_ref[head, :] = buf_ref[head, :] + rows[:16]
    buf_ref[pl.ds(pl.multiple_of(base + 16, 16), rows.shape[0] - 16), :] = rows[16:]


def unpack(rows_of, wet, rank, offset, limit):
    base, hot = segment(wet, rank, offset, limit)
    return lax.dot_general(
        hot, rows_of(base, hot.shape[0]), (((0,), (0,)), ((), ())), preferred_element_type=F32
    ).astype(BF16)


def column(depth_row):
    cols = depth_row.shape[1]
    return jnp.broadcast_to(depth_row, (cols, cols)).T


def widen(x, width):
    return jnp.concatenate([x] * (width // x.shape[1]), axis=1)


def stencil(taps, weight_ref, cols):
    count, width = taps[0].shape
    x = jnp.concatenate(taps, axis=1)
    sums = [
        jnp.dot(x, weight_ref[:, dc].reshape(3 * width, -1), preferred_element_type=F32)
        for dc in range(3)
    ]
    col = lax.broadcasted_iota(jnp.int32, (count, 1), 0) % cols
    left = jnp.where(col == 0, 0.0, pltpu.roll(sums[0], 1, axis=0))
    right = jnp.where(col == cols - 1, 0.0, pltpu.roll(sums[2], count - 1, axis=0))
    return sums[1] + left + right


def normalise(mixed):
    mf = mixed.astype(F32)
    mean = jnp.mean(mf * mf, axis=-1, keepdims=True)
    return (mf * lax.rsqrt(mean + EPS)).astype(BF16)


def prep_kernel(
    caps,
    side_ref,
    state_hbm,
    atm_hbm,
    depth_hbm,
    on_hbm,
    off_hbm,
    flag_ref,
    depth_ref,
    atm,
    rows_in,
    in_sem,
    out_sem,
    atm_sem,
    own_sem,
):
    _, lev, cells, width = state_hbm.shape
    rows, cols = depth_ref.shape
    own = atm_hbm.shape[1]
    sides = (on_hbm, off_hbm)
    load_depth = pltpu.make_async_copy(depth_hbm, depth_ref, own_sem.at[0])
    load_depth.start()
    loads, stores = [], []
    for k in (1, 0):
        at = pl.multiple_of(side_ref[k] * cols, cols)
        for l in range(lev):
            load = pltpu.make_async_copy(
                state_hbm.at[0, l, pl.ds(at, cols)], rows_in.at[k, l], in_sem.at[k, l]
            )
            load.start()
            loads.append((k, l, load))
    load_atm = pltpu.make_async_copy(atm_hbm.at[0], atm, own_sem.at[1])
    load_atm.start()
    load_depth.wait()
    d = depth_ref[...].astype(F32)
    pick = lambda k: jnp.where(side_ref[k] == 0, d[0:1], d[rows - 1 :])
    deep = [column(pick(k)) for k in range(2)]
    for k, l, load in loads:
        wet = widen((deep[k] > l).astype(F32).astype(BF16), width)
        load.wait()
        rows_in[k, l] = rows_in[k, l] * wet
        store = pltpu.make_async_copy(
            rows_in.at[k, l], sides[k].at[pl.ds(l * cols, cols)], out_sem.at[k, l]
        )
        store.start()
        stores.append(store)
    load_atm.wait()
    for k in (1, 0):
        store = pltpu.make_async_copy(
            atm, sides[k].at[pl.ds(lev * cols, own)], atm_sem.at[k]
        )
        store.start()
        stores.append(store)
    counts = [
        jnp.sum(jnp.maximum(d[1 : rows - 1] - 1.0, 0.0)),
        jnp.sum(jnp.maximum(pick(0) - 1.0, 0.0)),
        jnp.sum(pick(1)),
    ]
    over = jnp.int32(0)
    for count, cap in zip(counts, caps):
        over = over | (count > cap).astype(jnp.int32)
    flag_ref[0] = over
    for store in stores:
        store.wait()


def inner_kernel(
    cap,
    state,
    depth_ref,
    weight_hbm,
    mixed_hbm,
    normed_hbm,
    packed_hbm,
    weight,
    mixed,
    normed,
    packed,
    weight_sem,
    out_sem,
    packed_sem,
):
    _, lev, cells, width = state.shape
    rows, cols = depth_ref.shape
    load = pltpu.make_async_copy(weight_hbm, weight, weight_sem)
    load.start()
    packed[...] = jnp.zeros_like(packed)
    d = depth_ref[...].astype(F32)
    plans = [row_plan(d[r : r + 1], lev) for r in range(1, rows - 1)]
    place = offsets(plans, 1, lev)
    deep = jnp.concatenate([column(d[r : r + 1]) for r in range(rows)], axis=0)
    count = cells - 2 * cols
    stores = []
    for l in range(1, lev):
        wet = (deep > l).astype(F32)
        x = state[0, l] * widen(wet.astype(BF16), width)
        taps = [x[dr * cols : dr * cols + count] for dr in range(3)]
        if l == 1:
            load.wait()
        total = stencil(taps, weight, cols)
        new = taps[1].astype(F32) + widen(wet[cols : cols + count], width) * total
        new = new.astype(BF16)
        mixed[l - 1] = new
        tokens = normalise(new)
        normed[l - 1] = tokens
        for k, (buf, out) in enumerate(((mixed, mixed_hbm), (normed, normed_hbm))):
            store = pltpu.make_async_copy(buf.at[l - 1], out.at[l - 1], out_sem.at[l - 1, k])
            store.start()
            stores.append(store)
        for r, plan in enumerate(plans):
            pack(
                packed,
                plan[0][l : l + 1],
                plan[1][l : l + 1],
                place[l, r],
                cap,
                tokens[r * cols : (r + 1) * cols],
            )
        if l == lev - 1:
            store = pltpu.make_async_copy(packed.at[pl.ds(0, cap)], packed_hbm, packed_sem)
            store.start()
            stores.append(store)
    for store in stores:
        store.wait()


def surface_kernel(
    ids_ref,
    live_ref,
    side_ref,
    depth_ref,
    on_hbm,
    off_hbm,
    atm_ref,
    remap,
    base_hbm,
    edge_mixed_in,
    edge_normed_in,
    mixed_ref,
    normed_ref,
    far_ref,
    edge_mixed_hbm,
    edge_normed_hbm,
    base,
    window,
    forcing_ref,
    sem,
):
    rows, cols = depth_ref.shape
    _, own, width = atm_ref.shape
    blocks, pairs = remap.shape[0], remap.shape[1]
    on_at = jnp.where(side_ref[0] == 0, 0, 2 * own)
    copies = [
        pltpu.make_async_copy(
            on_hbm.at[pl.ds(on_hbm.shape[0] - own, own)],
            window.at[pl.ds(pl.multiple_of(on_at, own), own)],
            sem.at[0],
        ),
        pltpu.make_async_copy(
            off_hbm.at[pl.ds(off_hbm.shape[0] - own, own)],
            window.at[pl.ds(pl.multiple_of(2 * own - on_at, own), own)],
            sem.at[1],
        ),
        pltpu.make_async_copy(base_hbm, base, sem.at[4]),
    ]
    for copy in copies:
        copy.start()
    window[own : 2 * own] = atm_ref[0]
    d = depth_ref[...].astype(F32)
    near, far = side_ref[0], side_ref[1]
    rows_d = [d[r : r + 1] for r in range(1, rows - 1)]
    rows_d.append(jnp.where(near == 0, d[0:1], d[rows - 1 :]))
    wets = [widen((column(row) > 0).astype(F32), width) for row in rows_d]
    for copy in copies:
        copy.wait()
    for b in range(blocks):
        acc = jnp.zeros((cols, width), F32)
        for p in range(pairs):
            on = (p < live_ref[b]).astype(F32)
            start = pl.multiple_of(ids_ref[b, p] * cols, cols)
            acc = acc + on * jnp.dot(
                remap[b, p], window[pl.ds(start, cols), :], preferred_element_type=F32
            )
        forcing_ref[b] = acc
    for k, wet in enumerate(wets):
        at = slice(k * cols, (k + 1) * cols)
        forcing = forcing_ref[near] if k == rows - 2 else forcing_ref[k + 1]
        new = (base[at] + wet * forcing).astype(BF16)
        mixed_ref[0, at] = new
        normed_ref[0, at] = normalise(new)
    far_ref[...] = forcing_ref[far]
    at = pl.ds((rows - 2) * cols, cols)
    stores = [
        pltpu.make_async_copy(mixed_ref.at[0, at], edge_mixed_hbm.at[0, pl.ds(0, cols)], sem.at[2]),
        pltpu.make_async_copy(normed_ref.at[0, at], edge_normed_hbm.at[0, pl.ds(0, cols)], sem.at[3]),
    ]
    for store in stores:
        store.start()
    for store in stores:
        store.wait()


def row_kernel(cap, first, which, side_ref, state, depth_ref, weight_hbm, halo_hbm, *refs):
    refs = list(refs)
    forcing_hbm = None
    if not first:
        forcing_hbm = refs[0]
        refs = refs[3:]
    mixed_hbm, normed_hbm, packed_hbm = refs[:3]
    refs = refs[3:]
    base_ref = refs.pop(0) if first else None
    forcing_ref, weight, tap, mixed, normed, packed, weight_sem, halo_sem, out_sem, packed_sem = refs
    load = pltpu.make_async_copy(weight_hbm, weight, weight_sem)
    load.start()
    _, lev, cells, width = state.shape
    rows, cols = depth_ref.shape
    row = side_ref[which]
    top = row == 0
    beside = jnp.where(top, 1, rows - 2)
    outer = jnp.where(top, 0, 2)
    halo = pltpu.make_async_copy(
        halo_hbm.at[pl.ds(0, lev * cols)], tap.at[outer], halo_sem
    )
    halo.start()
    if not first:
        forcing = pltpu.make_async_copy(forcing_hbm, forcing_ref, packed_sem)
        forcing.start()
    packed[...] = jnp.zeros_like(packed)
    d = depth_ref[...].astype(F32)
    own_depth = jnp.where(top, d[0:1], d[rows - 1 :])
    plan = row_plan(own_depth, lev)
    place = offsets([plan], first, lev)
    deep = column(own_depth)
    deep_beside = column(jnp.where(top, d[1:2], d[rows - 2 : rows - 1]))
    at = pl.multiple_of(row * cols, cols)
    at_beside = pl.multiple_of(beside * cols, cols)
    wets = []
    for l in range(lev):
        rows_l = slice(l * cols, (l + 1) * cols)
        wet = (deep > l).astype(F32)
        wets.append(wet)
        wet_beside = (deep_beside > l).astype(F32)
        tap[1, rows_l] = state[0, l, pl.ds(at, cols)] * widen(wet.astype(BF16), width)
        tap[2 - outer, rows_l] = state[0, l, pl.ds(at_beside, cols)] * widen(
            wet_beside.astype(BF16), width
        )
    stores = []
    half = lev // 2
    load.wait()
    halo.wait()
    if not first:
        forcing.wait()
    for start in range(0, lev, half):
        rows_b = slice(start * cols, (start + half) * cols)
        taps = [tap[dr, rows_b] for dr in range(3)]
        total = stencil(taps, weight, cols)
        for k in range(half):
            l = start + k
            rows_k = slice(k * cols, (k + 1) * cols)
            part = total[rows_k]
            if l == 0 and not first:
                part = part + forcing_ref[...]
            new = taps[1][rows_k].astype(F32) + widen(wets[l], width) * part
            if l < first:
                base_ref[cells - 2 * cols :] = new
                continue
            new = new.astype(BF16)
            mixed[l - first] = new
            tokens = normalise(new)
            normed[l - first] = tokens
            pack(packed, plan[0][l : l + 1], plan[1][l : l + 1], place[l, 0], cap, tokens)
    if first:
        wet = (jnp.concatenate([column(d[r : r + 1]) for r in range(rows)], axis=0) > 0).astype(F32)
        x = state[0, 0] * widen(wet.astype(BF16), width)
        taps = [x[dr * cols : dr * cols + cells - 2 * cols] for dr in range(3)]
        inside = widen(wet[cols : cells - cols], width)
        base_ref[0 : cells - 2 * cols] = taps[1].astype(F32) + inside * stencil(taps, weight, cols)
    block = (pl.ds(first, lev - first), pl.ds(which * cols, cols))
    for k, (buf, out) in enumerate(((mixed, mixed_hbm), (normed, normed_hbm))):
        store = pltpu.make_async_copy(buf, out.at[block], out_sem.at[k])
        store.start()
        stores.append(store)
    store = pltpu.make_async_copy(packed.at[pl.ds(0, cap)], packed_hbm, packed_sem)
    store.start()
    stores.append(store)
    for store in stores:
        store.wait()


def attend_kernel(others, nparts, edges, flag_ref, side_ref, *refs):
    refs = list(refs)
    take = lambda k: [refs.pop(0) for _ in range(k)]
    own_normed = take(nparts)
    own_mixed = take(nparts)
    surf = take(others)
    packed = [take(others) for _ in range(1 + edges)]
    whole = take(others)
    depth_ref, qkv_ref, wo_ref = take(3)
    if edges:
        take(1)
    out_hbm, x_ref, mixed_ref, q_ref, k_ref, v_ref, att_ref, token_ref, new_ref = refs[:9]
    in_sem, out_sem, sem = refs[9:]
    steps, lev, count, width = q_ref.shape
    members = others + 1
    head = width // HEADS
    pair = 2 * head

    loads = []
    for kind, (parts, buf) in enumerate(((own_normed, x_ref), (own_mixed, mixed_ref))):
        for step in range(steps):
            at = 0
            for k, part in enumerate(parts):
                n = part.shape[0]
                load = pltpu.make_async_copy(
                    part.at[:, pl.ds(step * count, count)],
                    buf.at[step, pl.ds(at, n)],
                    in_sem.at[kind, step, k],
                )
                load.start()
                loads.append((kind, step, load))
                at += n

    def arrive(kind, step):
        for k, s, load in loads:
            if (k, s) == (kind, step):
                load.wait()

    d = depth_ref[...].astype(F32)
    last = d.shape[0] - 1
    if edges:
        rows_d = [jnp.where(side_ref[k] == 0, d[0:1], d[last:]) for k in range(2)]
    else:
        rows_d = [d[r : r + 1] for r in range(1, last)]
    plans = [row_plan(row, lev) for row in rows_d]
    if edges:
        near, far = offsets(plans[:1], 1, lev), offsets(plans[1:], 0, lev)
        place = [{l: at for (l, _), at in p.items()} for p in (near, far)]
    else:
        both = offsets(plans, 1, lev)
        place = [{l: both[l, step] for l in range(1, lev)} for step in range(steps)]

    def project(x, step, m):
        rows = slice(m * lev, (m + 1) * lev)
        kv = jnp.dot(x, qkv_ref[:, width:], preferred_element_type=F32).astype(BF16)
        k_ref[step, rows] = kv[:, :width].reshape(lev, count, width)
        v_ref[step, rows] = kv[:, width:].reshape(lev, count, width)

    for o in range(others):
        for step in range(steps):
            source = packed[step if edges else 0][o]
            window = lambda base, size: source[pl.ds(base, size), :]
            limit = source.shape[0] - count - 16
            wet, rank, _ = plans[step]
            if 0 not in place[step]:
                at = 0 if edges else step * count
                token_ref[step, 0] = surf[o][0, at : at + count]
            for l, at in place[step].items():
                token_ref[step, l] = unpack(window, wet[l : l + 1], rank[l : l + 1], at, limit)

        @pl.when(flag_ref[0] != 0)
        def _():
            first = lev - whole[o].shape[0]
            for step in range(steps):
                copy = pltpu.make_async_copy(
                    whole[o].at[:, pl.ds(step * count, count)],
                    token_ref.at[step, pl.ds(first, lev - first)],
                    sem,
                )
                copy.start()
                copy.wait()

        for step in range(steps):
            project(token_ref[step].reshape(-1, width), step, o + 1)

    nq, nk = lev * GROUP, members * lev * GROUP
    groups = count // GROUP
    lanes_n = lev * GROUP
    cell = lax.broadcasted_iota(jnp.int32, (groups, count), 1)
    mine = (cell // GROUP == lax.broadcasted_iota(jnp.int32, (groups, count), 0)).astype(F32)
    spread = lax.broadcasted_iota(jnp.int32, (count, lanes_n), 0) % GROUP
    spread = (spread == lax.broadcasted_iota(jnp.int32, (count, lanes_n), 1) % GROUP).astype(F32)
    key_level = lax.broadcasted_iota(jnp.int32, (groups, lanes_n), 1) // GROUP
    qc = lax.broadcasted_iota(jnp.int32, (nq, nk), 0) % GROUP
    kc = lax.broadcasted_iota(jnp.int32, (nq, nk), 1) % GROUP
    same = jnp.where(qc == kc, 0.0, NEG)
    lane = lax.broadcasted_iota(jnp.int32, (1, width), 1)
    scale = 1.0 / math.sqrt(head)
    masks = [jnp.where(lane // head == h, scale, 0.0).astype(BF16) for h in range(HEADS)]
    stores = []
    for step in range(steps):
        arrive(0, step)
        x = x_ref[step].reshape(-1, width)
        q = jnp.dot(x, qkv_ref[:, 0:width], preferred_element_type=F32).astype(BF16)
        q_ref[step] = q.reshape(lev, count, width)
        project(x, step, 0)
        key_depth = jnp.dot(
            (mine * rows_d[step]).astype(BF16), spread.astype(BF16), preferred_element_type=F32
        )
        key_bias = jnp.where(key_depth > key_level.astype(F32), 0.0, NEG)
        for g in range(groups):
            cells = slice(g * GROUP, (g + 1) * GROUP)
            bias = same + jnp.concatenate([key_bias[g : g + 1]] * members, axis=1)
            bias = jnp.concatenate([bias] * HEADS, axis=0)
            q = q_ref[step, :, cells].reshape(nq, width)
            q = jnp.concatenate([q * mask for mask in masks], axis=0)
            k = k_ref[step, :, cells].reshape(nk, width)
            v = v_ref[step, :, cells].reshape(nk, width)
            s = lax.dot_general(q, k, (((1,), (1,)), ((), ())), preferred_element_type=F32) + bias
            p = jnp.exp(s - jnp.max(s, axis=-1, keepdims=True))
            norm = 1.0 / jnp.sum(p, axis=-1, keepdims=True)
            p = p.astype(BF16)
            for h in range(HEADS // 2):
                lanes = slice(h * pair, (h + 1) * pair)
                rows = slice(h * 2 * nq, (h + 1) * 2 * nq)
                o = jnp.dot(p[rows], v[:, lanes], preferred_element_type=F32) * norm[rows]
                o = jnp.where(lane[:, :pair] < head, o[:nq], o[nq:])
                att_ref[step, :, cells, lanes] = o.astype(BF16).reshape(lev, GROUP, pair)
        proj = jnp.dot(
            att_ref[step].reshape(-1, width), wo_ref[...], preferred_element_type=F32
        )
        arrive(1, step)
        deep = column(rows_d[step])
        row = side_ref[step] if edges else step + 1
        for l in range(lev):
            rows = slice(l * count, (l + 1) * count)
            wet = widen((deep > l).astype(F32), width)
            new_ref[step, l] = (mixed_ref[step, l].astype(F32) + wet * proj[rows]).astype(BF16)
        at = pl.multiple_of(row * count, count)
        store = pltpu.make_async_copy(
            new_ref.at[step], out_hbm.at[0, :, pl.ds(at, count)], out_sem.at[step]
        )
        store.start()
        stores.append(store)
    for store in stores:
        store.wait()


def attend(
    flag, side, normed, mixed, surf, packed, whole, depth, qkv_weight, out_weight, out, shape
):
    edges = out is not None
    others, nparts = len(whole), len(mixed)
    lev = sum(p.shape[0] for p in mixed)
    width = shape[-1]
    cols = depth.shape[1]
    members = others + 1
    hbm = pl.BlockSpec(memory_space=pltpu.HBM)
    vmem = pl.BlockSpec(memory_space=pltpu.VMEM)
    smem = pl.BlockSpec(memory_space=pltpu.SMEM)
    stay = lambda x: pltpu.with_memory_space_constraint(x, pltpu.HBM)
    if edges:
        surf = [x[:, shape[2] - 2 * cols :] for x in surf]
    in_specs = [smem] * 2 + [hbm] * (2 * nparts) + [vmem] * (len(surf) + len(packed))
    in_specs += [hbm] * others + [vmem] * 3
    args = [flag, side] + [stay(x) for x in normed + mixed] + surf + packed
    args += [stay(x) for x in whole] + [depth, qkv_weight, out_weight]
    alias = {}
    if edges:
        in_specs.append(hbm)
        alias = {len(args): 0}
        args.append(stay(out))
    tokens = lev * cols * 2
    rows = pltpu.VMEM((2, lev, cols, width), BF16)
    keys = pltpu.VMEM((2, members * lev, cols, width), BF16)
    return pl.pallas_call(
        functools.partial(attend_kernel, others, nparts, edges),
        in_specs=in_specs,
        out_specs=hbm,
        scratch_shapes=[
            rows,
            rows,
            rows,
            keys,
            keys,
            rows,
            rows,
            rows,
            pltpu.SemaphoreType.DMA((2, 2, nparts)),
            pltpu.SemaphoreType.DMA((2,)),
            pltpu.SemaphoreType.DMA,
        ],
        out_shape=pltpu.HBM(shape, BF16),
        input_output_aliases=alias,
        compiler_params=params(24 if members <= 2 else 56),
        cost_estimate=cost(tokens * width * width * 8 * (members + 2), tokens * width * 2 * 5),
        name="attend",
    )(*args)


def body(
    atm_latent,
    ocean_state,
    depth,
    src_blocks,
    live,
    remap_weight,
    conv_weight,
    qkv_weight,
    out_weight,
):
    _, lev, cells, width = ocean_state.shape
    cols = remap_weight.shape[2]
    rows = cells // cols
    inner = cells - 2 * cols
    own = atm_latent.shape[1]
    atm_blk = own // cols
    tiles = lax.axis_size("tile")
    members = lax.axis_size("mem")
    tile = lax.axis_index("tile")

    def swap(x, first):
        pairs = [(i, i + 1) for i in range(first, tiles - 1, 2)]
        return lax.ppermute(x, "tile", pairs + [(b, a) for a, b in pairs])

    def exchange(x):
        return [
            lax.ppermute(x, "mem", [(i, (i + k) % members) for i in range(members)])
            for k in range(1, members)
        ]

    odd = tile % 2
    side = jnp.stack([(1 - odd) * (rows - 1), odd * (rows - 1)]).astype(jnp.int32)
    depth = depth.reshape(rows, cols)
    deep_cap = capacity((lev - 1) * inner, 0.5625)
    near_cap = capacity((lev - 1) * cols, 0.605)
    far_cap = capacity(lev * cols, 0.65625)

    hbm = pl.BlockSpec(memory_space=pltpu.HBM)
    anywhere = pl.BlockSpec(memory_space=pl.ANY)
    vmem = pl.BlockSpec(memory_space=pltpu.VMEM)
    smem = pl.BlockSpec(memory_space=pltpu.SMEM)
    tok = lambda *s: pltpu.HBM((*s, width), BF16)
    stay = lambda x: pltpu.with_memory_space_constraint(x, pltpu.HBM)
    conv_flops = lambda n, c: 2 * 9 * n * c * width * width
    dma = pltpu.SemaphoreType.DMA
    slack = cols + 16
    message = lev * cols + own
    on_msg, off_msg, flag = pl.pallas_call(
        functools.partial(prep_kernel, (deep_cap, near_cap, far_cap)),
        in_specs=[smem, hbm, hbm, hbm],
        out_specs=[hbm, hbm, smem],
        out_shape=[tok(message), tok(message), jax.ShapeDtypeStruct((1,), jnp.int32)],
        scratch_shapes=[
            pltpu.VMEM((rows, cols), jnp.int32),
            pltpu.VMEM((own, width), BF16),
            pltpu.VMEM((2, lev, cols, width), BF16),
            dma((2, lev)),
            dma((2, lev)),
            dma((2,)),
            dma((2,)),
        ],
        compiler_params=params(16),
        cost_estimate=cost(lev * cols * width * 4, lev * cols * width * 10),
        name="prep",
    )(side, stay(ocean_state), stay(atm_latent), stay(depth))
    off_halo = swap(off_msg, 1)
    on_halo = swap(on_msg, 0)

    deep_mixed, deep_normed, deep_packed = pl.pallas_call(
        functools.partial(inner_kernel, deep_cap),
        in_specs=[vmem, vmem, hbm],
        out_specs=[hbm] * 3,
        out_shape=[tok(lev - 1, inner), tok(lev - 1, inner), tok(deep_cap)],
        scratch_shapes=[
            pltpu.VMEM(conv_weight.shape, BF16),
            pltpu.VMEM((lev - 1, inner, width), BF16),
            pltpu.VMEM((lev - 1, inner, width), BF16),
            pltpu.VMEM((deep_cap + slack, width), BF16),
            dma,
            dma((lev - 1, 2)),
            dma,
        ],
        compiler_params=params(12),
        cost_estimate=cost(conv_flops(lev, inner), lev * inner * width * 8),
        name="inner",
    )(ocean_state, depth, stay(conv_weight))
    deep_others = exchange(deep_packed)

    whole_spec = lambda *sh: pl.BlockSpec(sh, lambda *_: (0,) * len(sh))
    row_f32 = pltpu.HBM((cols, width), F32)

    def row_conv(which, first, cap, halo, extra):
        n = lev - first
        base = pltpu.HBM((inner + cols, width), F32)
        return pl.pallas_call(
            functools.partial(row_kernel, cap, first, which),
            in_specs=[smem, vmem, vmem, hbm, anywhere] + [hbm] * len(extra),
            out_specs=[hbm] * 3 + [whole_spec(inner + cols, width)] * first,
            out_shape=[tok(lev, 2 * cols), tok(lev, 2 * cols), tok(cap)] + [base] * first,
            scratch_shapes=[
                pltpu.VMEM((cols, width), F32),
                pltpu.VMEM(conv_weight.shape, BF16),
                pltpu.VMEM((3, lev * cols, width), BF16),
                pltpu.VMEM((n, cols, width), BF16),
                pltpu.VMEM((n, cols, width), BF16),
                pltpu.VMEM((cap + slack, width), BF16),
                dma,
                dma,
                dma((2,)),
                dma,
            ],
            input_output_aliases={6: 0, 7: 1} if extra else {},
            compiler_params=params(12),
            cost_estimate=cost(conv_flops(lev, cols), lev * cols * width * 16),
            name="row",
        )(side, ocean_state, depth, stay(conv_weight), halo, *[stay(x) for x in extra])

    edge_mixed, edge_normed, near_packed, base = row_conv(0, 1, near_cap, on_halo, [])

    ids = jnp.clip(src_blocks - (tile - R) * atm_blk, 0, 3 * atm_blk - 1)
    surf_mixed, surf_normed, far_forcing, edge_mixed, edge_normed = pl.pallas_call(
        surface_kernel,
        in_specs=[smem] * 3 + [vmem] + [anywhere] * 2 + [vmem] * 2 + [hbm] * 3,
        out_specs=[whole_spec(1, inner + cols, width)] * 2 + [whole_spec(cols, width)] + [hbm] * 2,
        out_shape=[tok(1, inner + cols), tok(1, inner + cols), row_f32]
        + [tok(lev, 2 * cols)] * 2,
        scratch_shapes=[
            pltpu.VMEM((inner + cols, width), F32),
            pltpu.VMEM((3 * own, width), BF16),
            pltpu.VMEM((rows, cols, width), F32),
            dma((5,)),
        ],
        input_output_aliases={9: 3, 10: 4},
        compiler_params=params(12),
        cost_estimate=cost(conv_flops(1, inner), cells * width * 16),
        name="surface",
    )(
        ids,
        live,
        side,
        depth,
        on_halo,
        off_halo,
        atm_latent,
        remap_weight,
        stay(base),
        stay(edge_mixed),
        stay(edge_normed),
    )
    surf_others = exchange(surf_normed)
    near_others = exchange(near_packed)

    edge_mixed, edge_normed, far_packed = row_conv(
        1, 0, far_cap, off_halo, [far_forcing, edge_mixed, edge_normed]
    )
    far_others = exchange(far_packed)

    def unread(shape):
        return pl.pallas_call(
            lambda out_ref: None,
            out_specs=hbm,
            out_shape=pltpu.HBM(shape, BF16),
            name="unread",
        )()

    def send_all(*arrays):
        sizes = [x.shape[0] * x.shape[1] for x in arrays]
        joined = jnp.concatenate([x.reshape(-1, width) for x in arrays], axis=0)
        got = [[] for _ in arrays]
        for part in exchange(joined):
            at = 0
            for k, (x, size) in enumerate(zip(arrays, sizes)):
                got[k].append(part[at : at + size].reshape(x.shape))
                at += size
        return tuple(got)

    deep_whole, edge_whole = lax.cond(
        flag[0] > 0,
        send_all,
        lambda *a: tuple([unread(x.shape) for _ in range(members - 1)] for x in a),
        deep_normed,
        edge_normed,
    )
    shape = ocean_state.shape
    weights = (depth, qkv_weight, out_weight)
    out = attend(
        flag,
        side,
        [surf_normed, deep_normed],
        [surf_mixed, deep_mixed],
        surf_others,
        deep_others,
        deep_whole,
        *weights,
        None,
        shape,
    )
    return attend(
        flag,
        side,
        [edge_normed],
        [edge_mixed],
        surf_others,
        near_others + far_others,
        edge_whole,
        *weights,
        out,
        shape,
    )


def solution(mesh):
    return jax.shard_map(
        body,
        mesh=mesh,
        in_specs=(
            P("mem", "tile", None),
            P("mem", None, "tile", None),
            P("tile"),
            P("tile", None),
            P("tile"),
            P("tile", None, None, None),
            P(),
            P(),
            P(),
        ),
        out_specs=P("mem", None, "tile", None),
        check_vma=False,
    )
```

```python
import functools
import math

import jax
import jax.numpy as jnp
from jax import lax
from jax.experimental import pallas as pl
from jax.experimental.pallas import tpu as pltpu
from jax.sharding import PartitionSpec as P

HEADS = 4
R = 1
GROUP = 16
EPS = 1e-06
NEG = -1e30
F32 = jnp.float32
BF16 = jnp.bfloat16
MIB = 1024 * 1024


def params(mib, steps=0):
    return pltpu.CompilerParams(
        dimension_semantics=("arbitrary",) * steps if steps else None, vmem_limit_bytes=mib * MIB
    )


def cost(flops, nbytes):
    return pl.CostEstimate(flops=int(flops), bytes_accessed=int(nbytes), transcendentals=0)


def capacity(tokens, share):
    return -(-int(tokens * share) // 16) * 16


def row_plan(depth_row, lev):
    cols = depth_row.shape[1]
    level = lax.broadcasted_iota(jnp.int32, (lev, cols), 0).astype(F32)
    wet = (depth_row > level).astype(F32)
    upper = (
        lax.broadcasted_iota(jnp.int32, (cols, cols), 0)
        < lax.broadcasted_iota(jnp.int32, (cols, cols), 1)
    )
    upper = upper.astype(F32).astype(BF16)
    rank = jnp.dot(wet.astype(BF16), upper, preferred_element_type=F32)
    counts = [jnp.sum(wet[l : l + 1]).astype(jnp.int32) for l in range(lev)]
    return wet, rank, counts


def offsets(plans, first, lev):
    at, place = jnp.int32(0), {}
    for l in range(first, lev):
        for r, plan in enumerate(plans):
            place[l, r] = at
            at = at + plan[2][l]
    return place


def segment(wet, rank, offset, limit):
    cols = wet.shape[1]
    base = jnp.minimum((offset // 16) * 16, limit)
    target = jnp.where(wet > 0, rank + (offset - base).astype(F32), -1.0)
    slot = lax.broadcasted_iota(jnp.int32, (cols + 16, cols), 0).astype(F32)
    return pl.multiple_of(base, 16), (slot == target).astype(F32).astype(BF16)


def pack(buf_ref, wet, rank, offset, cap, tokens):
    base, hot = segment(wet, rank, offset, cap)
    rows = jnp.dot(hot, tokens, preferred_element_type=F32).astype(BF16)
    head = pl.ds(base, 16)
    buf_ref[head, :] = buf_ref[head, :] + rows[:16]
    buf_ref[pl.ds(pl.multiple_of(base + 16, 16), rows.shape[0] - 16), :] = rows[16:]


def unpack(rows_of, wet, rank, offset, limit):
    base, hot = segment(wet, rank, offset, limit)
    return lax.dot_general(
        hot, rows_of(base, hot.shape[0]), (((0,), (0,)), ((), ())), preferred_element_type=F32
    ).astype(BF16)


def column(depth_row):
    cols = depth_row.shape[1]
    return jnp.broadcast_to(depth_row, (cols, cols)).T


def widen(x, width):
    return jnp.concatenate([x] * (width // x.shape[1]), axis=1)


def stencil(taps, weight_ref, cols):
    count, width = taps[0].shape
    x = jnp.concatenate(taps, axis=1)
    sums = [
        jnp.dot(x, weight_ref[:, dc].reshape(3 * width, -1), preferred_element_type=F32)
        for dc in range(3)
    ]
    col = lax.broadcasted_iota(jnp.int32, (count, 1), 0) % cols
    left = jnp.where(col == 0, 0.0, pltpu.roll(sums[0], 1, axis=0))
    right = jnp.where(col == cols - 1, 0.0, pltpu.roll(sums[2], count - 1, axis=0))
    return sums[1] + left + right


def normalise(mixed):
    mf = mixed.astype(F32)
    mean = jnp.mean(mf * mf, axis=-1, keepdims=True)
    return (mf * lax.rsqrt(mean + EPS)).astype(BF16)


def prep_kernel(
    caps,
    side_ref,
    state_hbm,
    atm_hbm,
    depth_hbm,
    on_hbm,
    off_hbm,
    flag_ref,
    depth_ref,
    atm,
    rows_in,
    in_sem,
    out_sem,
    atm_sem,
    own_sem,
):
    _, lev, cells, width = state_hbm.shape
    rows, cols = depth_ref.shape
    own = atm_hbm.shape[1]
    sides = (on_hbm, off_hbm)
    load_depth = pltpu.make_async_copy(depth_hbm, depth_ref, own_sem.at[0])
    load_depth.start()
    loads, stores = [], []
    for k in (1, 0):
        at = pl.multiple_of(side_ref[k] * cols, cols)
        for l in range(lev):
            load = pltpu.make_async_copy(
                state_hbm.at[0, l, pl.ds(at, cols)], rows_in.at[k, l], in_sem.at[k, l]
            )
            load.start()
            loads.append((k, l, load))
    load_atm = pltpu.make_async_copy(atm_hbm.at[0], atm, own_sem.at[1])
    load_atm.start()
    load_depth.wait()
    d = depth_ref[...].astype(F32)
    pick = lambda k: jnp.where(side_ref[k] == 0, d[0:1], d[rows - 1 :])
    deep = [column(pick(k)) for k in range(2)]
    for k, l, load in loads:
        wet = widen((deep[k] > l).astype(F32).astype(BF16), width)
        load.wait()
        rows_in[k, l] = rows_in[k, l] * wet
        store = pltpu.make_async_copy(
            rows_in.at[k, l], sides[k].at[pl.ds(l * cols, cols)], out_sem.at[k, l]
        )
        store.start()
        stores.append(store)
    load_atm.wait()
    for k in (1, 0):
        store = pltpu.make_async_copy(
            atm, sides[k].at[pl.ds(lev * cols, own)], atm_sem.at[k]
        )
        store.start()
        stores.append(store)
    counts = [
        jnp.sum(jnp.maximum(d[1 : rows - 1] - 1.0, 0.0)),
        jnp.sum(jnp.maximum(pick(0) - 1.0, 0.0)),
        jnp.sum(pick(1)),
    ]
    over = jnp.int32(0)
    for count, cap in zip(counts, caps):
        over = over | (count > cap).astype(jnp.int32)
    flag_ref[0] = over
    for store in stores:
        store.wait()


def inner_kernel(
    cap,
    state,
    depth_ref,
    weight_hbm,
    mixed_hbm,
    normed_hbm,
    packed_hbm,
    weight,
    mixed,
    normed,
    packed,
    weight_sem,
    out_sem,
    packed_sem,
):
    _, lev, cells, width = state.shape
    rows, cols = depth_ref.shape
    load = pltpu.make_async_copy(weight_hbm, weight, weight_sem)
    load.start()
    packed[...] = jnp.zeros_like(packed)
    d = depth_ref[...].astype(F32)
    plans = [row_plan(d[r : r + 1], lev) for r in range(1, rows - 1)]
    place = offsets(plans, 1, lev)
    deep = jnp.concatenate([column(d[r : r + 1]) for r in range(rows)], axis=0)
    count = cells - 2 * cols
    stores = []
    for l in range(1, lev):
        wet = (deep > l).astype(F32)
        x = state[0, l] * widen(wet.astype(BF16), width)
        taps = [x[dr * cols : dr * cols + count] for dr in range(3)]
        if l == 1:
            load.wait()
        total = stencil(taps, weight, cols)
        new = taps[1].astype(F32) + widen(wet[cols : cols + count], width) * total
        new = new.astype(BF16)
        mixed[l - 1] = new
        tokens = normalise(new)
        normed[l - 1] = tokens
        for k, (buf, out) in enumerate(((mixed, mixed_hbm), (normed, normed_hbm))):
            store = pltpu.make_async_copy(buf.at[l - 1], out.at[l - 1], out_sem.at[l - 1, k])
            store.start()
            stores.append(store)
        for r, plan in enumerate(plans):
            pack(
                packed,
                plan[0][l : l + 1],
                plan[1][l : l + 1],
                place[l, r],
                cap,
                tokens[r * cols : (r + 1) * cols],
            )
        if l == lev - 1:
            store = pltpu.make_async_copy(packed.at[pl.ds(0, cap)], packed_hbm, packed_sem)
            store.start()
            stores.append(store)
    for store in stores:
        store.wait()


def surface_kernel(
    ids_ref,
    live_ref,
    side_ref,
    depth_ref,
    on_hbm,
    off_hbm,
    atm_ref,
    remap,
    base_hbm,
    edge_mixed_in,
    edge_normed_in,
    mixed_ref,
    normed_ref,
    far_ref,
    edge_mixed_hbm,
    edge_normed_hbm,
    base,
    window,
    forcing_ref,
    sem,
):
    rows, cols = depth_ref.shape
    _, own, width = atm_ref.shape
    blocks, pairs = remap.shape[0], remap.shape[1]
    on_at = jnp.where(side_ref[0] == 0, 0, 2 * own)
    copies = [
        pltpu.make_async_copy(
            on_hbm.at[pl.ds(on_hbm.shape[0] - own, own)],
            window.at[pl.ds(pl.multiple_of(on_at, own), own)],
            sem.at[0],
        ),
        pltpu.make_async_copy(
            off_hbm.at[pl.ds(off_hbm.shape[0] - own, own)],
            window.at[pl.ds(pl.multiple_of(2 * own - on_at, own), own)],
            sem.at[1],
        ),
        pltpu.make_async_copy(base_hbm, base, sem.at[4]),
    ]
    for copy in copies:
        copy.start()
    window[own : 2 * own] = atm_ref[0]
    d = depth_ref[...].astype(F32)
    near, far = side_ref[0], side_ref[1]
    rows_d = [d[r : r + 1] for r in range(1, rows - 1)]
    rows_d.append(jnp.where(near == 0, d[0:1], d[rows - 1 :]))
    wets = [widen((column(row) > 0).astype(F32), width) for row in rows_d]
    for copy in copies:
        copy.wait()
    for b in range(blocks):
        acc = jnp.zeros((cols, width), F32)
        for p in range(pairs):
            on = (p < live_ref[b]).astype(F32)
            start = pl.multiple_of(ids_ref[b, p] * cols, cols)
            acc = acc + on * jnp.dot(
                remap[b, p], window[pl.ds(start, cols), :], preferred_element_type=F32
            )
        forcing_ref[b] = acc
    for k, wet in enumerate(wets):
        at = slice(k * cols, (k + 1) * cols)
        forcing = forcing_ref[near] if k == rows - 2 else forcing_ref[k + 1]
        new = (base[at] + wet * forcing).astype(BF16)
        mixed_ref[0, at] = new
        normed_ref[0, at] = normalise(new)
    far_ref[...] = forcing_ref[far]
    at = pl.ds((rows - 2) * cols, cols)
    stores = [
        pltpu.make_async_copy(mixed_ref.at[0, at], edge_mixed_hbm.at[0, pl.ds(0, cols)], sem.at[2]),
        pltpu.make_async_copy(normed_ref.at[0, at], edge_normed_hbm.at[0, pl.ds(0, cols)], sem.at[3]),
    ]
    for store in stores:
        store.start()
    for store in stores:
        store.wait()


def row_kernel(cap, first, which, side_ref, state, depth_ref, weight_hbm, halo_hbm, *refs):
    refs = list(refs)
    forcing_hbm = None
    if not first:
        forcing_hbm = refs[0]
        refs = refs[3:]
    mixed_hbm, normed_hbm, packed_hbm = refs[:3]
    refs = refs[3:]
    base_ref = refs.pop(0) if first else None
    forcing_ref, weight, tap, mixed, normed, packed, weight_sem, halo_sem, out_sem, packed_sem = refs
    load = pltpu.make_async_copy(weight_hbm, weight, weight_sem)
    load.start()
    _, lev, cells, width = state.shape
    rows, cols = depth_ref.shape
    row = side_ref[which]
    top = row == 0
    beside = jnp.where(top, 1, rows - 2)
    outer = jnp.where(top, 0, 2)
    halo = pltpu.make_async_copy(
        halo_hbm.at[pl.ds(0, lev * cols)], tap.at[outer], halo_sem
    )
    halo.start()
    if not first:
        forcing = pltpu.make_async_copy(forcing_hbm, forcing_ref, packed_sem)
        forcing.start()
    packed[...] = jnp.zeros_like(packed)
    d = depth_ref[...].astype(F32)
    own_depth = jnp.where(top, d[0:1], d[rows - 1 :])
    plan = row_plan(own_depth, lev)
    place = offsets([plan], first, lev)
    deep = column(own_depth)
    deep_beside = column(jnp.where(top, d[1:2], d[rows - 2 : rows - 1]))
    at = pl.multiple_of(row * cols, cols)
    at_beside = pl.multiple_of(beside * cols, cols)
    wets = []
    for l in range(lev):
        rows_l = slice(l * cols, (l + 1) * cols)
        wet = (deep > l).astype(F32)
        wets.append(wet)
        wet_beside = (deep_beside > l).astype(F32)
        tap[1, rows_l] = state[0, l, pl.ds(at, cols)] * widen(wet.astype(BF16), width)
        tap[2 - outer, rows_l] = state[0, l, pl.ds(at_beside, cols)] * widen(
            wet_beside.astype(BF16), width
        )
    stores = []
    half = lev // 2
    load.wait()
    halo.wait()
    if not first:
        forcing.wait()
    for start in range(0, lev, half):
        rows_b = slice(start * cols, (start + half) * cols)
        taps = [tap[dr, rows_b] for dr in range(3)]
        total = stencil(taps, weight, cols)
        for k in range(half):
            l = start + k
            rows_k = slice(k * cols, (k + 1) * cols)
            part = total[rows_k]
            if l == 0 and not first:
                part = part + forcing_ref[...]
            new = taps[1][rows_k].astype(F32) + widen(wets[l], width) * part
            if l < first:
                base_ref[cells - 2 * cols :] = new
                continue
            new = new.astype(BF16)
            mixed[l - first] = new
            tokens = normalise(new)
            normed[l - first] = tokens
            pack(packed, plan[0][l : l + 1], plan[1][l : l + 1], place[l, 0], cap, tokens)
    if first:
        wet = (jnp.concatenate([column(d[r : r + 1]) for r in range(rows)], axis=0) > 0).astype(F32)
        x = state[0, 0] * widen(wet.astype(BF16), width)
        taps = [x[dr * cols : dr * cols + cells - 2 * cols] for dr in range(3)]
        inside = widen(wet[cols : cells - cols], width)
        base_ref[0 : cells - 2 * cols] = taps[1].astype(F32) + inside * stencil(taps, weight, cols)
    block = (pl.ds(first, lev - first), pl.ds(which * cols, cols))
    for k, (buf, out) in enumerate(((mixed, mixed_hbm), (normed, normed_hbm))):
        store = pltpu.make_async_copy(buf, out.at[block], out_sem.at[k])
        store.start()
        stores.append(store)
    store = pltpu.make_async_copy(packed.at[pl.ds(0, cap)], packed_hbm, packed_sem)
    store.start()
    stores.append(store)
    for store in stores:
        store.wait()


def attend_kernel(others, nparts, edges, flag_ref, side_ref, *refs):
    refs = list(refs)
    take = lambda k: [refs.pop(0) for _ in range(k)]
    own_normed = take(nparts)
    own_mixed = take(nparts)
    surf = take(others)
    packed = [take(others) for _ in range(1 + edges)]
    whole = take(others)
    depth_ref, qkv_hbm, wo_hbm = take(3)
    if edges:
        take(1)
    out_hbm, qkv_ref, wo_ref, x_ref, mixed_ref, q_ref, k_ref, v_ref, att_ref = refs[:9]
    token_ref, new_ref, in_sem, out_sem, sem, weight_sem = refs[9:]
    load_qkv = pltpu.make_async_copy(qkv_hbm, qkv_ref, weight_sem.at[0])
    load_wo = pltpu.make_async_copy(wo_hbm, wo_ref, weight_sem.at[1])
    load_qkv.start()
    load_wo.start()
    steps, lev, count, width = q_ref.shape
    members = others + 1
    head = width // HEADS
    pair = 2 * head

    loads = []
    for kind, (parts, buf) in enumerate(((own_normed, x_ref), (own_mixed, mixed_ref))):
        for step in range(steps):
            at = 0
            for k, part in enumerate(parts):
                n = part.shape[0]
                load = pltpu.make_async_copy(
                    part.at[:, pl.ds(step * count, count)],
                    buf.at[step, pl.ds(at, n)],
                    in_sem.at[kind, step, k],
                )
                load.start()
                loads.append((kind, step, load))
                at += n

    def arrive(kind, step):
        for k, s, load in loads:
            if (k, s) == (kind, step):
                load.wait()

    d = depth_ref[...].astype(F32)
    last = d.shape[0] - 1
    if edges:
        rows_d = [jnp.where(side_ref[k] == 0, d[0:1], d[last:]) for k in range(2)]
    else:
        rows_d = [d[r : r + 1] for r in range(1, last)]
    plans = [row_plan(row, lev) for row in rows_d]
    if edges:
        near, far = offsets(plans[:1], 1, lev), offsets(plans[1:], 0, lev)
        place = [{l: at for (l, _), at in p.items()} for p in (near, far)]
    else:
        both = offsets(plans, 1, lev)
        place = [{l: both[l, step] for l in range(1, lev)} for step in range(steps)]

    def project(x, step, m):
        rows = slice(m * lev, (m + 1) * lev)
        kv = jnp.dot(x, qkv_ref[:, width:], preferred_element_type=F32).astype(BF16)
        k_ref[step, rows] = kv[:, :width].reshape(lev, count, width)
        v_ref[step, rows] = kv[:, width:].reshape(lev, count, width)

    for o in range(others):
        for step in range(steps):
            source = packed[step if edges else 0][o]
            window = lambda base, size: source[pl.ds(base, size), :]
            limit = source.shape[0] - count - 16
            wet, rank, _ = plans[step]
            if 0 not in place[step]:
                at = surf[o].shape[1] - count if edges else step * count
                token_ref[step, 0] = surf[o][0, at : at + count]
            for l, at in place[step].items():
                token_ref[step, l] = unpack(window, wet[l : l + 1], rank[l : l + 1], at, limit)

        @pl.when(flag_ref[0] != 0)
        def _():
            first = lev - whole[o].shape[0]
            for step in range(steps):
                copy = pltpu.make_async_copy(
                    whole[o].at[:, pl.ds(step * count, count)],
                    token_ref.at[step, pl.ds(first, lev - first)],
                    sem,
                )
                copy.start()
                copy.wait()

        if o == 0:
            load_qkv.wait()
            load_wo.wait()
        for step in range(steps):
            project(token_ref[step].reshape(-1, width), step, o + 1)

    nq, nk = lev * GROUP, members * lev * GROUP
    groups = count // GROUP
    lanes_n = lev * GROUP
    cell = lax.broadcasted_iota(jnp.int32, (groups, count), 1)
    mine = (cell // GROUP == lax.broadcasted_iota(jnp.int32, (groups, count), 0)).astype(F32)
    spread = lax.broadcasted_iota(jnp.int32, (count, lanes_n), 0) % GROUP
    spread = (spread == lax.broadcasted_iota(jnp.int32, (count, lanes_n), 1) % GROUP).astype(F32)
    key_level = lax.broadcasted_iota(jnp.int32, (groups, lanes_n), 1) // GROUP
    qc = lax.broadcasted_iota(jnp.int32, (nq, nk), 0) % GROUP
    kc = lax.broadcasted_iota(jnp.int32, (nq, nk), 1) % GROUP
    same = jnp.where(qc == kc, 0.0, NEG)
    lane = lax.broadcasted_iota(jnp.int32, (1, width), 1)
    scale = 1.0 / math.sqrt(head)
    masks = [jnp.where(lane // head == h, scale, 0.0).astype(BF16) for h in range(HEADS)]
    stores = []
    for step in range(steps):
        arrive(0, step)
        x = x_ref[step].reshape(-1, width)
        q = jnp.dot(x, qkv_ref[:, 0:width], preferred_element_type=F32).astype(BF16)
        q_ref[step] = q.reshape(lev, count, width)
        project(x, step, 0)
        key_depth = jnp.dot(
            (mine * rows_d[step]).astype(BF16), spread.astype(BF16), preferred_element_type=F32
        )
        key_bias = jnp.where(key_depth > key_level.astype(F32), 0.0, NEG)
        for g in range(groups):
            cells = slice(g * GROUP, (g + 1) * GROUP)
            bias = same + jnp.concatenate([key_bias[g : g + 1]] * members, axis=1)
            bias = jnp.concatenate([bias] * HEADS, axis=0)
            q = q_ref[step, :, cells].reshape(nq, width)
            q = jnp.concatenate([q * mask for mask in masks], axis=0)
            k = k_ref[step, :, cells].reshape(nk, width)
            v = v_ref[step, :, cells].reshape(nk, width)
            s = lax.dot_general(q, k, (((1,), (1,)), ((), ())), preferred_element_type=F32) + bias
            p = jnp.exp(s - jnp.max(s, axis=-1, keepdims=True))
            norm = 1.0 / jnp.sum(p, axis=-1, keepdims=True)
            p = p.astype(BF16)
            for h in range(HEADS // 2):
                lanes = slice(h * pair, (h + 1) * pair)
                rows = slice(h * 2 * nq, (h + 1) * 2 * nq)
                o = jnp.dot(p[rows], v[:, lanes], preferred_element_type=F32) * norm[rows]
                o = jnp.where(lane[:, :pair] < head, o[:nq], o[nq:])
                att_ref[step, :, cells, lanes] = o.astype(BF16).reshape(lev, GROUP, pair)
        proj = jnp.dot(
            att_ref[step].reshape(-1, width), wo_ref[...], preferred_element_type=F32
        )
        arrive(1, step)
        deep = column(rows_d[step])
        row = side_ref[step] if edges else step + 1
        for l in range(lev):
            rows = slice(l * count, (l + 1) * count)
            wet = widen((deep > l).astype(F32), width)
            new_ref[step, l] = (mixed_ref[step, l].astype(F32) + wet * proj[rows]).astype(BF16)
        at = pl.multiple_of(row * count, count)
        store = pltpu.make_async_copy(
            new_ref.at[step], out_hbm.at[0, :, pl.ds(at, count)], out_sem.at[step]
        )
        store.start()
        stores.append(store)
    for store in stores:
        store.wait()


def attend(
    flag, side, normed, mixed, surf, packed, whole, depth, qkv_weight, out_weight, out, shape
):
    edges = out is not None
    others, nparts = len(whole), len(mixed)
    lev = sum(p.shape[0] for p in mixed)
    width = shape[-1]
    cols = depth.shape[1]
    members = others + 1
    hbm = pl.BlockSpec(memory_space=pltpu.HBM)
    vmem = pl.BlockSpec(memory_space=pltpu.VMEM)
    smem = pl.BlockSpec(memory_space=pltpu.SMEM)
    stay = lambda x: pltpu.with_memory_space_constraint(x, pltpu.HBM)
    in_specs = [smem] * 2 + [hbm] * (2 * nparts) + [vmem] * (len(surf) + len(packed))
    in_specs += [hbm] * others + [vmem] + [hbm] * 2
    args = [flag, side] + [stay(x) for x in normed + mixed] + surf + packed
    args += [stay(x) for x in whole] + [depth, stay(qkv_weight), stay(out_weight)]
    alias = {}
    if edges:
        in_specs.append(hbm)
        alias = {len(args): 0}
        args.append(stay(out))
    tokens = lev * cols * 2
    rows = pltpu.VMEM((2, lev, cols, width), BF16)
    keys = pltpu.VMEM((2, members * lev, cols, width), BF16)
    return pl.pallas_call(
        functools.partial(attend_kernel, others, nparts, edges),
        in_specs=in_specs,
        out_specs=hbm,
        scratch_shapes=[
            pltpu.VMEM(qkv_weight.shape, BF16),
            pltpu.VMEM(out_weight.shape, BF16),
            rows,
            rows,
            rows,
            keys,
            keys,
            rows,
            rows,
            rows,
            pltpu.SemaphoreType.DMA((2, 2, nparts)),
            pltpu.SemaphoreType.DMA((2,)),
            pltpu.SemaphoreType.DMA,
            pltpu.SemaphoreType.DMA((2,)),
        ],
        out_shape=pltpu.HBM(shape, BF16),
        input_output_aliases=alias,
        compiler_params=params(24 if members <= 2 else 56),
        cost_estimate=cost(tokens * width * width * 8 * (members + 2), tokens * width * 2 * 5),
        name="attend",
    )(*args)


def body(
    atm_latent,
    ocean_state,
    depth,
    src_blocks,
    live,
    remap_weight,
    conv_weight,
    qkv_weight,
    out_weight,
):
    _, lev, cells, width = ocean_state.shape
    cols = remap_weight.shape[2]
    rows = cells // cols
    inner = cells - 2 * cols
    own = atm_latent.shape[1]
    atm_blk = own // cols
    tiles = lax.axis_size("tile")
    members = lax.axis_size("mem")
    tile = lax.axis_index("tile")

    def swap(x, first):
        pairs = [(i, i + 1) for i in range(first, tiles - 1, 2)]
        return lax.ppermute(x, "tile", pairs + [(b, a) for a, b in pairs])

    def exchange(x):
        return [
            lax.ppermute(x, "mem", [(i, (i + k) % members) for i in range(members)])
            for k in range(1, members)
        ]

    odd = tile % 2
    side = jnp.stack([(1 - odd) * (rows - 1), odd * (rows - 1)]).astype(jnp.int32)
    depth = depth.reshape(rows, cols)
    deep_cap = capacity((lev - 1) * inner, 0.5625)
    near_cap = capacity((lev - 1) * cols, 0.605)
    far_cap = capacity(lev * cols, 0.65625)

    hbm = pl.BlockSpec(memory_space=pltpu.HBM)
    anywhere = pl.BlockSpec(memory_space=pl.ANY)
    vmem = pl.BlockSpec(memory_space=pltpu.VMEM)
    smem = pl.BlockSpec(memory_space=pltpu.SMEM)
    tok = lambda *s: pltpu.HBM((*s, width), BF16)
    stay = lambda x: pltpu.with_memory_space_constraint(x, pltpu.HBM)
    conv_flops = lambda n, c: 2 * 9 * n * c * width * width
    dma = pltpu.SemaphoreType.DMA
    slack = cols + 16
    message = lev * cols + own
    on_msg, off_msg, flag = pl.pallas_call(
        functools.partial(prep_kernel, (deep_cap, near_cap, far_cap)),
        in_specs=[smem, hbm, hbm, hbm],
        out_specs=[hbm, hbm, smem],
        out_shape=[tok(message), tok(message), jax.ShapeDtypeStruct((1,), jnp.int32)],
        scratch_shapes=[
            pltpu.VMEM((rows, cols), jnp.int32),
            pltpu.VMEM((own, width), BF16),
            pltpu.VMEM((2, lev, cols, width), BF16),
            dma((2, lev)),
            dma((2, lev)),
            dma((2,)),
            dma((2,)),
        ],
        compiler_params=params(16),
        cost_estimate=cost(lev * cols * width * 4, lev * cols * width * 10),
        name="prep",
    )(side, stay(ocean_state), stay(atm_latent), stay(depth))
    off_halo = swap(off_msg, 1)
    on_halo = swap(on_msg, 0)

    deep_mixed, deep_normed, deep_packed = pl.pallas_call(
        functools.partial(inner_kernel, deep_cap),
        in_specs=[vmem, vmem, hbm],
        out_specs=[hbm] * 3,
        out_shape=[tok(lev - 1, inner), tok(lev - 1, inner), tok(deep_cap)],
        scratch_shapes=[
            pltpu.VMEM(conv_weight.shape, BF16),
            pltpu.VMEM((lev - 1, inner, width), BF16),
            pltpu.VMEM((lev - 1, inner, width), BF16),
            pltpu.VMEM((deep_cap + slack, width), BF16),
            dma,
            dma((lev - 1, 2)),
            dma,
        ],
        compiler_params=params(12),
        cost_estimate=cost(conv_flops(lev, inner), lev * inner * width * 8),
        name="inner",
    )(ocean_state, depth, stay(conv_weight))
    deep_others = exchange(deep_packed)

    whole_spec = lambda *sh: pl.BlockSpec(sh, lambda *_: (0,) * len(sh))
    row_f32 = pltpu.HBM((cols, width), F32)

    def row_conv(which, first, cap, halo, extra):
        n = lev - first
        base = pltpu.HBM((inner + cols, width), F32)
        return pl.pallas_call(
            functools.partial(row_kernel, cap, first, which),
            in_specs=[smem, vmem, vmem, hbm, anywhere] + [hbm] * len(extra),
            out_specs=[hbm] * 3 + [whole_spec(inner + cols, width)] * first,
            out_shape=[tok(lev, 2 * cols), tok(lev, 2 * cols), tok(cap)] + [base] * first,
            scratch_shapes=[
                pltpu.VMEM((cols, width), F32),
                pltpu.VMEM(conv_weight.shape, BF16),
                pltpu.VMEM((3, lev * cols, width), BF16),
                pltpu.VMEM((n, cols, width), BF16),
                pltpu.VMEM((n, cols, width), BF16),
                pltpu.VMEM((cap + slack, width), BF16),
                dma,
                dma,
                dma((2,)),
                dma,
            ],
            input_output_aliases={6: 0, 7: 1} if extra else {},
            compiler_params=params(12),
            cost_estimate=cost(conv_flops(lev, cols), lev * cols * width * 16),
            name="row",
        )(side, ocean_state, depth, stay(conv_weight), halo, *[stay(x) for x in extra])

    edge_mixed, edge_normed, near_packed, base = row_conv(0, 1, near_cap, on_halo, [])

    ids = jnp.clip(src_blocks - (tile - R) * atm_blk, 0, 3 * atm_blk - 1)
    surf_mixed, surf_normed, far_forcing, edge_mixed, edge_normed = pl.pallas_call(
        surface_kernel,
        in_specs=[smem] * 3 + [vmem] + [anywhere] * 2 + [vmem] * 2 + [hbm] * 3,
        out_specs=[whole_spec(1, inner + cols, width)] * 2 + [whole_spec(cols, width)] + [hbm] * 2,
        out_shape=[tok(1, inner + cols), tok(1, inner + cols), row_f32]
        + [tok(lev, 2 * cols)] * 2,
        scratch_shapes=[
            pltpu.VMEM((inner + cols, width), F32),
            pltpu.VMEM((3 * own, width), BF16),
            pltpu.VMEM((rows, cols, width), F32),
            dma((5,)),
        ],
        input_output_aliases={9: 3, 10: 4},
        compiler_params=params(12),
        cost_estimate=cost(conv_flops(1, inner), cells * width * 16),
        name="surface",
    )(
        ids,
        live,
        side,
        depth,
        on_halo,
        off_halo,
        atm_latent,
        remap_weight,
        stay(base),
        stay(edge_mixed),
        stay(edge_normed),
    )
    surf_others = exchange(surf_normed)
    near_others = exchange(near_packed)

    edge_mixed, edge_normed, far_packed = row_conv(
        1, 0, far_cap, off_halo, [far_forcing, edge_mixed, edge_normed]
    )
    far_others = exchange(far_packed)

    def unread(shape):
        return pl.pallas_call(
            lambda out_ref: None,
            out_specs=hbm,
            out_shape=pltpu.HBM(shape, BF16),
            name="unread",
        )()

    def send_all(*arrays):
        sizes = [x.shape[0] * x.shape[1] for x in arrays]
        joined = jnp.concatenate([x.reshape(-1, width) for x in arrays], axis=0)
        got = [[] for _ in arrays]
        for part in exchange(joined):
            at = 0
            for k, (x, size) in enumerate(zip(arrays, sizes)):
                got[k].append(part[at : at + size].reshape(x.shape))
                at += size
        return tuple(got)

    deep_whole, edge_whole = lax.cond(
        flag[0] > 0,
        send_all,
        lambda *a: tuple([unread(x.shape) for _ in range(members - 1)] for x in a),
        deep_normed,
        edge_normed,
    )
    shape = ocean_state.shape
    weights = (depth, qkv_weight, out_weight)
    out = attend(
        flag,
        side,
        [surf_normed, deep_normed],
        [surf_mixed, deep_mixed],
        surf_others,
        deep_others,
        deep_whole,
        *weights,
        None,
        shape,
    )
    return attend(
        flag,
        side,
        [edge_normed],
        [edge_mixed],
        surf_others,
        near_others + far_others,
        edge_whole,
        *weights,
        out,
        shape,
    )


def solution(mesh):
    return jax.shard_map(
        body,
        mesh=mesh,
        in_specs=(
            P("mem", "tile", None),
            P("mem", None, "tile", None),
            P("tile"),
            P("tile", None),
            P("tile"),
            P("tile", None, None, None),
            P(),
            P(),
            P(),
        ),
        out_specs=P("mem", None, "tile", None),
        check_vma=False,
    )
```

```python
import functools
import math

import jax
import jax.numpy as jnp
from jax import lax
from jax.experimental import pallas as pl
from jax.experimental.pallas import tpu as pltpu
from jax.sharding import PartitionSpec as P

HEADS = 4
R = 1
GROUP = 16
EPS = 1e-06
NEG = -1e30
F32 = jnp.float32
BF16 = jnp.bfloat16
MIB = 1024 * 1024


def params(mib, steps=0):
    return pltpu.CompilerParams(
        dimension_semantics=("arbitrary",) * steps if steps else None, vmem_limit_bytes=mib * MIB
    )


def cost(flops, nbytes):
    return pl.CostEstimate(flops=int(flops), bytes_accessed=int(nbytes), transcendentals=0)


def capacity(tokens, share):
    return -(-int(tokens * share) // 16) * 16


def row_plan(depth_row, lev):
    cols = depth_row.shape[1]
    level = lax.broadcasted_iota(jnp.int32, (lev, cols), 0).astype(F32)
    wet = (depth_row > level).astype(F32)
    upper = (
        lax.broadcasted_iota(jnp.int32, (cols, cols), 0)
        < lax.broadcasted_iota(jnp.int32, (cols, cols), 1)
    )
    upper = upper.astype(F32).astype(BF16)
    rank = jnp.dot(wet.astype(BF16), upper, preferred_element_type=F32)
    counts = [jnp.sum(wet[l : l + 1]).astype(jnp.int32) for l in range(lev)]
    return wet, rank, counts


def offsets(plans, first, lev):
    at, place = jnp.int32(0), {}
    for l in range(first, lev):
        for r, plan in enumerate(plans):
            place[l, r] = at
            at = at + plan[2][l]
    return place


def segment(wet, rank, offset, limit):
    cols = wet.shape[1]
    base = jnp.minimum((offset // 16) * 16, limit)
    target = jnp.where(wet > 0, rank + (offset - base).astype(F32), -1.0)
    slot = lax.broadcasted_iota(jnp.int32, (cols + 16, cols), 0).astype(F32)
    return pl.multiple_of(base, 16), (slot == target).astype(F32).astype(BF16)


def pack(buf_ref, wet, rank, offset, cap, tokens):
    base, hot = segment(wet, rank, offset, cap)
    rows = jnp.dot(hot, tokens, preferred_element_type=F32).astype(BF16)
    head = pl.ds(base, 16)
    buf_ref[head, :] = buf_ref[head, :] + rows[:16]
    buf_ref[pl.ds(pl.multiple_of(base + 16, 16), rows.shape[0] - 16), :] = rows[16:]


def unpack(rows_of, wet, rank, offset, limit):
    base, hot = segment(wet, rank, offset, limit)
    return lax.dot_general(
        hot, rows_of(base, hot.shape[0]), (((0,), (0,)), ((), ())), preferred_element_type=F32
    ).astype(BF16)


def column(depth_row):
    cols = depth_row.shape[1]
    return jnp.broadcast_to(depth_row, (cols, cols)).T


def widen(x, width):
    return jnp.concatenate([x] * (width // x.shape[1]), axis=1)


def stencil(taps, weight_ref, cols):
    count, width = taps[0].shape
    x = jnp.concatenate(taps, axis=1)
    sums = [
        jnp.dot(x, weight_ref[:, dc].reshape(3 * width, -1), preferred_element_type=F32)
        for dc in range(3)
    ]
    col = lax.broadcasted_iota(jnp.int32, (count, 1), 0) % cols
    left = jnp.where(col == 0, 0.0, pltpu.roll(sums[0], 1, axis=0))
    right = jnp.where(col == cols - 1, 0.0, pltpu.roll(sums[2], count - 1, axis=0))
    return sums[1] + left + right


def normalise(mixed):
    mf = mixed.astype(F32)
    mean = jnp.mean(mf * mf, axis=-1, keepdims=True)
    return (mf * lax.rsqrt(mean + EPS)).astype(BF16)


def prep_kernel(
    caps,
    side_ref,
    state_hbm,
    atm_hbm,
    depth_hbm,
    on_hbm,
    off_hbm,
    flag_ref,
    depth_ref,
    atm,
    rows_in,
    in_sem,
    out_sem,
    atm_sem,
    own_sem,
):
    _, lev, cells, width = state_hbm.shape
    rows, cols = depth_ref.shape
    own = atm_hbm.shape[1]
    sides = (on_hbm, off_hbm)
    load_depth = pltpu.make_async_copy(depth_hbm, depth_ref, own_sem.at[0])
    load_depth.start()
    loads, stores = [], []
    for k in (1, 0):
        at = pl.multiple_of(side_ref[k] * cols, cols)
        for l in range(lev):
            load = pltpu.make_async_copy(
                state_hbm.at[0, l, pl.ds(at, cols)], rows_in.at[k, l], in_sem.at[k, l]
            )
            load.start()
            loads.append((k, l, load))
    load_atm = pltpu.make_async_copy(atm_hbm.at[0], atm, own_sem.at[1])
    load_atm.start()
    load_depth.wait()
    d = depth_ref[...].astype(F32)
    pick = lambda k: jnp.where(side_ref[k] == 0, d[0:1], d[rows - 1 :])
    deep = [column(pick(k)) for k in range(2)]
    for k, l, load in loads:
        wet = widen((deep[k] > l).astype(F32).astype(BF16), width)
        load.wait()
        rows_in[k, l] = rows_in[k, l] * wet
        store = pltpu.make_async_copy(
            rows_in.at[k, l], sides[k].at[pl.ds(l * cols, cols)], out_sem.at[k, l]
        )
        store.start()
        stores.append(store)
    load_atm.wait()
    for k in (1, 0):
        store = pltpu.make_async_copy(
            atm, sides[k].at[pl.ds(lev * cols, own)], atm_sem.at[k]
        )
        store.start()
        stores.append(store)
    counts = [
        jnp.sum(jnp.maximum(d[1 : rows - 1] - 1.0, 0.0)),
        jnp.sum(jnp.maximum(pick(0) - 1.0, 0.0)),
        jnp.sum(pick(1)),
    ]
    over = jnp.int32(0)
    for count, cap in zip(counts, caps):
        over = over | (count > cap).astype(jnp.int32)
    flag_ref[0] = over
    for store in stores:
        store.wait()


def inner_kernel(
    cap,
    state,
    depth_ref,
    weight_hbm,
    mixed_hbm,
    normed_hbm,
    packed_hbm,
    weight,
    mixed,
    normed,
    packed,
    weight_sem,
    out_sem,
    packed_sem,
):
    _, lev, cells, width = state.shape
    rows, cols = depth_ref.shape
    load = pltpu.make_async_copy(weight_hbm, weight, weight_sem)
    load.start()
    packed[...] = jnp.zeros_like(packed)
    d = depth_ref[...].astype(F32)
    plans = [row_plan(d[r : r + 1], lev) for r in range(1, rows - 1)]
    place = offsets(plans, 1, lev)
    deep = jnp.concatenate([column(d[r : r + 1]) for r in range(rows)], axis=0)
    count = cells - 2 * cols
    stores = []
    for l in range(1, lev):
        wet = (deep > l).astype(F32)
        x = state[0, l] * widen(wet.astype(BF16), width)
        taps = [x[dr * cols : dr * cols + count] for dr in range(3)]
        if l == 1:
            load.wait()
        total = stencil(taps, weight, cols)
        new = taps[1].astype(F32) + widen(wet[cols : cols + count], width) * total
        new = new.astype(BF16)
        mixed[l - 1] = new
        tokens = normalise(new)
        normed[l - 1] = tokens
        for k, (buf, out) in enumerate(((mixed, mixed_hbm), (normed, normed_hbm))):
            store = pltpu.make_async_copy(buf.at[l - 1], out.at[l - 1], out_sem.at[l - 1, k])
            store.start()
            stores.append(store)
        for r, plan in enumerate(plans):
            pack(
                packed,
                plan[0][l : l + 1],
                plan[1][l : l + 1],
                place[l, r],
                cap,
                tokens[r * cols : (r + 1) * cols],
            )
        if l == lev - 1:
            store = pltpu.make_async_copy(packed.at[pl.ds(0, cap)], packed_hbm, packed_sem)
            store.start()
            stores.append(store)
    for store in stores:
        store.wait()


def surface_kernel(
    ids_ref,
    live_ref,
    side_ref,
    depth_ref,
    on_hbm,
    off_hbm,
    atm_ref,
    remap,
    qkv_ref,
    wo_ref,
    base_hbm,
    edge_mixed_in,
    edge_normed_in,
    mixed_ref,
    normed_ref,
    far_ref,
    edge_mixed_hbm,
    edge_normed_hbm,
    base,
    window,
    forcing_ref,
    sem,
):
    rows, cols = depth_ref.shape
    _, own, width = atm_ref.shape
    blocks, pairs = remap.shape[0], remap.shape[1]
    on_at = jnp.where(side_ref[0] == 0, 0, 2 * own)
    copies = [
        pltpu.make_async_copy(
            on_hbm.at[pl.ds(on_hbm.shape[0] - own, own)],
            window.at[pl.ds(pl.multiple_of(on_at, own), own)],
            sem.at[0],
        ),
        pltpu.make_async_copy(
            off_hbm.at[pl.ds(off_hbm.shape[0] - own, own)],
            window.at[pl.ds(pl.multiple_of(2 * own - on_at, own), own)],
            sem.at[1],
        ),
        pltpu.make_async_copy(base_hbm, base, sem.at[4]),
    ]
    for copy in copies:
        copy.start()
    window[own : 2 * own] = atm_ref[0]
    d = depth_ref[...].astype(F32)
    near, far = side_ref[0], side_ref[1]
    rows_d = [d[r : r + 1] for r in range(1, rows - 1)]
    rows_d.append(jnp.where(near == 0, d[0:1], d[rows - 1 :]))
    wets = [widen((column(row) > 0).astype(F32), width) for row in rows_d]
    for copy in copies:
        copy.wait()
    for b in range(blocks):
        acc = jnp.zeros((cols, width), F32)
        for p in range(pairs):
            on = (p < live_ref[b]).astype(F32)
            start = pl.multiple_of(ids_ref[b, p] * cols, cols)
            acc = acc + on * jnp.dot(
                remap[b, p], window[pl.ds(start, cols), :], preferred_element_type=F32
            )
        forcing_ref[b] = acc
    for k, wet in enumerate(wets):
        at = slice(k * cols, (k + 1) * cols)
        forcing = forcing_ref[near] if k == rows - 2 else forcing_ref[k + 1]
        new = (base[at] + wet * forcing).astype(BF16)
        mixed_ref[0, at] = new
        normed_ref[0, at] = normalise(new)
    far_ref[...] = forcing_ref[far]
    at = pl.ds((rows - 2) * cols, cols)
    stores = [
        pltpu.make_async_copy(mixed_ref.at[0, at], edge_mixed_hbm.at[0, pl.ds(0, cols)], sem.at[2]),
        pltpu.make_async_copy(normed_ref.at[0, at], edge_normed_hbm.at[0, pl.ds(0, cols)], sem.at[3]),
    ]
    for store in stores:
        store.start()
    for store in stores:
        store.wait()


def row_kernel(cap, first, which, side_ref, state, depth_ref, weight_hbm, halo_hbm, *refs):
    refs = list(refs)
    forcing_hbm = None
    if not first:
        forcing_hbm = refs[0]
        refs = refs[3:]
    mixed_hbm, normed_hbm, packed_hbm = refs[:3]
    refs = refs[3:]
    base_ref = refs.pop(0) if first else None
    forcing_ref, weight, tap, mixed, normed, packed, weight_sem, halo_sem, out_sem, packed_sem = refs
    load = pltpu.make_async_copy(weight_hbm, weight, weight_sem)
    load.start()
    _, lev, cells, width = state.shape
    rows, cols = depth_ref.shape
    row = side_ref[which]
    top = row == 0
    beside = jnp.where(top, 1, rows - 2)
    outer = jnp.where(top, 0, 2)
    halo = pltpu.make_async_copy(
        halo_hbm.at[pl.ds(0, lev * cols)], tap.at[outer], halo_sem
    )
    halo.start()
    if not first:
        forcing = pltpu.make_async_copy(forcing_hbm, forcing_ref, packed_sem)
        forcing.start()
    packed[...] = jnp.zeros_like(packed)
    d = depth_ref[...].astype(F32)
    own_depth = jnp.where(top, d[0:1], d[rows - 1 :])
    plan = row_plan(own_depth, lev)
    place = offsets([plan], first, lev)
    deep = column(own_depth)
    deep_beside = column(jnp.where(top, d[1:2], d[rows - 2 : rows - 1]))
    at = pl.multiple_of(row * cols, cols)
    at_beside = pl.multiple_of(beside * cols, cols)
    wets = []
    for l in range(lev):
        rows_l = slice(l * cols, (l + 1) * cols)
        wet = (deep > l).astype(F32)
        wets.append(wet)
        wet_beside = (deep_beside > l).astype(F32)
        tap[1, rows_l] = state[0, l, pl.ds(at, cols)] * widen(wet.astype(BF16), width)
        tap[2 - outer, rows_l] = state[0, l, pl.ds(at_beside, cols)] * widen(
            wet_beside.astype(BF16), width
        )
    stores = []
    half = lev // 2
    load.wait()
    halo.wait()
    if not first:
        forcing.wait()
    for start in range(0, lev, half):
        rows_b = slice(start * cols, (start + half) * cols)
        taps = [tap[dr, rows_b] for dr in range(3)]
        total = stencil(taps, weight, cols)
        for k in range(half):
            l = start + k
            rows_k = slice(k * cols, (k + 1) * cols)
            part = total[rows_k]
            if l == 0 and not first:
                part = part + forcing_ref[...]
            new = taps[1][rows_k].astype(F32) + widen(wets[l], width) * part
            if l < first:
                base_ref[cells - 2 * cols :] = new
                continue
            new = new.astype(BF16)
            mixed[l - first] = new
            tokens = normalise(new)
            normed[l - first] = tokens
            pack(packed, plan[0][l : l + 1], plan[1][l : l + 1], place[l, 0], cap, tokens)
    if first:
        wet = (jnp.concatenate([column(d[r : r + 1]) for r in range(rows)], axis=0) > 0).astype(F32)
        x = state[0, 0] * widen(wet.astype(BF16), width)
        taps = [x[dr * cols : dr * cols + cells - 2 * cols] for dr in range(3)]
        inside = widen(wet[cols : cells - cols], width)
        base_ref[0 : cells - 2 * cols] = taps[1].astype(F32) + inside * stencil(taps, weight, cols)
    block = (pl.ds(first, lev - first), pl.ds(which * cols, cols))
    for k, (buf, out) in enumerate(((mixed, mixed_hbm), (normed, normed_hbm))):
        store = pltpu.make_async_copy(buf, out.at[block], out_sem.at[k])
        store.start()
        stores.append(store)
    store = pltpu.make_async_copy(packed.at[pl.ds(0, cap)], packed_hbm, packed_sem)
    store.start()
    stores.append(store)
    for store in stores:
        store.wait()


def attend_kernel(others, nparts, edges, flag_ref, side_ref, *refs):
    refs = list(refs)
    take = lambda k: [refs.pop(0) for _ in range(k)]
    own_normed = take(nparts)
    own_mixed = take(nparts)
    surf = take(others)
    packed = [take(others) for _ in range(1 + edges)]
    whole = take(others)
    depth_ref, qkv_ref, wo_ref = take(3)
    if edges:
        take(1)
    out_hbm, x_ref, mixed_ref, q_ref, k_ref, v_ref, att_ref, token_ref, new_ref = refs[:9]
    in_sem, out_sem, sem = refs[9:]
    steps, lev, count, width = q_ref.shape
    members = others + 1
    head = width // HEADS
    pair = 2 * head

    loads = []
    for kind, (parts, buf) in enumerate(((own_normed, x_ref), (own_mixed, mixed_ref))):
        for step in range(steps):
            at = 0
            for k, part in enumerate(parts):
                n = part.shape[0]
                load = pltpu.make_async_copy(
                    part.at[:, pl.ds(step * count, count)],
                    buf.at[step, pl.ds(at, n)],
                    in_sem.at[kind, step, k],
                )
                load.start()
                loads.append((kind, step, load))
                at += n

    def arrive(kind, step):
        for k, s, load in loads:
            if (k, s) == (kind, step):
                load.wait()

    d = depth_ref[...].astype(F32)
    last = d.shape[0] - 1
    if edges:
        rows_d = [jnp.where(side_ref[k] == 0, d[0:1], d[last:]) for k in range(2)]
    else:
        rows_d = [d[r : r + 1] for r in range(1, last)]
    plans = [row_plan(row, lev) for row in rows_d]
    if edges:
        near, far = offsets(plans[:1], 1, lev), offsets(plans[1:], 0, lev)
        place = [{l: at for (l, _), at in p.items()} for p in (near, far)]
    else:
        both = offsets(plans, 1, lev)
        place = [{l: both[l, step] for l in range(1, lev)} for step in range(steps)]

    def project(x, step, m):
        rows = slice(m * lev, (m + 1) * lev)
        kv = jnp.dot(x, qkv_ref[:, width:], preferred_element_type=F32).astype(BF16)
        k_ref[step, rows] = kv[:, :width].reshape(lev, count, width)
        v_ref[step, rows] = kv[:, width:].reshape(lev, count, width)

    for o in range(others):
        for step in range(steps):
            source = packed[step if edges else 0][o]
            window = lambda base, size: source[pl.ds(base, size), :]
            limit = source.shape[0] - count - 16
            wet, rank, _ = plans[step]
            if 0 not in place[step]:
                at = surf[o].shape[1] - count if edges else step * count
                token_ref[step, 0] = surf[o][0, at : at + count]
            for l, at in place[step].items():
                token_ref[step, l] = unpack(window, wet[l : l + 1], rank[l : l + 1], at, limit)

        @pl.when(flag_ref[0] != 0)
        def _():
            first = lev - whole[o].shape[0]
            for step in range(steps):
                copy = pltpu.make_async_copy(
                    whole[o].at[:, pl.ds(step * count, count)],
                    token_ref.at[step, pl.ds(first, lev - first)],
                    sem,
                )
                copy.start()
                copy.wait()

        for step in range(steps):
            project(token_ref[step].reshape(-1, width), step, o + 1)

    nq, nk = lev * GROUP, members * lev * GROUP
    groups = count // GROUP
    lanes_n = lev * GROUP
    cell = lax.broadcasted_iota(jnp.int32, (groups, count), 1)
    mine = (cell // GROUP == lax.broadcasted_iota(jnp.int32, (groups, count), 0)).astype(F32)
    spread = lax.broadcasted_iota(jnp.int32, (count, lanes_n), 0) % GROUP
    spread = (spread == lax.broadcasted_iota(jnp.int32, (count, lanes_n), 1) % GROUP).astype(F32)
    key_level = lax.broadcasted_iota(jnp.int32, (groups, lanes_n), 1) // GROUP
    qc = lax.broadcasted_iota(jnp.int32, (nq, nk), 0) % GROUP
    kc = lax.broadcasted_iota(jnp.int32, (nq, nk), 1) % GROUP
    same = jnp.where(qc == kc, 0.0, NEG)
    lane = lax.broadcasted_iota(jnp.int32, (1, width), 1)
    scale = 1.0 / math.sqrt(head)
    masks = [jnp.where(lane // head == h, scale, 0.0).astype(BF16) for h in range(HEADS)]
    stores = []
    for step in range(steps):
        arrive(0, step)
        x = x_ref[step].reshape(-1, width)
        q = jnp.dot(x, qkv_ref[:, 0:width], preferred_element_type=F32).astype(BF16)
        q_ref[step] = q.reshape(lev, count, width)
        project(x, step, 0)
        key_depth = jnp.dot(
            (mine * rows_d[step]).astype(BF16), spread.astype(BF16), preferred_element_type=F32
        )
        key_bias = jnp.where(key_depth > key_level.astype(F32), 0.0, NEG)
        for g in range(groups):
            cells = slice(g * GROUP, (g + 1) * GROUP)
            bias = same + jnp.concatenate([key_bias[g : g + 1]] * members, axis=1)
            bias = jnp.concatenate([bias] * HEADS, axis=0)
            q = q_ref[step, :, cells].reshape(nq, width)
            q = jnp.concatenate([q * mask for mask in masks], axis=0)
            k = k_ref[step, :, cells].reshape(nk, width)
            v = v_ref[step, :, cells].reshape(nk, width)
            s = lax.dot_general(q, k, (((1,), (1,)), ((), ())), preferred_element_type=F32) + bias
            p = jnp.exp(s - jnp.max(s, axis=-1, keepdims=True))
            norm = 1.0 / jnp.sum(p, axis=-1, keepdims=True)
            p = p.astype(BF16)
            for h in range(HEADS // 2):
                lanes = slice(h * pair, (h + 1) * pair)
                rows = slice(h * 2 * nq, (h + 1) * 2 * nq)
                o = jnp.dot(p[rows], v[:, lanes], preferred_element_type=F32) * norm[rows]
                o = jnp.where(lane[:, :pair] < head, o[:nq], o[nq:])
                att_ref[step, :, cells, lanes] = o.astype(BF16).reshape(lev, GROUP, pair)
        proj = jnp.dot(
            att_ref[step].reshape(-1, width), wo_ref[...], preferred_element_type=F32
        )
        arrive(1, step)
        deep = column(rows_d[step])
        row = side_ref[step] if edges else step + 1
        for l in range(lev):
            rows = slice(l * count, (l + 1) * count)
            wet = widen((deep > l).astype(F32), width)
            new_ref[step, l] = (mixed_ref[step, l].astype(F32) + wet * proj[rows]).astype(BF16)
        at = pl.multiple_of(row * count, count)
        store = pltpu.make_async_copy(
            new_ref.at[step], out_hbm.at[0, :, pl.ds(at, count)], out_sem.at[step]
        )
        store.start()
        stores.append(store)
    for store in stores:
        store.wait()


def attend(
    flag, side, normed, mixed, surf, packed, whole, depth, qkv_weight, out_weight, out, shape
):
    edges = out is not None
    others, nparts = len(whole), len(mixed)
    lev = sum(p.shape[0] for p in mixed)
    width = shape[-1]
    cols = depth.shape[1]
    members = others + 1
    hbm = pl.BlockSpec(memory_space=pltpu.HBM)
    vmem = pl.BlockSpec(memory_space=pltpu.VMEM)
    smem = pl.BlockSpec(memory_space=pltpu.SMEM)
    stay = lambda x: pltpu.with_memory_space_constraint(x, pltpu.HBM)
    in_specs = [smem] * 2 + [hbm] * (2 * nparts) + [vmem] * (len(surf) + len(packed))
    in_specs += [hbm] * others + [vmem] * 3
    args = [flag, side] + [stay(x) for x in normed + mixed] + surf + packed
    args += [stay(x) for x in whole] + [depth, qkv_weight, out_weight]
    alias = {}
    if edges:
        in_specs.append(hbm)
        alias = {len(args): 0}
        args.append(stay(out))
    tokens = lev * cols * 2
    rows = pltpu.VMEM((2, lev, cols, width), BF16)
    keys = pltpu.VMEM((2, members * lev, cols, width), BF16)
    return pl.pallas_call(
        functools.partial(attend_kernel, others, nparts, edges),
        in_specs=in_specs,
        out_specs=hbm,
        scratch_shapes=[
            rows,
            rows,
            rows,
            keys,
            keys,
            rows,
            rows,
            rows,
            pltpu.SemaphoreType.DMA((2, 2, nparts)),
            pltpu.SemaphoreType.DMA((2,)),
            pltpu.SemaphoreType.DMA,
        ],
        out_shape=pltpu.HBM(shape, BF16),
        input_output_aliases=alias,
        compiler_params=params(24 if members <= 2 else 56),
        cost_estimate=cost(tokens * width * width * 8 * (members + 2), tokens * width * 2 * 5),
        name="attend",
    )(*args)


def body(
    atm_latent,
    ocean_state,
    depth,
    src_blocks,
    live,
    remap_weight,
    conv_weight,
    qkv_weight,
    out_weight,
):
    _, lev, cells, width = ocean_state.shape
    cols = remap_weight.shape[2]
    rows = cells // cols
    inner = cells - 2 * cols
    own = atm_latent.shape[1]
    atm_blk = own // cols
    tiles = lax.axis_size("tile")
    members = lax.axis_size("mem")
    tile = lax.axis_index("tile")

    def swap(x, first):
        pairs = [(i, i + 1) for i in range(first, tiles - 1, 2)]
        return lax.ppermute(x, "tile", pairs + [(b, a) for a, b in pairs])

    def exchange(x):
        return [
            lax.ppermute(x, "mem", [(i, (i + k) % members) for i in range(members)])
            for k in range(1, members)
        ]

    odd = tile % 2
    side = jnp.stack([(1 - odd) * (rows - 1), odd * (rows - 1)]).astype(jnp.int32)
    depth = depth.reshape(rows, cols)
    deep_cap = capacity((lev - 1) * inner, 0.5625)
    near_cap = capacity((lev - 1) * cols, 0.605)
    far_cap = capacity(lev * cols, 0.65625)

    hbm = pl.BlockSpec(memory_space=pltpu.HBM)
    anywhere = pl.BlockSpec(memory_space=pl.ANY)
    vmem = pl.BlockSpec(memory_space=pltpu.VMEM)
    smem = pl.BlockSpec(memory_space=pltpu.SMEM)
    tok = lambda *s: pltpu.HBM((*s, width), BF16)
    stay = lambda x: pltpu.with_memory_space_constraint(x, pltpu.HBM)
    conv_flops = lambda n, c: 2 * 9 * n * c * width * width
    dma = pltpu.SemaphoreType.DMA
    slack = cols + 16
    message = lev * cols + own
    on_msg, off_msg, flag = pl.pallas_call(
        functools.partial(prep_kernel, (deep_cap, near_cap, far_cap)),
        in_specs=[smem, hbm, hbm, hbm],
        out_specs=[hbm, hbm, smem],
        out_shape=[tok(message), tok(message), jax.ShapeDtypeStruct((1,), jnp.int32)],
        scratch_shapes=[
            pltpu.VMEM((rows, cols), jnp.int32),
            pltpu.VMEM((own, width), BF16),
            pltpu.VMEM((2, lev, cols, width), BF16),
            dma((2, lev)),
            dma((2, lev)),
            dma((2,)),
            dma((2,)),
        ],
        compiler_params=params(16),
        cost_estimate=cost(lev * cols * width * 4, lev * cols * width * 10),
        name="prep",
    )(side, stay(ocean_state), stay(atm_latent), stay(depth))
    off_halo = swap(off_msg, 1)
    on_halo = swap(on_msg, 0)

    deep_mixed, deep_normed, deep_packed = pl.pallas_call(
        functools.partial(inner_kernel, deep_cap),
        in_specs=[vmem, vmem, hbm],
        out_specs=[hbm] * 3,
        out_shape=[tok(lev - 1, inner), tok(lev - 1, inner), tok(deep_cap)],
        scratch_shapes=[
            pltpu.VMEM(conv_weight.shape, BF16),
            pltpu.VMEM((lev - 1, inner, width), BF16),
            pltpu.VMEM((lev - 1, inner, width), BF16),
            pltpu.VMEM((deep_cap + slack, width), BF16),
            dma,
            dma((lev - 1, 2)),
            dma,
        ],
        compiler_params=params(12),
        cost_estimate=cost(conv_flops(lev, inner), lev * inner * width * 8),
        name="inner",
    )(ocean_state, depth, stay(conv_weight))
    deep_others = exchange(deep_packed)

    whole_spec = lambda *sh: pl.BlockSpec(sh, lambda *_: (0,) * len(sh))
    row_f32 = pltpu.HBM((cols, width), F32)

    def row_conv(which, first, cap, halo, extra):
        n = lev - first
        base = pltpu.HBM((inner + cols, width), F32)
        return pl.pallas_call(
            functools.partial(row_kernel, cap, first, which),
            in_specs=[smem, vmem, vmem, hbm, anywhere] + [hbm] * len(extra),
            out_specs=[hbm] * 3 + [whole_spec(inner + cols, width)] * first,
            out_shape=[tok(lev, 2 * cols), tok(lev, 2 * cols), tok(cap)] + [base] * first,
            scratch_shapes=[
                pltpu.VMEM((cols, width), F32),
                pltpu.VMEM(conv_weight.shape, BF16),
                pltpu.VMEM((3, lev * cols, width), BF16),
                pltpu.VMEM((n, cols, width), BF16),
                pltpu.VMEM((n, cols, width), BF16),
                pltpu.VMEM((cap + slack, width), BF16),
                dma,
                dma,
                dma((2,)),
                dma,
            ],
            input_output_aliases={6: 0, 7: 1} if extra else {},
            compiler_params=params(12),
            cost_estimate=cost(conv_flops(lev, cols), lev * cols * width * 16),
            name="row",
        )(side, ocean_state, depth, stay(conv_weight), halo, *[stay(x) for x in extra])

    edge_mixed, edge_normed, near_packed, base = row_conv(0, 1, near_cap, on_halo, [])

    ids = jnp.clip(src_blocks - (tile - R) * atm_blk, 0, 3 * atm_blk - 1)
    surf_mixed, surf_normed, far_forcing, edge_mixed, edge_normed = pl.pallas_call(
        surface_kernel,
        in_specs=[smem] * 3 + [vmem] + [anywhere] * 2 + [vmem] * 4 + [hbm] * 3,
        out_specs=[whole_spec(1, inner + cols, width)] * 2 + [whole_spec(cols, width)] + [hbm] * 2,
        out_shape=[tok(1, inner + cols), tok(1, inner + cols), row_f32]
        + [tok(lev, 2 * cols)] * 2,
        scratch_shapes=[
            pltpu.VMEM((inner + cols, width), F32),
            pltpu.VMEM((3 * own, width), BF16),
            pltpu.VMEM((rows, cols, width), F32),
            dma((5,)),
        ],
        input_output_aliases={11: 3, 12: 4},
        compiler_params=params(12),
        cost_estimate=cost(conv_flops(1, inner), cells * width * 16),
        name="surface",
    )(
        ids,
        live,
        side,
        depth,
        on_halo,
        off_halo,
        atm_latent,
        remap_weight,
        qkv_weight,
        out_weight,
        stay(base),
        stay(edge_mixed),
        stay(edge_normed),
    )
    surf_others = exchange(surf_normed)
    near_others = exchange(near_packed)

    edge_mixed, edge_normed, far_packed = row_conv(
        1, 0, far_cap, off_halo, [far_forcing, edge_mixed, edge_normed]
    )
    far_others = exchange(far_packed)

    def unread(shape):
        return pl.pallas_call(
            lambda out_ref: None,
            out_specs=hbm,
            out_shape=pltpu.HBM(shape, BF16),
            name="unread",
        )()

    def send_all(*arrays):
        sizes = [x.shape[0] * x.shape[1] for x in arrays]
        joined = jnp.concatenate([x.reshape(-1, width) for x in arrays], axis=0)
        got = [[] for _ in arrays]
        for part in exchange(joined):
            at = 0
            for k, (x, size) in enumerate(zip(arrays, sizes)):
                got[k].append(part[at : at + size].reshape(x.shape))
                at += size
        return tuple(got)

    deep_whole, edge_whole = lax.cond(
        flag[0] > 0,
        send_all,
        lambda *a: tuple([unread(x.shape) for _ in range(members - 1)] for x in a),
        deep_normed,
        edge_normed,
    )
    shape = ocean_state.shape
    weights = (depth, qkv_weight, out_weight)
    out = attend(
        flag,
        side,
        [surf_normed, deep_normed],
        [surf_mixed, deep_mixed],
        surf_others,
        deep_others,
        deep_whole,
        *weights,
        None,
        shape,
    )
    return attend(
        flag,
        side,
        [edge_normed],
        [edge_mixed],
        surf_others,
        near_others + far_others,
        edge_whole,
        *weights,
        out,
        shape,
    )


def solution(mesh):
    return jax.shard_map(
        body,
        mesh=mesh,
        in_specs=(
            P("mem", "tile", None),
            P("mem", None, "tile", None),
            P("tile"),
            P("tile", None),
            P("tile"),
            P("tile", None, None, None),
            P(),
            P(),
            P(),
        ),
        out_specs=P("mem", None, "tile", None),
        check_vma=False,
    )
```

```python
import functools
import math

import jax
import jax.numpy as jnp
from jax import lax
from jax.experimental import pallas as pl
from jax.experimental.pallas import tpu as pltpu
from jax.sharding import PartitionSpec as P

HEADS = 4
R = 1
GROUP = 16
EPS = 1e-06
NEG = -1e30
F32 = jnp.float32
BF16 = jnp.bfloat16
MIB = 1024 * 1024


def params(mib, steps=0):
    return pltpu.CompilerParams(
        dimension_semantics=("arbitrary",) * steps if steps else None, vmem_limit_bytes=mib * MIB
    )


def cost(flops, nbytes):
    return pl.CostEstimate(flops=int(flops), bytes_accessed=int(nbytes), transcendentals=0)


def capacity(tokens, share):
    return -(-int(tokens * share) // 16) * 16


def row_plan(depth_row, lev):
    cols = depth_row.shape[1]
    level = lax.broadcasted_iota(jnp.int32, (lev, cols), 0).astype(F32)
    wet = (depth_row > level).astype(F32)
    upper = (
        lax.broadcasted_iota(jnp.int32, (cols, cols), 0)
        < lax.broadcasted_iota(jnp.int32, (cols, cols), 1)
    )
    upper = upper.astype(F32).astype(BF16)
    rank = jnp.dot(wet.astype(BF16), upper, preferred_element_type=F32)
    counts = [jnp.sum(wet[l : l + 1]).astype(jnp.int32) for l in range(lev)]
    return wet, rank, counts


def offsets(plans, first, lev):
    at, place = jnp.int32(0), {}
    for l in range(first, lev):
        for r, plan in enumerate(plans):
            place[l, r] = at
            at = at + plan[2][l]
    return place


def segment(wet, rank, offset, limit):
    cols = wet.shape[1]
    base = jnp.minimum((offset // 16) * 16, limit)
    target = jnp.where(wet > 0, rank + (offset - base).astype(F32), -1.0)
    slot = lax.broadcasted_iota(jnp.int32, (cols + 16, cols), 0).astype(F32)
    return pl.multiple_of(base, 16), (slot == target).astype(F32).astype(BF16)


def pack(buf_ref, wet, rank, offset, cap, tokens):
    base, hot = segment(wet, rank, offset, cap)
    rows = jnp.dot(hot, tokens, preferred_element_type=F32).astype(BF16)
    head = pl.ds(base, 16)
    buf_ref[head, :] = buf_ref[head, :] + rows[:16]
    buf_ref[pl.ds(pl.multiple_of(base + 16, 16), rows.shape[0] - 16), :] = rows[16:]


def unpack(rows_of, wet, rank, offset, limit):
    base, hot = segment(wet, rank, offset, limit)
    return lax.dot_general(
        hot, rows_of(base, hot.shape[0]), (((0,), (0,)), ((), ())), preferred_element_type=F32
    ).astype(BF16)


def column(depth_row):
    cols = depth_row.shape[1]
    return jnp.broadcast_to(depth_row, (cols, cols)).T


def widen(x, width):
    return jnp.concatenate([x] * (width // x.shape[1]), axis=1)


def stencil(taps, weight_ref, cols):
    count, width = taps[0].shape
    x = jnp.concatenate(taps, axis=1)
    sums = [
        jnp.dot(x, weight_ref[:, dc].reshape(3 * width, -1), preferred_element_type=F32)
        for dc in range(3)
    ]
    col = lax.broadcasted_iota(jnp.int32, (count, 1), 0) % cols
    left = jnp.where(col == 0, 0.0, pltpu.roll(sums[0], 1, axis=0))
    right = jnp.where(col == cols - 1, 0.0, pltpu.roll(sums[2], count - 1, axis=0))
    return sums[1] + left + right


def normalise(mixed):
    mf = mixed.astype(F32)
    mean = jnp.mean(mf * mf, axis=-1, keepdims=True)
    return (mf * lax.rsqrt(mean + EPS)).astype(BF16)


def prep_kernel(
    caps,
    side_ref,
    state_hbm,
    atm_hbm,
    depth_hbm,
    on_hbm,
    off_hbm,
    flag_ref,
    depth_ref,
    atm,
    rows_in,
    in_sem,
    out_sem,
    atm_sem,
    own_sem,
):
    _, lev, cells, width = state_hbm.shape
    rows, cols = depth_ref.shape
    own = atm_hbm.shape[1]
    sides = (on_hbm, off_hbm)
    load_depth = pltpu.make_async_copy(depth_hbm, depth_ref, own_sem.at[0])
    load_depth.start()
    loads, stores = [], []
    for k in (1, 0):
        at = pl.multiple_of(side_ref[k] * cols, cols)
        for l in range(lev):
            load = pltpu.make_async_copy(
                state_hbm.at[0, l, pl.ds(at, cols)], rows_in.at[k, l], in_sem.at[k, l]
            )
            load.start()
            loads.append((k, l, load))
    load_atm = pltpu.make_async_copy(atm_hbm.at[0], atm, own_sem.at[1])
    load_atm.start()
    load_depth.wait()
    d = depth_ref[...].astype(F32)
    pick = lambda k: jnp.where(side_ref[k] == 0, d[0:1], d[rows - 1 :])
    deep = [column(pick(k)) for k in range(2)]
    for k, l, load in loads:
        wet = widen((deep[k] > l).astype(F32).astype(BF16), width)
        load.wait()
        rows_in[k, l] = rows_in[k, l] * wet
        store = pltpu.make_async_copy(
            rows_in.at[k, l], sides[k].at[pl.ds(l * cols, cols)], out_sem.at[k, l]
        )
        store.start()
        stores.append(store)
    load_atm.wait()
    for k in (1, 0):
        store = pltpu.make_async_copy(
            atm, sides[k].at[pl.ds(lev * cols, own)], atm_sem.at[k]
        )
        store.start()
        stores.append(store)
    counts = [
        jnp.sum(jnp.maximum(d[1 : rows - 1] - 1.0, 0.0)),
        jnp.sum(jnp.maximum(pick(0) - 1.0, 0.0)),
        jnp.sum(pick(1)),
    ]
    over = jnp.int32(0)
    for count, cap in zip(counts, caps):
        over = over | (count > cap).astype(jnp.int32)
    flag_ref[0] = over
    for store in stores:
        store.wait()


def inner_kernel(
    cap,
    state,
    depth_ref,
    weight_hbm,
    mixed_hbm,
    normed_hbm,
    packed_hbm,
    weight,
    mixed,
    normed,
    packed,
    weight_sem,
    out_sem,
    packed_sem,
):
    _, lev, cells, width = state.shape
    rows, cols = depth_ref.shape
    load = pltpu.make_async_copy(weight_hbm, weight, weight_sem)
    load.start()
    packed[...] = jnp.zeros_like(packed)
    d = depth_ref[...].astype(F32)
    plans = [row_plan(d[r : r + 1], lev) for r in range(1, rows - 1)]
    place = offsets(plans, 1, lev)
    deep = jnp.concatenate([column(d[r : r + 1]) for r in range(rows)], axis=0)
    count = cells - 2 * cols
    stores = []
    for l in range(1, lev):
        wet = (deep > l).astype(F32)
        x = state[0, l] * widen(wet.astype(BF16), width)
        taps = [x[dr * cols : dr * cols + count] for dr in range(3)]
        if l == 1:
            load.wait()
        total = stencil(taps, weight, cols)
        new = taps[1].astype(F32) + widen(wet[cols : cols + count], width) * total
        new = new.astype(BF16)
        mixed[l - 1] = new
        tokens = normalise(new)
        normed[l - 1] = tokens
        for k, (buf, out) in enumerate(((mixed, mixed_hbm), (normed, normed_hbm))):
            store = pltpu.make_async_copy(buf.at[l - 1], out.at[l - 1], out_sem.at[l - 1, k])
            store.start()
            stores.append(store)
        for r, plan in enumerate(plans):
            pack(
                packed,
                plan[0][l : l + 1],
                plan[1][l : l + 1],
                place[l, r],
                cap,
                tokens[r * cols : (r + 1) * cols],
            )
        if l == lev - 1:
            store = pltpu.make_async_copy(packed.at[pl.ds(0, cap)], packed_hbm, packed_sem)
            store.start()
            stores.append(store)
    for store in stores:
        store.wait()


def surface_kernel(
    ids_ref,
    live_ref,
    side_ref,
    depth_ref,
    on_hbm,
    off_hbm,
    atm_ref,
    remap,
    qkv_ref,
    wo_ref,
    base_hbm,
    edge_mixed_in,
    edge_normed_in,
    mixed_ref,
    normed_ref,
    far_ref,
    edge_mixed_hbm,
    edge_normed_hbm,
    base,
    window,
    forcing_ref,
    sem,
):
    rows, cols = depth_ref.shape
    _, own, width = atm_ref.shape
    blocks, pairs = remap.shape[0], remap.shape[1]
    on_at = jnp.where(side_ref[0] == 0, 0, 2 * own)
    copies = [
        pltpu.make_async_copy(
            on_hbm.at[pl.ds(on_hbm.shape[0] - own, own)],
            window.at[pl.ds(pl.multiple_of(on_at, own), own)],
            sem.at[0],
        ),
        pltpu.make_async_copy(
            off_hbm.at[pl.ds(off_hbm.shape[0] - own, own)],
            window.at[pl.ds(pl.multiple_of(2 * own - on_at, own), own)],
            sem.at[1],
        ),
        pltpu.make_async_copy(base_hbm, base, sem.at[4]),
    ]
    for copy in copies:
        copy.start()
    window[own : 2 * own] = atm_ref[0]
    d = depth_ref[...].astype(F32)
    near, far = side_ref[0], side_ref[1]
    rows_d = [d[r : r + 1] for r in range(1, rows - 1)]
    rows_d.append(jnp.where(near == 0, d[0:1], d[rows - 1 :]))
    wets = [widen((column(row) > 0).astype(F32), width) for row in rows_d]
    for copy in copies:
        copy.wait()
    for b in range(blocks):
        weights, picked = [], []
        for p in range(pairs):
            on = jnp.where(p < live_ref[b], 1.0, 0.0)
            weights.append(remap[b, p] * jnp.full((1, cols), on, F32).astype(BF16))
            start = pl.multiple_of(ids_ref[b, p] * cols, cols)
            picked.append(window[pl.ds(start, cols), :])
        acc = jnp.dot(
            jnp.concatenate(weights, axis=1),
            jnp.concatenate(picked, axis=0),
            preferred_element_type=F32,
        )
        forcing_ref[b] = acc
    for k, wet in enumerate(wets):
        at = slice(k * cols, (k + 1) * cols)
        forcing = forcing_ref[near] if k == rows - 2 else forcing_ref[k + 1]
        new = (base[at] + wet * forcing).astype(BF16)
        mixed_ref[0, at] = new
        normed_ref[0, at] = normalise(new)
    far_ref[...] = forcing_ref[far]
    at = pl.ds((rows - 2) * cols, cols)
    stores = [
        pltpu.make_async_copy(mixed_ref.at[0, at], edge_mixed_hbm.at[0, pl.ds(0, cols)], sem.at[2]),
        pltpu.make_async_copy(normed_ref.at[0, at], edge_normed_hbm.at[0, pl.ds(0, cols)], sem.at[3]),
    ]
    for store in stores:
        store.start()
    for store in stores:
        store.wait()


def row_kernel(cap, first, which, side_ref, state, depth_ref, weight_in, halo_hbm, *refs):
    refs = list(refs)
    forcing_hbm = None
    if not first:
        forcing_hbm = refs[0]
        refs = refs[3:]
    mixed_hbm, normed_hbm, packed_hbm = refs[:3]
    refs = refs[3:]
    base_ref = refs.pop(0) if first else None
    forcing_ref, weight, tap, mixed, normed, packed, weight_sem, halo_sem, out_sem, packed_sem = refs
    if first:
        load = pltpu.make_async_copy(weight_in, weight, weight_sem)
        load.start()
    else:
        weight = weight_in
    _, lev, cells, width = state.shape
    rows, cols = depth_ref.shape
    row = side_ref[which]
    top = row == 0
    beside = jnp.where(top, 1, rows - 2)
    outer = jnp.where(top, 0, 2)
    halo = pltpu.make_async_copy(
        halo_hbm.at[pl.ds(0, lev * cols)], tap.at[outer], halo_sem
    )
    halo.start()
    if not first:
        forcing = pltpu.make_async_copy(forcing_hbm, forcing_ref, packed_sem)
        forcing.start()
    packed[...] = jnp.zeros_like(packed)
    d = depth_ref[...].astype(F32)
    own_depth = jnp.where(top, d[0:1], d[rows - 1 :])
    plan = row_plan(own_depth, lev)
    place = offsets([plan], first, lev)
    deep = column(own_depth)
    deep_beside = column(jnp.where(top, d[1:2], d[rows - 2 : rows - 1]))
    at = pl.multiple_of(row * cols, cols)
    at_beside = pl.multiple_of(beside * cols, cols)
    wets = []
    for l in range(lev):
        rows_l = slice(l * cols, (l + 1) * cols)
        wet = (deep > l).astype(F32)
        wets.append(wet)
        wet_beside = (deep_beside > l).astype(F32)
        tap[1, rows_l] = state[0, l, pl.ds(at, cols)] * widen(wet.astype(BF16), width)
        tap[2 - outer, rows_l] = state[0, l, pl.ds(at_beside, cols)] * widen(
            wet_beside.astype(BF16), width
        )
    stores = []
    half = lev // 2
    if first:
        load.wait()
    halo.wait()
    if not first:
        forcing.wait()
    for start in range(0, lev, half):
        rows_b = slice(start * cols, (start + half) * cols)
        taps = [tap[dr, rows_b] for dr in range(3)]
        total = stencil(taps, weight, cols)
        for k in range(half):
            l = start + k
            rows_k = slice(k * cols, (k + 1) * cols)
            part = total[rows_k]
            if l == 0 and not first:
                part = part + forcing_ref[...]
            new = taps[1][rows_k].astype(F32) + widen(wets[l], width) * part
            if l < first:
                base_ref[cells - 2 * cols :] = new
                continue
            new = new.astype(BF16)
            mixed[l - first] = new
            tokens = normalise(new)
            normed[l - first] = tokens
            pack(packed, plan[0][l : l + 1], plan[1][l : l + 1], place[l, 0], cap, tokens)
    if first:
        wet = (jnp.concatenate([column(d[r : r + 1]) for r in range(rows)], axis=0) > 0).astype(F32)
        x = state[0, 0] * widen(wet.astype(BF16), width)
        taps = [x[dr * cols : dr * cols + cells - 2 * cols] for dr in range(3)]
        inside = widen(wet[cols : cells - cols], width)
        base_ref[0 : cells - 2 * cols] = taps[1].astype(F32) + inside * stencil(taps, weight, cols)
    block = (pl.ds(first, lev - first), pl.ds(which * cols, cols))
    for k, (buf, out) in enumerate(((mixed, mixed_hbm), (normed, normed_hbm))):
        store = pltpu.make_async_copy(buf, out.at[block], out_sem.at[k])
        store.start()
        stores.append(store)
    store = pltpu.make_async_copy(packed.at[pl.ds(0, cap)], packed_hbm, packed_sem)
    store.start()
    stores.append(store)
    for store in stores:
        store.wait()


def attend_kernel(others, nparts, edges, flag_ref, side_ref, *refs):
    refs = list(refs)
    take = lambda k: [refs.pop(0) for _ in range(k)]
    own_normed = take(nparts)
    own_mixed = take(nparts)
    surf = take(others)
    packed = [take(others) for _ in range(1 + edges)]
    whole = take(others)
    depth_ref, qkv_ref, wo_ref = take(3)
    if edges:
        take(1)
    out_hbm, x_ref, mixed_ref, q_ref, k_ref, v_ref, att_ref, token_ref, new_ref = refs[:9]
    in_sem, out_sem, sem = refs[9:]
    steps, lev, count, width = q_ref.shape
    members = others + 1
    head = width // HEADS
    pair = 2 * head

    loads = []
    for kind, (parts, buf) in enumerate(((own_normed, x_ref), (own_mixed, mixed_ref))):
        for step in range(steps):
            at = 0
            for k, part in enumerate(parts):
                n = part.shape[0]
                load = pltpu.make_async_copy(
                    part.at[:, pl.ds(step * count, count)],
                    buf.at[step, pl.ds(at, n)],
                    in_sem.at[kind, step, k],
                )
                load.start()
                loads.append((kind, step, load))
                at += n

    def arrive(kind, step):
        for k, s, load in loads:
            if (k, s) == (kind, step):
                load.wait()

    d = depth_ref[...].astype(F32)
    last = d.shape[0] - 1
    if edges:
        rows_d = [jnp.where(side_ref[k] == 0, d[0:1], d[last:]) for k in range(2)]
    else:
        rows_d = [d[r : r + 1] for r in range(1, last)]
    plans = [row_plan(row, lev) for row in rows_d]
    if edges:
        near, far = offsets(plans[:1], 1, lev), offsets(plans[1:], 0, lev)
        place = [{l: at for (l, _), at in p.items()} for p in (near, far)]
    else:
        both = offsets(plans, 1, lev)
        place = [{l: both[l, step] for l in range(1, lev)} for step in range(steps)]

    def project(x, step, m):
        rows = slice(m * lev, (m + 1) * lev)
        kv = jnp.dot(x, qkv_ref[:, width:], preferred_element_type=F32).astype(BF16)
        k_ref[step, rows] = kv[:, :width].reshape(lev, count, width)
        v_ref[step, rows] = kv[:, width:].reshape(lev, count, width)

    for o in range(others):
        for step in range(steps):
            source = packed[step if edges else 0][o]
            window = lambda base, size: source[pl.ds(base, size), :]
            limit = source.shape[0] - count - 16
            wet, rank, _ = plans[step]
            if 0 not in place[step]:
                at = surf[o].shape[1] - count if edges else step * count
                token_ref[step, 0] = surf[o][0, at : at + count]
            for l, at in place[step].items():
                token_ref[step, l] = unpack(window, wet[l : l + 1], rank[l : l + 1], at, limit)

        @pl.when(flag_ref[0] != 0)
        def _():
            first = lev - whole[o].shape[0]
            for step in range(steps):
                copy = pltpu.make_async_copy(
                    whole[o].at[:, pl.ds(step * count, count)],
                    token_ref.at[step, pl.ds(first, lev - first)],
                    sem,
                )
                copy.start()
                copy.wait()

        for step in range(steps):
            project(token_ref[step].reshape(-1, width), step, o + 1)

    nq, nk = lev * GROUP, members * lev * GROUP
    groups = count // GROUP
    lanes_n = lev * GROUP
    cell = lax.broadcasted_iota(jnp.int32, (groups, count), 1)
    mine = (cell // GROUP == lax.broadcasted_iota(jnp.int32, (groups, count), 0)).astype(F32)
    spread = lax.broadcasted_iota(jnp.int32, (count, lanes_n), 0) % GROUP
    spread = (spread == lax.broadcasted_iota(jnp.int32, (count, lanes_n), 1) % GROUP).astype(F32)
    key_level = lax.broadcasted_iota(jnp.int32, (groups, lanes_n), 1) // GROUP
    qc = lax.broadcasted_iota(jnp.int32, (nq, nk), 0) % GROUP
    kc = lax.broadcasted_iota(jnp.int32, (nq, nk), 1) % GROUP
    same = jnp.where(qc == kc, 0.0, NEG)
    lane = lax.broadcasted_iota(jnp.int32, (1, width), 1)
    scale = 1.0 / math.sqrt(head)
    masks = [jnp.where(lane // head == h, scale, 0.0).astype(BF16) for h in range(HEADS)]
    stores = []
    for step in range(steps):
        arrive(0, step)
        x = x_ref[step].reshape(-1, width)
        q = jnp.dot(x, qkv_ref[:, 0:width], preferred_element_type=F32).astype(BF16)
        q_ref[step] = q.reshape(lev, count, width)
        project(x, step, 0)
        key_depth = jnp.dot(
            (mine * rows_d[step]).astype(BF16), spread.astype(BF16), preferred_element_type=F32
        )
        key_bias = jnp.where(key_depth > key_level.astype(F32), 0.0, NEG)
        for g in range(groups):
            cells = slice(g * GROUP, (g + 1) * GROUP)
            bias = same + jnp.concatenate([key_bias[g : g + 1]] * members, axis=1)
            bias = jnp.concatenate([bias] * HEADS, axis=0)
            q = q_ref[step, :, cells].reshape(nq, width)
            q = jnp.concatenate([q * mask for mask in masks], axis=0)
            k = k_ref[step, :, cells].reshape(nk, width)
            v = v_ref[step, :, cells].reshape(nk, width)
            s = lax.dot_general(q, k, (((1,), (1,)), ((), ())), preferred_element_type=F32) + bias
            p = jnp.exp(s - jnp.max(s, axis=-1, keepdims=True))
            norm = 1.0 / jnp.sum(p, axis=-1, keepdims=True)
            p = p.astype(BF16)
            for h in range(HEADS // 2):
                lanes = slice(h * pair, (h + 1) * pair)
                rows = slice(h * 2 * nq, (h + 1) * 2 * nq)
                o = jnp.dot(p[rows], v[:, lanes], preferred_element_type=F32) * norm[rows]
                o = jnp.where(lane[:, :pair] < head, o[:nq], o[nq:])
                att_ref[step, :, cells, lanes] = o.astype(BF16).reshape(lev, GROUP, pair)
        proj = jnp.dot(
            att_ref[step].reshape(-1, width), wo_ref[...], preferred_element_type=F32
        )
        arrive(1, step)
        deep = column(rows_d[step])
        row = side_ref[step] if edges else step + 1
        for l in range(lev):
            rows = slice(l * count, (l + 1) * count)
            wet = widen((deep > l).astype(F32), width)
            new_ref[step, l] = (mixed_ref[step, l].astype(F32) + wet * proj[rows]).astype(BF16)
        at = pl.multiple_of(row * count, count)
        store = pltpu.make_async_copy(
            new_ref.at[step], out_hbm.at[0, :, pl.ds(at, count)], out_sem.at[step]
        )
        store.start()
        stores.append(store)
    for store in stores:
        store.wait()


def attend(
    flag, side, normed, mixed, surf, packed, whole, depth, qkv_weight, out_weight, out, shape
):
    edges = out is not None
    others, nparts = len(whole), len(mixed)
    lev = sum(p.shape[0] for p in mixed)
    width = shape[-1]
    cols = depth.shape[1]
    members = others + 1
    hbm = pl.BlockSpec(memory_space=pltpu.HBM)
    vmem = pl.BlockSpec(memory_space=pltpu.VMEM)
    smem = pl.BlockSpec(memory_space=pltpu.SMEM)
    stay = lambda x: pltpu.with_memory_space_constraint(x, pltpu.HBM)
    in_specs = [smem] * 2 + [hbm] * (2 * nparts) + [vmem] * (len(surf) + len(packed))
    in_specs += [hbm] * others + [vmem] * 3
    args = [flag, side] + [stay(x) for x in normed + mixed] + surf + packed
    args += [stay(x) for x in whole] + [depth, qkv_weight, out_weight]
    alias = {}
    if edges:
        in_specs.append(hbm)
        alias = {len(args): 0}
        args.append(stay(out))
    tokens = lev * cols * 2
    rows = pltpu.VMEM((2, lev, cols, width), BF16)
    keys = pltpu.VMEM((2, members * lev, cols, width), BF16)
    return pl.pallas_call(
        functools.partial(attend_kernel, others, nparts, edges),
        in_specs=in_specs,
        out_specs=hbm,
        scratch_shapes=[
            rows,
            rows,
            rows,
            keys,
            keys,
            rows,
            rows,
            rows,
            pltpu.SemaphoreType.DMA((2, 2, nparts)),
            pltpu.SemaphoreType.DMA((2,)),
            pltpu.SemaphoreType.DMA,
        ],
        out_shape=pltpu.HBM(shape, BF16),
        input_output_aliases=alias,
        compiler_params=params(24 if members <= 2 else 56),
        cost_estimate=cost(tokens * width * width * 8 * (members + 2), tokens * width * 2 * 5),
        name="attend",
    )(*args)


def body(
    atm_latent,
    ocean_state,
    depth,
    src_blocks,
    live,
    remap_weight,
    conv_weight,
    qkv_weight,
    out_weight,
):
    _, lev, cells, width = ocean_state.shape
    cols = remap_weight.shape[2]
    rows = cells // cols
    inner = cells - 2 * cols
    own = atm_latent.shape[1]
    atm_blk = own // cols
    tiles = lax.axis_size("tile")
    members = lax.axis_size("mem")
    tile = lax.axis_index("tile")

    def swap(x, first):
        pairs = [(i, i + 1) for i in range(first, tiles - 1, 2)]
        return lax.ppermute(x, "tile", pairs + [(b, a) for a, b in pairs])

    def exchange(x):
        return [
            lax.ppermute(x, "mem", [(i, (i + k) % members) for i in range(members)])
            for k in range(1, members)
        ]

    odd = tile % 2
    side = jnp.stack([(1 - odd) * (rows - 1), odd * (rows - 1)]).astype(jnp.int32)
    depth = depth.reshape(rows, cols)
    deep_cap = capacity((lev - 1) * inner, 0.5625)
    near_cap = capacity((lev - 1) * cols, 0.605)
    far_cap = capacity(lev * cols, 0.65625)

    hbm = pl.BlockSpec(memory_space=pltpu.HBM)
    anywhere = pl.BlockSpec(memory_space=pl.ANY)
    vmem = pl.BlockSpec(memory_space=pltpu.VMEM)
    smem = pl.BlockSpec(memory_space=pltpu.SMEM)
    tok = lambda *s: pltpu.HBM((*s, width), BF16)
    stay = lambda x: pltpu.with_memory_space_constraint(x, pltpu.HBM)
    conv_flops = lambda n, c: 2 * 9 * n * c * width * width
    dma = pltpu.SemaphoreType.DMA
    slack = cols + 16
    message = lev * cols + own
    on_msg, off_msg, flag = pl.pallas_call(
        functools.partial(prep_kernel, (deep_cap, near_cap, far_cap)),
        in_specs=[smem, hbm, hbm, hbm],
        out_specs=[hbm, hbm, smem],
        out_shape=[tok(message), tok(message), jax.ShapeDtypeStruct((1,), jnp.int32)],
        scratch_shapes=[
            pltpu.VMEM((rows, cols), jnp.int32),
            pltpu.VMEM((own, width), BF16),
            pltpu.VMEM((2, lev, cols, width), BF16),
            dma((2, lev)),
            dma((2, lev)),
            dma((2,)),
            dma((2,)),
        ],
        compiler_params=params(16),
        cost_estimate=cost(lev * cols * width * 4, lev * cols * width * 10),
        name="prep",
    )(side, stay(ocean_state), stay(atm_latent), stay(depth))
    off_halo = swap(off_msg, 1)
    on_halo = swap(on_msg, 0)

    deep_mixed, deep_normed, deep_packed = pl.pallas_call(
        functools.partial(inner_kernel, deep_cap),
        in_specs=[vmem, vmem, hbm],
        out_specs=[hbm] * 3,
        out_shape=[tok(lev - 1, inner), tok(lev - 1, inner), tok(deep_cap)],
        scratch_shapes=[
            pltpu.VMEM(conv_weight.shape, BF16),
            pltpu.VMEM((lev - 1, inner, width), BF16),
            pltpu.VMEM((lev - 1, inner, width), BF16),
            pltpu.VMEM((deep_cap + slack, width), BF16),
            dma,
            dma((lev - 1, 2)),
            dma,
        ],
        compiler_params=params(12),
        cost_estimate=cost(conv_flops(lev, inner), lev * inner * width * 8),
        name="inner",
    )(ocean_state, depth, stay(conv_weight))
    deep_others = exchange(deep_packed)

    whole_spec = lambda *sh: pl.BlockSpec(sh, lambda *_: (0,) * len(sh))
    row_f32 = pltpu.HBM((cols, width), F32)

    def row_conv(which, first, cap, halo, extra):
        n = lev - first
        base = pltpu.HBM((inner + cols, width), F32)
        return pl.pallas_call(
            functools.partial(row_kernel, cap, first, which),
            in_specs=[smem, vmem, vmem, hbm if first else vmem, anywhere] + [hbm] * len(extra),
            out_specs=[hbm] * 3 + [whole_spec(inner + cols, width)] * first,
            out_shape=[tok(lev, 2 * cols), tok(lev, 2 * cols), tok(cap)] + [base] * first,
            scratch_shapes=[
                pltpu.VMEM((cols, width), F32),
                pltpu.VMEM(conv_weight.shape, BF16),
                pltpu.VMEM((3, lev * cols, width), BF16),
                pltpu.VMEM((n, cols, width), BF16),
                pltpu.VMEM((n, cols, width), BF16),
                pltpu.VMEM((cap + slack, width), BF16),
                dma,
                dma,
                dma((2,)),
                dma,
            ],
            input_output_aliases={6: 0, 7: 1} if extra else {},
            compiler_params=params(12),
            cost_estimate=cost(conv_flops(lev, cols), lev * cols * width * 16),
            name="row",
        )(
            side,
            ocean_state,
            depth,
            stay(conv_weight) if first else conv_weight,
            halo,
            *[stay(x) for x in extra],
        )

    edge_mixed, edge_normed, near_packed, base = row_conv(0, 1, near_cap, on_halo, [])

    ids = jnp.clip(src_blocks - (tile - R) * atm_blk, 0, 3 * atm_blk - 1)
    surf_mixed, surf_normed, far_forcing, edge_mixed, edge_normed = pl.pallas_call(
        surface_kernel,
        in_specs=[smem] * 3 + [vmem] + [anywhere] * 2 + [vmem] * 4 + [hbm] * 3,
        out_specs=[whole_spec(1, inner + cols, width)] * 2 + [whole_spec(cols, width)] + [hbm] * 2,
        out_shape=[tok(1, inner + cols), tok(1, inner + cols), row_f32]
        + [tok(lev, 2 * cols)] * 2,
        scratch_shapes=[
            pltpu.VMEM((inner + cols, width), F32),
            pltpu.VMEM((3 * own, width), BF16),
            pltpu.VMEM((rows, cols, width), F32),
            dma((5,)),
        ],
        input_output_aliases={11: 3, 12: 4},
        compiler_params=params(12),
        cost_estimate=cost(conv_flops(1, inner), cells * width * 16),
        name="surface",
    )(
        ids,
        live,
        side,
        depth,
        on_halo,
        off_halo,
        atm_latent,
        remap_weight,
        qkv_weight,
        out_weight,
        stay(base),
        stay(edge_mixed),
        stay(edge_normed),
    )
    surf_others = exchange(surf_normed)
    near_others = exchange(near_packed)

    edge_mixed, edge_normed, far_packed = row_conv(
        1, 0, far_cap, off_halo, [far_forcing, edge_mixed, edge_normed]
    )
    far_others = exchange(far_packed)

    def unread(shape):
        return pl.pallas_call(
            lambda out_ref: None,
            out_specs=hbm,
            out_shape=pltpu.HBM(shape, BF16),
            name="unread",
        )()

    def send_all(*arrays):
        sizes = [x.shape[0] * x.shape[1] for x in arrays]
        joined = jnp.concatenate([x.reshape(-1, width) for x in arrays], axis=0)
        got = [[] for _ in arrays]
        for part in exchange(joined):
            at = 0
            for k, (x, size) in enumerate(zip(arrays, sizes)):
                got[k].append(part[at : at + size].reshape(x.shape))
                at += size
        return tuple(got)

    deep_whole, edge_whole = lax.cond(
        flag[0] > 0,
        send_all,
        lambda *a: tuple([unread(x.shape) for _ in range(members - 1)] for x in a),
        deep_normed,
        edge_normed,
    )
    shape = ocean_state.shape
    weights = (depth, qkv_weight, out_weight)
    out = attend(
        flag,
        side,
        [surf_normed, deep_normed],
        [surf_mixed, deep_mixed],
        surf_others,
        deep_others,
        deep_whole,
        *weights,
        None,
        shape,
    )
    return attend(
        flag,
        side,
        [edge_normed],
        [edge_mixed],
        surf_others,
        near_others + far_others,
        edge_whole,
        *weights,
        out,
        shape,
    )


def solution(mesh):
    return jax.shard_map(
        body,
        mesh=mesh,
        in_specs=(
            P("mem", "tile", None),
            P("mem", None, "tile", None),
            P("tile"),
            P("tile", None),
            P("tile"),
            P("tile", None, None, None),
            P(),
            P(),
            P(),
        ),
        out_specs=P("mem", None, "tile", None),
        check_vma=False,
    )
```

```python
import functools
import math

import jax
import jax.numpy as jnp
from jax import lax
from jax.experimental import pallas as pl
from jax.experimental.pallas import tpu as pltpu
from jax.sharding import PartitionSpec as P

HEADS = 4
R = 1
GROUP = 16
EPS = 1e-06
NEG = -1e30
F32 = jnp.float32
BF16 = jnp.bfloat16
MIB = 1024 * 1024


def params(mib, steps=0):
    return pltpu.CompilerParams(
        dimension_semantics=("arbitrary",) * steps if steps else None, vmem_limit_bytes=mib * MIB
    )


def cost(flops, nbytes):
    return pl.CostEstimate(flops=int(flops), bytes_accessed=int(nbytes), transcendentals=0)


def capacity(tokens, share):
    return -(-int(tokens * share) // 16) * 16


def row_plan(depth_row, lev):
    cols = depth_row.shape[1]
    level = lax.broadcasted_iota(jnp.int32, (lev, cols), 0).astype(F32)
    wet = (depth_row > level).astype(F32)
    upper = (
        lax.broadcasted_iota(jnp.int32, (cols, cols), 0)
        < lax.broadcasted_iota(jnp.int32, (cols, cols), 1)
    )
    upper = upper.astype(F32).astype(BF16)
    rank = jnp.dot(wet.astype(BF16), upper, preferred_element_type=F32)
    counts = [jnp.sum(wet[l : l + 1]).astype(jnp.int32) for l in range(lev)]
    return wet, rank, counts


def offsets(plans, first, lev):
    at, place = jnp.int32(0), {}
    for l in range(first, lev):
        for r, plan in enumerate(plans):
            place[l, r] = at
            at = at + plan[2][l]
    return place


def segment(wet, rank, offset, limit):
    cols = wet.shape[1]
    base = jnp.minimum((offset // 16) * 16, limit)
    target = jnp.where(wet > 0, rank + (offset - base).astype(F32), -1.0)
    slot = lax.broadcasted_iota(jnp.int32, (cols + 16, cols), 0).astype(F32)
    return pl.multiple_of(base, 16), (slot == target).astype(F32).astype(BF16)


def pack(buf_ref, wet, rank, offset, cap, tokens):
    base, hot = segment(wet, rank, offset, cap)
    rows = jnp.dot(hot, tokens, preferred_element_type=F32).astype(BF16)
    head = pl.ds(base, 16)
    buf_ref[head, :] = buf_ref[head, :] + rows[:16]
    buf_ref[pl.ds(pl.multiple_of(base + 16, 16), rows.shape[0] - 16), :] = rows[16:]


def unpack(rows_of, wet, rank, offset, limit):
    base, hot = segment(wet, rank, offset, limit)
    return lax.dot_general(
        hot, rows_of(base, hot.shape[0]), (((0,), (0,)), ((), ())), preferred_element_type=F32
    ).astype(BF16)


def column(depth_row):
    cols = depth_row.shape[1]
    return jnp.broadcast_to(depth_row, (cols, cols)).T


def widen(x, width):
    return jnp.concatenate([x] * (width // x.shape[1]), axis=1)


def stencil(taps, weight_ref, cols):
    count, width = taps[0].shape
    x = jnp.concatenate(taps, axis=1)
    sums = [
        jnp.dot(x, weight_ref[:, dc].reshape(3 * width, -1), preferred_element_type=F32)
        for dc in range(3)
    ]
    col = lax.broadcasted_iota(jnp.int32, (count, 1), 0) % cols
    left = jnp.where(col == 0, 0.0, pltpu.roll(sums[0], 1, axis=0))
    right = jnp.where(col == cols - 1, 0.0, pltpu.roll(sums[2], count - 1, axis=0))
    return sums[1] + left + right


def normalise(mixed):
    mf = mixed.astype(F32)
    mean = jnp.mean(mf * mf, axis=-1, keepdims=True)
    return (mf * lax.rsqrt(mean + EPS)).astype(BF16)


def prep_kernel(
    caps,
    side_ref,
    state_hbm,
    atm_hbm,
    depth_hbm,
    on_hbm,
    off_hbm,
    flag_ref,
    depth_ref,
    atm,
    rows_in,
    in_sem,
    out_sem,
    atm_sem,
    own_sem,
):
    _, lev, cells, width = state_hbm.shape
    rows, cols = depth_ref.shape
    own = atm_hbm.shape[1]
    sides = (on_hbm, off_hbm)
    load_depth = pltpu.make_async_copy(depth_hbm, depth_ref, own_sem.at[0])
    load_depth.start()
    loads, stores = [], []
    for k in (1, 0):
        at = pl.multiple_of(side_ref[k] * cols, cols)
        for l in range(lev):
            load = pltpu.make_async_copy(
                state_hbm.at[0, l, pl.ds(at, cols)], rows_in.at[k, l], in_sem.at[k, l]
            )
            load.start()
            loads.append((k, l, load))
    load_atm = pltpu.make_async_copy(atm_hbm.at[0], atm, own_sem.at[1])
    load_atm.start()
    load_depth.wait()
    d = depth_ref[...].astype(F32)
    pick = lambda k: jnp.where(side_ref[k] == 0, d[0:1], d[rows - 1 :])
    deep = [column(pick(k)) for k in range(2)]
    for k, l, load in loads:
        wet = widen((deep[k] > l).astype(F32).astype(BF16), width)
        load.wait()
        rows_in[k, l] = rows_in[k, l] * wet
        store = pltpu.make_async_copy(
            rows_in.at[k, l], sides[k].at[pl.ds(l * cols, cols)], out_sem.at[k, l]
        )
        store.start()
        stores.append(store)
    load_atm.wait()
    for k in (1, 0):
        store = pltpu.make_async_copy(
            atm, sides[k].at[pl.ds(lev * cols, own)], atm_sem.at[k]
        )
        store.start()
        stores.append(store)
    counts = [
        jnp.sum(jnp.maximum(d[1 : rows - 1] - 1.0, 0.0)),
        jnp.sum(jnp.maximum(pick(0) - 1.0, 0.0)),
        jnp.sum(pick(1)),
    ]
    over = jnp.int32(0)
    for count, cap in zip(counts, caps):
        over = over | (count > cap).astype(jnp.int32)
    flag_ref[0] = over
    for store in stores:
        store.wait()


def inner_kernel(
    cap,
    state,
    depth_ref,
    weight_hbm,
    mixed_hbm,
    normed_hbm,
    packed_hbm,
    weight,
    mixed,
    normed,
    packed,
    weight_sem,
    out_sem,
    packed_sem,
):
    _, lev, cells, width = state.shape
    rows, cols = depth_ref.shape
    load = pltpu.make_async_copy(weight_hbm, weight, weight_sem)
    load.start()
    packed[...] = jnp.zeros_like(packed)
    d = depth_ref[...].astype(F32)
    plans = [row_plan(d[r : r + 1], lev) for r in range(1, rows - 1)]
    place = offsets(plans, 1, lev)
    deep = jnp.concatenate([column(d[r : r + 1]) for r in range(rows)], axis=0)
    count = cells - 2 * cols
    stores = []
    for l in range(1, lev):
        wet = (deep > l).astype(F32)
        x = state[0, l] * widen(wet.astype(BF16), width)
        taps = [x[dr * cols : dr * cols + count] for dr in range(3)]
        if l == 1:
            load.wait()
        total = stencil(taps, weight, cols)
        new = taps[1].astype(F32) + widen(wet[cols : cols + count], width) * total
        new = new.astype(BF16)
        mixed[l - 1] = new
        tokens = normalise(new)
        normed[l - 1] = tokens
        for k, (buf, out) in enumerate(((mixed, mixed_hbm), (normed, normed_hbm))):
            store = pltpu.make_async_copy(buf.at[l - 1], out.at[l - 1], out_sem.at[l - 1, k])
            store.start()
            stores.append(store)
        for r, plan in enumerate(plans):
            pack(
                packed,
                plan[0][l : l + 1],
                plan[1][l : l + 1],
                place[l, r],
                cap,
                tokens[r * cols : (r + 1) * cols],
            )
        if l == lev - 1:
            store = pltpu.make_async_copy(packed.at[pl.ds(0, cap)], packed_hbm, packed_sem)
            store.start()
            stores.append(store)
    for store in stores:
        store.wait()


def surface_kernel(
    ids_ref,
    live_ref,
    side_ref,
    depth_ref,
    on_hbm,
    off_hbm,
    atm_ref,
    remap,
    qkv_ref,
    wo_ref,
    base_hbm,
    edge_mixed_in,
    edge_normed_in,
    mixed_ref,
    normed_ref,
    far_ref,
    edge_mixed_hbm,
    edge_normed_hbm,
    base,
    window,
    forcing_ref,
    sem,
):
    rows, cols = depth_ref.shape
    _, own, width = atm_ref.shape
    blocks, pairs = remap.shape[0], remap.shape[1]
    on_at = jnp.where(side_ref[0] == 0, 0, 2 * own)
    copies = [
        pltpu.make_async_copy(
            on_hbm.at[pl.ds(on_hbm.shape[0] - own, own)],
            window.at[pl.ds(pl.multiple_of(on_at, own), own)],
            sem.at[0],
        ),
        pltpu.make_async_copy(
            off_hbm.at[pl.ds(off_hbm.shape[0] - own, own)],
            window.at[pl.ds(pl.multiple_of(2 * own - on_at, own), own)],
            sem.at[1],
        ),
        pltpu.make_async_copy(base_hbm, base, sem.at[4]),
    ]
    for copy in copies:
        copy.start()
    window[own : 2 * own] = atm_ref[0]
    d = depth_ref[...].astype(F32)
    near, far = side_ref[0], side_ref[1]
    rows_d = [d[r : r + 1] for r in range(1, rows - 1)]
    rows_d.append(jnp.where(near == 0, d[0:1], d[rows - 1 :]))
    wets = [widen((column(row) > 0).astype(F32), width) for row in rows_d]
    for copy in copies:
        copy.wait()
    for b in range(blocks):
        weights, picked = [], []
        for p in range(pairs):
            on = jnp.where(p < live_ref[b], 1.0, 0.0)
            weights.append(remap[b, p] * jnp.full((1, cols), on, F32).astype(BF16))
            start = pl.multiple_of(ids_ref[b, p] * cols, cols)
            picked.append(window[pl.ds(start, cols), :])
        acc = jnp.dot(
            jnp.concatenate(weights, axis=1),
            jnp.concatenate(picked, axis=0),
            preferred_element_type=F32,
        )
        forcing_ref[b] = acc
    for k, wet in enumerate(wets):
        at = slice(k * cols, (k + 1) * cols)
        forcing = forcing_ref[near] if k == rows - 2 else forcing_ref[k + 1]
        new = (base[at] + wet * forcing).astype(BF16)
        mixed_ref[0, at] = new
        normed_ref[0, at] = normalise(new)
    far_ref[...] = forcing_ref[far]
    at = pl.ds((rows - 2) * cols, cols)
    stores = [
        pltpu.make_async_copy(mixed_ref.at[0, at], edge_mixed_hbm.at[0, pl.ds(0, cols)], sem.at[2]),
        pltpu.make_async_copy(normed_ref.at[0, at], edge_normed_hbm.at[0, pl.ds(0, cols)], sem.at[3]),
    ]
    for store in stores:
        store.start()
    for store in stores:
        store.wait()


def row_kernel(cap, first, which, side_ref, state, depth_ref, weight_in, halo_hbm, *refs):
    refs = list(refs)
    forcing_hbm = None
    if not first:
        forcing_hbm = refs[0]
        refs = refs[3:]
    mixed_hbm, normed_hbm, packed_hbm = refs[:3]
    refs = refs[3:]
    base_ref = refs.pop(0) if first else None
    forcing_ref, weight, tap, mixed, normed, packed, weight_sem, halo_sem, out_sem, packed_sem = refs
    if first:
        load = pltpu.make_async_copy(weight_in, weight, weight_sem)
        load.start()
    else:
        weight = weight_in
    _, lev, cells, width = state.shape
    rows, cols = depth_ref.shape
    row = side_ref[which]
    top = row == 0
    beside = jnp.where(top, 1, rows - 2)
    outer = jnp.where(top, 0, 2)
    halo = pltpu.make_async_copy(
        halo_hbm.at[pl.ds(0, lev * cols)], tap.at[outer], halo_sem
    )
    halo.start()
    if not first:
        forcing = pltpu.make_async_copy(forcing_hbm, forcing_ref, packed_sem)
        forcing.start()
    packed[...] = jnp.zeros_like(packed)
    d = depth_ref[...].astype(F32)
    own_depth = jnp.where(top, d[0:1], d[rows - 1 :])
    plan = row_plan(own_depth, lev)
    place = offsets([plan], first, lev)
    deep = column(own_depth)
    deep_beside = column(jnp.where(top, d[1:2], d[rows - 2 : rows - 1]))
    at = pl.multiple_of(row * cols, cols)
    at_beside = pl.multiple_of(beside * cols, cols)
    wets = []
    for l in range(lev):
        rows_l = slice(l * cols, (l + 1) * cols)
        wet = (deep > l).astype(F32)
        wets.append(wet)
        wet_beside = (deep_beside > l).astype(F32)
        tap[1, rows_l] = state[0, l, pl.ds(at, cols)] * widen(wet.astype(BF16), width)
        tap[2 - outer, rows_l] = state[0, l, pl.ds(at_beside, cols)] * widen(
            wet_beside.astype(BF16), width
        )
    stores = []
    half = lev // 2
    if first:
        load.wait()
    halo.wait()
    if not first:
        forcing.wait()
    for start in range(0, lev, half):
        rows_b = slice(start * cols, (start + half) * cols)
        taps = [tap[dr, rows_b] for dr in range(3)]
        total = stencil(taps, weight, cols)
        for k in range(half):
            l = start + k
            rows_k = slice(k * cols, (k + 1) * cols)
            part = total[rows_k]
            if l == 0 and not first:
                part = part + forcing_ref[...]
            new = taps[1][rows_k].astype(F32) + widen(wets[l], width) * part
            if l < first:
                base_ref[cells - 2 * cols :] = new
                continue
            new = new.astype(BF16)
            mixed[l - first] = new
            tokens = normalise(new)
            normed[l - first] = tokens
            pack(packed, plan[0][l : l + 1], plan[1][l : l + 1], place[l, 0], cap, tokens)
    if first:
        wet = (jnp.concatenate([column(d[r : r + 1]) for r in range(rows)], axis=0) > 0).astype(F32)
        x = state[0, 0] * widen(wet.astype(BF16), width)
        taps = [x[dr * cols : dr * cols + cells - 2 * cols] for dr in range(3)]
        inside = widen(wet[cols : cells - cols], width)
        base_ref[0 : cells - 2 * cols] = taps[1].astype(F32) + inside * stencil(taps, weight, cols)
    block = (pl.ds(first, lev - first), pl.ds(which * cols, cols))
    for k, (buf, out) in enumerate(((mixed, mixed_hbm), (normed, normed_hbm))):
        store = pltpu.make_async_copy(buf, out.at[block], out_sem.at[k])
        store.start()
        stores.append(store)
    store = pltpu.make_async_copy(packed.at[pl.ds(0, cap)], packed_hbm, packed_sem)
    store.start()
    stores.append(store)
    for store in stores:
        store.wait()


def attend_kernel(others, nparts, edges, flag_ref, side_ref, *refs):
    refs = list(refs)
    take = lambda k: [refs.pop(0) for _ in range(k)]
    own_normed = take(nparts)
    own_mixed = take(nparts)
    surf = take(others)
    packed = [take(others) for _ in range(1 + edges)]
    whole = take(others)
    depth_ref, qkv_ref, wo_ref = take(3)
    if edges:
        take(1)
    out_hbm, x_ref, mixed_ref, q_ref, k_ref, v_ref, att_ref, token_ref, new_ref = refs[:9]
    in_sem, out_sem, sem, got_sem, surf_buf = refs[9:14]
    pack_bufs = refs[14:]
    steps, lev, count, width = q_ref.shape
    got = []
    for o in range(others):
        copies = []
        for k, (source, buf) in enumerate(zip(packed, pack_bufs)):
            copies.append(pltpu.make_async_copy(source[o], buf.at[o], got_sem.at[o, k]))
        size = surf_buf.shape[1]
        at = surf[o].shape[1] - size if edges else 0
        copies.append(
            pltpu.make_async_copy(
                surf[o].at[0, pl.ds(at, size)], surf_buf.at[o], got_sem.at[o, len(packed)]
            )
        )
        got.append(copies)
    for copies in got:
        for copy in copies:
            copy.start()
    members = others + 1
    head = width // HEADS
    pair = 2 * head

    loads = []
    for kind, (parts, buf) in enumerate(((own_normed, x_ref), (own_mixed, mixed_ref))):
        for step in range(steps):
            at = 0
            for k, part in enumerate(parts):
                n = part.shape[0]
                load = pltpu.make_async_copy(
                    part.at[:, pl.ds(step * count, count)],
                    buf.at[step, pl.ds(at, n)],
                    in_sem.at[kind, step, k],
                )
                load.start()
                loads.append((kind, step, load))
                at += n

    def arrive(kind, step):
        for k, s, load in loads:
            if (k, s) == (kind, step):
                load.wait()

    d = depth_ref[...].astype(F32)
    last = d.shape[0] - 1
    if edges:
        rows_d = [jnp.where(side_ref[k] == 0, d[0:1], d[last:]) for k in range(2)]
    else:
        rows_d = [d[r : r + 1] for r in range(1, last)]
    plans = [row_plan(row, lev) for row in rows_d]
    if edges:
        near, far = offsets(plans[:1], 1, lev), offsets(plans[1:], 0, lev)
        place = [{l: at for (l, _), at in p.items()} for p in (near, far)]
    else:
        both = offsets(plans, 1, lev)
        place = [{l: both[l, step] for l in range(1, lev)} for step in range(steps)]

    def project(x, step, m):
        rows = slice(m * lev, (m + 1) * lev)
        kv = jnp.dot(x, qkv_ref[:, width:], preferred_element_type=F32).astype(BF16)
        k_ref[step, rows] = kv[:, :width].reshape(lev, count, width)
        v_ref[step, rows] = kv[:, width:].reshape(lev, count, width)

    for o in range(others):
        for copy in got[o]:
            copy.wait()
        for step in range(steps):
            buf = pack_bufs[step if edges else 0]
            window = lambda base, size: buf[o, pl.ds(base, size), :]
            limit = buf.shape[1] - count - 16
            wet, rank, _ = plans[step]
            if 0 not in place[step]:
                at = 0 if edges else step * count
                token_ref[step, 0] = surf_buf[o, at : at + count]
            for l, at in place[step].items():
                token_ref[step, l] = unpack(window, wet[l : l + 1], rank[l : l + 1], at, limit)

        @pl.when(flag_ref[0] != 0)
        def _():
            first = lev - whole[o].shape[0]
            for step in range(steps):
                copy = pltpu.make_async_copy(
                    whole[o].at[:, pl.ds(step * count, count)],
                    token_ref.at[step, pl.ds(first, lev - first)],
                    sem,
                )
                copy.start()
                copy.wait()

        for step in range(steps):
            project(token_ref[step].reshape(-1, width), step, o + 1)

    nq, nk = lev * GROUP, members * lev * GROUP
    groups = count // GROUP
    lanes_n = lev * GROUP
    cell = lax.broadcasted_iota(jnp.int32, (groups, count), 1)
    mine = (cell // GROUP == lax.broadcasted_iota(jnp.int32, (groups, count), 0)).astype(F32)
    spread = lax.broadcasted_iota(jnp.int32, (count, lanes_n), 0) % GROUP
    spread = (spread == lax.broadcasted_iota(jnp.int32, (count, lanes_n), 1) % GROUP).astype(F32)
    key_level = lax.broadcasted_iota(jnp.int32, (groups, lanes_n), 1) // GROUP
    qc = lax.broadcasted_iota(jnp.int32, (nq, nk), 0) % GROUP
    kc = lax.broadcasted_iota(jnp.int32, (nq, nk), 1) % GROUP
    same = jnp.where(qc == kc, 0.0, NEG)
    lane = lax.broadcasted_iota(jnp.int32, (1, width), 1)
    scale = 1.0 / math.sqrt(head)
    masks = [jnp.where(lane // head == h, scale, 0.0).astype(BF16) for h in range(HEADS)]
    stores = []
    for step in range(steps):
        arrive(0, step)
        x = x_ref[step].reshape(-1, width)
        q = jnp.dot(x, qkv_ref[:, 0:width], preferred_element_type=F32).astype(BF16)
        q_ref[step] = q.reshape(lev, count, width)
        project(x, step, 0)
        key_depth = jnp.dot(
            (mine * rows_d[step]).astype(BF16), spread.astype(BF16), preferred_element_type=F32
        )
        key_bias = jnp.where(key_depth > key_level.astype(F32), 0.0, NEG)
        for g in range(groups):
            cells = slice(g * GROUP, (g + 1) * GROUP)
            bias = same + jnp.concatenate([key_bias[g : g + 1]] * members, axis=1)
            bias = jnp.concatenate([bias] * HEADS, axis=0)
            q = q_ref[step, :, cells].reshape(nq, width)
            q = jnp.concatenate([q * mask for mask in masks], axis=0)
            k = k_ref[step, :, cells].reshape(nk, width)
            v = v_ref[step, :, cells].reshape(nk, width)
            s = lax.dot_general(q, k, (((1,), (1,)), ((), ())), preferred_element_type=F32) + bias
            p = jnp.exp(s - jnp.max(s, axis=-1, keepdims=True))
            norm = 1.0 / jnp.sum(p, axis=-1, keepdims=True)
            p = p.astype(BF16)
            for h in range(HEADS // 2):
                lanes = slice(h * pair, (h + 1) * pair)
                rows = slice(h * 2 * nq, (h + 1) * 2 * nq)
                o = jnp.dot(p[rows], v[:, lanes], preferred_element_type=F32) * norm[rows]
                o = jnp.where(lane[:, :pair] < head, o[:nq], o[nq:])
                att_ref[step, :, cells, lanes] = o.astype(BF16).reshape(lev, GROUP, pair)
        proj = jnp.dot(
            att_ref[step].reshape(-1, width), wo_ref[...], preferred_element_type=F32
        )
        arrive(1, step)
        deep = column(rows_d[step])
        row = side_ref[step] if edges else step + 1
        for l in range(lev):
            rows = slice(l * count, (l + 1) * count)
            wet = widen((deep > l).astype(F32), width)
            new_ref[step, l] = (mixed_ref[step, l].astype(F32) + wet * proj[rows]).astype(BF16)
        at = pl.multiple_of(row * count, count)
        store = pltpu.make_async_copy(
            new_ref.at[step], out_hbm.at[0, :, pl.ds(at, count)], out_sem.at[step]
        )
        store.start()
        stores.append(store)
    for store in stores:
        store.wait()


def attend(
    flag, side, normed, mixed, surf, packed, whole, depth, qkv_weight, out_weight, out, shape
):
    edges = out is not None
    others, nparts = len(whole), len(mixed)
    lev = sum(p.shape[0] for p in mixed)
    width = shape[-1]
    cols = depth.shape[1]
    members = others + 1
    hbm = pl.BlockSpec(memory_space=pltpu.HBM)
    vmem = pl.BlockSpec(memory_space=pltpu.VMEM)
    smem = pl.BlockSpec(memory_space=pltpu.SMEM)
    stay = lambda x: pltpu.with_memory_space_constraint(x, pltpu.HBM)
    anywhere = pl.BlockSpec(memory_space=pl.ANY)
    in_specs = [smem] * 2 + [hbm] * (2 * nparts) + [anywhere] * (len(surf) + len(packed))
    in_specs += [hbm] * others + [vmem] * 3
    args = [flag, side] + [stay(x) for x in normed + mixed] + surf + packed
    args += [stay(x) for x in whole] + [depth, qkv_weight, out_weight]
    alias = {}
    if edges:
        in_specs.append(hbm)
        alias = {len(args): 0}
        args.append(stay(out))
    tokens = lev * cols * 2
    rows = pltpu.VMEM((2, lev, cols, width), BF16)
    keys = pltpu.VMEM((2, members * lev, cols, width), BF16)
    return pl.pallas_call(
        functools.partial(attend_kernel, others, nparts, edges),
        in_specs=in_specs,
        out_specs=hbm,
        scratch_shapes=[
            rows,
            rows,
            rows,
            keys,
            keys,
            rows,
            rows,
            rows,
            pltpu.SemaphoreType.DMA((2, 2, nparts)),
            pltpu.SemaphoreType.DMA((2,)),
            pltpu.SemaphoreType.DMA,
            pltpu.SemaphoreType.DMA((others, 2 + edges)),
            pltpu.VMEM((others, cols if edges else 2 * cols, width), BF16),
        ]
        + [pltpu.VMEM((others, *p.shape), BF16) for p in packed[::others]],
        out_shape=pltpu.HBM(shape, BF16),
        input_output_aliases=alias,
        compiler_params=params(24 if members <= 2 else 56),
        cost_estimate=cost(tokens * width * width * 8 * (members + 2), tokens * width * 2 * 5),
        name="attend",
    )(*args)


def body(
    atm_latent,
    ocean_state,
    depth,
    src_blocks,
    live,
    remap_weight,
    conv_weight,
    qkv_weight,
    out_weight,
):
    _, lev, cells, width = ocean_state.shape
    cols = remap_weight.shape[2]
    rows = cells // cols
    inner = cells - 2 * cols
    own = atm_latent.shape[1]
    atm_blk = own // cols
    tiles = lax.axis_size("tile")
    members = lax.axis_size("mem")
    tile = lax.axis_index("tile")

    def swap(x, first):
        pairs = [(i, i + 1) for i in range(first, tiles - 1, 2)]
        return lax.ppermute(x, "tile", pairs + [(b, a) for a, b in pairs])

    def exchange(x):
        return [
            lax.ppermute(x, "mem", [(i, (i + k) % members) for i in range(members)])
            for k in range(1, members)
        ]

    odd = tile % 2
    side = jnp.stack([(1 - odd) * (rows - 1), odd * (rows - 1)]).astype(jnp.int32)
    depth = depth.reshape(rows, cols)
    deep_cap = capacity((lev - 1) * inner, 0.5625)
    near_cap = capacity((lev - 1) * cols, 0.605)
    far_cap = capacity(lev * cols, 0.65625)

    hbm = pl.BlockSpec(memory_space=pltpu.HBM)
    anywhere = pl.BlockSpec(memory_space=pl.ANY)
    vmem = pl.BlockSpec(memory_space=pltpu.VMEM)
    smem = pl.BlockSpec(memory_space=pltpu.SMEM)
    tok = lambda *s: pltpu.HBM((*s, width), BF16)
    stay = lambda x: pltpu.with_memory_space_constraint(x, pltpu.HBM)
    conv_flops = lambda n, c: 2 * 9 * n * c * width * width
    dma = pltpu.SemaphoreType.DMA
    slack = cols + 16
    message = lev * cols + own
    on_msg, off_msg, flag = pl.pallas_call(
        functools.partial(prep_kernel, (deep_cap, near_cap, far_cap)),
        in_specs=[smem, hbm, hbm, hbm],
        out_specs=[hbm, hbm, smem],
        out_shape=[tok(message), tok(message), jax.ShapeDtypeStruct((1,), jnp.int32)],
        scratch_shapes=[
            pltpu.VMEM((rows, cols), jnp.int32),
            pltpu.VMEM((own, width), BF16),
            pltpu.VMEM((2, lev, cols, width), BF16),
            dma((2, lev)),
            dma((2, lev)),
            dma((2,)),
            dma((2,)),
        ],
        compiler_params=params(16),
        cost_estimate=cost(lev * cols * width * 4, lev * cols * width * 10),
        name="prep",
    )(side, stay(ocean_state), stay(atm_latent), stay(depth))
    off_halo = swap(off_msg, 1)
    on_halo = swap(on_msg, 0)

    deep_mixed, deep_normed, deep_packed = pl.pallas_call(
        functools.partial(inner_kernel, deep_cap),
        in_specs=[vmem, vmem, hbm],
        out_specs=[hbm] * 3,
        out_shape=[tok(lev - 1, inner), tok(lev - 1, inner), tok(deep_cap)],
        scratch_shapes=[
            pltpu.VMEM(conv_weight.shape, BF16),
            pltpu.VMEM((lev - 1, inner, width), BF16),
            pltpu.VMEM((lev - 1, inner, width), BF16),
            pltpu.VMEM((deep_cap + slack, width), BF16),
            dma,
            dma((lev - 1, 2)),
            dma,
        ],
        compiler_params=params(12),
        cost_estimate=cost(conv_flops(lev, inner), lev * inner * width * 8),
        name="inner",
    )(ocean_state, depth, stay(conv_weight))
    deep_others = exchange(deep_packed)

    whole_spec = lambda *sh: pl.BlockSpec(sh, lambda *_: (0,) * len(sh))
    row_f32 = pltpu.HBM((cols, width), F32)

    def row_conv(which, first, cap, halo, extra):
        n = lev - first
        base = pltpu.HBM((inner + cols, width), F32)
        return pl.pallas_call(
            functools.partial(row_kernel, cap, first, which),
            in_specs=[smem, vmem, vmem, hbm if first else vmem, anywhere] + [hbm] * len(extra),
            out_specs=[hbm] * 3 + [whole_spec(inner + cols, width)] * first,
            out_shape=[tok(lev, 2 * cols), tok(lev, 2 * cols), tok(cap)] + [base] * first,
            scratch_shapes=[
                pltpu.VMEM((cols, width), F32),
                pltpu.VMEM(conv_weight.shape, BF16),
                pltpu.VMEM((3, lev * cols, width), BF16),
                pltpu.VMEM((n, cols, width), BF16),
                pltpu.VMEM((n, cols, width), BF16),
                pltpu.VMEM((cap + slack, width), BF16),
                dma,
                dma,
                dma((2,)),
                dma,
            ],
            input_output_aliases={6: 0, 7: 1} if extra else {},
            compiler_params=params(12),
            cost_estimate=cost(conv_flops(lev, cols), lev * cols * width * 16),
            name="row",
        )(
            side,
            ocean_state,
            depth,
            stay(conv_weight) if first else conv_weight,
            halo,
            *[stay(x) for x in extra],
        )

    edge_mixed, edge_normed, near_packed, base = row_conv(0, 1, near_cap, on_halo, [])

    ids = jnp.clip(src_blocks - (tile - R) * atm_blk, 0, 3 * atm_blk - 1)
    surf_mixed, surf_normed, far_forcing, edge_mixed, edge_normed = pl.pallas_call(
        surface_kernel,
        in_specs=[smem] * 3 + [vmem] + [anywhere] * 2 + [vmem] * 4 + [hbm] * 3,
        out_specs=[whole_spec(1, inner + cols, width)] * 2 + [whole_spec(cols, width)] + [hbm] * 2,
        out_shape=[tok(1, inner + cols), tok(1, inner + cols), row_f32]
        + [tok(lev, 2 * cols)] * 2,
        scratch_shapes=[
            pltpu.VMEM((inner + cols, width), F32),
            pltpu.VMEM((3 * own, width), BF16),
            pltpu.VMEM((rows, cols, width), F32),
            dma((5,)),
        ],
        input_output_aliases={11: 3, 12: 4},
        compiler_params=params(12),
        cost_estimate=cost(conv_flops(1, inner), cells * width * 16),
        name="surface",
    )(
        ids,
        live,
        side,
        depth,
        on_halo,
        off_halo,
        atm_latent,
        remap_weight,
        qkv_weight,
        out_weight,
        stay(base),
        stay(edge_mixed),
        stay(edge_normed),
    )
    surf_others = exchange(surf_normed)
    near_others = exchange(near_packed)

    edge_mixed, edge_normed, far_packed = row_conv(
        1, 0, far_cap, off_halo, [far_forcing, edge_mixed, edge_normed]
    )
    far_others = exchange(far_packed)

    def unread(shape):
        return pl.pallas_call(
            lambda out_ref: None,
            out_specs=hbm,
            out_shape=pltpu.HBM(shape, BF16),
            name="unread",
        )()

    def send_all(*arrays):
        sizes = [x.shape[0] * x.shape[1] for x in arrays]
        joined = jnp.concatenate([x.reshape(-1, width) for x in arrays], axis=0)
        got = [[] for _ in arrays]
        for part in exchange(joined):
            at = 0
            for k, (x, size) in enumerate(zip(arrays, sizes)):
                got[k].append(part[at : at + size].reshape(x.shape))
                at += size
        return tuple(got)

    deep_whole, edge_whole = lax.cond(
        flag[0] > 0,
        send_all,
        lambda *a: tuple([unread(x.shape) for _ in range(members - 1)] for x in a),
        deep_normed,
        edge_normed,
    )
    shape = ocean_state.shape
    weights = (depth, qkv_weight, out_weight)
    out = attend(
        flag,
        side,
        [surf_normed, deep_normed],
        [surf_mixed, deep_mixed],
        surf_others,
        deep_others,
        deep_whole,
        *weights,
        None,
        shape,
    )
    return attend(
        flag,
        side,
        [edge_normed],
        [edge_mixed],
        surf_others,
        near_others + far_others,
        edge_whole,
        *weights,
        out,
        shape,
    )


def solution(mesh):
    return jax.shard_map(
        body,
        mesh=mesh,
        in_specs=(
            P("mem", "tile", None),
            P("mem", None, "tile", None),
            P("tile"),
            P("tile", None),
            P("tile"),
            P("tile", None, None, None),
            P(),
            P(),
            P(),
        ),
        out_specs=P("mem", None, "tile", None),
        check_vma=False,
    )
```

```python
import functools
import math

import jax
import jax.numpy as jnp
from jax import lax
from jax.experimental import pallas as pl
from jax.experimental.pallas import tpu as pltpu
from jax.sharding import PartitionSpec as P

HEADS = 4
R = 1
GROUP = 16
EPS = 1e-06
NEG = -1e30
F32 = jnp.float32
BF16 = jnp.bfloat16
MIB = 1024 * 1024


def params(mib, steps=0):
    return pltpu.CompilerParams(
        dimension_semantics=("arbitrary",) * steps if steps else None, vmem_limit_bytes=mib * MIB
    )


def cost(flops, nbytes):
    return pl.CostEstimate(flops=int(flops), bytes_accessed=int(nbytes), transcendentals=0)


def capacity(tokens, share):
    return -(-int(tokens * share) // 16) * 16


def row_plan(depth_row, lev):
    cols = depth_row.shape[1]
    level = lax.broadcasted_iota(jnp.int32, (lev, cols), 0).astype(F32)
    wet = (depth_row > level).astype(F32)
    upper = (
        lax.broadcasted_iota(jnp.int32, (cols, cols), 0)
        < lax.broadcasted_iota(jnp.int32, (cols, cols), 1)
    )
    upper = upper.astype(F32).astype(BF16)
    rank = jnp.dot(wet.astype(BF16), upper, preferred_element_type=F32)
    counts = [jnp.sum(wet[l : l + 1]).astype(jnp.int32) for l in range(lev)]
    return wet, rank, counts


def offsets(plans, first, lev):
    at, place = jnp.int32(0), {}
    for l in range(first, lev):
        for r, plan in enumerate(plans):
            place[l, r] = at
            at = at + plan[2][l]
    return place


def segment(wet, rank, offset, limit):
    cols = wet.shape[1]
    base = jnp.minimum((offset // 16) * 16, limit)
    target = jnp.where(wet > 0, rank + (offset - base).astype(F32), -1.0)
    slot = lax.broadcasted_iota(jnp.int32, (cols + 16, cols), 0).astype(F32)
    return pl.multiple_of(base, 16), (slot == target).astype(F32).astype(BF16)


def pack(buf_ref, wet, rank, offset, cap, tokens):
    base, hot = segment(wet, rank, offset, cap)
    rows = jnp.dot(hot, tokens, preferred_element_type=F32).astype(BF16)
    head = pl.ds(base, 16)
    buf_ref[head, :] = buf_ref[head, :] + rows[:16]
    buf_ref[pl.ds(pl.multiple_of(base + 16, 16), rows.shape[0] - 16), :] = rows[16:]


def unpack(rows_of, wet, rank, offset, limit):
    base, hot = segment(wet, rank, offset, limit)
    return lax.dot_general(
        hot, rows_of(base, hot.shape[0]), (((0,), (0,)), ((), ())), preferred_element_type=F32
    ).astype(BF16)


def column(depth_row):
    cols = depth_row.shape[1]
    return jnp.broadcast_to(depth_row, (cols, cols)).T


def widen(x, width):
    return jnp.concatenate([x] * (width // x.shape[1]), axis=1)


def stencil(taps, weight_ref, cols):
    count, width = taps[0].shape
    x = jnp.concatenate(taps, axis=1)
    sums = [
        jnp.dot(x, weight_ref[:, dc].reshape(3 * width, -1), preferred_element_type=F32)
        for dc in range(3)
    ]
    col = lax.broadcasted_iota(jnp.int32, (count, 1), 0) % cols
    left = jnp.where(col == 0, 0.0, pltpu.roll(sums[0], 1, axis=0))
    right = jnp.where(col == cols - 1, 0.0, pltpu.roll(sums[2], count - 1, axis=0))
    return sums[1] + left + right


def normalise(mixed):
    mf = mixed.astype(F32)
    mean = jnp.mean(mf * mf, axis=-1, keepdims=True)
    return (mf * lax.rsqrt(mean + EPS)).astype(BF16)


def prep_kernel(
    caps,
    side_ref,
    state_hbm,
    atm_hbm,
    depth_hbm,
    on_hbm,
    off_hbm,
    flag_ref,
    depth_ref,
    atm,
    rows_in,
    in_sem,
    out_sem,
    atm_sem,
    own_sem,
):
    _, lev, cells, width = state_hbm.shape
    rows, cols = depth_ref.shape
    own = atm_hbm.shape[1]
    sides = (on_hbm, off_hbm)
    load_depth = pltpu.make_async_copy(depth_hbm, depth_ref, own_sem.at[0])
    load_depth.start()
    loads, stores = [], []
    for k in (1, 0):
        at = pl.multiple_of(side_ref[k] * cols, cols)
        for l in range(lev):
            load = pltpu.make_async_copy(
                state_hbm.at[0, l, pl.ds(at, cols)], rows_in.at[k, l], in_sem.at[k, l]
            )
            load.start()
            loads.append((k, l, load))
    load_atm = pltpu.make_async_copy(atm_hbm.at[0], atm, own_sem.at[1])
    load_atm.start()
    load_depth.wait()
    d = depth_ref[...].astype(F32)
    pick = lambda k: jnp.where(side_ref[k] == 0, d[0:1], d[rows - 1 :])
    deep = [column(pick(k)) for k in range(2)]
    counts = [
        jnp.sum(jnp.maximum(d[1 : rows - 1] - 1.0, 0.0)),
        jnp.sum(jnp.maximum(pick(0) - 1.0, 0.0)),
        jnp.sum(pick(1)),
    ]
    over = jnp.int32(0)
    for count, cap in zip(counts, caps):
        over = over | (count > cap).astype(jnp.int32)
    flag_ref[0] = over
    for k, l, load in loads:
        wet = widen((deep[k] > l).astype(F32).astype(BF16), width)
        load.wait()
        rows_in[k, l] = rows_in[k, l] * wet
        store = pltpu.make_async_copy(
            rows_in.at[k, l], sides[k].at[pl.ds(l * cols, cols)], out_sem.at[k, l]
        )
        store.start()
        stores.append(store)
    load_atm.wait()
    for k in (1, 0):
        store = pltpu.make_async_copy(
            atm, sides[k].at[pl.ds(lev * cols, own)], atm_sem.at[k]
        )
        store.start()
        stores.append(store)
    for store in stores:
        store.wait()


def inner_kernel(
    cap,
    state,
    depth_ref,
    weight_hbm,
    mixed_hbm,
    normed_hbm,
    packed_hbm,
    weight,
    mixed,
    normed,
    packed,
    weight_sem,
    out_sem,
    packed_sem,
):
    _, lev, cells, width = state.shape
    rows, cols = depth_ref.shape
    load = pltpu.make_async_copy(weight_hbm, weight, weight_sem)
    load.start()
    packed[...] = jnp.zeros_like(packed)
    d = depth_ref[...].astype(F32)
    plans = [row_plan(d[r : r + 1], lev) for r in range(1, rows - 1)]
    place = offsets(plans, 1, lev)
    deep = jnp.concatenate([column(d[r : r + 1]) for r in range(rows)], axis=0)
    count = cells - 2 * cols
    stores = []
    for l in range(1, lev):
        wet = (deep > l).astype(F32)
        x = state[0, l] * widen(wet.astype(BF16), width)
        taps = [x[dr * cols : dr * cols + count] for dr in range(3)]
        if l == 1:
            load.wait()
        total = stencil(taps, weight, cols)
        new = taps[1].astype(F32) + widen(wet[cols : cols + count], width) * total
        new = new.astype(BF16)
        mixed[l - 1] = new
        tokens = normalise(new)
        normed[l - 1] = tokens
        for k, (buf, out) in enumerate(((mixed, mixed_hbm), (normed, normed_hbm))):
            store = pltpu.make_async_copy(buf.at[l - 1], out.at[l - 1], out_sem.at[l - 1, k])
            store.start()
            stores.append(store)
        for r, plan in enumerate(plans):
            pack(
                packed,
                plan[0][l : l + 1],
                plan[1][l : l + 1],
                place[l, r],
                cap,
                tokens[r * cols : (r + 1) * cols],
            )
        if l == lev - 1:
            store = pltpu.make_async_copy(packed.at[pl.ds(0, cap)], packed_hbm, packed_sem)
            store.start()
            stores.append(store)
    for store in stores:
        store.wait()


def surface_kernel(
    ids_ref,
    live_ref,
    side_ref,
    depth_ref,
    on_hbm,
    off_hbm,
    atm_ref,
    remap,
    qkv_ref,
    wo_ref,
    base_hbm,
    edge_mixed_in,
    edge_normed_in,
    mixed_ref,
    normed_ref,
    far_ref,
    edge_mixed_hbm,
    edge_normed_hbm,
    base,
    window,
    forcing_ref,
    sem,
):
    rows, cols = depth_ref.shape
    _, own, width = atm_ref.shape
    blocks, pairs = remap.shape[0], remap.shape[1]
    on_at = jnp.where(side_ref[0] == 0, 0, 2 * own)
    copies = [
        pltpu.make_async_copy(
            on_hbm.at[pl.ds(on_hbm.shape[0] - own, own)],
            window.at[pl.ds(pl.multiple_of(on_at, own), own)],
            sem.at[0],
        ),
        pltpu.make_async_copy(
            off_hbm.at[pl.ds(off_hbm.shape[0] - own, own)],
            window.at[pl.ds(pl.multiple_of(2 * own - on_at, own), own)],
            sem.at[1],
        ),
        pltpu.make_async_copy(base_hbm, base, sem.at[4]),
    ]
    for copy in copies:
        copy.start()
    window[own : 2 * own] = atm_ref[0]
    d = depth_ref[...].astype(F32)
    near, far = side_ref[0], side_ref[1]
    rows_d = [d[r : r + 1] for r in range(1, rows - 1)]
    rows_d.append(jnp.where(near == 0, d[0:1], d[rows - 1 :]))
    wets = [widen((column(row) > 0).astype(F32), width) for row in rows_d]
    for copy in copies:
        copy.wait()
    for b in range(blocks):
        acc = jnp.zeros((cols, width), F32)
        for p in range(pairs):
            on = (p < live_ref[b]).astype(F32)
            start = pl.multiple_of(ids_ref[b, p] * cols, cols)
            acc = acc + on * jnp.dot(
                remap[b, p], window[pl.ds(start, cols), :], preferred_element_type=F32
            )
        forcing_ref[b] = acc
    for k, wet in enumerate(wets):
        at = slice(k * cols, (k + 1) * cols)
        forcing = forcing_ref[near] if k == rows - 2 else forcing_ref[k + 1]
        new = (base[at] + wet * forcing).astype(BF16)
        mixed_ref[0, at] = new
        normed_ref[0, at] = normalise(new)
    far_ref[...] = forcing_ref[far]
    at = pl.ds((rows - 2) * cols, cols)
    stores = [
        pltpu.make_async_copy(mixed_ref.at[0, at], edge_mixed_hbm.at[0, pl.ds(0, cols)], sem.at[2]),
        pltpu.make_async_copy(normed_ref.at[0, at], edge_normed_hbm.at[0, pl.ds(0, cols)], sem.at[3]),
    ]
    for store in stores:
        store.start()
    for store in stores:
        store.wait()


def row_kernel(cap, first, which, side_ref, state, depth_ref, weight_hbm, halo_hbm, *refs):
    refs = list(refs)
    forcing_hbm = None
    if not first:
        forcing_hbm = refs[0]
        refs = refs[3:]
    mixed_hbm, normed_hbm, packed_hbm = refs[:3]
    refs = refs[3:]
    base_ref = refs.pop(0) if first else None
    forcing_ref, weight, tap, mixed, normed, packed, weight_sem, halo_sem, out_sem, packed_sem = refs
    load = pltpu.make_async_copy(weight_hbm, weight, weight_sem)
    load.start()
    _, lev, cells, width = state.shape
    rows, cols = depth_ref.shape
    row = side_ref[which]
    top = row == 0
    beside = jnp.where(top, 1, rows - 2)
    outer = jnp.where(top, 0, 2)
    halo = pltpu.make_async_copy(
        halo_hbm.at[pl.ds(0, lev * cols)], tap.at[outer], halo_sem
    )
    halo.start()
    if not first:
        forcing = pltpu.make_async_copy(forcing_hbm, forcing_ref, packed_sem)
        forcing.start()
    packed[...] = jnp.zeros_like(packed)
    d = depth_ref[...].astype(F32)
    own_depth = jnp.where(top, d[0:1], d[rows - 1 :])
    plan = row_plan(own_depth, lev)
    place = offsets([plan], first, lev)
    deep = column(own_depth)
    deep_beside = column(jnp.where(top, d[1:2], d[rows - 2 : rows - 1]))
    at = pl.multiple_of(row * cols, cols)
    at_beside = pl.multiple_of(beside * cols, cols)
    wets = []
    for l in range(lev):
        rows_l = slice(l * cols, (l + 1) * cols)
        wet = (deep > l).astype(F32)
        wets.append(wet)
        wet_beside = (deep_beside > l).astype(F32)
        tap[1, rows_l] = state[0, l, pl.ds(at, cols)] * widen(wet.astype(BF16), width)
        tap[2 - outer, rows_l] = state[0, l, pl.ds(at_beside, cols)] * widen(
            wet_beside.astype(BF16), width
        )
    stores = []
    half = lev // 2
    load.wait()
    halo.wait()
    if not first:
        forcing.wait()
    for start in range(0, lev, half):
        rows_b = slice(start * cols, (start + half) * cols)
        taps = [tap[dr, rows_b] for dr in range(3)]
        total = stencil(taps, weight, cols)
        for k in range(half):
            l = start + k
            rows_k = slice(k * cols, (k + 1) * cols)
            part = total[rows_k]
            if l == 0 and not first:
                part = part + forcing_ref[...]
            new = taps[1][rows_k].astype(F32) + widen(wets[l], width) * part
            if l < first:
                base_ref[cells - 2 * cols :] = new
                continue
            new = new.astype(BF16)
            mixed[l - first] = new
            tokens = normalise(new)
            normed[l - first] = tokens
            pack(packed, plan[0][l : l + 1], plan[1][l : l + 1], place[l, 0], cap, tokens)
    if first:
        wet = (jnp.concatenate([column(d[r : r + 1]) for r in range(rows)], axis=0) > 0).astype(F32)
        x = state[0, 0] * widen(wet.astype(BF16), width)
        taps = [x[dr * cols : dr * cols + cells - 2 * cols] for dr in range(3)]
        inside = widen(wet[cols : cells - cols], width)
        base_ref[0 : cells - 2 * cols] = taps[1].astype(F32) + inside * stencil(taps, weight, cols)
    block = (pl.ds(first, lev - first), pl.ds(which * cols, cols))
    for k, (buf, out) in enumerate(((mixed, mixed_hbm), (normed, normed_hbm))):
        store = pltpu.make_async_copy(buf, out.at[block], out_sem.at[k])
        store.start()
        stores.append(store)
    store = pltpu.make_async_copy(packed.at[pl.ds(0, cap)], packed_hbm, packed_sem)
    store.start()
    stores.append(store)
    for store in stores:
        store.wait()


def attend_kernel(others, nparts, edges, flag_ref, side_ref, *refs):
    refs = list(refs)
    take = lambda k: [refs.pop(0) for _ in range(k)]
    own_normed = take(nparts)
    own_mixed = take(nparts)
    surf = take(others)
    packed = [take(others) for _ in range(1 + edges)]
    whole = take(others)
    depth_ref, qkv_ref, wo_ref = take(3)
    if edges:
        take(1)
    out_hbm, x_ref, mixed_ref, q_ref, k_ref, v_ref, att_ref, token_ref, new_ref = refs[:9]
    in_sem, out_sem, sem = refs[9:]
    steps, lev, count, width = q_ref.shape
    members = others + 1
    head = width // HEADS
    pair = 2 * head

    loads = []
    for kind, (parts, buf) in enumerate(((own_normed, x_ref), (own_mixed, mixed_ref))):
        for step in range(steps):
            at = 0
            for k, part in enumerate(parts):
                n = part.shape[0]
                load = pltpu.make_async_copy(
                    part.at[:, pl.ds(step * count, count)],
                    buf.at[step, pl.ds(at, n)],
                    in_sem.at[kind, step, k],
                )
                load.start()
                loads.append((kind, step, load))
                at += n

    def arrive(kind, step):
        for k, s, load in loads:
            if (k, s) == (kind, step):
                load.wait()

    d = depth_ref[...].astype(F32)
    last = d.shape[0] - 1
    if edges:
        rows_d = [jnp.where(side_ref[k] == 0, d[0:1], d[last:]) for k in range(2)]
    else:
        rows_d = [d[r : r + 1] for r in range(1, last)]
    plans = [row_plan(row, lev) for row in rows_d]
    if edges:
        near, far = offsets(plans[:1], 1, lev), offsets(plans[1:], 0, lev)
        place = [{l: at for (l, _), at in p.items()} for p in (near, far)]
    else:
        both = offsets(plans, 1, lev)
        place = [{l: both[l, step] for l in range(1, lev)} for step in range(steps)]

    def project(x, step, m):
        rows = slice(m * lev, (m + 1) * lev)
        kv = jnp.dot(x, qkv_ref[:, width:], preferred_element_type=F32).astype(BF16)
        k_ref[step, rows] = kv[:, :width].reshape(lev, count, width)
        v_ref[step, rows] = kv[:, width:].reshape(lev, count, width)

    for o in range(others):
        for step in range(steps):
            source = packed[step if edges else 0][o]
            window = lambda base, size: source[pl.ds(base, size), :]
            limit = source.shape[0] - count - 16
            wet, rank, _ = plans[step]
            if 0 not in place[step]:
                at = surf[o].shape[1] - count if edges else step * count
                token_ref[step, 0] = surf[o][0, at : at + count]
            for l, at in place[step].items():
                token_ref[step, l] = unpack(window, wet[l : l + 1], rank[l : l + 1], at, limit)

        @pl.when(flag_ref[0] != 0)
        def _():
            first = lev - whole[o].shape[0]
            for step in range(steps):
                copy = pltpu.make_async_copy(
                    whole[o].at[:, pl.ds(step * count, count)],
                    token_ref.at[step, pl.ds(first, lev - first)],
                    sem,
                )
                copy.start()
                copy.wait()

        for step in range(steps):
            project(token_ref[step].reshape(-1, width), step, o + 1)

    nq, nk = lev * GROUP, members * lev * GROUP
    groups = count // GROUP
    lanes_n = lev * GROUP
    cell = lax.broadcasted_iota(jnp.int32, (groups, count), 1)
    mine = (cell // GROUP == lax.broadcasted_iota(jnp.int32, (groups, count), 0)).astype(F32)
    spread = lax.broadcasted_iota(jnp.int32, (count, lanes_n), 0) % GROUP
    spread = (spread == lax.broadcasted_iota(jnp.int32, (count, lanes_n), 1) % GROUP).astype(F32)
    key_level = lax.broadcasted_iota(jnp.int32, (groups, lanes_n), 1) // GROUP
    qc = lax.broadcasted_iota(jnp.int32, (nq, nk), 0) % GROUP
    kc = lax.broadcasted_iota(jnp.int32, (nq, nk), 1) % GROUP
    same = jnp.where(qc == kc, 0.0, NEG)
    lane = lax.broadcasted_iota(jnp.int32, (1, width), 1)
    scale = 1.0 / math.sqrt(head)
    masks = [jnp.where(lane // head == h, scale, 0.0).astype(BF16) for h in range(HEADS)]
    stores = []
    for step in range(steps):
        arrive(0, step)
        x = x_ref[step].reshape(-1, width)
        q = jnp.dot(x, qkv_ref[:, 0:width], preferred_element_type=F32).astype(BF16)
        q_ref[step] = q.reshape(lev, count, width)
        project(x, step, 0)
        key_depth = jnp.dot(
            (mine * rows_d[step]).astype(BF16), spread.astype(BF16), preferred_element_type=F32
        )
        key_bias = jnp.where(key_depth > key_level.astype(F32), 0.0, NEG)
        for g in range(groups):
            cells = slice(g * GROUP, (g + 1) * GROUP)
            bias = same + jnp.concatenate([key_bias[g : g + 1]] * members, axis=1)
            bias = jnp.concatenate([bias] * HEADS, axis=0)
            q = q_ref[step, :, cells].reshape(nq, width)
            q = jnp.concatenate([q * mask for mask in masks], axis=0)
            k = k_ref[step, :, cells].reshape(nk, width)
            v = v_ref[step, :, cells].reshape(nk, width)
            s = lax.dot_general(q, k, (((1,), (1,)), ((), ())), preferred_element_type=F32) + bias
            p = jnp.exp(s - jnp.max(s, axis=-1, keepdims=True))
            norm = 1.0 / jnp.sum(p, axis=-1, keepdims=True)
            p = p.astype(BF16)
            for h in range(HEADS // 2):
                lanes = slice(h * pair, (h + 1) * pair)
                rows = slice(h * 2 * nq, (h + 1) * 2 * nq)
                o = jnp.dot(p[rows], v[:, lanes], preferred_element_type=F32) * norm[rows]
                o = jnp.where(lane[:, :pair] < head, o[:nq], o[nq:])
                att_ref[step, :, cells, lanes] = o.astype(BF16).reshape(lev, GROUP, pair)
        proj = jnp.dot(
            att_ref[step].reshape(-1, width), wo_ref[...], preferred_element_type=F32
        )
        arrive(1, step)
        deep = column(rows_d[step])
        row = side_ref[step] if edges else step + 1
        for l in range(lev):
            rows = slice(l * count, (l + 1) * count)
            wet = widen((deep > l).astype(F32), width)
            new_ref[step, l] = (mixed_ref[step, l].astype(F32) + wet * proj[rows]).astype(BF16)
        at = pl.multiple_of(row * count, count)
        store = pltpu.make_async_copy(
            new_ref.at[step], out_hbm.at[0, :, pl.ds(at, count)], out_sem.at[step]
        )
        store.start()
        stores.append(store)
    for store in stores:
        store.wait()


def attend(
    flag, side, normed, mixed, surf, packed, whole, depth, qkv_weight, out_weight, out, shape
):
    edges = out is not None
    others, nparts = len(whole), len(mixed)
    lev = sum(p.shape[0] for p in mixed)
    width = shape[-1]
    cols = depth.shape[1]
    members = others + 1
    hbm = pl.BlockSpec(memory_space=pltpu.HBM)
    vmem = pl.BlockSpec(memory_space=pltpu.VMEM)
    smem = pl.BlockSpec(memory_space=pltpu.SMEM)
    stay = lambda x: pltpu.with_memory_space_constraint(x, pltpu.HBM)
    in_specs = [smem] * 2 + [hbm] * (2 * nparts) + [vmem] * (len(surf) + len(packed))
    in_specs += [hbm] * others + [vmem] * 3
    args = [flag, side] + [stay(x) for x in normed + mixed] + surf + packed
    args += [stay(x) for x in whole] + [depth, qkv_weight, out_weight]
    alias = {}
    if edges:
        in_specs.append(hbm)
        alias = {len(args): 0}
        args.append(stay(out))
    tokens = lev * cols * 2
    rows = pltpu.VMEM((2, lev, cols, width), BF16)
    keys = pltpu.VMEM((2, members * lev, cols, width), BF16)
    return pl.pallas_call(
        functools.partial(attend_kernel, others, nparts, edges),
        in_specs=in_specs,
        out_specs=hbm,
        scratch_shapes=[
            rows,
            rows,
            rows,
            keys,
            keys,
            rows,
            rows,
            rows,
            pltpu.SemaphoreType.DMA((2, 2, nparts)),
            pltpu.SemaphoreType.DMA((2,)),
            pltpu.SemaphoreType.DMA,
        ],
        out_shape=pltpu.HBM(shape, BF16),
        input_output_aliases=alias,
        compiler_params=params(24 if members <= 2 else 56),
        cost_estimate=cost(tokens * width * width * 8 * (members + 2), tokens * width * 2 * 5),
        name="attend",
    )(*args)


def body(
    atm_latent,
    ocean_state,
    depth,
    src_blocks,
    live,
    remap_weight,
    conv_weight,
    qkv_weight,
    out_weight,
):
    _, lev, cells, width = ocean_state.shape
    cols = remap_weight.shape[2]
    rows = cells // cols
    inner = cells - 2 * cols
    own = atm_latent.shape[1]
    atm_blk = own // cols
    tiles = lax.axis_size("tile")
    members = lax.axis_size("mem")
    tile = lax.axis_index("tile")

    def swap(x, first):
        pairs = [(i, i + 1) for i in range(first, tiles - 1, 2)]
        return lax.ppermute(x, "tile", pairs + [(b, a) for a, b in pairs])

    def exchange(x):
        return [
            lax.ppermute(x, "mem", [(i, (i + k) % members) for i in range(members)])
            for k in range(1, members)
        ]

    odd = tile % 2
    side = jnp.stack([(1 - odd) * (rows - 1), odd * (rows - 1)]).astype(jnp.int32)
    depth = depth.reshape(rows, cols)
    deep_cap = capacity((lev - 1) * inner, 0.5625)
    near_cap = capacity((lev - 1) * cols, 0.605)
    far_cap = capacity(lev * cols, 0.65625)

    hbm = pl.BlockSpec(memory_space=pltpu.HBM)
    anywhere = pl.BlockSpec(memory_space=pl.ANY)
    vmem = pl.BlockSpec(memory_space=pltpu.VMEM)
    smem = pl.BlockSpec(memory_space=pltpu.SMEM)
    tok = lambda *s: pltpu.HBM((*s, width), BF16)
    stay = lambda x: pltpu.with_memory_space_constraint(x, pltpu.HBM)
    conv_flops = lambda n, c: 2 * 9 * n * c * width * width
    dma = pltpu.SemaphoreType.DMA
    slack = cols + 16
    message = lev * cols + own
    on_msg, off_msg, flag = pl.pallas_call(
        functools.partial(prep_kernel, (deep_cap, near_cap, far_cap)),
        in_specs=[smem, hbm, hbm, hbm],
        out_specs=[hbm, hbm, smem],
        out_shape=[tok(message), tok(message), jax.ShapeDtypeStruct((1,), jnp.int32)],
        scratch_shapes=[
            pltpu.VMEM((rows, cols), jnp.int32),
            pltpu.VMEM((own, width), BF16),
            pltpu.VMEM((2, lev, cols, width), BF16),
            dma((2, lev)),
            dma((2, lev)),
            dma((2,)),
            dma((2,)),
        ],
        compiler_params=params(16),
        cost_estimate=cost(lev * cols * width * 4, lev * cols * width * 10),
        name="prep",
    )(side, stay(ocean_state), stay(atm_latent), stay(depth))
    off_halo = swap(off_msg, 1)
    on_halo = swap(on_msg, 0)

    deep_mixed, deep_normed, deep_packed = pl.pallas_call(
        functools.partial(inner_kernel, deep_cap),
        in_specs=[vmem, vmem, hbm],
        out_specs=[hbm] * 3,
        out_shape=[tok(lev - 1, inner), tok(lev - 1, inner), tok(deep_cap)],
        scratch_shapes=[
            pltpu.VMEM(conv_weight.shape, BF16),
            pltpu.VMEM((lev - 1, inner, width), BF16),
            pltpu.VMEM((lev - 1, inner, width), BF16),
            pltpu.VMEM((deep_cap + slack, width), BF16),
            dma,
            dma((lev - 1, 2)),
            dma,
        ],
        compiler_params=params(12),
        cost_estimate=cost(conv_flops(lev, inner), lev * inner * width * 8),
        name="inner",
    )(ocean_state, depth, stay(conv_weight))
    deep_others = exchange(deep_packed)

    whole_spec = lambda *sh: pl.BlockSpec(sh, lambda *_: (0,) * len(sh))
    row_f32 = pltpu.HBM((cols, width), F32)

    def row_conv(which, first, cap, halo, extra):
        n = lev - first
        base = pltpu.HBM((inner + cols, width), F32)
        return pl.pallas_call(
            functools.partial(row_kernel, cap, first, which),
            in_specs=[smem, vmem, vmem, hbm, anywhere] + [hbm] * len(extra),
            out_specs=[hbm] * 3 + [whole_spec(inner + cols, width)] * first,
            out_shape=[tok(lev, 2 * cols), tok(lev, 2 * cols), tok(cap)] + [base] * first,
            scratch_shapes=[
                pltpu.VMEM((cols, width), F32),
                pltpu.VMEM(conv_weight.shape, BF16),
                pltpu.VMEM((3, lev * cols, width), BF16),
                pltpu.VMEM((n, cols, width), BF16),
                pltpu.VMEM((n, cols, width), BF16),
                pltpu.VMEM((cap + slack, width), BF16),
                dma,
                dma,
                dma((2,)),
                dma,
            ],
            input_output_aliases={6: 0, 7: 1} if extra else {},
            compiler_params=params(12),
            cost_estimate=cost(conv_flops(lev, cols), lev * cols * width * 16),
            name="row",
        )(side, ocean_state, depth, stay(conv_weight), halo, *[stay(x) for x in extra])

    edge_mixed, edge_normed, near_packed, base = row_conv(0, 1, near_cap, on_halo, [])

    ids = jnp.clip(src_blocks - (tile - R) * atm_blk, 0, 3 * atm_blk - 1)
    surf_mixed, surf_normed, far_forcing, edge_mixed, edge_normed = pl.pallas_call(
        surface_kernel,
        in_specs=[smem] * 3 + [vmem] + [anywhere] * 2 + [vmem] * 4 + [hbm] * 3,
        out_specs=[whole_spec(1, inner + cols, width)] * 2 + [whole_spec(cols, width)] + [hbm] * 2,
        out_shape=[tok(1, inner + cols), tok(1, inner + cols), row_f32]
        + [tok(lev, 2 * cols)] * 2,
        scratch_shapes=[
            pltpu.VMEM((inner + cols, width), F32),
            pltpu.VMEM((3 * own, width), BF16),
            pltpu.VMEM((rows, cols, width), F32),
            dma((5,)),
        ],
        input_output_aliases={11: 3, 12: 4},
        compiler_params=params(12),
        cost_estimate=cost(conv_flops(1, inner), cells * width * 16),
        name="surface",
    )(
        ids,
        live,
        side,
        depth,
        on_halo,
        off_halo,
        atm_latent,
        remap_weight,
        qkv_weight,
        out_weight,
        stay(base),
        stay(edge_mixed),
        stay(edge_normed),
    )
    surf_others = exchange(surf_normed)
    near_others = exchange(near_packed)

    edge_mixed, edge_normed, far_packed = row_conv(
        1, 0, far_cap, off_halo, [far_forcing, edge_mixed, edge_normed]
    )
    far_others = exchange(far_packed)

    def unread(shape):
        return pl.pallas_call(
            lambda out_ref: None,
            out_specs=hbm,
            out_shape=pltpu.HBM(shape, BF16),
            name="unread",
        )()

    def send_all(*arrays):
        sizes = [x.shape[0] * x.shape[1] for x in arrays]
        joined = jnp.concatenate([x.reshape(-1, width) for x in arrays], axis=0)
        got = [[] for _ in arrays]
        for part in exchange(joined):
            at = 0
            for k, (x, size) in enumerate(zip(arrays, sizes)):
                got[k].append(part[at : at + size].reshape(x.shape))
                at += size
        return tuple(got)

    deep_whole, edge_whole = lax.cond(
        flag[0] > 0,
        send_all,
        lambda *a: tuple([unread(x.shape) for _ in range(members - 1)] for x in a),
        deep_normed,
        edge_normed,
    )
    shape = ocean_state.shape
    weights = (depth, qkv_weight, out_weight)
    out = attend(
        flag,
        side,
        [surf_normed, deep_normed],
        [surf_mixed, deep_mixed],
        surf_others,
        deep_others,
        deep_whole,
        *weights,
        None,
        shape,
    )
    return attend(
        flag,
        side,
        [edge_normed],
        [edge_mixed],
        surf_others,
        near_others + far_others,
        edge_whole,
        *weights,
        out,
        shape,
    )


def solution(mesh):
    return jax.shard_map(
        body,
        mesh=mesh,
        in_specs=(
            P("mem", "tile", None),
            P("mem", None, "tile", None),
            P("tile"),
            P("tile", None),
            P("tile"),
            P("tile", None, None, None),
            P(),
            P(),
            P(),
        ),
        out_specs=P("mem", None, "tile", None),
        check_vma=False,
    )
```

```python
import functools
import math

import jax
import jax.numpy as jnp
from jax import lax
from jax.experimental import pallas as pl
from jax.experimental.pallas import tpu as pltpu
from jax.sharding import PartitionSpec as P

HEADS = 4
R = 1
GROUP = 16
EPS = 1e-06
NEG = -1e30
F32 = jnp.float32
BF16 = jnp.bfloat16
MIB = 1024 * 1024


def params(mib, steps=0):
    return pltpu.CompilerParams(
        dimension_semantics=("arbitrary",) * steps if steps else None, vmem_limit_bytes=mib * MIB
    )


def cost(flops, nbytes):
    return pl.CostEstimate(flops=int(flops), bytes_accessed=int(nbytes), transcendentals=0)


def capacity(tokens, share):
    return -(-int(tokens * share) // 16) * 16


def row_plan(depth_row, lev):
    cols = depth_row.shape[1]
    level = lax.broadcasted_iota(jnp.int32, (lev, cols), 0).astype(F32)
    wet = (depth_row > level).astype(F32)
    upper = (
        lax.broadcasted_iota(jnp.int32, (cols, cols), 0)
        < lax.broadcasted_iota(jnp.int32, (cols, cols), 1)
    )
    upper = upper.astype(F32).astype(BF16)
    rank = jnp.dot(wet.astype(BF16), upper, preferred_element_type=F32)
    counts = [jnp.sum(wet[l : l + 1]).astype(jnp.int32) for l in range(lev)]
    return wet, rank, counts


def offsets(plans, first, lev):
    at, place = jnp.int32(0), {}
    for l in range(first, lev):
        for r, plan in enumerate(plans):
            place[l, r] = at
            at = at + plan[2][l]
    return place


def segment(wet, rank, offset, limit):
    cols = wet.shape[1]
    base = jnp.minimum((offset // 16) * 16, limit)
    target = jnp.where(wet > 0, rank + (offset - base).astype(F32), -1.0)
    slot = lax.broadcasted_iota(jnp.int32, (cols + 16, cols), 0).astype(F32)
    return pl.multiple_of(base, 16), (slot == target).astype(F32).astype(BF16)


def pack(buf_ref, wet, rank, offset, cap, tokens):
    base, hot = segment(wet, rank, offset, cap)
    rows = jnp.dot(hot, tokens, preferred_element_type=F32).astype(BF16)
    head = pl.ds(base, 16)
    buf_ref[head, :] = buf_ref[head, :] + rows[:16]
    buf_ref[pl.ds(pl.multiple_of(base + 16, 16), rows.shape[0] - 16), :] = rows[16:]


def unpack(rows_of, wet, rank, offset, limit):
    base, hot = segment(wet, rank, offset, limit)
    return lax.dot_general(
        hot, rows_of(base, hot.shape[0]), (((0,), (0,)), ((), ())), preferred_element_type=F32
    ).astype(BF16)


def column(depth_row):
    cols = depth_row.shape[1]
    return jnp.broadcast_to(depth_row, (cols, cols)).T


def widen(x, width):
    return jnp.concatenate([x] * (width // x.shape[1]), axis=1)


def stencil(taps, weight_ref, cols):
    count, width = taps[0].shape
    x = jnp.concatenate(taps, axis=1)
    sums = [
        jnp.dot(x, weight_ref[:, dc].reshape(3 * width, -1), preferred_element_type=F32)
        for dc in range(3)
    ]
    col = lax.broadcasted_iota(jnp.int32, (count, 1), 0) % cols
    left = jnp.where(col == 0, 0.0, pltpu.roll(sums[0], 1, axis=0))
    right = jnp.where(col == cols - 1, 0.0, pltpu.roll(sums[2], count - 1, axis=0))
    return sums[1] + left + right


def normalise(mixed):
    mf = mixed.astype(F32)
    mean = jnp.mean(mf * mf, axis=-1, keepdims=True)
    return (mf * lax.rsqrt(mean + EPS)).astype(BF16)


def prep_kernel(
    caps,
    side_ref,
    state_hbm,
    atm_hbm,
    depth_hbm,
    on_hbm,
    off_hbm,
    flag_ref,
    depth_ref,
    atm,
    rows_in,
    in_sem,
    out_sem,
    atm_sem,
    own_sem,
):
    _, lev, cells, width = state_hbm.shape
    rows, cols = depth_ref.shape
    own = atm_hbm.shape[1]
    sides = (on_hbm, off_hbm)
    load_depth = pltpu.make_async_copy(depth_hbm, depth_ref, own_sem.at[0])
    load_depth.start()
    loads, stores = [], []
    for k in (1, 0):
        at = pl.multiple_of(side_ref[k] * cols, cols)
        half = lev // 2
        for l in range(0, lev, half):
            load = pltpu.make_async_copy(
                state_hbm.at[0, pl.ds(l, half), pl.ds(at, cols)],
                rows_in.at[k, pl.ds(l, half)],
                in_sem.at[k, l],
            )
            load.start()
            loads.append((k, l, load))
    load_atm = pltpu.make_async_copy(atm_hbm.at[0], atm, own_sem.at[1])
    load_atm.start()
    load_depth.wait()
    d = depth_ref[...].astype(F32)
    pick = lambda k: jnp.where(side_ref[k] == 0, d[0:1], d[rows - 1 :])
    deep = [column(pick(k)) for k in range(2)]
    counts = [
        jnp.sum(jnp.maximum(d[1 : rows - 1] - 1.0, 0.0)),
        jnp.sum(jnp.maximum(pick(0) - 1.0, 0.0)),
        jnp.sum(pick(1)),
    ]
    over = jnp.int32(0)
    for count, cap in zip(counts, caps):
        over = over | (count > cap).astype(jnp.int32)
    flag_ref[0] = over
    for k, l, load in loads:
        load.wait()
        for level in range(l, l + half):
            wet = widen((deep[k] > level).astype(F32).astype(BF16), width)
            rows_in[k, level] = rows_in[k, level] * wet
            store = pltpu.make_async_copy(
                rows_in.at[k, level], sides[k].at[pl.ds(level * cols, cols)], out_sem.at[k, level]
            )
            store.start()
            stores.append(store)
    load_atm.wait()
    for k in (1, 0):
        store = pltpu.make_async_copy(
            atm, sides[k].at[pl.ds(lev * cols, own)], atm_sem.at[k]
        )
        store.start()
        stores.append(store)
    for store in stores:
        store.wait()


def inner_kernel(
    cap,
    state,
    depth_ref,
    weight_hbm,
    mixed_hbm,
    normed_hbm,
    packed_hbm,
    weight,
    mixed,
    normed,
    packed,
    weight_sem,
    out_sem,
    packed_sem,
):
    _, lev, cells, width = state.shape
    rows, cols = depth_ref.shape
    load = pltpu.make_async_copy(weight_hbm, weight, weight_sem)
    load.start()
    packed[...] = jnp.zeros_like(packed)
    d = depth_ref[...].astype(F32)
    plans = [row_plan(d[r : r + 1], lev) for r in range(1, rows - 1)]
    place = offsets(plans, 1, lev)
    deep = jnp.concatenate([column(d[r : r + 1]) for r in range(rows)], axis=0)
    count = cells - 2 * cols
    stores = []
    for l in range(1, lev):
        wet = (deep > l).astype(F32)
        x = state[0, l] * widen(wet.astype(BF16), width)
        taps = [x[dr * cols : dr * cols + count] for dr in range(3)]
        if l == 1:
            load.wait()
        total = stencil(taps, weight, cols)
        new = taps[1].astype(F32) + widen(wet[cols : cols + count], width) * total
        new = new.astype(BF16)
        mixed[l - 1] = new
        tokens = normalise(new)
        normed[l - 1] = tokens
        for k, (buf, out) in enumerate(((mixed, mixed_hbm), (normed, normed_hbm))):
            store = pltpu.make_async_copy(buf.at[l - 1], out.at[l - 1], out_sem.at[l - 1, k])
            store.start()
            stores.append(store)
        for r, plan in enumerate(plans):
            pack(
                packed,
                plan[0][l : l + 1],
                plan[1][l : l + 1],
                place[l, r],
                cap,
                tokens[r * cols : (r + 1) * cols],
            )
        if l == lev - 1:
            store = pltpu.make_async_copy(packed.at[pl.ds(0, cap)], packed_hbm, packed_sem)
            store.start()
            stores.append(store)
    for store in stores:
        store.wait()


def surface_kernel(
    ids_ref,
    live_ref,
    side_ref,
    depth_ref,
    on_hbm,
    off_hbm,
    atm_ref,
    remap,
    qkv_ref,
    wo_ref,
    base_hbm,
    edge_mixed_in,
    edge_normed_in,
    mixed_ref,
    normed_ref,
    far_ref,
    edge_mixed_hbm,
    edge_normed_hbm,
    base,
    window,
    forcing_ref,
    sem,
):
    rows, cols = depth_ref.shape
    _, own, width = atm_ref.shape
    blocks, pairs = remap.shape[0], remap.shape[1]
    on_at = jnp.where(side_ref[0] == 0, 0, 2 * own)
    copies = [
        pltpu.make_async_copy(
            on_hbm.at[pl.ds(on_hbm.shape[0] - own, own)],
            window.at[pl.ds(pl.multiple_of(on_at, own), own)],
            sem.at[0],
        ),
        pltpu.make_async_copy(
            off_hbm.at[pl.ds(off_hbm.shape[0] - own, own)],
            window.at[pl.ds(pl.multiple_of(2 * own - on_at, own), own)],
            sem.at[1],
        ),
        pltpu.make_async_copy(base_hbm, base, sem.at[4]),
    ]
    for copy in copies:
        copy.start()
    window[own : 2 * own] = atm_ref[0]
    d = depth_ref[...].astype(F32)
    near, far = side_ref[0], side_ref[1]
    rows_d = [d[r : r + 1] for r in range(1, rows - 1)]
    rows_d.append(jnp.where(near == 0, d[0:1], d[rows - 1 :]))
    wets = [widen((column(row) > 0).astype(F32), width) for row in rows_d]
    for copy in copies:
        copy.wait()
    for b in range(blocks):
        acc = jnp.zeros((cols, width), F32)
        for p in range(pairs):
            on = (p < live_ref[b]).astype(F32)
            start = pl.multiple_of(ids_ref[b, p] * cols, cols)
            acc = acc + on * jnp.dot(
                remap[b, p], window[pl.ds(start, cols), :], preferred_element_type=F32
            )
        forcing_ref[b] = acc
    for k, wet in enumerate(wets):
        at = slice(k * cols, (k + 1) * cols)
        forcing = forcing_ref[near] if k == rows - 2 else forcing_ref[k + 1]
        new = (base[at] + wet * forcing).astype(BF16)
        mixed_ref[0, at] = new
        normed_ref[0, at] = normalise(new)
    far_ref[...] = forcing_ref[far]
    at = pl.ds((rows - 2) * cols, cols)
    stores = [
        pltpu.make_async_copy(mixed_ref.at[0, at], edge_mixed_hbm.at[0, pl.ds(0, cols)], sem.at[2]),
        pltpu.make_async_copy(normed_ref.at[0, at], edge_normed_hbm.at[0, pl.ds(0, cols)], sem.at[3]),
    ]
    for store in stores:
        store.start()
    for store in stores:
        store.wait()


def row_kernel(cap, first, which, side_ref, state, depth_ref, weight_hbm, halo_hbm, *refs):
    refs = list(refs)
    forcing_hbm = None
    if not first:
        forcing_hbm = refs[0]
        refs = refs[3:]
    mixed_hbm, normed_hbm, packed_hbm = refs[:3]
    refs = refs[3:]
    base_ref = refs.pop(0) if first else None
    forcing_ref, weight, tap, mixed, normed, packed, weight_sem, halo_sem, out_sem, packed_sem = refs
    load = pltpu.make_async_copy(weight_hbm, weight, weight_sem)
    load.start()
    _, lev, cells, width = state.shape
    rows, cols = depth_ref.shape
    row = side_ref[which]
    top = row == 0
    beside = jnp.where(top, 1, rows - 2)
    outer = jnp.where(top, 0, 2)
    halo = pltpu.make_async_copy(
        halo_hbm.at[pl.ds(0, lev * cols)], tap.at[outer], halo_sem
    )
    halo.start()
    if not first:
        forcing = pltpu.make_async_copy(forcing_hbm, forcing_ref, packed_sem)
        forcing.start()
    packed[...] = jnp.zeros_like(packed)
    d = depth_ref[...].astype(F32)
    own_depth = jnp.where(top, d[0:1], d[rows - 1 :])
    plan = row_plan(own_depth, lev)
    place = offsets([plan], first, lev)
    deep = column(own_depth)
    deep_beside = column(jnp.where(top, d[1:2], d[rows - 2 : rows - 1]))
    at = pl.multiple_of(row * cols, cols)
    at_beside = pl.multiple_of(beside * cols, cols)
    wets = []
    for l in range(lev):
        rows_l = slice(l * cols, (l + 1) * cols)
        wet = (deep > l).astype(F32)
        wets.append(wet)
        wet_beside = (deep_beside > l).astype(F32)
        tap[1, rows_l] = state[0, l, pl.ds(at, cols)] * widen(wet.astype(BF16), width)
        tap[2 - outer, rows_l] = state[0, l, pl.ds(at_beside, cols)] * widen(
            wet_beside.astype(BF16), width
        )
    stores = []
    half = lev // 2
    load.wait()
    halo.wait()
    if not first:
        forcing.wait()
    for start in range(0, lev, half):
        rows_b = slice(start * cols, (start + half) * cols)
        taps = [tap[dr, rows_b] for dr in range(3)]
        total = stencil(taps, weight, cols)
        for k in range(half):
            l = start + k
            rows_k = slice(k * cols, (k + 1) * cols)
            part = total[rows_k]
            if l == 0 and not first:
                part = part + forcing_ref[...]
            new = taps[1][rows_k].astype(F32) + widen(wets[l], width) * part
            if l < first:
                base_ref[cells - 2 * cols :] = new
                continue
            new = new.astype(BF16)
            mixed[l - first] = new
            tokens = normalise(new)
            normed[l - first] = tokens
            pack(packed, plan[0][l : l + 1], plan[1][l : l + 1], place[l, 0], cap, tokens)
    if first:
        wet = (jnp.concatenate([column(d[r : r + 1]) for r in range(rows)], axis=0) > 0).astype(F32)
        x = state[0, 0] * widen(wet.astype(BF16), width)
        taps = [x[dr * cols : dr * cols + cells - 2 * cols] for dr in range(3)]
        inside = widen(wet[cols : cells - cols], width)
        base_ref[0 : cells - 2 * cols] = taps[1].astype(F32) + inside * stencil(taps, weight, cols)
    block = (pl.ds(first, lev - first), pl.ds(which * cols, cols))
    for k, (buf, out) in enumerate(((mixed, mixed_hbm), (normed, normed_hbm))):
        store = pltpu.make_async_copy(buf, out.at[block], out_sem.at[k])
        store.start()
        stores.append(store)
    store = pltpu.make_async_copy(packed.at[pl.ds(0, cap)], packed_hbm, packed_sem)
    store.start()
    stores.append(store)
    for store in stores:
        store.wait()


def attend_kernel(others, nparts, edges, flag_ref, side_ref, *refs):
    refs = list(refs)
    take = lambda k: [refs.pop(0) for _ in range(k)]
    own_normed = take(nparts)
    own_mixed = take(nparts)
    surf = take(others)
    packed = [take(others) for _ in range(1 + edges)]
    whole = take(others)
    depth_ref, qkv_ref, wo_ref = take(3)
    if edges:
        take(1)
    out_hbm, x_ref, mixed_ref, q_ref, k_ref, v_ref, att_ref, token_ref, new_ref = refs[:9]
    in_sem, out_sem, sem = refs[9:]
    steps, lev, count, width = q_ref.shape
    members = others + 1
    head = width // HEADS
    pair = 2 * head

    loads = []
    for kind, (parts, buf) in enumerate(((own_normed, x_ref), (own_mixed, mixed_ref))):
        for step in range(steps):
            at = 0
            for k, part in enumerate(parts):
                n = part.shape[0]
                load = pltpu.make_async_copy(
                    part.at[:, pl.ds(step * count, count)],
                    buf.at[step, pl.ds(at, n)],
                    in_sem.at[kind, step, k],
                )
                load.start()
                loads.append((kind, step, load))
                at += n

    def arrive(kind, step):
        for k, s, load in loads:
            if (k, s) == (kind, step):
                load.wait()

    d = depth_ref[...].astype(F32)
    last = d.shape[0] - 1
    if edges:
        rows_d = [jnp.where(side_ref[k] == 0, d[0:1], d[last:]) for k in range(2)]
    else:
        rows_d = [d[r : r + 1] for r in range(1, last)]
    plans = [row_plan(row, lev) for row in rows_d]
    if edges:
        near, far = offsets(plans[:1], 1, lev), offsets(plans[1:], 0, lev)
        place = [{l: at for (l, _), at in p.items()} for p in (near, far)]
    else:
        both = offsets(plans, 1, lev)
        place = [{l: both[l, step] for l in range(1, lev)} for step in range(steps)]

    def project(x, step, m):
        rows = slice(m * lev, (m + 1) * lev)
        kv = jnp.dot(x, qkv_ref[:, width:], preferred_element_type=F32).astype(BF16)
        k_ref[step, rows] = kv[:, :width].reshape(lev, count, width)
        v_ref[step, rows] = kv[:, width:].reshape(lev, count, width)

    for o in range(others):
        for step in range(steps):
            source = packed[step if edges else 0][o]
            window = lambda base, size: source[pl.ds(base, size), :]
            limit = source.shape[0] - count - 16
            wet, rank, _ = plans[step]
            if 0 not in place[step]:
                at = surf[o].shape[1] - count if edges else step * count
                token_ref[step, 0] = surf[o][0, at : at + count]
            for l, at in place[step].items():
                token_ref[step, l] = unpack(window, wet[l : l + 1], rank[l : l + 1], at, limit)

        @pl.when(flag_ref[0] != 0)
        def _():
            first = lev - whole[o].shape[0]
            for step in range(steps):
                copy = pltpu.make_async_copy(
                    whole[o].at[:, pl.ds(step * count, count)],
                    token_ref.at[step, pl.ds(first, lev - first)],
                    sem,
                )
                copy.start()
                copy.wait()

        for step in range(steps):
            project(token_ref[step].reshape(-1, width), step, o + 1)

    nq, nk = lev * GROUP, members * lev * GROUP
    groups = count // GROUP
    lanes_n = lev * GROUP
    cell = lax.broadcasted_iota(jnp.int32, (groups, count), 1)
    mine = (cell // GROUP == lax.broadcasted_iota(jnp.int32, (groups, count), 0)).astype(F32)
    spread = lax.broadcasted_iota(jnp.int32, (count, lanes_n), 0) % GROUP
    spread = (spread == lax.broadcasted_iota(jnp.int32, (count, lanes_n), 1) % GROUP).astype(F32)
    key_level = lax.broadcasted_iota(jnp.int32, (groups, lanes_n), 1) // GROUP
    qc = lax.broadcasted_iota(jnp.int32, (nq, nk), 0) % GROUP
    kc = lax.broadcasted_iota(jnp.int32, (nq, nk), 1) % GROUP
    same = jnp.where(qc == kc, 0.0, NEG)
    lane = lax.broadcasted_iota(jnp.int32, (1, width), 1)
    scale = 1.0 / math.sqrt(head)
    masks = [jnp.where(lane // head == h, scale, 0.0).astype(BF16) for h in range(HEADS)]
    stores = []
    for step in range(steps):
        arrive(0, step)
        x = x_ref[step].reshape(-1, width)
        q = jnp.dot(x, qkv_ref[:, 0:width], preferred_element_type=F32).astype(BF16)
        q_ref[step] = q.reshape(lev, count, width)
        project(x, step, 0)
        key_depth = jnp.dot(
            (mine * rows_d[step]).astype(BF16), spread.astype(BF16), preferred_element_type=F32
        )
        key_bias = jnp.where(key_depth > key_level.astype(F32), 0.0, NEG)
        for g in range(groups):
            cells = slice(g * GROUP, (g + 1) * GROUP)
            bias = same + jnp.concatenate([key_bias[g : g + 1]] * members, axis=1)
            bias = jnp.concatenate([bias] * HEADS, axis=0)
            q = q_ref[step, :, cells].reshape(nq, width)
            q = jnp.concatenate([q * mask for mask in masks], axis=0)
            k = k_ref[step, :, cells].reshape(nk, width)
            v = v_ref[step, :, cells].reshape(nk, width)
            s = lax.dot_general(q, k, (((1,), (1,)), ((), ())), preferred_element_type=F32) + bias
            p = jnp.exp(s - jnp.max(s, axis=-1, keepdims=True))
            norm = 1.0 / jnp.sum(p, axis=-1, keepdims=True)
            p = p.astype(BF16)
            for h in range(HEADS // 2):
                lanes = slice(h * pair, (h + 1) * pair)
                rows = slice(h * 2 * nq, (h + 1) * 2 * nq)
                o = jnp.dot(p[rows], v[:, lanes], preferred_element_type=F32) * norm[rows]
                o = jnp.where(lane[:, :pair] < head, o[:nq], o[nq:])
                att_ref[step, :, cells, lanes] = o.astype(BF16).reshape(lev, GROUP, pair)
        proj = jnp.dot(
            att_ref[step].reshape(-1, width), wo_ref[...], preferred_element_type=F32
        )
        arrive(1, step)
        deep = column(rows_d[step])
        row = side_ref[step] if edges else step + 1
        for l in range(lev):
            rows = slice(l * count, (l + 1) * count)
            wet = widen((deep > l).astype(F32), width)
            new_ref[step, l] = (mixed_ref[step, l].astype(F32) + wet * proj[rows]).astype(BF16)
        at = pl.multiple_of(row * count, count)
        store = pltpu.make_async_copy(
            new_ref.at[step], out_hbm.at[0, :, pl.ds(at, count)], out_sem.at[step]
        )
        store.start()
        stores.append(store)
    for store in stores:
        store.wait()


def attend(
    flag, side, normed, mixed, surf, packed, whole, depth, qkv_weight, out_weight, out, shape
):
    edges = out is not None
    others, nparts = len(whole), len(mixed)
    lev = sum(p.shape[0] for p in mixed)
    width = shape[-1]
    cols = depth.shape[1]
    members = others + 1
    hbm = pl.BlockSpec(memory_space=pltpu.HBM)
    vmem = pl.BlockSpec(memory_space=pltpu.VMEM)
    smem = pl.BlockSpec(memory_space=pltpu.SMEM)
    stay = lambda x: pltpu.with_memory_space_constraint(x, pltpu.HBM)
    in_specs = [smem] * 2 + [hbm] * (2 * nparts) + [vmem] * (len(surf) + len(packed))
    in_specs += [hbm] * others + [vmem] * 3
    args = [flag, side] + [stay(x) for x in normed + mixed] + surf + packed
    args += [stay(x) for x in whole] + [depth, qkv_weight, out_weight]
    alias = {}
    if edges:
        in_specs.append(hbm)
        alias = {len(args): 0}
        args.append(stay(out))
    tokens = lev * cols * 2
    rows = pltpu.VMEM((2, lev, cols, width), BF16)
    keys = pltpu.VMEM((2, members * lev, cols, width), BF16)
    return pl.pallas_call(
        functools.partial(attend_kernel, others, nparts, edges),
        in_specs=in_specs,
        out_specs=hbm,
        scratch_shapes=[
            rows,
            rows,
            rows,
            keys,
            keys,
            rows,
            rows,
            rows,
            pltpu.SemaphoreType.DMA((2, 2, nparts)),
            pltpu.SemaphoreType.DMA((2,)),
            pltpu.SemaphoreType.DMA,
        ],
        out_shape=pltpu.HBM(shape, BF16),
        input_output_aliases=alias,
        compiler_params=params(24 if members <= 2 else 56),
        cost_estimate=cost(tokens * width * width * 8 * (members + 2), tokens * width * 2 * 5),
        name="attend",
    )(*args)


def body(
    atm_latent,
    ocean_state,
    depth,
    src_blocks,
    live,
    remap_weight,
    conv_weight,
    qkv_weight,
    out_weight,
):
    _, lev, cells, width = ocean_state.shape
    cols = remap_weight.shape[2]
    rows = cells // cols
    inner = cells - 2 * cols
    own = atm_latent.shape[1]
    atm_blk = own // cols
    tiles = lax.axis_size("tile")
    members = lax.axis_size("mem")
    tile = lax.axis_index("tile")

    def swap(x, first):
        pairs = [(i, i + 1) for i in range(first, tiles - 1, 2)]
        return lax.ppermute(x, "tile", pairs + [(b, a) for a, b in pairs])

    def exchange(x):
        return [
            lax.ppermute(x, "mem", [(i, (i + k) % members) for i in range(members)])
            for k in range(1, members)
        ]

    odd = tile % 2
    side = jnp.stack([(1 - odd) * (rows - 1), odd * (rows - 1)]).astype(jnp.int32)
    depth = depth.reshape(rows, cols)
    deep_cap = capacity((lev - 1) * inner, 0.5625)
    near_cap = capacity((lev - 1) * cols, 0.605)
    far_cap = capacity(lev * cols, 0.65625)

    hbm = pl.BlockSpec(memory_space=pltpu.HBM)
    anywhere = pl.BlockSpec(memory_space=pl.ANY)
    vmem = pl.BlockSpec(memory_space=pltpu.VMEM)
    smem = pl.BlockSpec(memory_space=pltpu.SMEM)
    tok = lambda *s: pltpu.HBM((*s, width), BF16)
    stay = lambda x: pltpu.with_memory_space_constraint(x, pltpu.HBM)
    conv_flops = lambda n, c: 2 * 9 * n * c * width * width
    dma = pltpu.SemaphoreType.DMA
    slack = cols + 16
    message = lev * cols + own
    on_msg, off_msg, flag = pl.pallas_call(
        functools.partial(prep_kernel, (deep_cap, near_cap, far_cap)),
        in_specs=[smem, hbm, hbm, hbm],
        out_specs=[hbm, hbm, smem],
        out_shape=[tok(message), tok(message), jax.ShapeDtypeStruct((1,), jnp.int32)],
        scratch_shapes=[
            pltpu.VMEM((rows, cols), jnp.int32),
            pltpu.VMEM((own, width), BF16),
            pltpu.VMEM((2, lev, cols, width), BF16),
            dma((2, lev)),
            dma((2, lev)),
            dma((2,)),
            dma((2,)),
        ],
        compiler_params=params(16),
        cost_estimate=cost(lev * cols * width * 4, lev * cols * width * 10),
        name="prep",
    )(side, stay(ocean_state), stay(atm_latent), stay(depth))
    off_halo = swap(off_msg, 1)
    on_halo = swap(on_msg, 0)

    deep_mixed, deep_normed, deep_packed = pl.pallas_call(
        functools.partial(inner_kernel, deep_cap),
        in_specs=[vmem, vmem, hbm],
        out_specs=[hbm] * 3,
        out_shape=[tok(lev - 1, inner), tok(lev - 1, inner), tok(deep_cap)],
        scratch_shapes=[
            pltpu.VMEM(conv_weight.shape, BF16),
            pltpu.VMEM((lev - 1, inner, width), BF16),
            pltpu.VMEM((lev - 1, inner, width), BF16),
            pltpu.VMEM((deep_cap + slack, width), BF16),
            dma,
            dma((lev - 1, 2)),
            dma,
        ],
        compiler_params=params(12),
        cost_estimate=cost(conv_flops(lev, inner), lev * inner * width * 8),
        name="inner",
    )(ocean_state, depth, stay(conv_weight))
    deep_others = exchange(deep_packed)

    whole_spec = lambda *sh: pl.BlockSpec(sh, lambda *_: (0,) * len(sh))
    row_f32 = pltpu.HBM((cols, width), F32)

    def row_conv(which, first, cap, halo, extra):
        n = lev - first
        base = pltpu.HBM((inner + cols, width), F32)
        return pl.pallas_call(
            functools.partial(row_kernel, cap, first, which),
            in_specs=[smem, vmem, vmem, hbm, anywhere] + [hbm] * len(extra),
            out_specs=[hbm] * 3 + [whole_spec(inner + cols, width)] * first,
            out_shape=[tok(lev, 2 * cols), tok(lev, 2 * cols), tok(cap)] + [base] * first,
            scratch_shapes=[
                pltpu.VMEM((cols, width), F32),
                pltpu.VMEM(conv_weight.shape, BF16),
                pltpu.VMEM((3, lev * cols, width), BF16),
                pltpu.VMEM((n, cols, width), BF16),
                pltpu.VMEM((n, cols, width), BF16),
                pltpu.VMEM((cap + slack, width), BF16),
                dma,
                dma,
                dma((2,)),
                dma,
            ],
            input_output_aliases={6: 0, 7: 1} if extra else {},
            compiler_params=params(12),
            cost_estimate=cost(conv_flops(lev, cols), lev * cols * width * 16),
            name="row",
        )(side, ocean_state, depth, stay(conv_weight), halo, *[stay(x) for x in extra])

    edge_mixed, edge_normed, near_packed, base = row_conv(0, 1, near_cap, on_halo, [])

    ids = jnp.clip(src_blocks - (tile - R) * atm_blk, 0, 3 * atm_blk - 1)
    surf_mixed, surf_normed, far_forcing, edge_mixed, edge_normed = pl.pallas_call(
        surface_kernel,
        in_specs=[smem] * 3 + [vmem] + [anywhere] * 2 + [vmem] * 4 + [hbm] * 3,
        out_specs=[whole_spec(1, inner + cols, width)] * 2 + [whole_spec(cols, width)] + [hbm] * 2,
        out_shape=[tok(1, inner + cols), tok(1, inner + cols), row_f32]
        + [tok(lev, 2 * cols)] * 2,
        scratch_shapes=[
            pltpu.VMEM((inner + cols, width), F32),
            pltpu.VMEM((3 * own, width), BF16),
            pltpu.VMEM((rows, cols, width), F32),
            dma((5,)),
        ],
        input_output_aliases={11: 3, 12: 4},
        compiler_params=params(12),
        cost_estimate=cost(conv_flops(1, inner), cells * width * 16),
        name="surface",
    )(
        ids,
        live,
        side,
        depth,
        on_halo,
        off_halo,
        atm_latent,
        remap_weight,
        qkv_weight,
        out_weight,
        stay(base),
        stay(edge_mixed),
        stay(edge_normed),
    )
    surf_others = exchange(surf_normed)
    near_others = exchange(near_packed)

    edge_mixed, edge_normed, far_packed = row_conv(
        1, 0, far_cap, off_halo, [far_forcing, edge_mixed, edge_normed]
    )
    far_others = exchange(far_packed)

    def unread(shape):
        return pl.pallas_call(
            lambda out_ref: None,
            out_specs=hbm,
            out_shape=pltpu.HBM(shape, BF16),
            name="unread",
        )()

    def send_all(*arrays):
        sizes = [x.shape[0] * x.shape[1] for x in arrays]
        joined = jnp.concatenate([x.reshape(-1, width) for x in arrays], axis=0)
        got = [[] for _ in arrays]
        for part in exchange(joined):
            at = 0
            for k, (x, size) in enumerate(zip(arrays, sizes)):
                got[k].append(part[at : at + size].reshape(x.shape))
                at += size
        return tuple(got)

    deep_whole, edge_whole = lax.cond(
        flag[0] > 0,
        send_all,
        lambda *a: tuple([unread(x.shape) for _ in range(members - 1)] for x in a),
        deep_normed,
        edge_normed,
    )
    shape = ocean_state.shape
    weights = (depth, qkv_weight, out_weight)
    out = attend(
        flag,
        side,
        [surf_normed, deep_normed],
        [surf_mixed, deep_mixed],
        surf_others,
        deep_others,
        deep_whole,
        *weights,
        None,
        shape,
    )
    return attend(
        flag,
        side,
        [edge_normed],
        [edge_mixed],
        surf_others,
        near_others + far_others,
        edge_whole,
        *weights,
        out,
        shape,
    )


def solution(mesh):
    return jax.shard_map(
        body,
        mesh=mesh,
        in_specs=(
            P("mem", "tile", None),
            P("mem", None, "tile", None),
            P("tile"),
            P("tile", None),
            P("tile"),
            P("tile", None, None, None),
            P(),
            P(),
            P(),
        ),
        out_specs=P("mem", None, "tile", None),
        check_vma=False,
    )
```
